32 devices in a mesh: ctx: 8 (over z, core), shard: 4 (over y, x).
Axes of the slice: x: 2, y: 2, z: 4, core: 2. Of those that a mesh axis runs over, the one named last changes fastest.
Arguments:
- tokens: bfloat16 [4, 2048, 2048], P('shard', 'ctx'), may hold values from -6 to 6
- doc_ids: int32 [4, 2048], P('shard', 'ctx'), may hold values from 0 to 7, never falling along the last dimension, each value on 1 to 1024 neighbouring positions
- routes: int32 [4, 2048, 8], P('shard', 'ctx'), may hold values from 0 to 15, all different within a row; in each aligned block of 256 rows (0 to 255, 256 to 511, ..., all dimensions but the last counted through in order) at most 256 rows name the same one
- attn_gain: bfloat16 [2048], P(('ctx', 'shard')), may hold values from 0.099609375 to 1.8984375
- w_query: bfloat16 [2048, 2048], P(('ctx', 'shard')), may hold values from -0.125 to 0.125
- w_key: bfloat16 [2048, 2048], P(('ctx', 'shard')), may hold values from -0.125 to 0.125
- w_value: bfloat16 [2048, 2048], P(('ctx', 'shard')), may hold values from -0.125 to 0.125
- query_gain: bfloat16 [2048], P(('ctx', 'shard')), may hold values from 0.7 to 3.8, as said below
- key_gain: bfloat16 [2048], P(('ctx', 'shard')), may hold values from 0.099609375 to 1.8984375
- w_out: bfloat16 [2048, 2048], P(('ctx', 'shard')), may hold values from -3 to 3
- ffn_gain: bfloat16 [2048], P(('ctx', 'shard')), may hold values from 0.099609375 to 1.8984375
- w_router: bfloat16 [2048, 16], P(('ctx', 'shard')), may hold values from -0.0625 to 0.0625
- w_gate: bfloat16 [16, 2048, 1024], P('shard', 'ctx'), may hold values from -0.125 to 0.125
- w_up: bfloat16 [16, 2048, 1024], P('shard', 'ctx'), may hold values from -0.125 to 0.125
- w_down: bfloat16 [16, 1024, 2048], P('shard', None, 'ctx'), may hold values from -1 to 1
- clip_threshold: float32 [], replicated, may hold values from 0.1 to 1
- cotangent: bfloat16 [4, 2048, 2048], P('shard', 'ctx'), may hold values from -6 to 6
Outputs:
- output: bfloat16 [4, 2048, 2048], P('shard', 'ctx')
- input_grad: float32 [4, 2048, 2048], P('shard', 'ctx')
- attn_gain_grad: float32 [2048], P(('ctx', 'shard'))
- w_query_grad: float32 [2048, 2048], P(('ctx', 'shard'))
- w_key_grad: float32 [2048, 2048], P(('ctx', 'shard'))
- w_value_grad: float32 [2048, 2048], P(('ctx', 'shard'))
- query_gain_grad: float32 [2048], P(('ctx', 'shard'))
- key_gain_grad: float32 [2048], P(('ctx', 'shard'))
- w_out_grad: float32 [2048, 2048], P(('ctx', 'shard'))
- ffn_gain_grad: float32 [2048], P(('ctx', 'shard'))
- w_router_grad: float32 [2048, 16], P(('ctx', 'shard'))
- w_gate_grad: float32 [16, 2048, 1024], P('shard', 'ctx')
- w_up_grad: float32 [16, 2048, 1024], P('shard', 'ctx')
- w_down_grad: float32 [16, 1024, 2048], P('shard', None, 'ctx')
- query_clipped: bfloat16 [2048, 2048], P(('ctx', 'shard'))
- key_clipped: bfloat16 [2048, 2048], P(('ctx', 'shard'))
- clip_factors: float32 [16], replicated
The draws below stay inside these ranges and needn't reach their ends.
Inputs may be any that keep to these rules, and one draw needn't show every extreme that they name: `routes`: each token names 8 different experts. In each aligned block of 256 tokens of a sequence (the tokens of one device) no expert is named more than 256 times, and in some blocks one is named exactly 256 times. `doc_ids`: document numbers never fall along a sequence; a document has at most 1024 tokens, and in each sequence one has exactly that many. `query_gain`: Positive.
All inputs are finite; a program needn't handle non-finite values.
Results may differ from the reference program's by a relative error of at most 0.02.
The reference program's roundings to bfloat16 on the way count: a program that leaves them out, or rounds other values in their place, can miss the bound.
Values may be sent and summed in bfloat16 or wider, within the bound.
A program may use at most 384 MiB of HBM per device.

```python
import math
import jax
import jax.numpy as jnp
import numpy as np
from jax import lax

D = 2048
HEADS = 16
HEAD = 128
FF = 1024
TOP = 8
SEQ_LEN = 2048
DOCS = 8
EXPERTS = 16
SEQS = 4
CTX_TOK = 256
CAP = 256


def draw_query_gain(key, part):
    order_key = jax.random.fold_in(key, 11)
    column_key = jax.random.fold_in(key, 12)
    order = jax.random.permutation(order_key, HEADS).astype(jnp.float32)
    head_scale = 3.0 ** (order / max(HEADS - 1, 1))
    column = 1.0 + 0.1 * jnp.clip(jax.random.normal(column_key, (D,), jnp.float32), -2.5, 2.5)
    return (jnp.repeat(head_scale, HEAD) * column).astype(jnp.bfloat16)


def block_levels(own_key, extent, cuts, low, high):
    loudness, own = 1.0, jax.random.fold_in(own_key, 6)
    for position, blocks in cuts:
        steps = jnp.exp(jax.random.uniform(jax.random.fold_in(own, position), (blocks,), jnp.float32, low / len(cuts), high / len(cuts)))
        loudness = loudness * jnp.repeat(steps, extent[position] // blocks).reshape([-1 if axis == position else 1 for axis in range(len(extent))])
    return loudness


def split_up(count, total, bound, lean):
    portions = [(1 << 20) // math.isqrt(grade ** lean) + 1 for grade in range(2, count + 1)]
    surplus, holding = total - bound - (count - 1), [1] * (count - 1)
    while surplus > 0:
        free = [i for i in range(count - 1) if holding[i] < bound]
        pool, budget = sum([portions[i] for i in free]), surplus
        for i in free:
            addition = min(bound - holding[i], max(1, budget * portions[i] // pool), surplus)
            holding[i] = holding[i] + addition
            surplus = surplus - addition
    return np.array([bound] + holding)


def uneven(key, number_of, total, reach, skew):
    if number_of == 2:
        one = jax.random.randint(key, (), max(1, total - reach), min(reach, total - 1) + 1)
        return jnp.stack([one, total - one])
    tallies = jnp.asarray(split_up(number_of, total, reach, skew), jnp.int32)
    pairs = (number_of - 1) // 2
    source_of, receiver = tallies[1:1 + 2 * pairs:2], tallies[2:2 + 2 * pairs:2]
    slack = jnp.minimum(source_of - 1, reach - receiver)
    passed = jax.random.randint(jax.random.fold_in(key, 1), (pairs,), 0, 1 << 20) % (slack + 1)
    tallies = tallies.at[1:1 + 2 * pairs:2].set(source_of - passed).at[2:2 + 2 * pairs:2].set(receiver + passed)
    return tallies[jax.random.permutation(jax.random.fold_in(key, 2), number_of)]


def shared_out(key, own, number, rows, number_of, top, bound, skew):
    ranking = jax.random.permutation(key, number_of)
    heavy_load, ordinary = shares(number_of, rows * top, bound, skew, True), shares(number_of, rows * top, bound, skew, False)
    places = jnp.arange(number_of)

    def named(sizes, offset_by):
        used = int((sizes > 0).sum())
        fixed = max(1, used // 4)
        shifted = fixed + (places - fixed + offset_by * (used - fixed)) % max(1, number_of - fixed)
        return jnp.zeros((number_of,), jnp.int32).at[ranking[jnp.where(places < fixed, places, shifted)]].set(jnp.asarray(sizes, jnp.int32))

    sizes = jnp.where(number % 4 == 0, named(heavy_load, number // 4), named(ordinary, number - number // 4 - 1))
    mixed = jax.random.permutation(jax.random.fold_in(own, 3), number_of)
    donor, receiver = mixed[0:number_of // 2 * 2:2], mixed[1:number_of // 2 * 2:2]
    room = jnp.minimum(sizes[donor] - 1, bound - sizes[receiver]) // 2
    room = jnp.where((donor == ranking[0]) | (receiver == ranking[0]) | (sizes[receiver] == 0), 0, jnp.maximum(room, 0))
    shifted = jax.random.randint(jax.random.fold_in(own, 4), (number_of // 2,), 0, 1 << 20) % (room + 1)
    sizes = sizes.at[donor].add(-shifted).at[receiver].add(shifted)
    items = jnp.searchsorted(jnp.cumsum(sizes), jnp.arange(rows * top), side="right").astype(jnp.int32)
    table = items.reshape(top, rows).T
    table = table[jax.random.permutation(jax.random.fold_in(own, 1), rows)]
    offset_by = jax.random.randint(jax.random.fold_in(own, 2), (rows, 1), 0, top)
    return jnp.take_along_axis(table, (jnp.arange(top)[None, :] + offset_by) % top, axis=1)


def shares(count, total, most, skew, full):
    loads = [(1 << 20) // math.isqrt(grade ** skew) + 1 for grade in range(1, count + 1)]
    largest = most if full else min(most, max(-(-total // count), total * loads[0] // sum(loads)))
    least = 1 if total - largest >= count - 1 else 0
    given, surplus = [largest] + [least] * (count - 1), total - largest - least * (count - 1)
    while surplus > 0:
        candidates = [i for i in range(1, count) if given[i] < largest] or [i for i in range(1, count) if given[i] < most]
        whole, remaining = sum([loads[i] for i in candidates]), surplus
        for i in candidates:
            extra = min(most - given[i], max(1, remaining * loads[i] // whole), surplus)
            given[i] = given[i] + extra
            surplus = surplus - extra
    return np.array(given)


def noise(own_key, shape, deviation, limit, shards=(), kind=jnp.bfloat16):
    factor_of = block_levels(own_key, shape, shards, -0.22, 0.18) if shards else 1.0
    array = jax.random.normal(own_key, shape, jnp.float32) * deviation * factor_of
    return jnp.minimum(jnp.maximum(array, -limit), limit).astype(kind)


def setup_inputs(seed: int = 0) -> dict:
    arg_keys = jax.random.split(jax.random.key(seed), 18)
    tokens = noise(arg_keys[0], (SEQS, SEQ_LEN, D), 1.0, 6.0, ((0, 4), (1, 8)))
    doc_ids = jax.vmap(lambda own: jnp.searchsorted(jnp.cumsum(uneven(own, DOCS, SEQ_LEN, SEQ_LEN // 2, 2)), jnp.arange(SEQ_LEN), side="right"))(jax.random.split(arg_keys[1], SEQS)).reshape((SEQS, SEQ_LEN)).astype(jnp.int32)
    routes_keys = jax.random.split(jax.random.fold_in(arg_keys[2], 1), SEQS * SEQ_LEN // CTX_TOK)
    routes_turns = jax.random.permutation(jax.random.fold_in(arg_keys[2], 3), SEQS * SEQ_LEN // CTX_TOK)
    routes = jax.vmap(lambda own, number: shared_out(jax.random.fold_in(arg_keys[2], 2), own, number, CTX_TOK, EXPERTS, TOP, CAP, 1))(routes_keys, routes_turns).reshape((SEQS, SEQ_LEN, TOP))
    attn_gain = jnp.clip(1.0 + 0.18 * jax.random.normal(arg_keys[3], (D,), jnp.float32), 0.099609375, 1.8984375).astype(jnp.bfloat16)
    w_query = noise(arg_keys[4], (D, D), D ** -0.5, 0.125, ((0, 32),))
    w_key = noise(arg_keys[5], (D, D), D ** -0.5, 0.125, ((0, 32),))
    w_value = noise(arg_keys[6], (D, D), D ** -0.5, 0.125, ((0, 32),))
    query_gain = draw_query_gain(jax.random.fold_in(arg_keys[17], 71), 0)
    key_gain = jnp.clip(1.0 + 0.18 * jax.random.normal(arg_keys[8], (D,), jnp.float32), 0.099609375, 1.8984375).astype(jnp.bfloat16)
    w_out = noise(arg_keys[9], (D, D), (max(D // 512, 1)) ** -0.5, 3.0, ((0, 32),))
    ffn_gain = jnp.clip(1.0 + 0.18 * jax.random.normal(arg_keys[10], (D,), jnp.float32), 0.099609375, 1.8984375).astype(jnp.bfloat16)
    w_router = noise(arg_keys[11], (D, EXPERTS), (4 * D) ** -0.5, 0.0625, ((0, 32),))
    w_gate = noise(arg_keys[12], (EXPERTS, D, FF), D ** -0.5, 0.125, ((0, 4), (1, 8)))
    w_up = noise(arg_keys[13], (EXPERTS, D, FF), D ** -0.5, 0.125, ((0, 4), (1, 8)))
    w_down = noise(arg_keys[14], (EXPERTS, FF, D), (max(FF // 32, 1)) ** -0.5, 1.0, ((0, 4), (2, 8)))
    clip_threshold = jnp.clip(jnp.exp(jax.random.uniform(arg_keys[15], (), jnp.float32, math.log(0.1), math.log(1.0))), 0.1, 1.0)
    cotangent = noise(arg_keys[16], (SEQS, SEQ_LEN, D), 1.0, 6.0, ((0, 4), (1, 8)))
    return dict(tokens=tokens, doc_ids=doc_ids, routes=routes, attn_gain=attn_gain, w_query=w_query, w_key=w_key, w_value=w_value, query_gain=query_gain, key_gain=key_gain, w_out=w_out, ffn_gain=ffn_gain, w_router=w_router, w_gate=w_gate, w_up=w_up, w_down=w_down, clip_threshold=clip_threshold, cotangent=cotangent)


norm_eps = 1e-06
rope_base = 10000.0
highest = lax.Precision.HIGHEST

@jax.custom_vjp
def low(v):
    return lax.optimization_barrier(v.astype(jnp.bfloat16)).astype(jnp.float32)

@jax.custom_vjp
def low_back(v):
    return v

def low_keep(v):
    return (low(v), None)

def low_pass(kept, grad):
    return (grad,)

def back_keep(v):
    return (v, None)

def back_low(kept, grad):
    return (low(grad),)
low.defvjp(low_keep, low_pass)
low_back.defvjp(back_keep, back_low)

def matmul(left_op, right_op):
    return jnp.dot(left_op, right_op, precision=highest, preferred_element_type=jnp.float32)

def rms_scale(values, gain_vec):
    inverse = lax.rsqrt(lax.optimization_barrier(jnp.mean(values * values, axis=-1, keepdims=True)) + norm_eps)
    return values * inverse * gain_vec

def rotary(values, positions, head_count):
    row_count, model_width = values.shape
    half_size = model_width // head_count // 2
    inverse_freq = rope_base ** (-jnp.arange(half_size).astype(jnp.float32) / half_size)
    angles = positions.astype(jnp.float32)[:, None] * inverse_freq[None, :]
    cosine = jnp.cos(angles)[:, None, :]
    sine_vals = jnp.sin(angles)[:, None, :]
    paired = values.reshape(row_count, head_count, 2, half_size)
    first_half = paired[:, :, 0, :]
    second_half = paired[:, :, 1, :]
    turned = jnp.stack([first_half * cosine - second_half * sine_vals, second_half * cosine + first_half * sine_vals], axis=2)
    return turned.reshape(row_count, model_width)

def layer_sequence(params, tokens_seq, docs_seq, routes_seq):
    attn_gain, w_query, w_key, w_value, query_gain, key_gain, w_out, ffn_gain, w_router, w_gate, w_up, w_down = params
    seq_rows, model_width = tokens_seq.shape
    positions = jnp.arange(seq_rows).astype(jnp.int32)
    scale_qk = HEAD ** (-0.5)
    normed_one = low(rms_scale(tokens_seq, attn_gain))
    queries = low_back(matmul(normed_one, w_query))
    keys_lin = low_back(matmul(normed_one, w_key))
    values_b = low(low_back(matmul(normed_one, w_value)))
    queries_r = low(rotary(rms_scale(queries, query_gain), positions, HEADS))
    keys_r = low(rotary(rms_scale(keys_lin, key_gain), positions, HEADS))
    same_doc = docs_seq[:, None] == docs_seq[None, :]

    def one_head(head_idx):
        col_start = head_idx * HEAD
        query_h = lax.dynamic_slice_in_dim(queries_r, col_start, HEAD, 1)
        key_h = lax.dynamic_slice_in_dim(keys_r, col_start, HEAD, 1)
        value_h = lax.dynamic_slice_in_dim(values_b, col_start, HEAD, 1)
        scores = low_back(scale_qk * matmul(query_h, key_h.T))
        masked = jnp.where(same_doc, scores, -1e+30)
        row_top = lax.optimization_barrier(jnp.max(masked, axis=1, keepdims=True))
        weights = jnp.exp(masked - row_top)
        row_total = lax.optimization_barrier(jnp.sum(weights, axis=1, keepdims=True))
        prob_vals = low(weights / row_total)
        return (matmul(prob_vals, value_h), jnp.max(row_top))
    mixed_heads, head_peaks = lax.map(jax.checkpoint(one_head), jnp.arange(HEADS).astype(jnp.int32))
    mixed_all = low(low_back(mixed_heads.transpose(1, 0, 2).reshape(seq_rows, model_width)))
    after_attn = tokens_seq + low_back(matmul(mixed_all, w_out))
    normed_two = low(rms_scale(after_attn, ffn_gain))
    logits = low_back(matmul(normed_two, w_router))
    logit_top = lax.optimization_barrier(jnp.max(logits, axis=1, keepdims=True))
    logit_exp = jnp.exp(logits - logit_top)
    router_probs = logit_exp / lax.optimization_barrier(jnp.sum(logit_exp, axis=1, keepdims=True))
    chosen = (routes_seq[:, :, None] == jnp.arange(EXPERTS).astype(jnp.int32)[None, None, :]).astype(jnp.float32)
    selected = lax.optimization_barrier(jnp.sum(router_probs[:, None, :] * chosen, axis=2))
    gate_vals = selected / lax.optimization_barrier(jnp.sum(selected, axis=1, keepdims=True))
    per_expert = lax.optimization_barrier(jnp.sum(gate_vals[:, :, None] * chosen, axis=1))

    def expert_step(total_moe, expert_item):
        gate_w, up_w, down_w, weight_col = expert_item
        expert_in = low_back(normed_two)
        gate_h = low_back(matmul(expert_in, gate_w))
        up_h = low_back(matmul(expert_in, up_w))
        act_vals = low(gate_h * jax.nn.sigmoid(gate_h) * up_h)
        result = low(low_back(matmul(act_vals, down_w)))
        return (total_moe + weight_col[:, None] * result, None)
    moe_sum, _ = lax.scan(jax.checkpoint(expert_step), jnp.zeros((seq_rows, model_width), jnp.float32), (w_gate, w_up, w_down, per_expert.T))
    return (after_attn + moe_sum, head_peaks)

def reference(tokens, doc_ids, routes, attn_gain, w_query, w_key, w_value, query_gain, key_gain, w_out, ffn_gain, w_router, w_gate, w_up, w_down, clip_threshold, cotangent):
    params = tuple((member.astype(jnp.float32) for member in (attn_gain, w_query, w_key, w_value, query_gain, key_gain, w_out, ffn_gain, w_router, w_gate, w_up, w_down)))
    inputs = tokens.astype(jnp.float32)

    def forward(weight_set, token_rows):

        def per_sequence(seq_item):
            seq_tokens, seq_docs, seq_routes = seq_item
            return jax.checkpoint(layer_sequence)(weight_set, seq_tokens, seq_docs, seq_routes)
        outputs, peaks_all = lax.map(per_sequence, (token_rows, doc_ids, routes))
        return (outputs, lax.optimization_barrier(jnp.max(peaks_all, axis=0)))
    outputs, pullback, peak_all = jax.vjp(forward, params, inputs, has_aux=True)
    weight_grads, input_grad = pullback(cotangent.astype(jnp.float32))
    threshold = clip_threshold.astype(jnp.float32)
    clip_factors = jnp.sqrt(threshold / jnp.maximum(peak_all, threshold))
    col_scale = jnp.repeat(clip_factors, HEAD)
    query_clipped = (params[1] * col_scale[None, :]).astype(jnp.bfloat16)
    key_clipped = (params[2] * col_scale[None, :]).astype(jnp.bfloat16)
    return (outputs.astype(jnp.bfloat16), input_grad, weight_grads[0], weight_grads[1], weight_grads[2], weight_grads[3], weight_grads[4], weight_grads[5], weight_grads[6], weight_grads[7], weight_grads[8], weight_grads[9], weight_grads[10], weight_grads[11], query_clipped, key_clipped, clip_factors)
```

```python
import functools

import jax
import jax.numpy as jnp
from jax import lax
from jax.experimental import pallas as pl
from jax.experimental.pallas import tpu as pltpu
from jax.sharding import PartitionSpec as P

HEADS = 16
HEAD = 128
SCALE = HEAD ** (-0.5)
Q_BLOCK = 256
LANES = 128
EXPERT_GROUP = 2

norm_eps = 1e-06
rope_base = 10000.0
f32 = jnp.float32
bf16 = jnp.bfloat16


def dot(a, b):
    return jnp.dot(a, b, preferred_element_type=f32)


def contract_rows(a, b):
    return lax.dot_general(a, b, (((0,), (0,)), ((), ())), preferred_element_type=f32)


def contract_cols(a, b):
    return lax.dot_general(a, b, (((1,), (1,)), ((), ())), preferred_element_type=f32)


def inverse_rms(values):
    return lax.rsqrt(jnp.mean(values * values, axis=-1, keepdims=True) + norm_eps)


def rope_tables(count):
    half = HEAD // 2
    freq = rope_base ** (-jnp.arange(half).astype(f32) / half)
    angles = jnp.arange(count).astype(f32)[:, None] * freq[None, :]
    return jnp.cos(angles), jnp.sin(angles)


def rotate(values, cosine, sine):
    parts = []
    for col in range(0, values.shape[1], HEAD):
        a = values[:, col : col + HEAD // 2]
        b = values[:, col + HEAD // 2 : col + HEAD]
        parts += [a * cosine - b * sine, b * cosine + a * sine]
    return jnp.concatenate(parts, axis=1)


def attend_forward_kernel(q_ref, k_ref, v_ref, doc_q_ref, doc_k_ref, o_ref, lse_ref, peak_ref):
    s = SCALE * contract_cols(q_ref[...], k_ref[...])
    s = jnp.where(doc_q_ref[...] == doc_k_ref[...], s, -1e30)
    top = jnp.max(s, axis=1, keepdims=True)
    e = jnp.exp(s - top)
    total = jnp.sum(e, axis=1, keepdims=True)
    p = (e * (1.0 / total)).astype(bf16)
    o_ref[...] = dot(p, v_ref[...]).astype(bf16)
    lse_ref[0] = top + jnp.log(total)
    peak = jnp.broadcast_to(jnp.max(top, axis=0, keepdims=True), peak_ref.shape[1:])

    @pl.when(pl.program_id(1) == 0)
    def _():
        peak_ref[0] = peak

    @pl.when(pl.program_id(1) > 0)
    def _():
        peak_ref[0] = jnp.maximum(peak_ref[0], peak)


def attend_backward_kernel(
    q_ref, k_ref, v_ref, doc_q_ref, doc_k_ref, lse_ref, do_ref, dq_ref, dk_ref, dv_ref
):
    q, k, v, do = q_ref[...], k_ref[...], v_ref[...], do_ref[...]
    s = SCALE * contract_cols(q, k)
    p = jnp.where(doc_q_ref[...] == doc_k_ref[...], jnp.exp(s - lse_ref[0]), 0.0)
    dp = contract_cols(do, v)
    inner = jnp.sum(p * dp, axis=1, keepdims=True)
    ds = (p * (dp - inner)).astype(bf16)
    dq_ref[...] = SCALE * dot(ds, k)
    dk = SCALE * contract_rows(ds, q)
    dv = contract_rows(p.astype(bf16), do)

    @pl.when(pl.program_id(1) == 0)
    def _():
        dk_ref[...] = dk
        dv_ref[...] = dv

    @pl.when(pl.program_id(1) > 0)
    def _():
        dk_ref[...] += dk
        dv_ref[...] += dv


def attend_specs(count):
    block = pl.BlockSpec((Q_BLOCK, HEAD), lambda h, i: (i, h))
    whole = pl.BlockSpec((count, HEAD), lambda h, i: (0, h))
    doc_q = pl.BlockSpec((Q_BLOCK, 1), lambda h, i: (i, 0))
    doc_k = pl.BlockSpec((1, count), lambda h, i: (0, 0))
    lse = pl.BlockSpec((1, Q_BLOCK, 1), lambda h, i: (h, i, 0))
    return block, whole, doc_q, doc_k, lse


def attend_forward(q, k, v, docs):
    count, width = q.shape
    heads = width // HEAD
    block, whole, doc_q, doc_k, lse = attend_specs(count)
    return pl.pallas_call(
        attend_forward_kernel,
        grid=(heads, count // Q_BLOCK),
        in_specs=[block, whole, whole, doc_q, doc_k],
        out_specs=[block, lse, pl.BlockSpec((1, 8, 128), lambda h, i: (h, 0, 0))],
        out_shape=[
            jax.ShapeDtypeStruct((count, width), bf16),
            jax.ShapeDtypeStruct((heads, count, 1), f32),
            jax.ShapeDtypeStruct((heads, 8, 128), f32),
        ],
        compiler_params=pltpu.CompilerParams(vmem_limit_bytes=48 << 20),
        cost_estimate=pl.CostEstimate(
            flops=4 * count * count * width,
            transcendentals=heads * count * count,
            bytes_accessed=8 * count * width,
        ),
    )(q, k, v, docs[:, None], docs[None, :])


def attend_backward(q, k, v, docs, log_total, grad):
    count, width = q.shape
    heads = width // HEAD
    block, whole, doc_q, doc_k, lse = attend_specs(count)
    return pl.pallas_call(
        attend_backward_kernel,
        grid=(heads, count // Q_BLOCK),
        in_specs=[block, whole, whole, doc_q, doc_k, lse, block],
        out_specs=[block, whole, whole],
        out_shape=[jax.ShapeDtypeStruct((count, width), f32)] * 3,
        compiler_params=pltpu.CompilerParams(vmem_limit_bytes=56 << 20),
        cost_estimate=pl.CostEstimate(
            flops=10 * count * count * width,
            transcendentals=heads * count * count,
            bytes_accessed=20 * count * width,
        ),
    )(q, k, v, docs[:, None], docs[None, :], log_total, grad)


MESH = pl.DeviceIdType.MESH
ANY = pl.BlockSpec(memory_space=pl.ANY)
VMEM = pl.BlockSpec(memory_space=pltpu.VMEM)


def greet(axis, peers):
    barrier = pltpu.get_barrier_semaphore()
    for there, peer in peers:

        @pl.when(there)
        def _():
            pl.semaphore_signal(barrier, inc=1, device_id={axis: peer}, device_id_type=MESH)

    pl.semaphore_wait(barrier, sum(there.astype(jnp.int32) for there, _ in peers))


def ring_peers(axis):
    n, me = lax.axis_size(axis), lax.axis_index(axis)
    return [lax.rem(me + k, n) for k in range(n)], [lax.rem(me + n - k, n) for k in range(n)]


def greet_ring(axis):
    barrier = pltpu.get_barrier_semaphore()
    to, _ = ring_peers(axis)
    for peer in to[1:]:
        pl.semaphore_signal(barrier, inc=1, device_id={axis: peer}, device_id_type=MESH)
    pl.semaphore_wait(barrier, len(to) - 1)


def exchange_kernel(axis, count, *refs):
    ins, outs = refs[:count], refs[count : 2 * count]
    own_sem, send, recv = refs[2 * count :]
    me = lax.axis_index(axis)
    to, source = ring_peers(axis)
    greet_ring(axis)
    copies = []
    for k in range(1, len(to)):
        for i in range(count):
            copies.append(
                pltpu.make_async_remote_copy(
                    src_ref=ins[i].at[to[k]],
                    dst_ref=outs[i].at[me],
                    send_sem=send.at[i, k],
                    recv_sem=recv.at[i, k],
                    device_id={axis: to[k]},
                    device_id_type=MESH,
                )
            )
            copies[-1].start()
    own = [
        pltpu.make_async_copy(ins[i].at[me], outs[i].at[me], own_sem.at[i]) for i in range(count)
    ]
    for copy in own:
        copy.start()
    for copy in own:
        copy.wait()
    for k in range(1, len(to)):
        for i in range(count):
            pltpu.make_async_remote_copy(
                src_ref=ins[i].at[to[k]],
                dst_ref=outs[i].at[source[k]],
                send_sem=send.at[i, k],
                recv_sem=recv.at[i, k],
                device_id={axis: to[k]},
                device_id_type=MESH,
            ).wait()


def gather_kernel(axis, count, *refs):
    ins, outs = refs[:count], refs[count : 2 * count]
    own_sem, send, recv = refs[2 * count :]
    me = lax.axis_index(axis)
    to, source = ring_peers(axis)
    greet_ring(axis)
    for i in range(count):
        for k in range(1, len(to)):
            pltpu.make_async_remote_copy(
                src_ref=ins[i],
                dst_ref=outs[i].at[me],
                send_sem=send.at[i, k],
                recv_sem=recv.at[i, k],
                device_id={axis: to[k]},
                device_id_type=MESH,
            ).start()
    own = [pltpu.make_async_copy(ins[i], outs[i].at[me], own_sem.at[i]) for i in range(count)]
    for copy in own:
        copy.start()
    for copy in own:
        copy.wait()
    for i in range(count):
        for k in range(1, len(to)):
            pltpu.make_async_remote_copy(
                src_ref=ins[i],
                dst_ref=outs[i].at[source[k]],
                send_sem=send.at[i, k],
                recv_sem=recv.at[i, k],
                device_id={axis: to[k]},
                device_id_type=MESH,
            ).wait()


def reduce_kernel(axis, count, *refs):
    ins, outs, bufs = refs[:count], refs[count : 2 * count], refs[2 * count : 3 * count]
    send, recv = refs[3 * count :]
    me = lax.axis_index(axis)
    to, _ = ring_peers(axis)
    greet_ring(axis)

    def copy(i, k):
        return pltpu.make_async_remote_copy(
            src_ref=ins[i].at[to[k]],
            dst_ref=bufs[i].at[k - 1],
            send_sem=send.at[i, k],
            recv_sem=recv.at[i, k],
            device_id={axis: to[k]},
            device_id_type=MESH,
        )

    for i in range(count):
        for k in range(1, len(to)):
            copy(i, k).start()
    for i in range(count):
        for k in range(1, len(to)):
            copy(i, k).wait_recv()
        rows = outs[i].shape[0]
        step = 8 if rows % 32 else 32

        @pl.loop(0, rows // step)
        def _(j):
            at = pl.ds(pl.multiple_of(j * step, step), step)
            total = ins[i][me, at].astype(f32)
            for k in range(1, len(to)):
                total = total + bufs[i][k - 1, at].astype(f32)
            outs[i][at] = total

    for i in range(count):
        for k in range(1, len(to)):
            copy(i, k).wait_send()


def many_sum_kernel(axis, x_ref, o_ref, buf, send, recv):
    me = lax.axis_index(axis)
    to, source = ring_peers(axis)
    greet_ring(axis)

    def copy(k):
        return pltpu.make_async_remote_copy(
            src_ref=x_ref,
            dst_ref=buf.at[k - 1],
            send_sem=send.at[k],
            recv_sem=recv.at[k],
            device_id={axis: to[k]},
            device_id_type=MESH,
        )

    for k in range(1, len(to)):
        copy(k).start()
    total = x_ref[...]
    for k in range(1, len(to)):
        copy(k).wait_recv()
        total = total + buf[k - 1]
    o_ref[...] = total
    for k in range(1, len(to)):
        copy(k).wait_send()


def line_gather_kernel(chunks, x_ref, o_ref, own_sem, send_r, send_l, send_p, recv_r, recv_l, recv_p):
    n, me = lax.axis_size("ctx") // 2, lax.axis_index("ctx")
    place, core = lax.div(me, 2), lax.rem(me, 2)
    partner = me + 1 - 2 * core
    not_first, not_last = place > 0, place < n - 1
    rows = x_ref.shape[0] // chunks
    greet("ctx", [(place >= 0, partner), (not_last, me + 2), (not_first, me - 2)])
    own = pltpu.make_async_copy(x_ref, o_ref.at[me], own_sem)
    own.start()

    def copy(block, k, c, target, send, recv):
        part = pl.ds(c * rows, rows)
        return pltpu.make_async_remote_copy(
            src_ref=x_ref.at[part] if k == 0 else o_ref.at[block, part],
            dst_ref=o_ref.at[block, part],
            send_sem=send,
            recv_sem=recv,
            device_id={"ctx": target},
            device_id_type=MESH,
        )

    def right(k, c):
        return copy(me - 2 * k, k, c, me + 2, send_r.at[k, c], recv_r.at[k, c])

    def left(k, c):
        return copy(me + 2 * k, k, c, me - 2, send_l.at[k, c], recv_l.at[k, c])

    def across(k, c, sign):
        i = k if sign < 0 else n - 1 + k
        return copy(me + sign * 2 * k, k, c, partner, send_p.at[i, c], recv_p.at[i, c])

    def arrived(block, c, recv):
        part = pl.ds(c * rows, rows)
        pltpu.make_async_remote_copy(
            src_ref=x_ref.at[part],
            dst_ref=o_ref.at[block, part],
            send_sem=own_sem,
            recv_sem=recv,
            device_id={"ctx": partner},
            device_id_type=MESH,
        ).wait_recv()

    for k in range(n):
        for c in range(chunks):

            @pl.when(place >= k)
            def _():
                if k:
                    arrived(me - 2 * k, c, recv_r.at[k - 1, c])

                @pl.when(not_last)
                def _():
                    right(k, c).start()

                across(k, c, -1).start()

            @pl.when(place + k <= n - 1)
            def _():
                if k:
                    arrived(me + 2 * k, c, recv_l.at[k - 1, c])

                @pl.when(not_first)
                def _():
                    left(k, c).start()

                if k:
                    across(k, c, 1).start()

    own.wait()
    for k in range(n):
        for c in range(chunks):

            @pl.when(place >= k)
            def _():
                @pl.when(not_last)
                def _():
                    right(k, c).wait_send()

                across(k, c, -1).wait_send()
                arrived(partner - 2 * k, c, recv_p.at[k, c])

            @pl.when(place + k <= n - 1)
            def _():
                @pl.when(not_first)
                def _():
                    left(k, c).wait_send()

                if k:
                    across(k, c, 1).wait_send()
                    arrived(partner + 2 * k, c, recv_p.at[n - 1 + k, c])


def line_reduce_kernel(
    chunks, x_ref, o_ref, pair, from_left, from_right, out, send_p, recv_p, send_s, recv_r, recv_l
):
    n, me = lax.axis_size("ctx") // 2, lax.axis_index("ctx")
    place, core = lax.div(me, 2), lax.rem(me, 2)
    partner = me + 1 - 2 * core
    not_first, not_last = place > 0, place < n - 1
    rows = x_ref.shape[1] // chunks
    greet("ctx", [(place >= 0, partner), (not_last, me + 2), (not_first, me - 2)])
    order = []
    for j in range(n):
        order += [p for p in (n - 1 - j, j) if p not in order]

    def at(c):
        return pl.ds(c * rows, rows)

    def across(p, c):
        return pltpu.make_async_remote_copy(
            src_ref=x_ref.at[2 * p + 1 - core, at(c)],
            dst_ref=pair.at[p, at(c)],
            send_sem=send_p.at[p, c],
            recv_sem=recv_p.at[p, c],
            device_id={"ctx": partner},
            device_id_type=MESH,
        )

    def right(p, c):
        return pltpu.make_async_remote_copy(
            src_ref=out.at[p, at(c)],
            dst_ref=from_left.at[p, at(c)],
            send_sem=send_s.at[p, c],
            recv_sem=recv_r.at[p, c],
            device_id={"ctx": me + 2},
            device_id_type=MESH,
        )

    def left(p, c):
        return pltpu.make_async_remote_copy(
            src_ref=out.at[p, at(c)],
            dst_ref=from_right.at[p, at(c)],
            send_sem=send_s.at[p, c],
            recv_sem=recv_l.at[p, c],
            device_id={"ctx": me - 2},
            device_id_type=MESH,
        )

    for p in order:
        for c in range(chunks):
            across(p, c).start()
    for p in order:
        for c in range(chunks):
            across(p, c).wait_recv()

            @pl.when(place < p)
            def _():
                total = x_ref[2 * p + core, at(c)].astype(f32) + pair[p, at(c)].astype(f32)

                @pl.when(not_first)
                def _():
                    right(p, c).wait_recv()
                    out[p, at(c)] = (total + from_left[p, at(c)].astype(f32)).astype(bf16)

                @pl.when(place == 0)
                def _():
                    out[p, at(c)] = total.astype(bf16)

                right(p, c).start()

            @pl.when(place > p)
            def _():
                total = x_ref[2 * p + core, at(c)].astype(f32) + pair[p, at(c)].astype(f32)

                @pl.when(not_last)
                def _():
                    left(p, c).wait_recv()
                    out[p, at(c)] = (total + from_right[p, at(c)].astype(f32)).astype(bf16)

                @pl.when(place == n - 1)
                def _():
                    out[p, at(c)] = total.astype(bf16)

                left(p, c).start()

    for p in range(n):
        for c in range(chunks):

            @pl.when(place == p)
            def _():
                o_ref[at(c)] = x_ref[2 * p + core, at(c)].astype(f32) + pair[p, at(c)].astype(f32)
                if p > 0:
                    right(p, c).wait_recv()
                    o_ref[at(c)] += from_left[p, at(c)].astype(f32)
                if p < n - 1:
                    left(p, c).wait_recv()
                    o_ref[at(c)] += from_right[p, at(c)].astype(f32)

    for p in range(n):
        for c in range(chunks):
            across(p, c).wait_send()

            @pl.when(place < p)
            def _():
                right(p, c).wait_send()

            @pl.when(place > p)
            def _():
                left(p, c).wait_send()


def remote_params(collective_id, megabytes=None):
    limit = None if megabytes is None else megabytes << 20
    return pltpu.CompilerParams(
        collective_id=collective_id, has_side_effects=True, vmem_limit_bytes=limit
    )


def direct_call(kernel, axis, collective_id, arrays, shapes):
    count = len(arrays)
    n = lax.axis_size(axis)
    sem = pltpu.SemaphoreType.DMA
    return pl.pallas_call(
        functools.partial(kernel, axis, count),
        out_shape=[jax.ShapeDtypeStruct(s, a.dtype) for s, a in zip(shapes, arrays)],
        in_specs=[ANY] * count,
        out_specs=[ANY] * count,
        scratch_shapes=[sem((count,)), sem((count, n)), sem((count, n))],
        compiler_params=remote_params(collective_id, 8),
    )(*arrays)


def exchange(axis, collective_id, *arrays):
    return direct_call(exchange_kernel, axis, collective_id, arrays, [a.shape for a in arrays])


def gather(axis, collective_id, *arrays):
    n = lax.axis_size(axis)
    return direct_call(gather_kernel, axis, collective_id, arrays, [(n, *a.shape) for a in arrays])


def reduce(axis, collective_id, *arrays):
    count, n = len(arrays), lax.axis_size(axis)
    sem = pltpu.SemaphoreType.DMA
    return pl.pallas_call(
        functools.partial(reduce_kernel, axis, count),
        out_shape=[jax.ShapeDtypeStruct(a.shape[1:], f32) for a in arrays],
        in_specs=[VMEM] * count,
        out_specs=[VMEM] * count,
        scratch_shapes=[pltpu.VMEM((n - 1, *a.shape[1:]), a.dtype) for a in arrays]
        + [sem((count, n)), sem((count, n))],
        compiler_params=remote_params(collective_id, 48),
    )(*arrays)


def many_sum(axis, collective_id, x):
    n = lax.axis_size(axis)
    sem = pltpu.SemaphoreType.DMA
    return pl.pallas_call(
        functools.partial(many_sum_kernel, axis),
        out_shape=jax.ShapeDtypeStruct(x.shape, x.dtype),
        in_specs=[VMEM],
        out_specs=VMEM,
        scratch_shapes=[pltpu.VMEM((n - 1, *x.shape), x.dtype), sem((n,)), sem((n,))],
        compiler_params=remote_params(collective_id, 8),
    )(x)


LINE_CHUNKS = 4


def line_gather(collective_id, x):
    n_ctx = lax.axis_size("ctx")
    n = n_ctx // 2
    sem = pltpu.SemaphoreType.DMA
    return pl.pallas_call(
        functools.partial(line_gather_kernel, LINE_CHUNKS),
        out_shape=jax.ShapeDtypeStruct((n_ctx, *x.shape), x.dtype),
        in_specs=[ANY],
        out_specs=ANY,
        scratch_shapes=[
            sem,
            sem((n, LINE_CHUNKS)),
            sem((n, LINE_CHUNKS)),
            sem((2 * n - 1, LINE_CHUNKS)),
            sem((n, LINE_CHUNKS)),
            sem((n, LINE_CHUNKS)),
            sem((2 * n - 1, LINE_CHUNKS)),
        ],
        compiler_params=remote_params(collective_id, 8),
    )(x)


def line_reduce(collective_id, x):
    n_ctx, rows, width = x.shape
    n = n_ctx // 2
    sem = pltpu.SemaphoreType.DMA
    return pl.pallas_call(
        functools.partial(line_reduce_kernel, LINE_CHUNKS),
        out_shape=jax.ShapeDtypeStruct((rows, width), f32),
        in_specs=[VMEM],
        out_specs=VMEM,
        scratch_shapes=[pltpu.VMEM((n, rows, width), bf16)] * 4 + [sem((n, LINE_CHUNKS))] * 5,
        compiler_params=remote_params(collective_id, 40),
    )(x)


def per_device(
    tokens,
    doc_ids,
    routes,
    attn_gain,
    w_query,
    w_key,
    w_value,
    query_gain,
    key_gain,
    w_out,
    ffn_gain,
    w_router,
    w_gate,
    w_up,
    w_down,
    clip_threshold,
    cotangent,
):
    both = ("ctx", "shard")
    n_ctx, n_shard = lax.axis_size("ctx"), lax.axis_size("shard")
    ctx, shard = lax.axis_index("ctx"), lax.axis_index("shard")
    x_own = tokens[0]
    rows, width = x_own.shape
    part = w_query.shape[0]
    cols = width // n_ctx
    heads = cols // HEAD
    count = rows * n_ctx
    local = w_gate.shape[0]
    experts = local * n_shard

    top = routes.shape[2]
    spare = jnp.zeros((part, LANES - 4 - experts - rows // part * (1 + top)), bf16)
    small = jnp.concatenate(
        [
            jnp.stack([attn_gain, query_gain, key_gain, ffn_gain], axis=1),
            w_router,
            doc_ids.reshape(part, rows // part).astype(bf16),
            routes.reshape(part, rows // part * top).astype(bf16),
            spare,
        ],
        axis=1,
    )
    packed = jnp.concatenate(
        [
            jnp.stack([w_query, w_key, w_value], axis=1)
            .reshape(part, 3, n_ctx, cols)
            .transpose(2, 0, 1, 3)
            .reshape(n_ctx, part, 3 * cols),
            jnp.broadcast_to(small[None], (n_ctx, part, LANES)),
        ],
        axis=2,
    )
    (packed,) = exchange("ctx", 1, packed)
    grad_own = cotangent[0]
    packed, out_w_own, grad_all = gather("shard", 2, packed, w_out, grad_own)
    packed = packed.transpose(1, 0, 2, 3)
    weights = packed[..., : 3 * cols].reshape(width, 3 * cols)
    small_all = packed[..., 3 * cols :]
    out_w_own = out_w_own.reshape(cols, width)
    grad_all = grad_all.reshape(n_shard * rows, width)
    gains = small_all[..., : 4 + experts].reshape(width, 4 + experts)
    gain_attn, gain_query, gain_key, gain_ffn = (gains[:, i].astype(f32) for i in range(4))
    router_w = gains[:, 4:]
    gain_query = lax.dynamic_slice_in_dim(gain_query, ctx * cols, cols)
    gain_key = lax.dynamic_slice_in_dim(gain_key, ctx * cols, cols)
    tail = small_all[..., 4 + experts :].astype(jnp.int32)
    docs = lax.dynamic_index_in_dim(tail[..., : rows // part], shard, 1, False).reshape(count)
    routes_all = lax.dynamic_index_in_dim(
        tail[..., rows // part : rows // part * (1 + top)], ctx, 0, False
    ).reshape(n_shard * rows, top)
    x_all = line_gather(3, x_own).reshape(count, width)
    w_gate, w_up, w_down, x_all = lax.optimization_barrier((w_gate, w_up, w_down, x_all))
    groups = [slice(g, g + EXPERT_GROUP) for g in range(0, local, EXPERT_GROUP)]
    wide_w, down_w = [], []
    for g in groups:
        both_own = jnp.concatenate([w_gate[g], w_up[g]], axis=2)
        wide_w.append(lax.all_gather(both_own, "ctx", axis=1, tiled=True))
        down_w.append(lax.all_gather(w_down[g], "ctx", axis=2, tiled=True))

    x_wide = x_all.astype(f32)
    inverse_one = inverse_rms(x_wide)
    hidden_one = (x_wide * inverse_one * gain_attn).astype(bf16)
    linear = dot(hidden_one, weights)
    query_lin, key_lin = linear[:, :cols], linear[:, cols : 2 * cols]
    value = linear[:, 2 * cols :].astype(bf16)
    squares = jnp.stack(
        [jnp.sum(query_lin * query_lin, axis=1), jnp.sum(key_lin * key_lin, axis=1)]
    )
    squares = many_sum("ctx", 4, squares)
    inverse_qk = lax.rsqrt(squares / width + norm_eps)
    inverse_q, inverse_k = inverse_qk[0][:, None], inverse_qk[1][:, None]
    cosine, sine = rope_tables(count)
    query_n, key_n = query_lin * inverse_q, key_lin * inverse_k
    query = rotate(query_n * gain_query, cosine, sine).astype(bf16)
    key = rotate(key_n * gain_key, cosine, sine).astype(bf16)
    mixed, log_total, peaks = attend_forward(query, key, value, docs)
    x_f = x_own.astype(f32)
    mixed_out = dot(mixed, out_w_own).astype(bf16).reshape(n_ctx, rows, width)
    after = x_f + line_reduce(5, mixed_out)
    inverse_two = inverse_rms(after)
    normed_two = after * inverse_two
    hidden_two = (normed_two * gain_ffn).astype(bf16)

    hidden_all, peaks = gather("shard", 6, hidden_two, peaks)
    hidden_all = hidden_all.reshape(n_shard * rows, width)
    peaks = jnp.max(peaks, axis=0)[:, 0, 0]
    logits = dot(hidden_all, router_w)
    named = jnp.any(routes_all[:, :, None] == jnp.arange(experts)[None, None, :], axis=1)
    probs = jax.nn.softmax(logits, axis=1)
    selected = jnp.where(named, probs, 0.0)
    selected_sum = jnp.sum(selected, axis=1, keepdims=True)
    gates = selected / selected_sum
    gates_own = lax.dynamic_slice_in_dim(gates, shard * local, local, 1)
    named_own = lax.dynamic_slice_in_dim(named, shard * local, local, 1)
    grad_wide = grad_all.astype(f32)
    moe_part = jnp.zeros(grad_all.shape, f32)
    back_part = jnp.zeros(grad_all.shape, f32)
    grad_gates, grad_wide_w, grad_down_w = [], [], []
    for e in range(local):
        group, member = divmod(e, EXPERT_GROUP)
        wide, down = wide_w[group][member], down_w[group][member]
        gate_col = gates_own[:, e : e + 1]
        hidden = dot(hidden_all, wide)
        ff = hidden.shape[1] // 2
        gate_h, up_h = hidden[:, :ff], hidden[:, ff:]
        sig = jax.nn.sigmoid(gate_h)
        silu = gate_h * sig
        act = (silu * up_h).astype(bf16)
        result = dot(act, down).astype(bf16).astype(f32)
        moe_part = moe_part + gate_col * result
        grad_gates.append(
            jnp.where(named_own[:, e], jnp.sum(grad_wide * result, axis=1), 0.0)
        )
        grad_y = (gate_col * grad_wide).astype(bf16)
        grad_act = contract_cols(grad_y, down)
        grad_h = jnp.concatenate(
            [grad_act * up_h * sig * (1.0 + gate_h * (1.0 - sig)), grad_act * silu], axis=1
        ).astype(bf16)
        back_part = back_part + contract_cols(grad_h, wide).astype(bf16).astype(f32)
        grad_down_w.append(contract_rows(act, grad_y).astype(bf16))
        grad_wide_w.append(contract_rows(hidden_all, grad_h).astype(bf16))
    wide_grads = [
        lax.psum_scatter(jnp.stack(grad_wide_w[g]), "ctx", scatter_dimension=1, tiled=True)
        for g in groups
    ]
    down_grads = [
        lax.psum_scatter(jnp.stack(grad_down_w[g]), "ctx", scatter_dimension=2, tiled=True)
        for g in groups
    ]
    (back_sum,) = reduce("shard", 7, back_part.astype(bf16).reshape(n_shard, rows, width))
    grad_gates = lax.all_to_all(
        jnp.stack(grad_gates, axis=1), "shard", split_axis=0, concat_axis=1, tiled=True
    )

    def own_rows(u):
        return lax.dynamic_slice_in_dim(u, shard * rows, rows, 0)

    gates_t, probs_t, named_t, sum_t = map(own_rows, (gates, probs, named, selected_sum))
    grad_selected = (
        grad_gates - jnp.sum(gates_t * grad_gates, axis=1, keepdims=True)
    ) / sum_t
    grad_probs = jnp.where(named_t, grad_selected, 0.0)
    grad_logits = (
        probs_t * (grad_probs - jnp.sum(probs_t * grad_probs, axis=1, keepdims=True))
    ).astype(bf16)
    grad_router = contract_rows(hidden_two, grad_logits)
    grad_hidden = back_sum + contract_cols(grad_logits, router_w)
    grad_gain_ffn = jnp.sum(grad_hidden * normed_two, axis=0)
    scaled_two = grad_hidden * gain_ffn
    grad_after = grad_own.astype(f32) + inverse_two * (
        scaled_two - normed_two * jnp.mean(scaled_two * normed_two, axis=1, keepdims=True)
    )

    grad_attn = line_gather(3, grad_after.astype(bf16)).reshape(count, width)
    grad_mixed = contract_cols(grad_attn, out_w_own).astype(bf16)
    grad_out_w = contract_rows(mixed, grad_attn)
    grad_query_rot, grad_key_rot, grad_value = attend_backward(
        query, key, value, docs, log_total, grad_mixed
    )
    grad_query_n = rotate(grad_query_rot, cosine, -sine)
    grad_key_n = rotate(grad_key_rot, cosine, -sine)
    grad_gain_query = jnp.sum(grad_query_n * query_n, axis=0)
    grad_gain_key = jnp.sum(grad_key_n * key_n, axis=0)
    scaled_q, scaled_k = grad_query_n * gain_query, grad_key_n * gain_key
    peak_row = lax.dynamic_update_slice_in_dim(jnp.zeros((count,), f32), peaks, ctx * heads, 0)
    inner = jnp.stack(
        [jnp.sum(scaled_q * query_n, axis=1), jnp.sum(scaled_k * key_n, axis=1), peak_row]
    )
    inner = many_sum("ctx", 8, inner)
    peak_all = inner[2, :HEADS]
    inner = inner / width
    grad_linear = jnp.concatenate(
        [
            inverse_q * (scaled_q - query_n * inner[0][:, None]),
            inverse_k * (scaled_k - key_n * inner[1][:, None]),
            grad_value,
        ],
        axis=1,
    ).astype(bf16)
    grad_weights = contract_rows(hidden_one, grad_linear)
    hidden_part = contract_cols(grad_linear, weights)
    grad_gain_attn = jnp.sum(hidden_part * (x_wide * inverse_one), axis=0)
    grad_small = jnp.concatenate(
        [jnp.stack([grad_gain_attn, grad_gain_ffn], axis=1), grad_router], axis=1
    )
    grad_small = jnp.pad(grad_small, ((0, 0), (0, LANES - 2 - experts)))
    grad_weights = (
        jnp.concatenate([grad_weights, grad_small], axis=1)
        .astype(bf16)
        .reshape(n_ctx, n_shard, part, 3 * cols + LANES)
        .transpose(1, 0, 2, 3)
        .reshape(n_shard, n_ctx * part, 3 * cols + LANES)
    )
    grad_gain_qk = jnp.pad(
        jnp.stack([grad_gain_query, grad_gain_key], axis=1), ((0, 0), (0, LANES - 2))
    )
    grad_out_w = (
        jnp.concatenate([grad_out_w, grad_gain_qk], axis=1)
        .astype(bf16)
        .reshape(n_shard, part, width + LANES)
    )
    moe_part = moe_part.astype(bf16).reshape(n_shard, rows, width)
    grad_weights, grad_out_w, moe_sum = reduce("shard", 9, grad_weights, grad_out_w, moe_part)
    output = (after + moe_sum).astype(bf16)
    grad_weights = grad_weights.reshape(n_ctx, part, 3 * cols + LANES)
    (grad_weights,) = exchange("ctx", 10, grad_weights)
    grad_small = jnp.sum(grad_weights[..., 3 * cols :], axis=0)
    grad_weights = (
        grad_weights[..., : 3 * cols]
        .reshape(n_ctx, part, 3, cols)
        .transpose(2, 1, 0, 3)
        .reshape(3, part, width)
    )
    grad_hidden_one = line_reduce(5, hidden_part.astype(bf16).reshape(n_ctx, rows, width))
    inverse_own = inverse_rms(x_f)
    normed_own = x_f * inverse_own
    scaled_one = grad_hidden_one * gain_attn
    grad_inputs = grad_after + inverse_own * (
        scaled_one - normed_own * jnp.mean(scaled_one * normed_own, axis=1, keepdims=True)
    )

    wide_grads = jnp.concatenate(wide_grads, axis=0)
    factors = jnp.sqrt(clip_threshold / jnp.maximum(peak_all, clip_threshold))
    col_scale = jnp.repeat(factors, HEAD)
    query_clipped = (w_query.astype(f32) * col_scale[None, :]).astype(bf16)
    key_clipped = (w_key.astype(f32) * col_scale[None, :]).astype(bf16)
    return (
        output[None],
        grad_inputs[None],
        grad_small[:, 0],
        grad_weights[0],
        grad_weights[1],
        grad_weights[2],
        grad_out_w[:, width],
        grad_out_w[:, width + 1],
        grad_out_w[:, :width],
        grad_small[:, 1],
        grad_small[:, 2 : 2 + experts],
        wide_grads[..., :ff].astype(f32),
        wide_grads[..., ff:].astype(f32),
        jnp.concatenate(down_grads, axis=0).astype(f32),
        query_clipped,
        key_clipped,
        factors,
    )


def solution(mesh):
    both = ("ctx", "shard")
    return jax.shard_map(
        per_device,
        mesh=mesh,
        in_specs=(
            P("shard", "ctx", None),
            P("shard", "ctx"),
            P("shard", "ctx", None),
            P(both),
            P(both, None),
            P(both, None),
            P(both, None),
            P(both),
            P(both),
            P(both, None),
            P(both),
            P(both, None),
            P("shard", "ctx", None),
            P("shard", "ctx", None),
            P("shard", None, "ctx"),
            P(),
            P("shard", "ctx", None),
        ),
        out_specs=(
            P("shard", "ctx", None),
            P("shard", "ctx", None),
            P(both),
            P(both, None),
            P(both, None),
            P(both, None),
            P(both),
            P(both),
            P(both, None),
            P(both),
            P(both, None),
            P("shard", "ctx", None),
            P("shard", "ctx", None),
            P("shard", None, "ctx"),
            P(both, None),
            P(both, None),
            P(),
        ),
        check_vma=False,
    )
```

```python
import functools

import jax
import jax.numpy as jnp
from jax import lax
from jax.experimental import pallas as pl
from jax.experimental.pallas import tpu as pltpu
from jax.sharding import PartitionSpec as P

HEADS = 16
HEAD = 128
SCALE = HEAD ** (-0.5)
Q_BLOCK = 256
LANES = 128

norm_eps = 1e-06
rope_base = 10000.0
f32 = jnp.float32
bf16 = jnp.bfloat16


def dot(a, b):
    return jnp.dot(a, b, preferred_element_type=f32)


def contract_rows(a, b):
    return lax.dot_general(a, b, (((0,), (0,)), ((), ())), preferred_element_type=f32)


def contract_cols(a, b):
    return lax.dot_general(a, b, (((1,), (1,)), ((), ())), preferred_element_type=f32)


def inverse_rms(values):
    return lax.rsqrt(jnp.mean(values * values, axis=-1, keepdims=True) + norm_eps)


def rope_tables(count):
    half = HEAD // 2
    freq = rope_base ** (-jnp.arange(half).astype(f32) / half)
    angles = jnp.arange(count).astype(f32)[:, None] * freq[None, :]
    return jnp.cos(angles), jnp.sin(angles)


def rotate(values, cosine, sine):
    parts = []
    for col in range(0, values.shape[1], HEAD):
        a = values[:, col : col + HEAD // 2]
        b = values[:, col + HEAD // 2 : col + HEAD]
        parts += [a * cosine - b * sine, b * cosine + a * sine]
    return jnp.concatenate(parts, axis=1)


def attend_forward_kernel(q_ref, k_ref, v_ref, doc_q_ref, doc_k_ref, o_ref, lse_ref, peak_ref):
    s = SCALE * contract_cols(q_ref[...], k_ref[...])
    s = jnp.where(doc_q_ref[...] == doc_k_ref[...], s, -1e30)
    top = jnp.max(s, axis=1, keepdims=True)
    e = jnp.exp(s - top)
    total = jnp.sum(e, axis=1, keepdims=True)
    p = (e * (1.0 / total)).astype(bf16)
    o_ref[...] = dot(p, v_ref[...]).astype(bf16)
    lse_ref[0] = top + jnp.log(total)
    peak = jnp.broadcast_to(jnp.max(top, axis=0, keepdims=True), peak_ref.shape[1:])

    @pl.when(pl.program_id(1) == 0)
    def _():
        peak_ref[0] = peak

    @pl.when(pl.program_id(1) > 0)
    def _():
        peak_ref[0] = jnp.maximum(peak_ref[0], peak)


def attend_backward_kernel(
    q_ref, k_ref, v_ref, doc_q_ref, doc_k_ref, lse_ref, do_ref, dq_ref, dk_ref, dv_ref
):
    q, k, v, do = q_ref[...], k_ref[...], v_ref[...], do_ref[...]
    s = SCALE * contract_cols(q, k)
    p = jnp.where(doc_q_ref[...] == doc_k_ref[...], jnp.exp(s - lse_ref[0]), 0.0)
    dp = contract_cols(do, v)
    inner = jnp.sum(p * dp, axis=1, keepdims=True)
    ds = (p * (dp - inner)).astype(bf16)
    dq_ref[...] = SCALE * dot(ds, k)
    dk = SCALE * contract_rows(ds, q)
    dv = contract_rows(p.astype(bf16), do)

    @pl.when(pl.program_id(1) == 0)
    def _():
        dk_ref[...] = dk
        dv_ref[...] = dv

    @pl.when(pl.program_id(1) > 0)
    def _():
        dk_ref[...] += dk
        dv_ref[...] += dv


def attend_specs(count):
    block = pl.BlockSpec((Q_BLOCK, HEAD), lambda h, i: (i, h))
    whole = pl.BlockSpec((count, HEAD), lambda h, i: (0, h))
    doc_q = pl.BlockSpec((Q_BLOCK, 1), lambda h, i: (i, 0))
    doc_k = pl.BlockSpec((1, count), lambda h, i: (0, 0))
    lse = pl.BlockSpec((1, Q_BLOCK, 1), lambda h, i: (h, i, 0))
    return block, whole, doc_q, doc_k, lse


def attend_forward(q, k, v, docs):
    count, width = q.shape
    heads = width // HEAD
    block, whole, doc_q, doc_k, lse = attend_specs(count)
    return pl.pallas_call(
        attend_forward_kernel,
        grid=(heads, count // Q_BLOCK),
        in_specs=[block, whole, whole, doc_q, doc_k],
        out_specs=[block, lse, pl.BlockSpec((1, 8, 128), lambda h, i: (h, 0, 0))],
        out_shape=[
            jax.ShapeDtypeStruct((count, width), bf16),
            jax.ShapeDtypeStruct((heads, count, 1), f32),
            jax.ShapeDtypeStruct((heads, 8, 128), f32),
        ],
        compiler_params=pltpu.CompilerParams(vmem_limit_bytes=48 << 20),
        cost_estimate=pl.CostEstimate(
            flops=4 * count * count * width,
            transcendentals=heads * count * count,
            bytes_accessed=8 * count * width,
        ),
    )(q, k, v, docs[:, None], docs[None, :])


def attend_backward(q, k, v, docs, log_total, grad):
    count, width = q.shape
    heads = width // HEAD
    block, whole, doc_q, doc_k, lse = attend_specs(count)
    return pl.pallas_call(
        attend_backward_kernel,
        grid=(heads, count // Q_BLOCK),
        in_specs=[block, whole, whole, doc_q, doc_k, lse, block],
        out_specs=[block, whole, whole],
        out_shape=[jax.ShapeDtypeStruct((count, width), f32)] * 3,
        compiler_params=pltpu.CompilerParams(vmem_limit_bytes=56 << 20),
        cost_estimate=pl.CostEstimate(
            flops=10 * count * count * width,
            transcendentals=heads * count * count,
            bytes_accessed=20 * count * width,
        ),
    )(q, k, v, docs[:, None], docs[None, :], log_total, grad)


MESH = pl.DeviceIdType.MESH
ANY = pl.BlockSpec(memory_space=pl.ANY)
VMEM = pl.BlockSpec(memory_space=pltpu.VMEM)


def ring_peers(axis):
    n, me = lax.axis_size(axis), lax.axis_index(axis)
    return [lax.rem(me + k, n) for k in range(n)], [lax.rem(me + n - k, n) for k in range(n)]


class Greeting:
    def __init__(self):
        self.barrier, self.total = pltpu.get_barrier_semaphore(), 0

    def ring(self, axis):
        to, _ = ring_peers(axis)
        for peer in to[1:]:
            pl.semaphore_signal(
                self.barrier, inc=1, device_id={axis: peer}, device_id_type=MESH
            )
        self.total = self.total + len(to) - 1
        return self

    def line(self):
        line = Line()
        for there, peer in (
            (line.place >= 0, line.partner),
            (line.not_last, line.me + 2),
            (line.not_first, line.me - 2),
        ):

            @pl.when(there)
            def _():
                pl.semaphore_signal(
                    self.barrier, inc=1, device_id={"ctx": peer}, device_id_type=MESH
                )

            self.total = self.total + there.astype(jnp.int32)
        return self

    def pair(self):
        pl.semaphore_signal(
            self.barrier, inc=1, device_id={"ctx": Pair().peer}, device_id_type=MESH
        )
        self.total = self.total + 1
        return self

    def wait(self):
        pl.semaphore_wait(self.barrier, self.total)


class Line:
    def __init__(self):
        self.n, self.me = lax.axis_size("ctx") // 2, lax.axis_index("ctx")
        self.place, self.core = lax.div(self.me, 2), lax.rem(self.me, 2)
        self.partner = self.me + 1 - 2 * self.core
        self.not_first, self.not_last = self.place > 0, self.place < self.n - 1


class Direct:
    def __init__(self, axis, source, target, send, recv):
        self.axis, self.source, self.target = axis, source, target
        self.send, self.recv = send, recv
        self.me = lax.axis_index(axis)
        self.to, self.origin = ring_peers(axis)

    def copy(self, k, sender):
        return pltpu.make_async_remote_copy(
            src_ref=self.source(self.to[k]),
            dst_ref=self.target(sender, k),
            send_sem=self.send.at[k],
            recv_sem=self.recv.at[k],
            device_id={self.axis: self.to[k]},
            device_id_type=MESH,
        )

    def start(self):
        for k in range(1, len(self.to)):
            self.copy(k, self.me).start()

    def wait_recv(self):
        for k in range(1, len(self.to)):
            self.copy(k, self.origin[k]).wait_recv()

    def wait_send(self):
        for k in range(1, len(self.to)):
            self.copy(k, self.me).wait_send()


class LineGather:
    def __init__(self, pieces, own_sem, send_r, send_l, send_p, recv_r, recv_l, recv_p):
        self.line, self.pieces, self.own_sem = Line(), pieces, own_sem
        self.send_r, self.send_l, self.send_p = send_r, send_l, send_p
        self.recv_r, self.recv_l, self.recv_p = recv_r, recv_l, recv_p

    def own(self, c):
        source, target = self.pieces[c]
        return pltpu.make_async_copy(source, target(self.line.me), self.own_sem.at[c])

    def copy(self, block, k, c, target_device, send, recv):
        source, target = self.pieces[c]
        return pltpu.make_async_remote_copy(
            src_ref=source if k == 0 else target(block),
            dst_ref=target(block),
            send_sem=send,
            recv_sem=recv,
            device_id={"ctx": target_device},
            device_id_type=MESH,
        )

    def right(self, k, c):
        me = self.line.me
        return self.copy(me - 2 * k, k, c, me + 2, self.send_r.at[k, c], self.recv_r.at[k, c])

    def left(self, k, c):
        me = self.line.me
        return self.copy(me + 2 * k, k, c, me - 2, self.send_l.at[k, c], self.recv_l.at[k, c])

    def across(self, k, c, sign):
        line = self.line
        i = k if sign < 0 else line.n - 1 + k
        return self.copy(
            line.me + sign * 2 * k, k, c, line.partner, self.send_p.at[i, c], self.recv_p.at[i, c]
        )

    def arrived(self, block, c, recv):
        source, target = self.pieces[c]
        pltpu.make_async_remote_copy(
            src_ref=source,
            dst_ref=target(block),
            send_sem=recv,
            recv_sem=recv,
            device_id={"ctx": self.line.partner},
            device_id_type=MESH,
        ).wait_recv()

    def start(self):
        for c in range(len(self.pieces)):
            self.own(c).start()

    def hop(self, k):
        line = self.line
        for c in range(len(self.pieces)):

            @pl.when(line.place >= k)
            def _():
                if k:
                    self.arrived(line.me - 2 * k, c, self.recv_r.at[k - 1, c])

                @pl.when(line.not_last)
                def _():
                    self.right(k, c).start()

                self.across(k, c, -1).start()

            @pl.when(line.place + k <= line.n - 1)
            def _():
                if k:
                    self.arrived(line.me + 2 * k, c, self.recv_l.at[k - 1, c])

                @pl.when(line.not_first)
                def _():
                    self.left(k, c).start()

                if k:
                    self.across(k, c, 1).start()

    def finish(self, skip_own=None):
        line = self.line
        for c in range(len(self.pieces)):
            if c != skip_own:
                self.own(c).wait()
        for k in range(line.n):
            for c in range(len(self.pieces)):

                @pl.when(line.place >= k)
                def _():
                    @pl.when(line.not_last)
                    def _():
                        self.right(k, c).wait_send()

                    self.across(k, c, -1).wait_send()
                    self.arrived(line.partner - 2 * k, c, self.recv_p.at[k, c])

                @pl.when(line.place + k <= line.n - 1)
                def _():
                    @pl.when(line.not_first)
                    def _():
                        self.left(k, c).wait_send()

                    if k:
                        self.across(k, c, 1).wait_send()
                        self.arrived(line.partner + 2 * k, c, self.recv_p.at[line.n - 1 + k, c])


def line_gather_scratch(n, pieces):
    sem = pltpu.SemaphoreType.DMA
    one, two = sem((n, pieces)), sem((2 * n - 1, pieces))
    return [sem((pieces,)), one, one, two, one, one, two]


class LineReduce:
    def __init__(
        self, chunks, x, o, pair, from_left, from_right, out, send_p, recv_p, send_s, recv_r, recv_l
    ):
        self.line, self.chunks = Line(), chunks
        self.x, self.o, self.pair, self.out = x, o, pair, out
        self.from_left, self.from_right = from_left, from_right
        self.send_p, self.recv_p, self.send_s = send_p, recv_p, send_s
        self.recv_r, self.recv_l = recv_r, recv_l
        self.order = []
        for j in range(self.line.n):
            self.order += [p for p in (self.line.n - 1 - j, j) if p not in self.order]

    def at(self, c):
        rows = self.x.shape[1] // self.chunks
        return pl.ds(c * rows, rows)

    def across(self, p, c):
        line, at = self.line, self.at(c)
        return pltpu.make_async_remote_copy(
            src_ref=self.x.at[2 * p + 1 - line.core, at],
            dst_ref=self.pair.at[p, at],
            send_sem=self.send_p.at[p, c],
            recv_sem=self.recv_p.at[p, c],
            device_id={"ctx": line.partner},
            device_id_type=MESH,
        )

    def along(self, p, c, step, buffer, recv):
        at = self.at(c)
        return pltpu.make_async_remote_copy(
            src_ref=self.out.at[p, at],
            dst_ref=buffer.at[p, at],
            send_sem=self.send_s.at[p, c],
            recv_sem=recv.at[p, c],
            device_id={"ctx": self.line.me + step},
            device_id_type=MESH,
        )

    def right(self, p, c):
        return self.along(p, c, 2, self.from_left, self.recv_r)

    def left(self, p, c):
        return self.along(p, c, -2, self.from_right, self.recv_l)

    def start(self):
        for p in self.order:
            for c in range(self.chunks):
                self.across(p, c).start()

    def both(self, p, c):
        at = self.at(c)
        return self.x[2 * p + self.line.core, at].astype(f32) + self.pair[p, at].astype(f32)

    def pass_on(self):
        line = self.line
        for p in self.order:
            for c in range(self.chunks):
                at = self.at(c)
                self.across(p, c).wait_recv()

                @pl.when(line.place < p)
                def _():
                    @pl.when(line.not_first)
                    def _():
                        self.right(p, c).wait_recv()
                        total = self.both(p, c) + self.from_left[p, at].astype(f32)
                        self.out[p, at] = total.astype(bf16)

                    @pl.when(line.place == 0)
                    def _():
                        self.out[p, at] = self.both(p, c).astype(bf16)

                    self.right(p, c).start()

                @pl.when(line.place > p)
                def _():
                    @pl.when(line.not_last)
                    def _():
                        self.left(p, c).wait_recv()
                        total = self.both(p, c) + self.from_right[p, at].astype(f32)
                        self.out[p, at] = total.astype(bf16)

                    @pl.when(line.place == line.n - 1)
                    def _():
                        self.out[p, at] = self.both(p, c).astype(bf16)

                    self.left(p, c).start()

    def finish(self):
        line = self.line
        for p in range(line.n):
            for c in range(self.chunks):
                at = self.at(c)

                @pl.when(line.place == p)
                def _():
                    self.o[at] = self.both(p, c)
                    if p > 0:
                        self.right(p, c).wait_recv()
                        self.o[at] += self.from_left[p, at].astype(f32)
                    if p < line.n - 1:
                        self.left(p, c).wait_recv()
                        self.o[at] += self.from_right[p, at].astype(f32)

        for p in range(line.n):
            for c in range(self.chunks):
                self.across(p, c).wait_send()

                @pl.when(line.place < p)
                def _():
                    self.right(p, c).wait_send()

                @pl.when(line.place > p)
                def _():
                    self.left(p, c).wait_send()


def add_up(x, buf, o, me):
    rows = x.shape[1]
    step = 8 if rows % 32 else 32

    @pl.loop(0, rows // step)
    def _(j):
        at = pl.ds(pl.multiple_of(j * step, step), step)
        total = x[me, at].astype(f32)
        for k in range(buf.shape[0]):
            total = total + buf[k, at].astype(f32)
        o[at] = total.astype(o.dtype)


def block_of(ref):
    return lambda device: ref.at[device]


def block_from(ref):
    return lambda device, k: ref.at[device]


def whole_of(ref):
    return lambda device: ref


def buffer_of(ref):
    return lambda device, k: ref.at[k - 1]


def row_pieces(source, target, chunks):
    rows = source.shape[0] // chunks
    return [
        (source.at[pl.ds(c * rows, rows)], lambda b, c=c: target.at[b, pl.ds(c * rows, rows)])
        for c in range(chunks)
    ]


def start_kernel(
    x, w, w_query, w_key, w_value, small, x_all, w_all, packed_mid, packed_all,
    own_sem, ex_send, ex_recv, pk_send, pk_recv, w_send, w_recv, f_send, f_recv,
    *line_sems,
):
    shard, ctx = lax.axis_index("shard"), lax.axis_index("ctx")
    n_ctx = lax.axis_size("ctx")
    cols = w_query.shape[1] // n_ctx
    Greeting().ring("ctx").ring("shard").wait()

    def columns(ref):
        return lambda d: ref.at[:, pl.ds(pl.multiple_of(d * cols, HEAD), cols)]

    def place(i):
        stop = packed_mid.shape[2] if i == 3 else (i + 1) * cols
        return lambda d, k: packed_mid.at[d, :, i * cols : stop]

    sources = [columns(w_query), columns(w_key), columns(w_value), whole_of(small)]
    swaps = [
        Direct("ctx", source, place(i), ex_send.at[i], ex_recv.at[i])
        for i, source in enumerate(sources)
    ]
    spread = Direct(
        "shard", whole_of(packed_mid), lambda d, k: packed_all.at[:, d], pk_send, pk_recv
    )
    pieces = row_pieces(x, x_all, LINE_CHUNKS) + [(w, lambda b: w_all.at[b, shard])]
    line = LineGather(pieces, *line_sems)
    at = line.line
    own = [
        pltpu.make_async_copy(source(ctx), place(i)(ctx, 0), own_sem.at[i])
        for i, source in enumerate(sources)
    ]
    spread_own = pltpu.make_async_copy(packed_mid, packed_all.at[:, shard], own_sem.at[4])
    for swap in swaps:
        swap.start()
    for copy in own:
        copy.start()
    line.start()
    line.hop(0)
    for swap in swaps:
        swap.wait_recv()
    for copy in own:
        copy.wait()
    spread.start()
    spread_own.start()
    for k in range(1, at.n):
        line.hop(k)

    to, origin = ring_peers("shard")

    def row(k, p, sender):
        block = 2 * p + at.core
        return pltpu.make_async_remote_copy(
            src_ref=w_all.at[block, shard],
            dst_ref=w_all.at[block, sender],
            send_sem=w_send.at[k, p],
            recv_sem=w_recv.at[k, p],
            device_id={"shard": to[k]},
            device_id_type=MESH,
        )

    def forward(k, p, core):
        block = w_all.at[2 * p + core, origin[k]]
        return pltpu.make_async_remote_copy(
            src_ref=block,
            dst_ref=block,
            send_sem=f_send.at[k, p],
            recv_sem=f_recv.at[k, p],
            device_id={"ctx": at.partner},
            device_id_type=MESH,
        )

    some = [(k, p) for k in range(1, len(to)) for p in range(at.n)]
    line.own(LINE_CHUNKS).wait()
    for k, p in some:
        row(k, p, shard).start()
    for k, p in some:
        row(k, p, origin[k]).wait_recv()
        forward(k, p, at.core).start()
    line.finish(skip_own=LINE_CHUNKS)
    for k, p in some:
        row(k, p, shard).wait_send()
        forward(k, p, at.core).wait_send()
        forward(k, p, 1 - at.core).wait_recv()
    spread.wait_recv()
    for direct in (*swaps, spread):
        direct.wait_send()
    spread_own.wait()


def exchange_kernel(axis, x, o, own_sem, send, recv):
    me = lax.axis_index(axis)
    Greeting().ring(axis).wait()
    swap = Direct(axis, block_of(x), block_from(o), send, recv)
    swap.start()
    own = pltpu.make_async_copy(x.at[me], o.at[me], own_sem)
    own.start()
    own.wait()
    swap.wait_recv()
    swap.wait_send()


class Pair:
    def __init__(self):
        ctx, half = lax.axis_index("ctx"), lax.axis_size("ctx") // 2
        self.role = lax.div(ctx, half)
        self.peer = ctx + half - 2 * half * self.role

    def copy(self, source, target, send, recv):
        return pltpu.make_async_remote_copy(
            src_ref=source,
            dst_ref=target,
            send_sem=send,
            recv_sem=recv,
            device_id={"ctx": self.peer},
            device_id_type=MESH,
        )


def pair_gather_kernel(x, peaks, o, peaks_all, own_sem, send, recv, pair_send, pair_recv):
    shard, pair = lax.axis_index("shard"), Pair()
    Greeting().ring("shard").pair().wait()
    role = pair.role
    own_rows = Direct(
        "shard", whole_of(x), lambda d, k: o.at[d, role], send.at[0], recv.at[0]
    )
    peer_rows = Direct(
        "shard",
        lambda d: o.at[shard, 1 - role],
        lambda d, k: o.at[d, 1 - role],
        send.at[1],
        recv.at[1],
    )
    tops = Direct("shard", whole_of(peaks), block_from(peaks_all), send.at[2], recv.at[2])
    across = pair.copy(x, o.at[shard, role], pair_send, pair_recv)
    arrive = pair.copy(x, o.at[shard, 1 - role], pair_send, pair_recv)
    across.start()
    own_rows.start()
    tops.start()
    own = [
        pltpu.make_async_copy(x, o.at[shard, role], own_sem.at[0]),
        pltpu.make_async_copy(peaks, peaks_all.at[shard], own_sem.at[1]),
    ]
    for copy in own:
        copy.start()
    arrive.wait_recv()
    peer_rows.start()
    for copy in own:
        copy.wait()
    across.wait_send()
    for direct in (own_rows, peer_rows, tops):
        direct.wait_recv()
        direct.wait_send()


class PairReduce:
    def __init__(self, x, o, buf, part, peer, send, recv, pair_send, pair_recv):
        self.x, self.o, self.buf, self.part, self.peer = x, o, buf, part, peer
        self.pair = Pair()
        theirs, mine = 1 - self.pair.role, self.pair.role
        self.first = Direct(
            "shard",
            lambda d: x.at[d, theirs],
            lambda d, k: buf.at[0, k - 1],
            send.at[0],
            recv.at[0],
        )
        self.second = Direct(
            "shard", lambda d: x.at[d, mine], lambda d, k: buf.at[1, k - 1], send.at[1], recv.at[1]
        )
        self.across = self.pair.copy(part, peer, pair_send, pair_recv)

    def start(self):
        self.first.start()
        self.second.start()

    def add_up(self, half, role, o, more=None):
        x, buf, shard = self.x, self.buf, self.first.me
        rows = x.shape[2]
        step = 8 if rows % 32 else 32

        @pl.loop(0, rows // step)
        def _(j):
            at = pl.ds(pl.multiple_of(j * step, step), step)
            total = x[shard, role, at].astype(f32)
            for k in range(buf.shape[1]):
                total = total + buf[half, k, at].astype(f32)
            if more is not None:
                total = total + more[at].astype(f32)
            o[at] = total.astype(o.dtype)

    def turn(self):
        self.first.wait_recv()
        self.add_up(0, 1 - self.pair.role, self.part)
        self.across.start()

    def finish(self):
        self.second.wait_recv()
        self.across.wait_recv()
        self.add_up(1, self.pair.role, self.o, self.peer)
        self.across.wait_send()
        self.first.wait_send()
        self.second.wait_send()


def pair_reduce_scratch(n_shard, x):
    sem = pltpu.SemaphoreType.DMA
    return [
        pltpu.VMEM((2, n_shard - 1, *x.shape[2:]), x.dtype),
        pltpu.VMEM(x.shape[2:], x.dtype),
        pltpu.VMEM(x.shape[2:], x.dtype),
        sem((2, n_shard)),
        sem((2, n_shard)),
        sem,
        sem,
    ]


def pair_reduce_kernel(count, *refs):
    ins, outs, rest = refs[:count], refs[count : 2 * count], refs[2 * count :]
    Greeting().ring("shard").pair().wait()
    all_of = [PairReduce(ins[i], outs[i], *rest[7 * i : 7 * i + 7]) for i in range(count)]
    for one in all_of:
        one.start()
    for one in all_of:
        one.turn()
    for one in all_of:
        one.finish()


def many_sum_kernel(axis, x, o, buf, send, recv):
    Greeting().ring(axis).wait()
    direct = Direct(axis, whole_of(x), buffer_of(buf), send, recv)
    direct.start()
    direct.wait_recv()
    total = x[...]
    for k in range(buf.shape[0]):
        total = total + buf[k]
    o[...] = total
    direct.wait_send()


def middle_kernel(x, y, x_all, y_sum, *rest):
    Greeting().ring("ctx").ring("shard").wait()
    returns = PairReduce(y, y_sum, *rest[:7])
    line = LineGather(row_pieces(x, x_all, LINE_CHUNKS), *rest[7:])
    returns.start()
    line.start()
    for k in range(line.line.n):
        line.hop(k)
    returns.turn()
    returns.finish()
    line.finish()


def end_kernel(
    x, wide, out, x_sum, wide_all, out_sum, wide_buf, out_buf, wide_sum,
    own_sem, wide_send, wide_recv, out_send, out_recv, swap_send, swap_recv, *line_refs,
):
    ctx = lax.axis_index("ctx")
    Greeting().ring("ctx").ring("shard").wait()
    wides = Direct("shard", block_of(wide), buffer_of(wide_buf), wide_send, wide_recv)
    outs = Direct("shard", block_of(out), buffer_of(out_buf), out_send, out_recv)
    swap = Direct("ctx", block_of(wide_sum), block_from(wide_all), swap_send, swap_recv)
    line = LineReduce(LINE_CHUNKS, x, x_sum, *line_refs)
    line.start()
    wides.start()
    outs.start()
    line.pass_on()
    wides.wait_recv()
    for b in range(lax.axis_size("ctx")):
        rows = wide_sum.shape[1]
        total = wide[wides.me, b * rows : (b + 1) * rows].astype(f32)
        for k in range(wide_buf.shape[0]):
            total = total + wide_buf[k, b * rows : (b + 1) * rows].astype(f32)
        wide_sum[b] = total.astype(bf16)
    swap.start()
    own = pltpu.make_async_copy(wide_sum.at[ctx], wide_all.at[ctx], own_sem)
    own.start()
    outs.wait_recv()
    add_up(out, out_buf, out_sum, outs.me)
    line.finish()
    own.wait()
    swap.wait_recv()
    for direct in (swap, wides, outs):
        direct.wait_send()


def remote_params(collective_id, megabytes):
    return pltpu.CompilerParams(
        collective_id=collective_id, has_side_effects=True, vmem_limit_bytes=megabytes << 20
    )


LINE_CHUNKS = 4


def start_call(collective_id, x, w, w_query, w_key, w_value, small):
    n_ctx, n_shard = lax.axis_size("ctx"), lax.axis_size("shard")
    n = n_ctx // 2
    packed = (w.shape[0], 3 * w.shape[1] // n_ctx + small.shape[1])
    sem = pltpu.SemaphoreType.DMA
    return pl.pallas_call(
        start_kernel,
        out_shape=[
            jax.ShapeDtypeStruct((n_ctx, *x.shape), bf16),
            jax.ShapeDtypeStruct((n_ctx, n_shard, *w.shape), bf16),
            jax.ShapeDtypeStruct((n_ctx, *packed), bf16),
            jax.ShapeDtypeStruct((n_ctx, n_shard, *packed), bf16),
        ],
        in_specs=[ANY] * 6,
        out_specs=[ANY] * 4,
        scratch_shapes=[sem((5,)), sem((4, n_ctx)), sem((4, n_ctx))]
        + [sem((n_shard,))] * 2
        + [sem((n_shard, n))] * 4
        + line_gather_scratch(n, LINE_CHUNKS + 1),
        compiler_params=remote_params(collective_id, 8),
    )(x, w, w_query, w_key, w_value, small)


def exchange(axis, collective_id, x):
    n = lax.axis_size(axis)
    sem = pltpu.SemaphoreType.DMA
    return pl.pallas_call(
        functools.partial(exchange_kernel, axis),
        out_shape=jax.ShapeDtypeStruct(x.shape, x.dtype),
        in_specs=[ANY],
        out_specs=ANY,
        scratch_shapes=[sem, sem((n,)), sem((n,))],
        compiler_params=remote_params(collective_id, 8),
    )(x)


def pair_gather(collective_id, x, peaks):
    n = lax.axis_size("shard")
    sem = pltpu.SemaphoreType.DMA
    return pl.pallas_call(
        pair_gather_kernel,
        out_shape=[
            jax.ShapeDtypeStruct((n, 2, *x.shape), x.dtype),
            jax.ShapeDtypeStruct((n, *peaks.shape), peaks.dtype),
        ],
        in_specs=[ANY] * 2,
        out_specs=[ANY] * 2,
        scratch_shapes=[sem((2,)), sem((3, n)), sem((3, n)), sem, sem],
        compiler_params=remote_params(collective_id, 8),
    )(x, peaks)


def pair_reduce(collective_id, *arrays):
    n = lax.axis_size("shard")
    return pl.pallas_call(
        functools.partial(pair_reduce_kernel, len(arrays)),
        out_shape=[jax.ShapeDtypeStruct(a.shape[2:], f32) for a in arrays],
        in_specs=[VMEM] * len(arrays),
        out_specs=[VMEM] * len(arrays),
        scratch_shapes=sum((pair_reduce_scratch(n, a) for a in arrays), []),
        compiler_params=remote_params(collective_id, 40),
    )(*arrays)


def many_sum(axis, collective_id, x):
    n = lax.axis_size(axis)
    sem = pltpu.SemaphoreType.DMA
    return pl.pallas_call(
        functools.partial(many_sum_kernel, axis),
        out_shape=jax.ShapeDtypeStruct(x.shape, x.dtype),
        in_specs=[VMEM],
        out_specs=VMEM,
        scratch_shapes=[pltpu.VMEM((n - 1, *x.shape), x.dtype), sem((n,)), sem((n,))],
        compiler_params=remote_params(collective_id, 8),
    )(x)


def middle_call(collective_id, x, y):
    n_ctx, n_shard = lax.axis_size("ctx"), lax.axis_size("shard")
    return pl.pallas_call(
        middle_kernel,
        out_shape=[
            jax.ShapeDtypeStruct((n_ctx, *x.shape), x.dtype),
            jax.ShapeDtypeStruct(y.shape[2:], f32),
        ],
        in_specs=[ANY, VMEM],
        out_specs=[ANY, VMEM],
        scratch_shapes=pair_reduce_scratch(n_shard, y)
        + line_gather_scratch(n_ctx // 2, LINE_CHUNKS),
        compiler_params=remote_params(collective_id, 40),
    )(x, y)


def end_call(collective_id, x, wide, out):
    n_ctx, rows, width = x.shape
    n_shard = lax.axis_size("shard")
    n = n_ctx // 2
    wide_rows, wide_cols = wide.shape[1] // n_ctx, wide.shape[2]
    sem = pltpu.SemaphoreType.DMA
    return pl.pallas_call(
        end_kernel,
        out_shape=[
            jax.ShapeDtypeStruct((rows, width), f32),
            jax.ShapeDtypeStruct((n_ctx, wide_rows, wide_cols), bf16),
            jax.ShapeDtypeStruct(out.shape[1:], f32),
        ],
        in_specs=[VMEM] * 3,
        out_specs=[VMEM] * 3,
        scratch_shapes=[
            pltpu.VMEM((n_shard - 1, *wide.shape[1:]), bf16),
            pltpu.VMEM((n_shard - 1, *out.shape[1:]), bf16),
            pltpu.VMEM((n_ctx, wide_rows, wide_cols), bf16),
            sem,
        ]
        + [sem((n_shard,))] * 4
        + [sem((n_ctx,))] * 2
        + [pltpu.VMEM((n, rows, width), bf16)] * 4
        + [sem((n, LINE_CHUNKS))] * 5,
        compiler_params=remote_params(collective_id, 48),
    )(x, wide, out)


def per_device(
    tokens,
    doc_ids,
    routes,
    attn_gain,
    w_query,
    w_key,
    w_value,
    query_gain,
    key_gain,
    w_out,
    ffn_gain,
    w_router,
    w_gate,
    w_up,
    w_down,
    clip_threshold,
    cotangent,
):
    both = ("ctx", "shard")
    n_ctx, n_shard = lax.axis_size("ctx"), lax.axis_size("shard")
    ctx, shard = lax.axis_index("ctx"), lax.axis_index("shard")
    x_own = tokens[0]
    rows, width = x_own.shape
    part = w_query.shape[0]
    cols = width // n_ctx
    heads = cols // HEAD
    count = rows * n_ctx
    local = w_gate.shape[0]
    experts = local * n_shard

    top = routes.shape[2]
    spare = jnp.zeros((part, LANES - 4 - experts - rows // part * (1 + top)), bf16)
    small = jnp.concatenate(
        [
            jnp.stack([attn_gain, query_gain, key_gain, ffn_gain], axis=1),
            w_router,
            doc_ids.reshape(part, rows // part).astype(bf16),
            routes.reshape(part, rows // part * top).astype(bf16),
            spare,
        ],
        axis=1,
    )
    grad_own = cotangent[0]
    x_all, out_w, _, packed = start_call(
        1, x_own, w_out, w_query, w_key, w_value, small
    )
    x_all = x_all.reshape(count, width)
    out_w = out_w.reshape(width, width)
    weights = packed[..., : 3 * cols].reshape(width, 3 * cols)
    small_all = packed[..., 3 * cols :]
    out_w_own = lax.dynamic_slice_in_dim(out_w, ctx * cols, cols, 0)
    gains = small_all[..., : 4 + experts].reshape(width, 4 + experts)
    gain_attn, gain_query, gain_key, gain_ffn = (gains[:, i].astype(f32) for i in range(4))
    router_w = gains[:, 4:]
    gain_query = lax.dynamic_slice_in_dim(gain_query, ctx * cols, cols)
    gain_key = lax.dynamic_slice_in_dim(gain_key, ctx * cols, cols)
    tail = small_all[..., 4 + experts :].astype(jnp.int32)
    docs = lax.dynamic_index_in_dim(tail[..., : rows // part], shard, 1, False).reshape(count)
    span = n_ctx // 2
    role = lax.div(ctx, span)
    routes_all = tail[..., rows // part : rows // part * (1 + top)].reshape(
        n_ctx, n_shard, rows, top
    )
    routes_all = jnp.stack(
        [lax.dynamic_index_in_dim(routes_all, ctx + span * (r - role), 0, False) for r in (0, 1)],
        axis=1,
    ).reshape(2 * n_shard * rows, top)

    def swap(u):
        both = lax.all_gather(
            u, "ctx", axis=0, axis_index_groups=[[i, i + span] for i in range(span)]
        )
        return lax.dynamic_index_in_dim(both, 1 - role, 0, False)

    def in_order(mine, theirs):
        return jnp.where(role == 0, jnp.stack([mine, theirs]), jnp.stack([theirs, mine]))

    half = local // 2
    ff = w_gate.shape[2]
    own_w = jnp.concatenate([w_gate, w_up, w_down.transpose(0, 2, 1)], axis=2)
    keep_w = lax.dynamic_slice_in_dim(own_w, role * half, half, 0)
    give_w = lax.dynamic_slice_in_dim(own_w, (1 - role) * half, half, 0)
    spans = [list(range(r * span, (r + 1) * span)) for r in (0, 1)]
    early = [swap(give_w[e]) for e in range(half)] + [swap(grad_own)]
    x_all, early[0], early[-1] = lax.optimization_barrier((x_all, early[0], early[-1]))
    expert_w = [
        lax.all_gather(
            in_order(keep_w[e], early[e]),
            "ctx",
            axis=1,
            tiled=True,
            axis_index_groups=spans,
        ).reshape(width, 3 * ff)
        for e in range(half)
    ]

    grad_all = lax.all_gather(in_order(grad_own, early[-1]), "shard", axis=0, tiled=False)
    grad_all = grad_all.reshape(2 * n_shard * rows, width)

    x_wide = x_all.astype(f32)
    inverse_one = inverse_rms(x_wide)
    hidden_one = (x_wide * inverse_one * gain_attn).astype(bf16)
    linear = dot(hidden_one, weights)
    query_lin, key_lin = linear[:, :cols], linear[:, cols : 2 * cols]
    value = linear[:, 2 * cols :].astype(bf16)
    squares = jnp.stack(
        [jnp.sum(query_lin * query_lin, axis=1), jnp.sum(key_lin * key_lin, axis=1)]
    )
    squares = many_sum("ctx", 6, squares)
    inverse_qk = lax.rsqrt(squares / width + norm_eps)
    inverse_q, inverse_k = inverse_qk[0][:, None], inverse_qk[1][:, None]
    cosine, sine = rope_tables(count)
    query_n, key_n = query_lin * inverse_q, key_lin * inverse_k
    query = rotate(query_n * gain_query, cosine, sine).astype(bf16)
    key = rotate(key_n * gain_key, cosine, sine).astype(bf16)
    mixed, log_total, peaks = attend_forward(query, key, value, docs)
    x_f = x_own.astype(f32)
    mixed_own = exchange("ctx", 2, mixed.reshape(n_ctx, rows, cols))
    mixed_own = mixed_own.transpose(1, 0, 2).reshape(rows, width)
    after = x_f + dot(mixed_own, out_w)
    inverse_two = inverse_rms(after)
    normed_two = after * inverse_two
    hidden_two = (normed_two * gain_ffn).astype(bf16)

    hidden_all, peaks = pair_gather(3, hidden_two, peaks)
    hidden_all = hidden_all.reshape(2 * n_shard * rows, width)
    peaks = jnp.max(peaks, axis=0)[:, 0, 0]
    logits = dot(hidden_all, router_w)
    named = jnp.any(routes_all[:, :, None] == jnp.arange(experts)[None, None, :], axis=1)
    probs = jax.nn.softmax(logits, axis=1)
    selected = jnp.where(named, probs, 0.0)
    selected_sum = jnp.sum(selected, axis=1, keepdims=True)
    gates = selected / selected_sum
    first = shard * local + role * half
    gates_own = lax.dynamic_slice_in_dim(gates, first, half, 1)
    named_own = lax.dynamic_slice_in_dim(named, first, half, 1)
    grad_wide = grad_all.astype(f32)
    moe_part = jnp.zeros(grad_all.shape, f32)
    back_part = jnp.zeros(grad_all.shape, f32)
    grad_gates, expert_grads = [], []
    for e in range(half):
        wide, down = expert_w[e][:, : 2 * ff], expert_w[e][:, 2 * ff :]
        gate_col = gates_own[:, e : e + 1]
        hidden = dot(hidden_all, wide)
        gate_h, up_h = hidden[:, :ff], hidden[:, ff:]
        sig = jax.nn.sigmoid(gate_h)
        silu = gate_h * sig
        act = (silu * up_h).astype(bf16)
        result = contract_cols(act, down).astype(bf16).astype(f32)
        moe_part = moe_part + gate_col * result
        grad_gates.append(
            jnp.where(named_own[:, e], jnp.sum(grad_wide * result, axis=1), 0.0)
        )
        grad_y = (gate_col * grad_wide).astype(bf16)
        grad_act = dot(grad_y, down)
        grad_h = jnp.concatenate(
            [grad_act * up_h * sig * (1.0 + gate_h * (1.0 - sig)), grad_act * silu], axis=1
        ).astype(bf16)
        back_part = back_part + contract_cols(grad_h, wide).astype(bf16).astype(f32)
        grad_w = [
            contract_rows(hidden_all, grad_h).astype(bf16),
            contract_rows(grad_y, act).astype(bf16),
        ]
        hidden_all, back_part, grad_w = lax.optimization_barrier((hidden_all, back_part, grad_w))
        expert_grads.append(
            [
                lax.psum_scatter(
                    u.reshape(2, width // 2, -1),
                    "ctx",
                    scatter_dimension=1,
                    tiled=True,
                    axis_index_groups=spans,
                )
                for u in grad_w
            ]
        )
    slots = jnp.stack(grad_gates).reshape(half, n_shard, 2, rows).transpose(1, 2, 0, 3)
    grad_gates = lax.dynamic_update_slice_in_dim(
        jnp.zeros((n_shard, 2, experts, rows), f32), slots, first, 2
    )
    back_sum, grad_gates = pair_reduce(
        4, back_part.astype(bf16).reshape(n_shard, 2, rows, width), grad_gates
    )
    grad_gates = grad_gates.T
    def own_rows(u):
        return lax.dynamic_slice_in_dim(u, (2 * shard + role) * rows, rows, 0)

    gates_t, probs_t, named_t, sum_t = map(own_rows, (gates, probs, named, selected_sum))
    grad_selected = (
        grad_gates - jnp.sum(gates_t * grad_gates, axis=1, keepdims=True)
    ) / sum_t
    grad_probs = jnp.where(named_t, grad_selected, 0.0)
    grad_logits = (
        probs_t * (grad_probs - jnp.sum(probs_t * grad_probs, axis=1, keepdims=True))
    ).astype(bf16)
    grad_router = contract_rows(hidden_two, grad_logits)
    grad_hidden = back_sum + contract_cols(grad_logits, router_w)
    grad_gain_ffn = jnp.sum(grad_hidden * normed_two, axis=0)
    scaled_two = grad_hidden * gain_ffn
    grad_after = grad_own.astype(f32) + inverse_two * (
        scaled_two - normed_two * jnp.mean(scaled_two * normed_two, axis=1, keepdims=True)
    )

    moe_part = moe_part.astype(bf16).reshape(n_shard, 2, rows, width)
    grad_attn, moe_sum = middle_call(5, grad_after.astype(bf16), moe_part)
    grad_attn = grad_attn.reshape(count, width)
    output = (after + moe_sum).astype(bf16)
    grad_mixed = contract_cols(grad_attn, out_w_own).astype(bf16)
    grad_out_w = contract_rows(mixed, grad_attn)
    grad_query_rot, grad_key_rot, grad_value = attend_backward(
        query, key, value, docs, log_total, grad_mixed
    )
    grad_query_rot, expert_grads = lax.optimization_barrier((grad_query_rot, expert_grads))
    kept = [[lax.dynamic_index_in_dim(u, role, 0, False) for u in sums] for sums in expert_grads]
    peers = swap(
        jnp.stack(
            [
                jnp.concatenate(
                    [lax.dynamic_index_in_dim(u, 1 - role, 0, False) for u in sums], axis=1
                )
                for sums in expert_grads
            ]
        )
    )
    peers = [(peer[:, : 2 * ff], peer[:, 2 * ff :]) for peer in peers]
    both_halves = [
        in_order(jnp.stack([k[i] for k in kept]), jnp.stack([p[i] for p in peers]))
        .reshape(local, width // n_ctx, -1)
        .astype(f32)
        for i in (0, 1)
    ]
    grad_query_n = rotate(grad_query_rot, cosine, -sine)
    grad_key_n = rotate(grad_key_rot, cosine, -sine)
    grad_gain_query = jnp.sum(grad_query_n * query_n, axis=0)
    grad_gain_key = jnp.sum(grad_key_n * key_n, axis=0)
    scaled_q, scaled_k = grad_query_n * gain_query, grad_key_n * gain_key
    peak_row = lax.dynamic_update_slice_in_dim(jnp.zeros((count,), f32), peaks, ctx * heads, 0)
    inner = jnp.stack(
        [jnp.sum(scaled_q * query_n, axis=1), jnp.sum(scaled_k * key_n, axis=1), peak_row]
    )
    inner = many_sum("ctx", 7, inner)
    peak_all = inner[2, :HEADS]
    inner = inner / width
    grad_linear = jnp.concatenate(
        [
            inverse_q * (scaled_q - query_n * inner[0][:, None]),
            inverse_k * (scaled_k - key_n * inner[1][:, None]),
            grad_value,
        ],
        axis=1,
    ).astype(bf16)
    grad_weights = contract_rows(hidden_one, grad_linear)
    hidden_part = contract_cols(grad_linear, weights)
    grad_gain_attn = jnp.sum(hidden_part * (x_wide * inverse_one), axis=0)
    grad_small = jnp.concatenate(
        [jnp.stack([grad_gain_attn, grad_gain_ffn], axis=1), grad_router], axis=1
    )
    grad_small = jnp.pad(grad_small, ((0, 0), (0, LANES - 2 - experts)))
    grad_weights = (
        jnp.concatenate([grad_weights, grad_small], axis=1)
        .astype(bf16)
        .reshape(n_ctx, n_shard, part, 3 * cols + LANES)
        .transpose(1, 0, 2, 3)
        .reshape(n_shard, n_ctx * part, 3 * cols + LANES)
    )
    grad_gain_qk = jnp.pad(
        jnp.stack([grad_gain_query, grad_gain_key], axis=1), ((0, 0), (0, LANES - 2))
    )
    grad_out_w = (
        jnp.concatenate([grad_out_w, grad_gain_qk], axis=1)
        .astype(bf16)
        .reshape(n_shard, part, width + LANES)
    )
    grad_hidden_one, grad_weights, grad_out_w = end_call(
        8, hidden_part.astype(bf16).reshape(n_ctx, rows, width), grad_weights, grad_out_w
    )
    grad_weights = grad_weights.astype(f32)
    grad_small = jnp.sum(grad_weights[..., 3 * cols :], axis=0)
    grad_weights = (
        grad_weights[..., : 3 * cols]
        .reshape(n_ctx, part, 3, cols)
        .transpose(2, 1, 0, 3)
        .reshape(3, part, width)
    )
    inverse_own = inverse_rms(x_f)
    normed_own = x_f * inverse_own
    scaled_one = grad_hidden_one * gain_attn
    grad_inputs = grad_after + inverse_own * (
        scaled_one - normed_own * jnp.mean(scaled_one * normed_own, axis=1, keepdims=True)
    )

    factors = jnp.sqrt(clip_threshold / jnp.maximum(peak_all, clip_threshold))
    col_scale = jnp.repeat(factors, HEAD)
    query_clipped = (w_query.astype(f32) * col_scale[None, :]).astype(bf16)
    key_clipped = (w_key.astype(f32) * col_scale[None, :]).astype(bf16)
    return (
        output[None],
        grad_inputs[None],
        grad_small[:, 0],
        grad_weights[0],
        grad_weights[1],
        grad_weights[2],
        grad_out_w[:, width],
        grad_out_w[:, width + 1],
        grad_out_w[:, :width],
        grad_small[:, 1],
        grad_small[:, 2 : 2 + experts],
        both_halves[0][..., :ff],
        both_halves[0][..., ff:],
        both_halves[1].transpose(0, 2, 1),
        query_clipped,
        key_clipped,
        factors,
    )


def solution(mesh):
    both = ("ctx", "shard")
    return jax.shard_map(
        per_device,
        mesh=mesh,
        in_specs=(
            P("shard", "ctx", None),
            P("shard", "ctx"),
            P("shard", "ctx", None),
            P(both),
            P(both, None),
            P(both, None),
            P(both, None),
            P(both),
            P(both),
            P(both, None),
            P(both),
            P(both, None),
            P("shard", "ctx", None),
            P("shard", "ctx", None),
            P("shard", None, "ctx"),
            P(),
            P("shard", "ctx", None),
        ),
        out_specs=(
            P("shard", "ctx", None),
            P("shard", "ctx", None),
            P(both),
            P(both, None),
            P(both, None),
            P(both, None),
            P(both),
            P(both),
            P(both, None),
            P(both),
            P(both, None),
            P("shard", "ctx", None),
            P("shard", "ctx", None),
            P("shard", None, "ctx"),
            P(both, None),
            P(both, None),
            P(),
        ),
        check_vma=False,
    )
```

```python
import functools

import jax
import jax.numpy as jnp
from jax import lax
from jax.experimental import pallas as pl
from jax.experimental.pallas import tpu as pltpu
from jax.sharding import PartitionSpec as P

HEADS = 16
HEAD = 128
SCALE = HEAD ** (-0.5)
Q_BLOCK = 256
LANES = 128

norm_eps = 1e-06
rope_base = 10000.0
f32 = jnp.float32
bf16 = jnp.bfloat16


def dot(a, b):
    return jnp.dot(a, b, preferred_element_type=f32)


def contract_rows(a, b):
    return lax.dot_general(a, b, (((0,), (0,)), ((), ())), preferred_element_type=f32)


def contract_cols(a, b):
    return lax.dot_general(a, b, (((1,), (1,)), ((), ())), preferred_element_type=f32)


def inverse_rms(values):
    return lax.rsqrt(jnp.mean(values * values, axis=-1, keepdims=True) + norm_eps)


def rope_tables(count):
    half = HEAD // 2
    freq = rope_base ** (-jnp.arange(half).astype(f32) / half)
    angles = jnp.arange(count).astype(f32)[:, None] * freq[None, :]
    return jnp.cos(angles), jnp.sin(angles)


def rotate(values, cosine, sine):
    parts = []
    for col in range(0, values.shape[1], HEAD):
        a = values[:, col : col + HEAD // 2]
        b = values[:, col + HEAD // 2 : col + HEAD]
        parts += [a * cosine - b * sine, b * cosine + a * sine]
    return jnp.concatenate(parts, axis=1)


def attend_forward_kernel(q_ref, k_ref, v_ref, doc_q_ref, doc_k_ref, o_ref, lse_ref, peak_ref):
    s = SCALE * contract_cols(q_ref[...], k_ref[...])
    s = jnp.where(doc_q_ref[...] == doc_k_ref[...], s, -1e30)
    top = jnp.max(s, axis=1, keepdims=True)
    e = jnp.exp(s - top)
    total = jnp.sum(e, axis=1, keepdims=True)
    p = (e * (1.0 / total)).astype(bf16)
    o_ref[...] = dot(p, v_ref[...]).astype(bf16)
    lse_ref[0] = top + jnp.log(total)
    peak = jnp.broadcast_to(jnp.max(top, axis=0, keepdims=True), peak_ref.shape[1:])

    @pl.when(pl.program_id(1) == 0)
    def _():
        peak_ref[0] = peak

    @pl.when(pl.program_id(1) > 0)
    def _():
        peak_ref[0] = jnp.maximum(peak_ref[0], peak)


def attend_backward_kernel(
    q_ref, k_ref, v_ref, doc_q_ref, doc_k_ref, lse_ref, do_ref, dq_ref, dk_ref, dv_ref
):
    q, k, v, do = q_ref[...], k_ref[...], v_ref[...], do_ref[...]
    s = SCALE * contract_cols(q, k)
    p = jnp.where(doc_q_ref[...] == doc_k_ref[...], jnp.exp(s - lse_ref[0]), 0.0)
    dp = contract_cols(do, v)
    inner = jnp.sum(p * dp, axis=1, keepdims=True)
    ds = (p * (dp - inner)).astype(bf16)
    dq_ref[...] = SCALE * dot(ds, k)
    dk = SCALE * contract_rows(ds, q)
    dv = contract_rows(p.astype(bf16), do)

    @pl.when(pl.program_id(1) == 0)
    def _():
        dk_ref[...] = dk
        dv_ref[...] = dv

    @pl.when(pl.program_id(1) > 0)
    def _():
        dk_ref[...] += dk
        dv_ref[...] += dv


def attend_specs(count):
    block = pl.BlockSpec((Q_BLOCK, HEAD), lambda h, i: (i, h))
    whole = pl.BlockSpec((count, HEAD), lambda h, i: (0, h))
    doc_q = pl.BlockSpec((Q_BLOCK, 1), lambda h, i: (i, 0))
    doc_k = pl.BlockSpec((1, count), lambda h, i: (0, 0))
    lse = pl.BlockSpec((1, Q_BLOCK, 1), lambda h, i: (h, i, 0))
    return block, whole, doc_q, doc_k, lse


def attend_forward(q, k, v, docs):
    count, width = q.shape
    heads = width // HEAD
    block, whole, doc_q, doc_k, lse = attend_specs(count)
    return pl.pallas_call(
        attend_forward_kernel,
        grid=(heads, count // Q_BLOCK),
        in_specs=[block, whole, whole, doc_q, doc_k],
        out_specs=[block, lse, pl.BlockSpec((1, 8, 128), lambda h, i: (h, 0, 0))],
        out_shape=[
            jax.ShapeDtypeStruct((count, width), bf16),
            jax.ShapeDtypeStruct((heads, count, 1), f32),
            jax.ShapeDtypeStruct((heads, 8, 128), f32),
        ],
        compiler_params=pltpu.CompilerParams(vmem_limit_bytes=48 << 20),
        cost_estimate=pl.CostEstimate(
            flops=4 * count * count * width,
            transcendentals=heads * count * count,
            bytes_accessed=8 * count * width,
        ),
    )(q, k, v, docs[:, None], docs[None, :])


def attend_backward(q, k, v, docs, log_total, grad):
    count, width = q.shape
    heads = width // HEAD
    block, whole, doc_q, doc_k, lse = attend_specs(count)
    return pl.pallas_call(
        attend_backward_kernel,
        grid=(heads, count // Q_BLOCK),
        in_specs=[block, whole, whole, doc_q, doc_k, lse, block],
        out_specs=[block, whole, whole],
        out_shape=[jax.ShapeDtypeStruct((count, width), f32)] * 3,
        compiler_params=pltpu.CompilerParams(vmem_limit_bytes=56 << 20),
        cost_estimate=pl.CostEstimate(
            flops=10 * count * count * width,
            transcendentals=heads * count * count,
            bytes_accessed=20 * count * width,
        ),
    )(q, k, v, docs[:, None], docs[None, :], log_total, grad)


MESH = pl.DeviceIdType.MESH
ANY = pl.BlockSpec(memory_space=pl.ANY)
VMEM = pl.BlockSpec(memory_space=pltpu.VMEM)


def ring_peers(axis):
    n, me = lax.axis_size(axis), lax.axis_index(axis)
    return [lax.rem(me + k, n) for k in range(n)], [lax.rem(me + n - k, n) for k in range(n)]


class Greeting:
    def __init__(self):
        self.barrier, self.total = pltpu.get_barrier_semaphore(), 0

    def ring(self, axis):
        to, _ = ring_peers(axis)
        for peer in to[1:]:
            pl.semaphore_signal(
                self.barrier, inc=1, device_id={axis: peer}, device_id_type=MESH
            )
        self.total = self.total + len(to) - 1
        return self

    def line(self):
        line = Line()
        for there, peer in (
            (line.place >= 0, line.partner),
            (line.not_last, line.me + 2),
            (line.not_first, line.me - 2),
        ):

            @pl.when(there)
            def _():
                pl.semaphore_signal(
                    self.barrier, inc=1, device_id={"ctx": peer}, device_id_type=MESH
                )

            self.total = self.total + there.astype(jnp.int32)
        return self

    def pair(self):
        pl.semaphore_signal(
            self.barrier, inc=1, device_id={"ctx": Pair().peer}, device_id_type=MESH
        )
        self.total = self.total + 1
        return self

    def wait(self):
        pl.semaphore_wait(self.barrier, self.total)


class Line:
    def __init__(self):
        self.n, self.me = lax.axis_size("ctx") // 2, lax.axis_index("ctx")
        self.place, self.core = lax.div(self.me, 2), lax.rem(self.me, 2)
        self.partner = self.me + 1 - 2 * self.core
        self.not_first, self.not_last = self.place > 0, self.place < self.n - 1


class Direct:
    def __init__(self, axis, source, target, send, recv):
        self.axis, self.source, self.target = axis, source, target
        self.send, self.recv = send, recv
        self.me = lax.axis_index(axis)
        self.to, self.origin = ring_peers(axis)

    def copy(self, k, sender):
        return pltpu.make_async_remote_copy(
            src_ref=self.source(self.to[k]),
            dst_ref=self.target(sender, k),
            send_sem=self.send.at[k],
            recv_sem=self.recv.at[k],
            device_id={self.axis: self.to[k]},
            device_id_type=MESH,
        )

    def start(self):
        for k in range(1, len(self.to)):
            self.copy(k, self.me).start()

    def wait_recv(self):
        for k in range(1, len(self.to)):
            self.copy(k, self.origin[k]).wait_recv()

    def wait_send(self):
        for k in range(1, len(self.to)):
            self.copy(k, self.me).wait_send()


class LineGather:
    def __init__(self, pieces, own_sem, send_r, send_l, send_p, recv_r, recv_l, recv_p):
        self.line, self.pieces, self.own_sem = Line(), pieces, own_sem
        self.send_r, self.send_l, self.send_p = send_r, send_l, send_p
        self.recv_r, self.recv_l, self.recv_p = recv_r, recv_l, recv_p

    def own(self, c):
        source, target = self.pieces[c]
        return pltpu.make_async_copy(source, target(self.line.me), self.own_sem.at[c])

    def copy(self, block, k, c, target_device, send, recv):
        source, target = self.pieces[c]
        return pltpu.make_async_remote_copy(
            src_ref=source if k == 0 else target(block),
            dst_ref=target(block),
            send_sem=send,
            recv_sem=recv,
            device_id={"ctx": target_device},
            device_id_type=MESH,
        )

    def right(self, k, c):
        me = self.line.me
        return self.copy(me - 2 * k, k, c, me + 2, self.send_r.at[k, c], self.recv_r.at[k, c])

    def left(self, k, c):
        me = self.line.me
        return self.copy(me + 2 * k, k, c, me - 2, self.send_l.at[k, c], self.recv_l.at[k, c])

    def across(self, k, c, sign):
        line = self.line
        i = k if sign < 0 else line.n - 1 + k
        return self.copy(
            line.me + sign * 2 * k, k, c, line.partner, self.send_p.at[i, c], self.recv_p.at[i, c]
        )

    def arrived(self, block, c, recv):
        source, target = self.pieces[c]
        pltpu.make_async_remote_copy(
            src_ref=source,
            dst_ref=target(block),
            send_sem=recv,
            recv_sem=recv,
            device_id={"ctx": self.line.partner},
            device_id_type=MESH,
        ).wait_recv()

    def start(self):
        for c in range(len(self.pieces)):
            self.own(c).start()

    def hop(self, k):
        line = self.line
        for c in range(len(self.pieces)):

            @pl.when(line.place >= k)
            def _():
                if k:
                    self.arrived(line.me - 2 * k, c, self.recv_r.at[k - 1, c])

                @pl.when(line.not_last)
                def _():
                    self.right(k, c).start()

                self.across(k, c, -1).start()

            @pl.when(line.place + k <= line.n - 1)
            def _():
                if k:
                    self.arrived(line.me + 2 * k, c, self.recv_l.at[k - 1, c])

                @pl.when(line.not_first)
                def _():
                    self.left(k, c).start()

                if k:
                    self.across(k, c, 1).start()

    def finish(self, skip_own=None):
        line = self.line
        for c in range(len(self.pieces)):
            if c != skip_own:
                self.own(c).wait()
        for k in range(line.n):
            for c in range(len(self.pieces)):

                @pl.when(line.place >= k)
                def _():
                    @pl.when(line.not_last)
                    def _():
                        self.right(k, c).wait_send()

                    self.across(k, c, -1).wait_send()
                    self.arrived(line.partner - 2 * k, c, self.recv_p.at[k, c])

                @pl.when(line.place + k <= line.n - 1)
                def _():
                    @pl.when(line.not_first)
                    def _():
                        self.left(k, c).wait_send()

                    if k:
                        self.across(k, c, 1).wait_send()
                        self.arrived(line.partner + 2 * k, c, self.recv_p.at[line.n - 1 + k, c])


def line_gather_scratch(n, pieces):
    sem = pltpu.SemaphoreType.DMA
    one, two = sem((n, pieces)), sem((2 * n - 1, pieces))
    return [sem((pieces,)), one, one, two, one, one, two]


class LineReduce:
    def __init__(
        self, chunks, x, o, pair, from_left, from_right, send_p, recv_p, send_s, recv_r, recv_l
    ):
        self.line, self.chunks = Line(), chunks
        self.x, self.o, self.pair, self.out = x, o, pair, pair
        self.from_left, self.from_right = from_left, from_right
        self.send_p, self.recv_p, self.send_s = send_p, recv_p, send_s
        self.recv_r, self.recv_l = recv_r, recv_l
        self.order = []
        for j in range(self.line.n):
            self.order += [p for p in (self.line.n - 1 - j, j) if p not in self.order]

    def at(self, c):
        rows = self.x.shape[1] // self.chunks
        return pl.ds(c * rows, rows)

    def across(self, p, c):
        line, at = self.line, self.at(c)
        return pltpu.make_async_remote_copy(
            src_ref=self.x.at[2 * p + 1 - line.core, at],
            dst_ref=self.pair.at[p, at],
            send_sem=self.send_p.at[p, c],
            recv_sem=self.recv_p.at[p, c],
            device_id={"ctx": line.partner},
            device_id_type=MESH,
        )

    def along(self, p, c, step, buffer, recv):
        at = self.at(c)
        return pltpu.make_async_remote_copy(
            src_ref=self.out.at[p, at],
            dst_ref=buffer.at[p, at],
            send_sem=self.send_s.at[p, c],
            recv_sem=recv.at[p, c],
            device_id={"ctx": self.line.me + step},
            device_id_type=MESH,
        )

    def right(self, p, c):
        return self.along(p, c, 2, self.from_left, self.recv_r)

    def left(self, p, c):
        return self.along(p, c, -2, self.from_right, self.recv_l)

    def start(self):
        for p in self.order:
            for c in range(self.chunks):
                self.across(p, c).start()

    def both(self, p, c):
        at = self.at(c)
        return self.x[2 * p + self.line.core, at].astype(f32) + self.pair[p, at].astype(f32)

    def pass_on(self):
        line = self.line
        for p in self.order:
            for c in range(self.chunks):
                at = self.at(c)
                self.across(p, c).wait_recv()

                @pl.when(line.place < p)
                def _():
                    @pl.when(line.not_first)
                    def _():
                        self.right(p, c).wait_recv()
                        total = self.both(p, c) + self.from_left[p, at].astype(f32)
                        self.out[p, at] = total.astype(bf16)

                    @pl.when(line.place == 0)
                    def _():
                        self.out[p, at] = self.both(p, c).astype(bf16)

                    self.right(p, c).start()

                @pl.when(line.place > p)
                def _():
                    @pl.when(line.not_last)
                    def _():
                        self.left(p, c).wait_recv()
                        total = self.both(p, c) + self.from_right[p, at].astype(f32)
                        self.out[p, at] = total.astype(bf16)

                    @pl.when(line.place == line.n - 1)
                    def _():
                        self.out[p, at] = self.both(p, c).astype(bf16)

                    self.left(p, c).start()

    def finish(self):
        line = self.line
        for p in range(line.n):
            for c in range(self.chunks):
                at = self.at(c)

                @pl.when(line.place == p)
                def _():
                    self.o[at] = self.both(p, c)
                    if p > 0:
                        self.right(p, c).wait_recv()
                        self.o[at] += self.from_left[p, at].astype(f32)
                    if p < line.n - 1:
                        self.left(p, c).wait_recv()
                        self.o[at] += self.from_right[p, at].astype(f32)

        for p in range(line.n):
            for c in range(self.chunks):
                self.across(p, c).wait_send()

                @pl.when(line.place < p)
                def _():
                    self.right(p, c).wait_send()

                @pl.when(line.place > p)
                def _():
                    self.left(p, c).wait_send()


def add_up(x, buf, o, me):
    rows = x.shape[1]
    step = 8 if rows % 32 else 32

    @pl.loop(0, rows // step)
    def _(j):
        at = pl.ds(pl.multiple_of(j * step, step), step)
        total = x[me, at].astype(f32)
        for k in range(buf.shape[0]):
            total = total + buf[k, at].astype(f32)
        o[at] = total.astype(o.dtype)


def block_of(ref):
    return lambda device: ref.at[device]


def block_from(ref):
    return lambda device, k: ref.at[device]


def whole_of(ref):
    return lambda device: ref


def buffer_of(ref):
    return lambda device, k: ref.at[k - 1]


def row_pieces(source, target, chunks):
    rows = source.shape[0] // chunks
    return [
        (source.at[pl.ds(c * rows, rows)], lambda b, c=c: target.at[b, pl.ds(c * rows, rows)])
        for c in range(chunks)
    ]


def start_kernel(
    x, w, w_query, w_key, w_value, small, cot, x_all, w_all, heads_all, small_all, cot_all,
    heads_mid, small_mid, own_sem, ex_send, ex_recv, sp_send, sp_recv, w_send, w_recv, f_send,
    f_recv, *line_sems,
):
    shard, ctx = lax.axis_index("shard"), lax.axis_index("ctx")
    n_ctx = lax.axis_size("ctx")
    cols = w_query.shape[1] // n_ctx
    Greeting().ring("ctx").ring("shard").wait()

    def columns(ref):
        return lambda d: ref.at[:, pl.ds(pl.multiple_of(d * cols, HEAD), cols)]

    def place(i):
        if i == 3:
            return block_from(small_mid)
        return lambda d, k: heads_mid.at[d, :, i * cols : (i + 1) * cols]

    sources = [columns(w_query), columns(w_key), columns(w_value), whole_of(small)]
    swaps = [
        Direct("ctx", source, place(i), ex_send.at[i], ex_recv.at[i])
        for i, source in enumerate(sources)
    ]

    def by_shard(ref):
        return lambda d, k: ref.at[:, d]

    spreads = [
        Direct("shard", whole_of(heads_mid), by_shard(heads_all), sp_send.at[0], sp_recv.at[0]),
        Direct("shard", whole_of(small_mid), by_shard(small_all), sp_send.at[1], sp_recv.at[1]),
    ]
    other = Direct("shard", whole_of(cot), block_from(cot_all), sp_send.at[2], sp_recv.at[2])
    pieces = row_pieces(x, x_all, LINE_CHUNKS) + [(w, lambda b: w_all.at[b, shard])]
    line = LineGather(pieces, *line_sems)
    at = line.line
    own = [
        pltpu.make_async_copy(source(ctx), place(i)(ctx, 0), own_sem.at[i])
        for i, source in enumerate(sources)
    ]
    later = [
        pltpu.make_async_copy(heads_mid, heads_all.at[:, shard], own_sem.at[4]),
        pltpu.make_async_copy(small_mid, small_all.at[:, shard], own_sem.at[5]),
        pltpu.make_async_copy(cot, cot_all.at[shard], own_sem.at[6]),
    ]
    for swap in swaps:
        swap.start()
    for copy in own:
        copy.start()
    line.start()
    line.hop(0)
    for swap in swaps:
        swap.wait_recv()
    for copy in own:
        copy.wait()
    for one in (*spreads, other, *later):
        one.start()
    for k in range(1, at.n):
        line.hop(k)

    to, origin = ring_peers("shard")

    def row(k, p, sender):
        block = 2 * p + at.core
        return pltpu.make_async_remote_copy(
            src_ref=w_all.at[block, shard],
            dst_ref=w_all.at[block, sender],
            send_sem=w_send.at[k, p],
            recv_sem=w_recv.at[k, p],
            device_id={"shard": to[k]},
            device_id_type=MESH,
        )

    def forward(k, p, core):
        block = w_all.at[2 * p + core, origin[k]]
        return pltpu.make_async_remote_copy(
            src_ref=block,
            dst_ref=block,
            send_sem=f_send.at[k, p],
            recv_sem=f_recv.at[k, p],
            device_id={"ctx": at.partner},
            device_id_type=MESH,
        )

    some = [(k, p) for k in range(1, len(to)) for p in range(at.n)]
    line.own(LINE_CHUNKS).wait()
    for k, p in some:
        row(k, p, shard).start()
    for k, p in some:
        row(k, p, origin[k]).wait_recv()
        forward(k, p, at.core).start()
    line.finish(skip_own=LINE_CHUNKS)
    for k, p in some:
        row(k, p, shard).wait_send()
        forward(k, p, at.core).wait_send()
        forward(k, p, 1 - at.core).wait_recv()
    for direct in (*spreads, other):
        direct.wait_recv()
    for direct in (*swaps, *spreads, other):
        direct.wait_send()
    for copy in later:
        copy.wait()


def exchange_kernel(to_rows, x, o, own_sem, send, recv):
    n, me = lax.axis_size("ctx"), lax.axis_index("ctx")
    cols, rows = (x.shape[1] // n, x.shape[0]) if to_rows else (x.shape[1], o.shape[0])

    def row_block(ref):
        return lambda d, k=0: ref.at[pl.ds(pl.multiple_of(d * rows, rows), rows)]

    def column_block(ref):
        return lambda d, k=0: ref.at[:, pl.ds(pl.multiple_of(d * cols, cols), cols)]

    source, target = (
        (column_block(x), row_block(o)) if to_rows else (row_block(x), column_block(o))
    )
    Greeting().ring("ctx").wait()
    swap = Direct("ctx", source, target, send, recv)
    swap.start()
    own = pltpu.make_async_copy(source(me), target(me), own_sem)
    own.start()
    own.wait()
    swap.wait_recv()
    swap.wait_send()


class Pair:
    def __init__(self):
        ctx, half = lax.axis_index("ctx"), lax.axis_size("ctx") // 2
        self.role = lax.div(ctx, half)
        self.peer = ctx + half - 2 * half * self.role

    def copy(self, source, target, send, recv):
        return pltpu.make_async_remote_copy(
            src_ref=source,
            dst_ref=target,
            send_sem=send,
            recv_sem=recv,
            device_id={"ctx": self.peer},
            device_id_type=MESH,
        )


def pair_gather_kernel(x, peaks, o, peaks_all, own_sem, send, recv, pair_send, pair_recv):
    shard, pair = lax.axis_index("shard"), Pair()
    Greeting().ring("shard").pair().wait()
    own_rows = Direct(
        "shard", whole_of(x), lambda d, k: o.at[0, d], send.at[0], recv.at[0]
    )
    peer_rows = Direct(
        "shard", lambda d: o.at[1, shard], lambda d, k: o.at[1, d], send.at[1], recv.at[1]
    )
    tops = Direct("shard", whole_of(peaks), block_from(peaks_all), send.at[2], recv.at[2])
    across = pair.copy(x, o.at[1, shard], pair_send, pair_recv)
    across.start()
    own_rows.start()
    tops.start()
    own = [
        pltpu.make_async_copy(x, o.at[0, shard], own_sem.at[0]),
        pltpu.make_async_copy(peaks, peaks_all.at[shard], own_sem.at[1]),
    ]
    for copy in own:
        copy.start()
    across.wait_recv()
    peer_rows.start()
    for copy in own:
        copy.wait()
    across.wait_send()
    for direct in (own_rows, peer_rows, tops):
        direct.wait_recv()
        direct.wait_send()


class PairReduce:
    def __init__(self, x, o, buf, part, peer, send, recv, pair_send, pair_recv):
        self.x, self.o, self.buf, self.part, self.peer = x, o, buf, part, peer
        self.pair = Pair()
        self.first = Direct(
            "shard", lambda d: x.at[1, d], lambda d, k: buf.at[1, k - 1], send.at[1], recv.at[1]
        )
        self.second = Direct(
            "shard", lambda d: x.at[0, d], lambda d, k: buf.at[0, k - 1], send.at[0], recv.at[0]
        )
        self.across = self.pair.copy(part, peer, pair_send, pair_recv)

    def start(self):
        self.first.start()
        self.second.start()

    def add_up(self, half, o, more=None):
        x, buf, shard = self.x, self.buf, self.first.me
        rows = x.shape[2]
        step = 8 if rows % 32 else 32

        @pl.loop(0, rows // step)
        def _(j):
            at = pl.ds(pl.multiple_of(j * step, step), step)
            total = x[half, shard, at].astype(f32)
            for k in range(buf.shape[1]):
                total = total + buf[half, k, at].astype(f32)
            if more is not None:
                total = total + more[at].astype(f32)
            o[at] = total.astype(o.dtype)

    def turn(self):
        self.first.wait_recv()
        self.add_up(1, self.part)
        self.across.start()

    def finish(self):
        self.second.wait_recv()
        self.across.wait_recv()
        self.add_up(0, self.o, self.peer)
        self.across.wait_send()
        self.first.wait_send()
        self.second.wait_send()


def pair_reduce_scratch(n_shard, x):
    sem = pltpu.SemaphoreType.DMA
    return [
        pltpu.VMEM((2, n_shard - 1, *x.shape[2:]), x.dtype),
        pltpu.VMEM(x.shape[2:], x.dtype),
        pltpu.VMEM(x.shape[2:], x.dtype),
        sem((2, n_shard)),
        sem((2, n_shard)),
        sem,
        sem,
    ]


def pair_reduce_kernel(count, *refs):
    ins, outs, rest = refs[:count], refs[count : 2 * count], refs[2 * count :]
    Greeting().ring("shard").pair().wait()
    all_of = [PairReduce(ins[i], outs[i], *rest[7 * i : 7 * i + 7]) for i in range(count)]
    for one in all_of:
        one.start()
    for one in all_of:
        one.turn()
    for one in all_of:
        one.finish()


def many_sum_kernel(axis, x, o, buf, send, recv):
    Greeting().ring(axis).wait()
    direct = Direct(axis, whole_of(x), buffer_of(buf), send, recv)
    direct.start()
    direct.wait_recv()
    total = x[...]
    for k in range(buf.shape[0]):
        total = total + buf[k]
    o[...] = total
    direct.wait_send()


def end_kernel(
    x, wide, out, y, x_sum, wide_all, out_sum, y_sum, wide_buf, out_buf, wide_sum,
    own_sem, wide_send, wide_recv, out_send, out_recv, swap_send, swap_recv, *rest,
):
    ctx = lax.axis_index("ctx")
    Greeting().ring("ctx").ring("shard").wait()
    wides = Direct("shard", block_of(wide), buffer_of(wide_buf), wide_send, wide_recv)
    outs = Direct("shard", block_of(out), buffer_of(out_buf), out_send, out_recv)
    swap = Direct("ctx", block_of(wide_sum), block_from(wide_all), swap_send, swap_recv)
    line = LineReduce(LINE_CHUNKS, x, x_sum, *rest[7:])
    returns = PairReduce(y, y_sum, *rest[:7])
    line.start()
    wides.start()
    returns.start()
    outs.start()
    line.pass_on()
    wides.wait_recv()
    for b in range(lax.axis_size("ctx")):
        rows = wide_sum.shape[1]
        total = wide[wides.me, b * rows : (b + 1) * rows].astype(f32)
        for k in range(wide_buf.shape[0]):
            total = total + wide_buf[k, b * rows : (b + 1) * rows].astype(f32)
        wide_sum[b] = total.astype(bf16)
    swap.start()
    own = pltpu.make_async_copy(wide_sum.at[ctx], wide_all.at[ctx], own_sem)
    own.start()
    line.finish()
    returns.turn()
    outs.wait_recv()
    add_up(out, out_buf, out_sum, outs.me)
    returns.finish()
    own.wait()
    swap.wait_recv()
    for direct in (swap, wides, outs):
        direct.wait_send()


def remote_params(collective_id, megabytes):
    return pltpu.CompilerParams(
        collective_id=collective_id, has_side_effects=True, vmem_limit_bytes=megabytes << 20
    )


LINE_CHUNKS = 4


def start_call(collective_id, x, w, w_query, w_key, w_value, small, cot):
    n_ctx, n_shard = lax.axis_size("ctx"), lax.axis_size("shard")
    n = n_ctx // 2
    heads = (w.shape[0], 3 * w.shape[1] // n_ctx)
    sem = pltpu.SemaphoreType.DMA
    return pl.pallas_call(
        start_kernel,
        out_shape=[
            jax.ShapeDtypeStruct((n_ctx, *x.shape), bf16),
            jax.ShapeDtypeStruct((n_ctx, n_shard, *w.shape), bf16),
            jax.ShapeDtypeStruct((n_ctx, n_shard, *heads), bf16),
            jax.ShapeDtypeStruct((n_ctx, n_shard, *small.shape), bf16),
            jax.ShapeDtypeStruct((n_shard, *cot.shape), bf16),
        ],
        in_specs=[ANY] * 7,
        out_specs=[ANY] * 5,
        scratch_shapes=[
            pltpu.VMEM((n_ctx, *heads), bf16),
            pltpu.VMEM((n_ctx, *small.shape), bf16),
            sem((7,)),
            sem((4, n_ctx)),
            sem((4, n_ctx)),
        ]
        + [sem((3, n_shard))] * 2
        + [sem((n_shard, n))] * 4
        + line_gather_scratch(n, LINE_CHUNKS + 1),
        compiler_params=remote_params(collective_id, 8),
    )(x, w, w_query, w_key, w_value, small, cot)


def exchange(collective_id, x, to_rows):
    n = lax.axis_size("ctx")
    shape = (x.shape[0] * n, x.shape[1] // n) if to_rows else (x.shape[0] // n, x.shape[1] * n)
    sem = pltpu.SemaphoreType.DMA
    return pl.pallas_call(
        functools.partial(exchange_kernel, to_rows),
        out_shape=jax.ShapeDtypeStruct(shape, x.dtype),
        in_specs=[ANY],
        out_specs=ANY,
        scratch_shapes=[sem, sem((n,)), sem((n,))],
        compiler_params=remote_params(collective_id, 8),
    )(x)


def pair_gather(collective_id, x, peaks):
    n = lax.axis_size("shard")
    sem = pltpu.SemaphoreType.DMA
    return pl.pallas_call(
        pair_gather_kernel,
        out_shape=[
            jax.ShapeDtypeStruct((2, n, *x.shape), x.dtype),
            jax.ShapeDtypeStruct((n, *peaks.shape), peaks.dtype),
        ],
        in_specs=[ANY] * 2,
        out_specs=[ANY] * 2,
        scratch_shapes=[sem((2,)), sem((3, n)), sem((3, n)), sem, sem],
        compiler_params=remote_params(collective_id, 8),
    )(x, peaks)


def pair_reduce(collective_id, *arrays):
    n = lax.axis_size("shard")
    return pl.pallas_call(
        functools.partial(pair_reduce_kernel, len(arrays)),
        out_shape=[jax.ShapeDtypeStruct(a.shape[2:], f32) for a in arrays],
        in_specs=[VMEM] * len(arrays),
        out_specs=[VMEM] * len(arrays),
        scratch_shapes=sum((pair_reduce_scratch(n, a) for a in arrays), []),
        compiler_params=remote_params(collective_id, 40),
    )(*arrays)


def many_sum(axis, collective_id, x):
    n = lax.axis_size(axis)
    sem = pltpu.SemaphoreType.DMA
    return pl.pallas_call(
        functools.partial(many_sum_kernel, axis),
        out_shape=jax.ShapeDtypeStruct(x.shape, x.dtype),
        in_specs=[VMEM],
        out_specs=VMEM,
        scratch_shapes=[pltpu.VMEM((n - 1, *x.shape), x.dtype), sem((n,)), sem((n,))],
        compiler_params=remote_params(collective_id, 8),
    )(x)


def end_call(collective_id, x, wide, out, y):
    n_ctx, rows, width = x.shape
    n_shard = lax.axis_size("shard")
    n = n_ctx // 2
    wide_rows, wide_cols = wide.shape[1] // n_ctx, wide.shape[2]
    sem = pltpu.SemaphoreType.DMA
    return pl.pallas_call(
        end_kernel,
        out_shape=[
            jax.ShapeDtypeStruct((rows, width), f32),
            jax.ShapeDtypeStruct((n_ctx, wide_rows, wide_cols), bf16),
            jax.ShapeDtypeStruct(out.shape[1:], f32),
            jax.ShapeDtypeStruct(y.shape[2:], f32),
        ],
        in_specs=[VMEM] * 4,
        out_specs=[VMEM] * 4,
        scratch_shapes=[
            pltpu.VMEM((n_shard - 1, *wide.shape[1:]), bf16),
            pltpu.VMEM((n_shard - 1, *out.shape[1:]), bf16),
            pltpu.VMEM((n_ctx, wide_rows, wide_cols), bf16),
            sem,
        ]
        + [sem((n_shard,))] * 4
        + [sem((n_ctx,))] * 2
        + pair_reduce_scratch(n_shard, y)
        + [pltpu.VMEM((n, rows, width), bf16)] * 3
        + [sem((n, LINE_CHUNKS))] * 5,
        compiler_params=remote_params(collective_id, 56),
    )(x, wide, out, y)


def per_device(
    tokens,
    doc_ids,
    routes,
    attn_gain,
    w_query,
    w_key,
    w_value,
    query_gain,
    key_gain,
    w_out,
    ffn_gain,
    w_router,
    w_gate,
    w_up,
    w_down,
    clip_threshold,
    cotangent,
):
    both = ("ctx", "shard")
    n_ctx, n_shard = lax.axis_size("ctx"), lax.axis_size("shard")
    ctx, shard = lax.axis_index("ctx"), lax.axis_index("shard")
    x_own = tokens[0]
    rows, width = x_own.shape
    part = w_query.shape[0]
    cols = width // n_ctx
    heads = cols // HEAD
    count = rows * n_ctx
    local = w_gate.shape[0]
    experts = local * n_shard

    top = routes.shape[2]
    spare = jnp.zeros((part, LANES - 4 - experts - rows // part * (1 + top)), bf16)
    small = jnp.concatenate(
        [
            jnp.stack([attn_gain, query_gain, key_gain, ffn_gain], axis=1),
            w_router,
            doc_ids.reshape(part, rows // part).astype(bf16),
            routes.reshape(part, rows // part * top).astype(bf16),
            spare,
        ],
        axis=1,
    )
    grad_own = cotangent[0]
    x_all, out_w, weights, small_all, grad_mine = start_call(
        1, x_own, w_out, w_query, w_key, w_value, small, grad_own
    )
    x_all = x_all.reshape(count, width)
    out_w = out_w.reshape(width, width)
    weights = weights.reshape(width, 3 * cols)
    gains = small_all[..., : 4 + experts].reshape(width, 4 + experts)
    gain_attn, gain_query, gain_key, gain_ffn = (gains[:, i].astype(f32) for i in range(4))
    router_w = gains[:, 4:]
    gain_query = lax.dynamic_slice_in_dim(gain_query, ctx * cols, cols)
    gain_key = lax.dynamic_slice_in_dim(gain_key, ctx * cols, cols)
    tail = small_all[..., 4 + experts :].astype(jnp.int32)
    docs = lax.dynamic_index_in_dim(tail[..., : rows // part], shard, 1, False).reshape(count)
    span = n_ctx // 2
    role = lax.div(ctx, span)
    routes_all = tail[..., rows // part : rows // part * (1 + top)].reshape(
        n_ctx, n_shard, rows, top
    )
    routes_all = jnp.stack(
        [
            lax.dynamic_index_in_dim(routes_all, ctx, 0, False),
            lax.dynamic_index_in_dim(routes_all, lax.rem(ctx + span, n_ctx), 0, False),
        ]
    ).reshape(2 * n_shard * rows, top)

    def swap(u):
        both = lax.all_gather(
            u, "ctx", axis=0, axis_index_groups=[[i, i + span] for i in range(span)]
        )
        return lax.dynamic_index_in_dim(both, 1 - role, 0, False)

    def in_order(mine, theirs):
        return jnp.where(role == 0, jnp.stack([mine, theirs]), jnp.stack([theirs, mine]))

    half = local // 2
    ff = w_gate.shape[2]
    own_w = jnp.concatenate([w_gate, w_up, w_down.transpose(0, 2, 1)], axis=2)
    keep_w = lax.dynamic_slice_in_dim(own_w, role * half, half, 0)
    give_w = lax.dynamic_slice_in_dim(own_w, (1 - role) * half, half, 0)
    spans = [list(range(r * span, (r + 1) * span)) for r in (0, 1)]
    first_w = swap(give_w[0])
    x_all, first_w, later_w, later_grad = lax.optimization_barrier(
        (x_all, first_w, give_w[1:], grad_own)
    )
    grad_theirs = swap(later_grad)
    early = [first_w] + [swap(later_w[e]) for e in range(half - 1)]
    expert_w = [
        lax.all_gather(
            in_order(keep_w[e], early[e]),
            "ctx",
            axis=1,
            tiled=True,
            axis_index_groups=spans,
        ).reshape(width, 3 * ff)
        for e in range(half)
    ]

    x_wide = x_all.astype(f32)
    inverse_one = inverse_rms(x_wide)
    hidden_one = (x_wide * inverse_one * gain_attn).astype(bf16)
    linear = dot(hidden_one, weights)
    query_lin, key_lin = linear[:, :cols], linear[:, cols : 2 * cols]
    value = linear[:, 2 * cols :].astype(bf16)
    squares = jnp.stack(
        [jnp.sum(query_lin * query_lin, axis=1), jnp.sum(key_lin * key_lin, axis=1)]
    )
    squares = many_sum("ctx", 6, squares)
    inverse_qk = lax.rsqrt(squares / width + norm_eps)
    inverse_q, inverse_k = inverse_qk[0][:, None], inverse_qk[1][:, None]
    cosine, sine = rope_tables(count)
    query_n, key_n = query_lin * inverse_q, key_lin * inverse_k
    query = rotate(query_n * gain_query, cosine, sine).astype(bf16)
    key = rotate(key_n * gain_key, cosine, sine).astype(bf16)
    mixed, log_total, peaks = attend_forward(query, key, value, docs)
    mixed, grad_theirs = lax.optimization_barrier((mixed, grad_theirs))
    grad_theirs = lax.all_gather(grad_theirs, "shard", axis=0, tiled=True)
    grad_mine = grad_mine.reshape(n_shard * rows, width)
    x_f = x_own.astype(f32)
    after = x_f + dot(exchange(2, mixed, False), out_w)
    inverse_two = inverse_rms(after)
    normed_two = after * inverse_two
    hidden_two = (normed_two * gain_ffn).astype(bf16)

    hidden_all, peaks = pair_gather(3, hidden_two, peaks)
    hidden_all = hidden_all.reshape(2 * n_shard * rows, width)
    peaks = jnp.max(peaks, axis=0)[:, 0, 0]
    logits = dot(hidden_all, router_w)
    named = jnp.any(routes_all[:, :, None] == jnp.arange(experts)[None, None, :], axis=1)
    probs = jax.nn.softmax(logits, axis=1)
    selected = jnp.where(named, probs, 0.0)
    selected_sum = jnp.sum(selected, axis=1, keepdims=True)
    gates = selected / selected_sum
    first = shard * local + role * half
    gates_own = lax.dynamic_slice_in_dim(gates, first, half, 1)
    named_own = lax.dynamic_slice_in_dim(named, first, half, 1)
    moe_part = jnp.zeros(hidden_all.shape, f32)
    back_part = jnp.zeros(hidden_all.shape, f32)

    def by_half(function, *arrays):
        split = grad_mine.shape[0]
        return jnp.concatenate(
            [
                function(grad_mine.astype(f32), *(u[:split] for u in arrays)),
                function(grad_theirs.astype(f32), *(u[split:] for u in arrays)),
            ]
        )

    grad_gates, expert_grads = [], []
    for e in range(half):
        wide, down = expert_w[e][:, : 2 * ff], expert_w[e][:, 2 * ff :]
        gate_col = gates_own[:, e : e + 1]
        hidden = dot(hidden_all, wide)
        gate_h, up_h = hidden[:, :ff], hidden[:, ff:]
        sig = jax.nn.sigmoid(gate_h)
        silu = gate_h * sig
        act = (silu * up_h).astype(bf16)
        result = contract_cols(act, down).astype(bf16).astype(f32)
        moe_part = moe_part + gate_col * result
        along = by_half(lambda d, u: jnp.sum(d * u, axis=1), result)
        grad_gates.append(jnp.where(named_own[:, e], along, 0.0))
        grad_y = by_half(lambda d, u: (u * d).astype(bf16), gate_col)
        grad_act = dot(grad_y, down)
        grad_h = jnp.concatenate(
            [grad_act * up_h * sig * (1.0 + gate_h * (1.0 - sig)), grad_act * silu], axis=1
        ).astype(bf16)
        back_part = back_part + contract_cols(grad_h, wide).astype(bf16).astype(f32)
        grad_w = [
            contract_rows(hidden_all, grad_h).astype(bf16),
            contract_rows(grad_y, act).astype(bf16),
        ]
        hidden_all, back_part, grad_w = lax.optimization_barrier((hidden_all, back_part, grad_w))
        expert_grads.append(
            [
                lax.psum_scatter(
                    u.reshape(2, width // 2, -1),
                    "ctx",
                    scatter_dimension=1,
                    tiled=True,
                    axis_index_groups=spans,
                )
                for u in grad_w
            ]
        )
    slots = jnp.stack(grad_gates).reshape(half, 2, n_shard, rows).transpose(1, 2, 0, 3)
    grad_gates = lax.dynamic_update_slice_in_dim(
        jnp.zeros((2, n_shard, experts, rows), f32), slots, first, 2
    )
    back_sum, grad_gates = pair_reduce(
        4, back_part.astype(bf16).reshape(2, n_shard, rows, width), grad_gates
    )
    grad_gates = grad_gates.T
    def own_rows(u):
        return lax.dynamic_slice_in_dim(u, shard * rows, rows, 0)

    gates_t, probs_t, named_t, sum_t = map(own_rows, (gates, probs, named, selected_sum))
    grad_selected = (
        grad_gates - jnp.sum(gates_t * grad_gates, axis=1, keepdims=True)
    ) / sum_t
    grad_probs = jnp.where(named_t, grad_selected, 0.0)
    grad_logits = (
        probs_t * (grad_probs - jnp.sum(probs_t * grad_probs, axis=1, keepdims=True))
    ).astype(bf16)
    grad_router = contract_rows(hidden_two, grad_logits)
    grad_hidden = back_sum + contract_cols(grad_logits, router_w)
    grad_gain_ffn = jnp.sum(grad_hidden * normed_two, axis=0)
    scaled_two = grad_hidden * gain_ffn
    grad_after = grad_own.astype(f32) + inverse_two * (
        scaled_two - normed_two * jnp.mean(scaled_two * normed_two, axis=1, keepdims=True)
    )

    grad_attn_own = grad_after.astype(bf16)
    to_gather, expert_grads = lax.optimization_barrier((grad_attn_own, expert_grads))
    grad_attn = lax.all_gather(to_gather, "ctx", axis=0, tiled=True)
    grad_mixed = exchange(5, contract_cols(grad_attn_own, out_w).astype(bf16), True)
    grad_mixed, expert_grads = lax.optimization_barrier((grad_mixed, expert_grads))
    grad_out_w = contract_rows(mixed, grad_attn)
    grad_query_rot, grad_key_rot, grad_value = attend_backward(
        query, key, value, docs, log_total, grad_mixed
    )
    kept = [[lax.dynamic_index_in_dim(u, role, 0, False) for u in sums] for sums in expert_grads]
    peers = swap(
        jnp.stack(
            [
                jnp.concatenate(
                    [lax.dynamic_index_in_dim(u, 1 - role, 0, False) for u in sums], axis=1
                )
                for sums in expert_grads
            ]
        )
    )
    peers = [(peer[:, : 2 * ff], peer[:, 2 * ff :]) for peer in peers]
    both_halves = [
        in_order(jnp.stack([k[i] for k in kept]), jnp.stack([p[i] for p in peers]))
        .reshape(local, width // n_ctx, -1)
        .astype(f32)
        for i in (0, 1)
    ]
    grad_query_n = rotate(grad_query_rot, cosine, -sine)
    grad_key_n = rotate(grad_key_rot, cosine, -sine)
    grad_gain_query = jnp.sum(grad_query_n * query_n, axis=0)
    grad_gain_key = jnp.sum(grad_key_n * key_n, axis=0)
    scaled_q, scaled_k = grad_query_n * gain_query, grad_key_n * gain_key
    peak_row = lax.dynamic_update_slice_in_dim(jnp.zeros((count,), f32), peaks, ctx * heads, 0)
    inner = jnp.stack(
        [jnp.sum(scaled_q * query_n, axis=1), jnp.sum(scaled_k * key_n, axis=1), peak_row]
    )
    inner = many_sum("ctx", 7, inner)
    peak_all = inner[2, :HEADS]
    inner = inner / width
    grad_linear = jnp.concatenate(
        [
            inverse_q * (scaled_q - query_n * inner[0][:, None]),
            inverse_k * (scaled_k - key_n * inner[1][:, None]),
            grad_value,
        ],
        axis=1,
    ).astype(bf16)
    grad_weights = contract_rows(hidden_one, grad_linear)
    hidden_part = contract_cols(grad_linear, weights)
    grad_gain_attn = jnp.sum(hidden_part * (x_wide * inverse_one), axis=0)
    grad_small = jnp.concatenate(
        [jnp.stack([grad_gain_attn, grad_gain_ffn], axis=1), grad_router], axis=1
    )
    grad_small = jnp.pad(grad_small, ((0, 0), (0, LANES - 2 - experts)))
    grad_weights = (
        jnp.concatenate([grad_weights, grad_small], axis=1)
        .astype(bf16)
        .reshape(n_ctx, n_shard, part, 3 * cols + LANES)
        .transpose(1, 0, 2, 3)
        .reshape(n_shard, n_ctx * part, 3 * cols + LANES)
    )
    grad_gain_qk = jnp.pad(
        jnp.stack([grad_gain_query, grad_gain_key], axis=1), ((0, 0), (0, LANES - 2))
    )
    grad_out_w = (
        jnp.concatenate([grad_out_w, grad_gain_qk], axis=1)
        .astype(bf16)
        .reshape(n_shard, part, width + LANES)
    )
    grad_hidden_one, grad_weights, grad_out_w, moe_sum = end_call(
        8,
        hidden_part.astype(bf16).reshape(n_ctx, rows, width),
        grad_weights,
        grad_out_w,
        moe_part.astype(bf16).reshape(2, n_shard, rows, width),
    )
    output = (after + moe_sum).astype(bf16)
    grad_weights = grad_weights.astype(f32)
    grad_small = jnp.sum(grad_weights[..., 3 * cols :], axis=0)
    grad_weights = (
        grad_weights[..., : 3 * cols]
        .reshape(n_ctx, part, 3, cols)
        .transpose(2, 1, 0, 3)
        .reshape(3, part, width)
    )
    inverse_own = inverse_rms(x_f)
    normed_own = x_f * inverse_own
    scaled_one = grad_hidden_one * gain_attn
    grad_inputs = grad_after + inverse_own * (
        scaled_one - normed_own * jnp.mean(scaled_one * normed_own, axis=1, keepdims=True)
    )

    factors = jnp.sqrt(clip_threshold / jnp.maximum(peak_all, clip_threshold))
    col_scale = jnp.repeat(factors, HEAD)
    query_clipped = (w_query.astype(f32) * col_scale[None, :]).astype(bf16)
    key_clipped = (w_key.astype(f32) * col_scale[None, :]).astype(bf16)
    return (
        output[None],
        grad_inputs[None],
        grad_small[:, 0],
        grad_weights[0],
        grad_weights[1],
        grad_weights[2],
        grad_out_w[:, width],
        grad_out_w[:, width + 1],
        grad_out_w[:, :width],
        grad_small[:, 1],
        grad_small[:, 2 : 2 + experts],
        both_halves[0][..., :ff],
        both_halves[0][..., ff:],
        both_halves[1].transpose(0, 2, 1),
        query_clipped,
        key_clipped,
        factors,
    )


def solution(mesh):
    both = ("ctx", "shard")
    return jax.shard_map(
        per_device,
        mesh=mesh,
        in_specs=(
            P("shard", "ctx", None),
            P("shard", "ctx"),
            P("shard", "ctx", None),
            P(both),
            P(both, None),
            P(both, None),
            P(both, None),
            P(both),
            P(both),
            P(both, None),
            P(both),
            P(both, None),
            P("shard", "ctx", None),
            P("shard", "ctx", None),
            P("shard", None, "ctx"),
            P(),
            P("shard", "ctx", None),
        ),
        out_specs=(
            P("shard", "ctx", None),
            P("shard", "ctx", None),
            P(both),
            P(both, None),
            P(both, None),
            P(both, None),
            P(both),
            P(both),
            P(both, None),
            P(both),
            P(both, None),
            P("shard", "ctx", None),
            P("shard", "ctx", None),
            P("shard", None, "ctx"),
            P(both, None),
            P(both, None),
            P(),
        ),
        check_vma=False,
    )
```

```python
import functools

import jax
import jax.numpy as jnp
from jax import lax
from jax.experimental import pallas as pl
from jax.experimental.pallas import tpu as pltpu
from jax.sharding import PartitionSpec as P

HEADS = 16
HEAD = 128
SCALE = HEAD ** (-0.5)
Q_BLOCK = 256
LANES = 128

norm_eps = 1e-06
rope_base = 10000.0
f32 = jnp.float32
bf16 = jnp.bfloat16


def dot(a, b):
    return jnp.dot(a, b, preferred_element_type=f32)


def contract_rows(a, b):
    return lax.dot_general(a, b, (((0,), (0,)), ((), ())), preferred_element_type=f32)


def contract_cols(a, b):
    return lax.dot_general(a, b, (((1,), (1,)), ((), ())), preferred_element_type=f32)


def inverse_rms(values):
    return lax.rsqrt(jnp.mean(values * values, axis=-1, keepdims=True) + norm_eps)


def rope_tables(count):
    half = HEAD // 2
    freq = rope_base ** (-jnp.arange(half).astype(f32) / half)
    angles = jnp.arange(count).astype(f32)[:, None] * freq[None, :]
    return jnp.cos(angles), jnp.sin(angles)


def rotate(values, cosine, sine):
    parts = []
    for col in range(0, values.shape[1], HEAD):
        a = values[:, col : col + HEAD // 2]
        b = values[:, col + HEAD // 2 : col + HEAD]
        parts += [a * cosine - b * sine, b * cosine + a * sine]
    return jnp.concatenate(parts, axis=1)


def attend_forward_kernel(q_ref, k_ref, v_ref, doc_q_ref, doc_k_ref, o_ref, lse_ref, peak_ref):
    s = SCALE * contract_cols(q_ref[...], k_ref[...])
    s = jnp.where(doc_q_ref[...] == doc_k_ref[...], s, -1e30)
    top = jnp.max(s, axis=1, keepdims=True)
    e = jnp.exp(s - top)
    total = jnp.sum(e, axis=1, keepdims=True)
    p = (e * (1.0 / total)).astype(bf16)
    o_ref[...] = dot(p, v_ref[...]).astype(bf16)
    lse_ref[0] = top + jnp.log(total)
    peak = jnp.broadcast_to(jnp.max(top, axis=0, keepdims=True), peak_ref.shape[1:])

    @pl.when(pl.program_id(1) == 0)
    def _():
        peak_ref[0] = peak

    @pl.when(pl.program_id(1) > 0)
    def _():
        peak_ref[0] = jnp.maximum(peak_ref[0], peak)


def attend_backward_kernel(
    q_ref, k_ref, v_ref, doc_q_ref, doc_k_ref, lse_ref, do_ref, dq_ref, dk_ref, dv_ref
):
    q, k, v, do = q_ref[...], k_ref[...], v_ref[...], do_ref[...]
    s = SCALE * contract_cols(q, k)
    p = jnp.where(doc_q_ref[...] == doc_k_ref[...], jnp.exp(s - lse_ref[0]), 0.0)
    dp = contract_cols(do, v)
    inner = jnp.sum(p * dp, axis=1, keepdims=True)
    ds = (p * (dp - inner)).astype(bf16)
    dq_ref[...] = SCALE * dot(ds, k)
    dk = SCALE * contract_rows(ds, q)
    dv = contract_rows(p.astype(bf16), do)

    @pl.when(pl.program_id(1) == 0)
    def _():
        dk_ref[...] = dk
        dv_ref[...] = dv

    @pl.when(pl.program_id(1) > 0)
    def _():
        dk_ref[...] += dk
        dv_ref[...] += dv


def attend_specs(count):
    block = pl.BlockSpec((Q_BLOCK, HEAD), lambda h, i: (i, h))
    whole = pl.BlockSpec((count, HEAD), lambda h, i: (0, h))
    doc_q = pl.BlockSpec((Q_BLOCK, 1), lambda h, i: (i, 0))
    doc_k = pl.BlockSpec((1, count), lambda h, i: (0, 0))
    lse = pl.BlockSpec((1, Q_BLOCK, 1), lambda h, i: (h, i, 0))
    return block, whole, doc_q, doc_k, lse


def attend_forward(q, k, v, docs):
    count, width = q.shape
    heads = width // HEAD
    block, whole, doc_q, doc_k, lse = attend_specs(count)
    return pl.pallas_call(
        attend_forward_kernel,
        grid=(heads, count // Q_BLOCK),
        in_specs=[block, whole, whole, doc_q, doc_k],
        out_specs=[block, lse, pl.BlockSpec((1, 8, 128), lambda h, i: (h, 0, 0))],
        out_shape=[
            jax.ShapeDtypeStruct((count, width), bf16),
            jax.ShapeDtypeStruct((heads, count, 1), f32),
            jax.ShapeDtypeStruct((heads, 8, 128), f32),
        ],
        compiler_params=pltpu.CompilerParams(vmem_limit_bytes=48 << 20),
        cost_estimate=pl.CostEstimate(
            flops=4 * count * count * width,
            transcendentals=heads * count * count,
            bytes_accessed=8 * count * width,
        ),
    )(q, k, v, docs[:, None], docs[None, :])


def attend_backward(q, k, v, docs, log_total, grad):
    count, width = q.shape
    heads = width // HEAD
    block, whole, doc_q, doc_k, lse = attend_specs(count)
    return pl.pallas_call(
        attend_backward_kernel,
        grid=(heads, count // Q_BLOCK),
        in_specs=[block, whole, whole, doc_q, doc_k, lse, block],
        out_specs=[block, whole, whole],
        out_shape=[jax.ShapeDtypeStruct((count, width), f32)] * 3,
        compiler_params=pltpu.CompilerParams(vmem_limit_bytes=56 << 20),
        cost_estimate=pl.CostEstimate(
            flops=10 * count * count * width,
            transcendentals=heads * count * count,
            bytes_accessed=20 * count * width,
        ),
    )(q, k, v, docs[:, None], docs[None, :], log_total, grad)


MESH = pl.DeviceIdType.MESH
ANY = pl.BlockSpec(memory_space=pl.ANY)
VMEM = pl.BlockSpec(memory_space=pltpu.VMEM)


def ring_peers(axis):
    n, me = lax.axis_size(axis), lax.axis_index(axis)
    return [lax.rem(me + k, n) for k in range(n)], [lax.rem(me + n - k, n) for k in range(n)]


class Greeting:
    def __init__(self):
        self.barrier, self.total = pltpu.get_barrier_semaphore(), 0

    def ring(self, axis):
        to, _ = ring_peers(axis)
        for peer in to[1:]:
            pl.semaphore_signal(
                self.barrier, inc=1, device_id={axis: peer}, device_id_type=MESH
            )
        self.total = self.total + len(to) - 1
        return self

    def line(self):
        line = Line()
        for there, peer in (
            (line.place >= 0, line.partner),
            (line.not_last, line.me + 2),
            (line.not_first, line.me - 2),
        ):

            @pl.when(there)
            def _():
                pl.semaphore_signal(
                    self.barrier, inc=1, device_id={"ctx": peer}, device_id_type=MESH
                )

            self.total = self.total + there.astype(jnp.int32)
        return self

    def pair(self):
        pl.semaphore_signal(
            self.barrier, inc=1, device_id={"ctx": Pair().peer}, device_id_type=MESH
        )
        self.total = self.total + 1
        return self

    def wait(self):
        pl.semaphore_wait(self.barrier, self.total)


class Line:
    def __init__(self):
        self.n, self.me = lax.axis_size("ctx") // 2, lax.axis_index("ctx")
        self.place, self.core = lax.div(self.me, 2), lax.rem(self.me, 2)
        self.partner = self.me + 1 - 2 * self.core
        self.not_first, self.not_last = self.place > 0, self.place < self.n - 1


class Direct:
    def __init__(self, axis, source, target, send, recv):
        self.axis, self.source, self.target = axis, source, target
        self.send, self.recv = send, recv
        self.me = lax.axis_index(axis)
        self.to, self.origin = ring_peers(axis)

    def copy(self, k, sender):
        return pltpu.make_async_remote_copy(
            src_ref=self.source(self.to[k]),
            dst_ref=self.target(sender, k),
            send_sem=self.send.at[k],
            recv_sem=self.recv.at[k],
            device_id={self.axis: self.to[k]},
            device_id_type=MESH,
        )

    def start(self):
        for k in range(1, len(self.to)):
            self.copy(k, self.me).start()

    def wait_recv(self):
        for k in range(1, len(self.to)):
            self.copy(k, self.origin[k]).wait_recv()

    def wait_send(self):
        for k in range(1, len(self.to)):
            self.copy(k, self.me).wait_send()


class LineGather:
    def __init__(self, pieces, own_sem, send_r, send_l, send_p, recv_r, recv_l, recv_p):
        self.line, self.pieces, self.own_sem = Line(), pieces, own_sem
        self.send_r, self.send_l, self.send_p = send_r, send_l, send_p
        self.recv_r, self.recv_l, self.recv_p = recv_r, recv_l, recv_p

    def own(self, c):
        source, target = self.pieces[c]
        return pltpu.make_async_copy(source, target(self.line.me), self.own_sem.at[c])

    def copy(self, block, k, c, target_device, send, recv):
        source, target = self.pieces[c]
        return pltpu.make_async_remote_copy(
            src_ref=source if k == 0 else target(block),
            dst_ref=target(block),
            send_sem=send,
            recv_sem=recv,
            device_id={"ctx": target_device},
            device_id_type=MESH,
        )

    def right(self, k, c):
        me = self.line.me
        return self.copy(me - 2 * k, k, c, me + 2, self.send_r.at[k, c], self.recv_r.at[k, c])

    def left(self, k, c):
        me = self.line.me
        return self.copy(me + 2 * k, k, c, me - 2, self.send_l.at[k, c], self.recv_l.at[k, c])

    def across(self, k, c, sign):
        line = self.line
        i = k if sign < 0 else line.n - 1 + k
        return self.copy(
            line.me + sign * 2 * k, k, c, line.partner, self.send_p.at[i, c], self.recv_p.at[i, c]
        )

    def arrived(self, block, c, recv):
        source, target = self.pieces[c]
        pltpu.make_async_remote_copy(
            src_ref=source,
            dst_ref=target(block),
            send_sem=recv,
            recv_sem=recv,
            device_id={"ctx": self.line.partner},
            device_id_type=MESH,
        ).wait_recv()

    def start(self):
        for c in range(len(self.pieces)):
            self.own(c).start()

    def hop(self, k):
        line = self.line
        for c in range(len(self.pieces)):

            @pl.when(line.place >= k)
            def _():
                if k:
                    self.arrived(line.me - 2 * k, c, self.recv_r.at[k - 1, c])

                @pl.when(line.not_last)
                def _():
                    self.right(k, c).start()

                self.across(k, c, -1).start()

            @pl.when(line.place + k <= line.n - 1)
            def _():
                if k:
                    self.arrived(line.me + 2 * k, c, self.recv_l.at[k - 1, c])

                @pl.when(line.not_first)
                def _():
                    self.left(k, c).start()

                if k:
                    self.across(k, c, 1).start()

    def finish(self, skip_own=None):
        line = self.line
        for c in range(len(self.pieces)):
            if c != skip_own:
                self.own(c).wait()
        for k in range(line.n):
            for c in range(len(self.pieces)):

                @pl.when(line.place >= k)
                def _():
                    @pl.when(line.not_last)
                    def _():
                        self.right(k, c).wait_send()

                    self.across(k, c, -1).wait_send()
                    self.arrived(line.partner - 2 * k, c, self.recv_p.at[k, c])

                @pl.when(line.place + k <= line.n - 1)
                def _():
                    @pl.when(line.not_first)
                    def _():
                        self.left(k, c).wait_send()

                    if k:
                        self.across(k, c, 1).wait_send()
                        self.arrived(line.partner + 2 * k, c, self.recv_p.at[line.n - 1 + k, c])


def line_gather_scratch(n, pieces):
    sem = pltpu.SemaphoreType.DMA
    one, two = sem((n, pieces)), sem((2 * n - 1, pieces))
    return [sem((pieces,)), one, one, two, one, one, two]


class LineReduce:
    def __init__(
        self, chunks, x, o, pair, from_left, from_right, send_p, recv_p, send_s, recv_r, recv_l
    ):
        self.line, self.chunks = Line(), chunks
        self.x, self.o, self.pair, self.out = x, o, pair, pair
        self.from_left, self.from_right = from_left, from_right
        self.send_p, self.recv_p, self.send_s = send_p, recv_p, send_s
        self.recv_r, self.recv_l = recv_r, recv_l
        self.order = []
        for j in range(self.line.n):
            self.order += [p for p in (self.line.n - 1 - j, j) if p not in self.order]

    def at(self, c):
        rows = self.x.shape[1] // self.chunks
        return pl.ds(c * rows, rows)

    def across(self, p, c):
        line, at = self.line, self.at(c)
        return pltpu.make_async_remote_copy(
            src_ref=self.x.at[2 * p + 1 - line.core, at],
            dst_ref=self.pair.at[p, at],
            send_sem=self.send_p.at[p, c],
            recv_sem=self.recv_p.at[p, c],
            device_id={"ctx": line.partner},
            device_id_type=MESH,
        )

    def along(self, p, c, step, buffer, recv):
        at = self.at(c)
        return pltpu.make_async_remote_copy(
            src_ref=self.out.at[p, at],
            dst_ref=buffer.at[p, at],
            send_sem=self.send_s.at[p, c],
            recv_sem=recv.at[p, c],
            device_id={"ctx": self.line.me + step},
            device_id_type=MESH,
        )

    def right(self, p, c):
        return self.along(p, c, 2, self.from_left, self.recv_r)

    def left(self, p, c):
        return self.along(p, c, -2, self.from_right, self.recv_l)

    def start(self):
        for p in self.order:
            for c in range(self.chunks):
                self.across(p, c).start()

    def both(self, p, c):
        at = self.at(c)
        return self.x[2 * p + self.line.core, at].astype(f32) + self.pair[p, at].astype(f32)

    def pass_on(self):
        line = self.line
        for p in self.order:
            for c in range(self.chunks):
                at = self.at(c)
                self.across(p, c).wait_recv()

                @pl.when(line.place < p)
                def _():
                    @pl.when(line.not_first)
                    def _():
                        self.right(p, c).wait_recv()
                        total = self.both(p, c) + self.from_left[p, at].astype(f32)
                        self.out[p, at] = total.astype(bf16)

                    @pl.when(line.place == 0)
                    def _():
                        self.out[p, at] = self.both(p, c).astype(bf16)

                    self.right(p, c).start()

                @pl.when(line.place > p)
                def _():
                    @pl.when(line.not_last)
                    def _():
                        self.left(p, c).wait_recv()
                        total = self.both(p, c) + self.from_right[p, at].astype(f32)
                        self.out[p, at] = total.astype(bf16)

                    @pl.when(line.place == line.n - 1)
                    def _():
                        self.out[p, at] = self.both(p, c).astype(bf16)

                    self.left(p, c).start()

    def finish(self):
        line = self.line
        for p in range(line.n):
            for c in range(self.chunks):
                at = self.at(c)

                @pl.when(line.place == p)
                def _():
                    self.o[at] = self.both(p, c)
                    if p > 0:
                        self.right(p, c).wait_recv()
                        self.o[at] += self.from_left[p, at].astype(f32)
                    if p < line.n - 1:
                        self.left(p, c).wait_recv()
                        self.o[at] += self.from_right[p, at].astype(f32)

        for p in range(line.n):
            for c in range(self.chunks):
                self.across(p, c).wait_send()

                @pl.when(line.place < p)
                def _():
                    self.right(p, c).wait_send()

                @pl.when(line.place > p)
                def _():
                    self.left(p, c).wait_send()


def add_up(x, buf, o, me):
    rows = x.shape[1]
    step = 8 if rows % 32 else 32

    @pl.loop(0, rows // step)
    def _(j):
        at = pl.ds(pl.multiple_of(j * step, step), step)
        total = x[me, at].astype(f32)
        for k in range(buf.shape[0]):
            total = total + buf[k, at].astype(f32)
        o[at] = total.astype(o.dtype)


def block_of(ref):
    return lambda device: ref.at[device]


def block_from(ref):
    return lambda device, k: ref.at[device]


def whole_of(ref):
    return lambda device: ref


def buffer_of(ref):
    return lambda device, k: ref.at[k - 1]


def row_pieces(source, target, chunks):
    rows = source.shape[0] // chunks
    return [
        (source.at[pl.ds(c * rows, rows)], lambda b, c=c: target.at[b, pl.ds(c * rows, rows)])
        for c in range(chunks)
    ]


def start_kernel(
    x, w, w_query, w_key, w_value, small, cot, x_all, w_all, heads_all, small_all, cot_all,
    heads_mid, small_mid, own_sem, ex_send, ex_recv, sp_send, sp_recv, w_send, w_recv, f_send,
    f_recv, *line_sems,
):
    shard, ctx = lax.axis_index("shard"), lax.axis_index("ctx")
    n_ctx = lax.axis_size("ctx")
    cols = w_query.shape[1] // n_ctx
    Greeting().ring("ctx").ring("shard").wait()

    def columns(ref):
        return lambda d: ref.at[:, pl.ds(pl.multiple_of(d * cols, HEAD), cols)]

    def place(i):
        if i == 3:
            return block_from(small_mid)
        return lambda d, k: heads_mid.at[d, :, i * cols : (i + 1) * cols]

    sources = [columns(w_query), columns(w_key), columns(w_value), whole_of(small)]
    swaps = [
        Direct("ctx", source, place(i), ex_send.at[i], ex_recv.at[i])
        for i, source in enumerate(sources)
    ]

    def by_shard(ref):
        return lambda d, k: ref.at[:, d]

    spreads = [
        Direct("shard", whole_of(heads_mid), by_shard(heads_all), sp_send.at[0], sp_recv.at[0]),
        Direct("shard", whole_of(small_mid), by_shard(small_all), sp_send.at[1], sp_recv.at[1]),
    ]
    other = Direct("shard", whole_of(cot), block_from(cot_all), sp_send.at[2], sp_recv.at[2])
    pieces = row_pieces(x, x_all, LINE_CHUNKS) + [(w, lambda b: w_all.at[b, shard])]
    line = LineGather(pieces, *line_sems)
    at = line.line
    own = [
        pltpu.make_async_copy(source(ctx), place(i)(ctx, 0), own_sem.at[i])
        for i, source in enumerate(sources)
    ]
    later = [
        pltpu.make_async_copy(heads_mid, heads_all.at[:, shard], own_sem.at[4]),
        pltpu.make_async_copy(small_mid, small_all.at[:, shard], own_sem.at[5]),
        pltpu.make_async_copy(cot, cot_all.at[shard], own_sem.at[6]),
    ]
    for swap in swaps:
        swap.start()
    for copy in own:
        copy.start()
    line.start()
    line.hop(0)
    for swap in swaps:
        swap.wait_recv()
    for copy in own:
        copy.wait()
    for one in (*spreads, other, *later):
        one.start()
    for k in range(1, at.n):
        line.hop(k)

    to, origin = ring_peers("shard")

    def row(k, p, sender):
        block = 2 * p + at.core
        return pltpu.make_async_remote_copy(
            src_ref=w_all.at[block, shard],
            dst_ref=w_all.at[block, sender],
            send_sem=w_send.at[k, p],
            recv_sem=w_recv.at[k, p],
            device_id={"shard": to[k]},
            device_id_type=MESH,
        )

    def forward(k, p, core):
        block = w_all.at[2 * p + core, origin[k]]
        return pltpu.make_async_remote_copy(
            src_ref=block,
            dst_ref=block,
            send_sem=f_send.at[k, p],
            recv_sem=f_recv.at[k, p],
            device_id={"ctx": at.partner},
            device_id_type=MESH,
        )

    some = [(k, p) for k in range(1, len(to)) for p in range(at.n)]
    line.own(LINE_CHUNKS).wait()
    for k, p in some:
        row(k, p, shard).start()
    for k, p in some:
        row(k, p, origin[k]).wait_recv()
        forward(k, p, at.core).start()
    line.finish(skip_own=LINE_CHUNKS)
    for k, p in some:
        row(k, p, shard).wait_send()
        forward(k, p, at.core).wait_send()
        forward(k, p, 1 - at.core).wait_recv()
    for direct in (*spreads, other):
        direct.wait_recv()
    for direct in (*swaps, *spreads, other):
        direct.wait_send()
    for copy in later:
        copy.wait()


def exchange_kernel(to_rows, x, o, own_sem, send, recv):
    n, me = lax.axis_size("ctx"), lax.axis_index("ctx")
    cols, rows = (x.shape[1] // n, x.shape[0]) if to_rows else (x.shape[1], o.shape[0])

    def row_block(ref):
        return lambda d, k=0: ref.at[pl.ds(pl.multiple_of(d * rows, rows), rows)]

    def column_block(ref):
        return lambda d, k=0: ref.at[:, pl.ds(pl.multiple_of(d * cols, cols), cols)]

    source, target = (
        (column_block(x), row_block(o)) if to_rows else (row_block(x), column_block(o))
    )
    Greeting().ring("ctx").wait()
    swap = Direct("ctx", source, target, send, recv)
    swap.start()
    own = pltpu.make_async_copy(source(me), target(me), own_sem)
    own.start()
    own.wait()
    swap.wait_recv()
    swap.wait_send()


class Pair:
    def __init__(self):
        ctx, half = lax.axis_index("ctx"), lax.axis_size("ctx") // 2
        self.role = lax.div(ctx, half)
        self.peer = ctx + half - 2 * half * self.role

    def copy(self, source, target, send, recv):
        return pltpu.make_async_remote_copy(
            src_ref=source,
            dst_ref=target,
            send_sem=send,
            recv_sem=recv,
            device_id={"ctx": self.peer},
            device_id_type=MESH,
        )


def pair_gather_kernel(x, peaks, o, peaks_all, own_sem, send, recv, pair_send, pair_recv):
    shard, pair = lax.axis_index("shard"), Pair()
    Greeting().ring("shard").pair().wait()
    own_rows = Direct(
        "shard", whole_of(x), lambda d, k: o.at[0, d], send.at[0], recv.at[0]
    )
    peer_rows = Direct(
        "shard", lambda d: o.at[1, shard], lambda d, k: o.at[1, d], send.at[1], recv.at[1]
    )
    tops = Direct("shard", whole_of(peaks), block_from(peaks_all), send.at[2], recv.at[2])
    across = pair.copy(x, o.at[1, shard], pair_send, pair_recv)
    across.start()
    own_rows.start()
    tops.start()
    own = [
        pltpu.make_async_copy(x, o.at[0, shard], own_sem.at[0]),
        pltpu.make_async_copy(peaks, peaks_all.at[shard], own_sem.at[1]),
    ]
    for copy in own:
        copy.start()
    across.wait_recv()
    peer_rows.start()
    for copy in own:
        copy.wait()
    across.wait_send()
    for direct in (own_rows, peer_rows, tops):
        direct.wait_recv()
        direct.wait_send()


class PairReduce:
    def __init__(self, x, o, buf, part, peer, send, recv, pair_send, pair_recv):
        self.x, self.o, self.buf, self.part, self.peer = x, o, buf, part, peer
        self.pair = Pair()
        self.first = Direct(
            "shard", lambda d: x.at[1, d], lambda d, k: buf.at[1, k - 1], send.at[1], recv.at[1]
        )
        self.second = Direct(
            "shard", lambda d: x.at[0, d], lambda d, k: buf.at[0, k - 1], send.at[0], recv.at[0]
        )
        self.across = self.pair.copy(part, peer, pair_send, pair_recv)

    def start(self):
        self.first.start()
        self.second.start()

    def add_up(self, half, o, more=None):
        x, buf, shard = self.x, self.buf, self.first.me
        rows = x.shape[2]
        step = 8 if rows % 32 else 32

        @pl.loop(0, rows // step)
        def _(j):
            at = pl.ds(pl.multiple_of(j * step, step), step)
            total = x[half, shard, at].astype(f32)
            for k in range(buf.shape[1]):
                total = total + buf[half, k, at].astype(f32)
            if more is not None:
                total = total + more[at].astype(f32)
            o[at] = total.astype(o.dtype)

    def turn(self):
        self.first.wait_recv()
        self.add_up(1, self.part)
        self.across.start()

    def finish(self):
        self.second.wait_recv()
        self.across.wait_recv()
        self.add_up(0, self.o, self.peer)
        self.across.wait_send()
        self.first.wait_send()
        self.second.wait_send()


def pair_reduce_scratch(n_shard, x):
    sem = pltpu.SemaphoreType.DMA
    return [
        pltpu.VMEM((2, n_shard - 1, *x.shape[2:]), x.dtype),
        pltpu.VMEM(x.shape[2:], x.dtype),
        pltpu.VMEM(x.shape[2:], x.dtype),
        sem((2, n_shard)),
        sem((2, n_shard)),
        sem,
        sem,
    ]


def pair_reduce_kernel(count, *refs):
    ins, outs, rest = refs[:count], refs[count : 2 * count], refs[2 * count :]
    Greeting().ring("shard").pair().wait()
    all_of = [PairReduce(ins[i], outs[i], *rest[7 * i : 7 * i + 7]) for i in range(count)]
    for one in all_of:
        one.start()
    for one in all_of:
        one.turn()
    for one in all_of:
        one.finish()


def many_sum_kernel(axis, x, o, buf, send, recv):
    Greeting().ring(axis).wait()
    direct = Direct(axis, whole_of(x), buffer_of(buf), send, recv)
    direct.start()
    direct.wait_recv()
    total = x[...]
    for k in range(buf.shape[0]):
        total = total + buf[k]
    o[...] = total
    direct.wait_send()


def end_kernel(
    x, wide, out, y, x_sum, wide_all, out_sum, y_sum, wide_buf, out_buf, wide_sum,
    own_sem, wide_send, wide_recv, out_send, out_recv, swap_send, swap_recv, *rest,
):
    ctx = lax.axis_index("ctx")
    Greeting().ring("ctx").ring("shard").wait()
    wides = Direct("shard", block_of(wide), buffer_of(wide_buf), wide_send, wide_recv)
    outs = Direct("shard", block_of(out), buffer_of(out_buf), out_send, out_recv)
    swap = Direct("ctx", block_of(wide_sum), block_from(wide_all), swap_send, swap_recv)
    line = LineReduce(LINE_CHUNKS, x, x_sum, *rest[7:])
    returns = PairReduce(y, y_sum, *rest[:7])
    line.start()
    wides.start()
    returns.start()
    outs.start()
    line.pass_on()
    wides.wait_recv()
    for b in range(lax.axis_size("ctx")):
        rows = wide_sum.shape[1]
        total = wide[wides.me, b * rows : (b + 1) * rows].astype(f32)
        for k in range(wide_buf.shape[0]):
            total = total + wide_buf[k, b * rows : (b + 1) * rows].astype(f32)
        wide_sum[b] = total.astype(bf16)
    swap.start()
    own = pltpu.make_async_copy(wide_sum.at[ctx], wide_all.at[ctx], own_sem)
    own.start()
    line.finish()
    returns.turn()
    outs.wait_recv()
    add_up(out, out_buf, out_sum, outs.me)
    returns.finish()
    own.wait()
    swap.wait_recv()
    for direct in (swap, wides, outs):
        direct.wait_send()


def remote_params(collective_id, megabytes):
    return pltpu.CompilerParams(
        collective_id=collective_id, has_side_effects=True, vmem_limit_bytes=megabytes << 20
    )


LINE_CHUNKS = 4


def start_call(collective_id, x, w, w_query, w_key, w_value, small, cot):
    n_ctx, n_shard = lax.axis_size("ctx"), lax.axis_size("shard")
    n = n_ctx // 2
    heads = (w.shape[0], 3 * w.shape[1] // n_ctx)
    sem = pltpu.SemaphoreType.DMA
    return pl.pallas_call(
        start_kernel,
        out_shape=[
            jax.ShapeDtypeStruct((n_ctx, *x.shape), bf16),
            jax.ShapeDtypeStruct((n_ctx, n_shard, *w.shape), bf16),
            jax.ShapeDtypeStruct((n_ctx, n_shard, *heads), bf16),
            jax.ShapeDtypeStruct((n_ctx, n_shard, *small.shape), bf16),
            jax.ShapeDtypeStruct((n_shard, *cot.shape), bf16),
        ],
        in_specs=[ANY] * 7,
        out_specs=[ANY] * 5,
        scratch_shapes=[
            pltpu.VMEM((n_ctx, *heads), bf16),
            pltpu.VMEM((n_ctx, *small.shape), bf16),
            sem((7,)),
            sem((4, n_ctx)),
            sem((4, n_ctx)),
        ]
        + [sem((3, n_shard))] * 2
        + [sem((n_shard, n))] * 4
        + line_gather_scratch(n, LINE_CHUNKS + 1),
        compiler_params=remote_params(collective_id, 8),
    )(x, w, w_query, w_key, w_value, small, cot)


def exchange(collective_id, x, to_rows):
    n = lax.axis_size("ctx")
    shape = (x.shape[0] * n, x.shape[1] // n) if to_rows else (x.shape[0] // n, x.shape[1] * n)
    sem = pltpu.SemaphoreType.DMA
    return pl.pallas_call(
        functools.partial(exchange_kernel, to_rows),
        out_shape=jax.ShapeDtypeStruct(shape, x.dtype),
        in_specs=[ANY],
        out_specs=ANY,
        scratch_shapes=[sem, sem((n,)), sem((n,))],
        compiler_params=remote_params(collective_id, 8),
    )(x)


def pair_gather(collective_id, x, peaks):
    n = lax.axis_size("shard")
    sem = pltpu.SemaphoreType.DMA
    return pl.pallas_call(
        pair_gather_kernel,
        out_shape=[
            jax.ShapeDtypeStruct((2, n, *x.shape), x.dtype),
            jax.ShapeDtypeStruct((n, *peaks.shape), peaks.dtype),
        ],
        in_specs=[ANY] * 2,
        out_specs=[ANY] * 2,
        scratch_shapes=[sem((2,)), sem((3, n)), sem((3, n)), sem, sem],
        compiler_params=remote_params(collective_id, 8),
    )(x, peaks)


def pair_reduce(collective_id, *arrays):
    n = lax.axis_size("shard")
    return pl.pallas_call(
        functools.partial(pair_reduce_kernel, len(arrays)),
        out_shape=[jax.ShapeDtypeStruct(a.shape[2:], f32) for a in arrays],
        in_specs=[VMEM] * len(arrays),
        out_specs=[VMEM] * len(arrays),
        scratch_shapes=sum((pair_reduce_scratch(n, a) for a in arrays), []),
        compiler_params=remote_params(collective_id, 40),
    )(*arrays)


def many_sum(axis, collective_id, x):
    n = lax.axis_size(axis)
    sem = pltpu.SemaphoreType.DMA
    return pl.pallas_call(
        functools.partial(many_sum_kernel, axis),
        out_shape=jax.ShapeDtypeStruct(x.shape, x.dtype),
        in_specs=[VMEM],
        out_specs=VMEM,
        scratch_shapes=[pltpu.VMEM((n - 1, *x.shape), x.dtype), sem((n,)), sem((n,))],
        compiler_params=remote_params(collective_id, 8),
    )(x)


def end_call(collective_id, x, wide, out, y):
    n_ctx, rows, width = x.shape
    n_shard = lax.axis_size("shard")
    n = n_ctx // 2
    wide_rows, wide_cols = wide.shape[1] // n_ctx, wide.shape[2]
    sem = pltpu.SemaphoreType.DMA
    return pl.pallas_call(
        end_kernel,
        out_shape=[
            jax.ShapeDtypeStruct((rows, width), f32),
            jax.ShapeDtypeStruct((n_ctx, wide_rows, wide_cols), bf16),
            jax.ShapeDtypeStruct(out.shape[1:], f32),
            jax.ShapeDtypeStruct(y.shape[2:], f32),
        ],
        in_specs=[VMEM] * 4,
        out_specs=[VMEM] * 4,
        scratch_shapes=[
            pltpu.VMEM((n_shard - 1, *wide.shape[1:]), bf16),
            pltpu.VMEM((n_shard - 1, *out.shape[1:]), bf16),
            pltpu.VMEM((n_ctx, wide_rows, wide_cols), bf16),
            sem,
        ]
        + [sem((n_shard,))] * 4
        + [sem((n_ctx,))] * 2
        + pair_reduce_scratch(n_shard, y)
        + [pltpu.VMEM((n, rows, width), bf16)] * 3
        + [sem((n, LINE_CHUNKS))] * 5,
        compiler_params=remote_params(collective_id, 56),
    )(x, wide, out, y)


def per_device(
    tokens,
    doc_ids,
    routes,
    attn_gain,
    w_query,
    w_key,
    w_value,
    query_gain,
    key_gain,
    w_out,
    ffn_gain,
    w_router,
    w_gate,
    w_up,
    w_down,
    clip_threshold,
    cotangent,
):
    both = ("ctx", "shard")
    n_ctx, n_shard = lax.axis_size("ctx"), lax.axis_size("shard")
    ctx, shard = lax.axis_index("ctx"), lax.axis_index("shard")
    x_own = tokens[0]
    rows, width = x_own.shape
    part = w_query.shape[0]
    cols = width // n_ctx
    heads = cols // HEAD
    count = rows * n_ctx
    local = w_gate.shape[0]
    experts = local * n_shard

    top = routes.shape[2]
    spare = jnp.zeros((part, LANES - 4 - experts - rows // part * (1 + top)), bf16)
    small = jnp.concatenate(
        [
            jnp.stack([attn_gain, query_gain, key_gain, ffn_gain], axis=1),
            w_router,
            doc_ids.reshape(part, rows // part).astype(bf16),
            routes.reshape(part, rows // part * top).astype(bf16),
            spare,
        ],
        axis=1,
    )
    grad_own = cotangent[0]
    x_all, out_w, weights, small_all, grad_mine = start_call(
        1, x_own, w_out, w_query, w_key, w_value, small, grad_own
    )
    x_all = x_all.reshape(count, width)
    out_w = out_w.reshape(width, width)
    weights = weights.reshape(width, 3 * cols)
    gains = small_all[..., : 4 + experts].reshape(width, 4 + experts)
    gain_attn, gain_query, gain_key, gain_ffn = (gains[:, i].astype(f32) for i in range(4))
    router_w = gains[:, 4:]
    gain_query = lax.dynamic_slice_in_dim(gain_query, ctx * cols, cols)
    gain_key = lax.dynamic_slice_in_dim(gain_key, ctx * cols, cols)
    tail = small_all[..., 4 + experts :].astype(jnp.int32)
    docs = lax.dynamic_index_in_dim(tail[..., : rows // part], shard, 1, False).reshape(count)
    span = n_ctx // 2
    role = lax.div(ctx, span)
    routes_all = tail[..., rows // part : rows // part * (1 + top)].reshape(
        n_ctx, n_shard, rows, top
    )
    routes_all = jnp.stack(
        [
            lax.dynamic_index_in_dim(routes_all, ctx, 0, False),
            lax.dynamic_index_in_dim(routes_all, lax.rem(ctx + span, n_ctx), 0, False),
        ]
    ).reshape(2 * n_shard * rows, top)

    def swap(u):
        return lax.ppermute(u, "ctx", [(i, (i + span) % n_ctx) for i in range(n_ctx)])

    def queued_swap(u):
        both = lax.all_gather(
            u, "ctx", axis=0, axis_index_groups=[[i, i + span] for i in range(span)]
        )
        return lax.dynamic_index_in_dim(both, 1 - role, 0, False)

    def in_order(mine, theirs):
        return jnp.where(role == 0, jnp.stack([mine, theirs]), jnp.stack([theirs, mine]))

    half = local // 2
    ff = w_gate.shape[2]
    own_w = jnp.concatenate([w_gate, w_up, w_down.transpose(0, 2, 1)], axis=2)
    keep_w = lax.dynamic_slice_in_dim(own_w, role * half, half, 0)
    give_w = lax.dynamic_slice_in_dim(own_w, (1 - role) * half, half, 0)
    spans = [list(range(r * span, (r + 1) * span)) for r in (0, 1)]
    first_w = swap(give_w[0])
    x_all, first_w, later_w, later_grad = lax.optimization_barrier(
        (x_all, first_w, give_w[1:], grad_own)
    )
    grad_theirs = swap(later_grad)
    early = [first_w] + [queued_swap(later_w[e]) for e in range(half - 1)]
    def expert_weights(e, theirs):
        return lax.all_gather(
            in_order(keep_w[e], theirs),
            "ctx",
            axis=1,
            tiled=True,
            axis_index_groups=spans,
        ).reshape(width, 3 * ff)

    expert_w = [expert_weights(0, early[0])]

    x_wide = x_all.astype(f32)
    inverse_one = inverse_rms(x_wide)
    hidden_one = (x_wide * inverse_one * gain_attn).astype(bf16)
    linear = dot(hidden_one, weights)
    query_lin, key_lin = linear[:, :cols], linear[:, cols : 2 * cols]
    value = linear[:, 2 * cols :].astype(bf16)
    squares = jnp.stack(
        [jnp.sum(query_lin * query_lin, axis=1), jnp.sum(key_lin * key_lin, axis=1)]
    )
    squares = many_sum("ctx", 6, squares)
    inverse_qk = lax.rsqrt(squares / width + norm_eps)
    inverse_q, inverse_k = inverse_qk[0][:, None], inverse_qk[1][:, None]
    cosine, sine = rope_tables(count)
    query_n, key_n = query_lin * inverse_q, key_lin * inverse_k
    query = rotate(query_n * gain_query, cosine, sine).astype(bf16)
    key = rotate(key_n * gain_key, cosine, sine).astype(bf16)
    mixed, log_total, peaks = attend_forward(query, key, value, docs)
    grad_mine = grad_mine.reshape(n_shard * rows, width)
    x_f = x_own.astype(f32)
    after = x_f + dot(exchange(2, mixed, False), out_w)
    inverse_two = inverse_rms(after)
    normed_two = after * inverse_two
    hidden_two = (normed_two * gain_ffn).astype(bf16)

    hidden_all, peaks = pair_gather(3, hidden_two, peaks)
    hidden_all, early, grad_theirs = lax.optimization_barrier(
        (hidden_all, early[1:], grad_theirs)
    )
    grad_theirs = lax.all_gather(grad_theirs, "shard", axis=0, tiled=True)
    expert_w += [expert_weights(e + 1, u) for e, u in enumerate(early)]
    hidden_all = hidden_all.reshape(2 * n_shard * rows, width)
    peaks = jnp.max(peaks, axis=0)[:, 0, 0]
    logits = dot(hidden_all, router_w)
    named = jnp.any(routes_all[:, :, None] == jnp.arange(experts)[None, None, :], axis=1)
    probs = jax.nn.softmax(logits, axis=1)
    selected = jnp.where(named, probs, 0.0)
    selected_sum = jnp.sum(selected, axis=1, keepdims=True)
    gates = selected / selected_sum
    first = shard * local + role * half
    gates_own = lax.dynamic_slice_in_dim(gates, first, half, 1)
    named_own = lax.dynamic_slice_in_dim(named, first, half, 1)
    moe_part = jnp.zeros(hidden_all.shape, f32)
    back_part = jnp.zeros(hidden_all.shape, f32)

    def by_half(grad_theirs, function, *arrays):
        split = grad_mine.shape[0]
        return jnp.concatenate(
            [
                function(grad_mine.astype(f32), *(u[:split] for u in arrays)),
                function(grad_theirs.astype(f32), *(u[split:] for u in arrays)),
            ]
        )

    grad_gates, expert_grads = [], []
    for e in range(half):
        wide, down = expert_w[e][:, : 2 * ff], expert_w[e][:, 2 * ff :]
        gate_col = gates_own[:, e : e + 1]
        hidden = dot(hidden_all, wide)
        gate_h, up_h = hidden[:, :ff], hidden[:, ff:]
        sig = jax.nn.sigmoid(gate_h)
        silu = gate_h * sig
        act = (silu * up_h).astype(bf16)
        if e == 0:
            act, grad_theirs = lax.optimization_barrier((act, grad_theirs))
        result = contract_cols(act, down).astype(bf16).astype(f32)
        moe_part = moe_part + gate_col * result
        along = by_half(grad_theirs, lambda d, u: jnp.sum(d * u, axis=1), result)
        grad_gates.append(jnp.where(named_own[:, e], along, 0.0))
        grad_y = by_half(grad_theirs, lambda d, u: (u * d).astype(bf16), gate_col)
        grad_act = dot(grad_y, down)
        grad_h = jnp.concatenate(
            [grad_act * up_h * sig * (1.0 + gate_h * (1.0 - sig)), grad_act * silu], axis=1
        ).astype(bf16)
        back_part = back_part + contract_cols(grad_h, wide).astype(bf16).astype(f32)
        grad_w = [
            contract_rows(hidden_all, grad_h).astype(bf16),
            contract_rows(grad_y, act).astype(bf16),
        ]
        hidden_all, back_part, grad_w, expert_grads = lax.optimization_barrier(
            (hidden_all, back_part, grad_w, expert_grads)
        )
        expert_grads.append(
            [
                lax.psum_scatter(
                    u.reshape(2, width // 2, -1),
                    "ctx",
                    scatter_dimension=1,
                    tiled=True,
                    axis_index_groups=spans,
                )
                for u in grad_w
            ]
        )
    slots = jnp.stack(grad_gates).reshape(half, 2, n_shard, rows).transpose(1, 2, 0, 3)
    grad_gates = lax.dynamic_update_slice_in_dim(
        jnp.zeros((2, n_shard, experts, rows), f32), slots, first, 2
    )
    back_sum, grad_gates = pair_reduce(
        4, back_part.astype(bf16).reshape(2, n_shard, rows, width), grad_gates
    )
    grad_gates = grad_gates.T
    def own_rows(u):
        return lax.dynamic_slice_in_dim(u, shard * rows, rows, 0)

    gates_t, probs_t, named_t, sum_t = map(own_rows, (gates, probs, named, selected_sum))
    grad_selected = (
        grad_gates - jnp.sum(gates_t * grad_gates, axis=1, keepdims=True)
    ) / sum_t
    grad_probs = jnp.where(named_t, grad_selected, 0.0)
    grad_logits = (
        probs_t * (grad_probs - jnp.sum(probs_t * grad_probs, axis=1, keepdims=True))
    ).astype(bf16)
    grad_router = contract_rows(hidden_two, grad_logits)
    grad_hidden = back_sum + contract_cols(grad_logits, router_w)
    grad_gain_ffn = jnp.sum(grad_hidden * normed_two, axis=0)
    scaled_two = grad_hidden * gain_ffn
    grad_after = grad_own.astype(f32) + inverse_two * (
        scaled_two - normed_two * jnp.mean(scaled_two * normed_two, axis=1, keepdims=True)
    )

    grad_attn_own = grad_after.astype(bf16)
    to_gather, expert_grads = lax.optimization_barrier((grad_attn_own, expert_grads))
    grad_attn = lax.all_gather(to_gather, "ctx", axis=0, tiled=True)
    grad_mixed = exchange(5, contract_cols(grad_attn_own, out_w).astype(bf16), True)
    grad_attn, expert_grads = lax.optimization_barrier((grad_attn, expert_grads))
    grad_out_w = contract_rows(mixed, grad_attn)
    grad_query_rot, grad_key_rot, grad_value = attend_backward(
        query, key, value, docs, log_total, grad_mixed
    )
    kept = [[lax.dynamic_index_in_dim(u, role, 0, False) for u in sums] for sums in expert_grads]
    peers = queued_swap(
        jnp.stack(
            [
                jnp.concatenate(
                    [lax.dynamic_index_in_dim(u, 1 - role, 0, False) for u in sums], axis=1
                )
                for sums in expert_grads
            ]
        )
    )
    peers = [(peer[:, : 2 * ff], peer[:, 2 * ff :]) for peer in peers]
    both_halves = [
        in_order(jnp.stack([k[i] for k in kept]), jnp.stack([p[i] for p in peers]))
        .reshape(local, width // n_ctx, -1)
        .astype(f32)
        for i in (0, 1)
    ]
    grad_query_n = rotate(grad_query_rot, cosine, -sine)
    grad_key_n = rotate(grad_key_rot, cosine, -sine)
    grad_gain_query = jnp.sum(grad_query_n * query_n, axis=0)
    grad_gain_key = jnp.sum(grad_key_n * key_n, axis=0)
    scaled_q, scaled_k = grad_query_n * gain_query, grad_key_n * gain_key
    peak_row = lax.dynamic_update_slice_in_dim(jnp.zeros((count,), f32), peaks, ctx * heads, 0)
    inner = jnp.stack(
        [jnp.sum(scaled_q * query_n, axis=1), jnp.sum(scaled_k * key_n, axis=1), peak_row]
    )
    inner = many_sum("ctx", 7, inner)
    peak_all = inner[2, :HEADS]
    inner = inner / width
    grad_linear = jnp.concatenate(
        [
            inverse_q * (scaled_q - query_n * inner[0][:, None]),
            inverse_k * (scaled_k - key_n * inner[1][:, None]),
            grad_value,
        ],
        axis=1,
    ).astype(bf16)
    grad_weights = contract_rows(hidden_one, grad_linear)
    hidden_part = contract_cols(grad_linear, weights)
    grad_gain_attn = jnp.sum(hidden_part * (x_wide * inverse_one), axis=0)
    grad_small = jnp.concatenate(
        [jnp.stack([grad_gain_attn, grad_gain_ffn], axis=1), grad_router], axis=1
    )
    grad_small = jnp.pad(grad_small, ((0, 0), (0, LANES - 2 - experts)))
    grad_weights = (
        jnp.concatenate([grad_weights, grad_small], axis=1)
        .astype(bf16)
        .reshape(n_ctx, n_shard, part, 3 * cols + LANES)
        .transpose(1, 0, 2, 3)
        .reshape(n_shard, n_ctx * part, 3 * cols + LANES)
    )
    grad_gain_qk = jnp.pad(
        jnp.stack([grad_gain_query, grad_gain_key], axis=1), ((0, 0), (0, LANES - 2))
    )
    grad_out_w = (
        jnp.concatenate([grad_out_w, grad_gain_qk], axis=1)
        .astype(bf16)
        .reshape(n_shard, part, width + LANES)
    )
    grad_hidden_one, grad_weights, grad_out_w, moe_sum = end_call(
        8,
        hidden_part.astype(bf16).reshape(n_ctx, rows, width),
        grad_weights,
        grad_out_w,
        moe_part.astype(bf16).reshape(2, n_shard, rows, width),
    )
    output = (after + moe_sum).astype(bf16)
    grad_weights = grad_weights.astype(f32)
    grad_small = jnp.sum(grad_weights[..., 3 * cols :], axis=0)
    grad_weights = (
        grad_weights[..., : 3 * cols]
        .reshape(n_ctx, part, 3, cols)
        .transpose(2, 1, 0, 3)
        .reshape(3, part, width)
    )
    inverse_own = inverse_rms(x_f)
    normed_own = x_f * inverse_own
    scaled_one = grad_hidden_one * gain_attn
    grad_inputs = grad_after + inverse_own * (
        scaled_one - normed_own * jnp.mean(scaled_one * normed_own, axis=1, keepdims=True)
    )

    factors = jnp.sqrt(clip_threshold / jnp.maximum(peak_all, clip_threshold))
    col_scale = jnp.repeat(factors, HEAD)
    query_clipped = (w_query.astype(f32) * col_scale[None, :]).astype(bf16)
    key_clipped = (w_key.astype(f32) * col_scale[None, :]).astype(bf16)
    return (
        output[None],
        grad_inputs[None],
        grad_small[:, 0],
        grad_weights[0],
        grad_weights[1],
        grad_weights[2],
        grad_out_w[:, width],
        grad_out_w[:, width + 1],
        grad_out_w[:, :width],
        grad_small[:, 1],
        grad_small[:, 2 : 2 + experts],
        both_halves[0][..., :ff],
        both_halves[0][..., ff:],
        both_halves[1].transpose(0, 2, 1),
        query_clipped,
        key_clipped,
        factors,
    )


def solution(mesh):
    both = ("ctx", "shard")
    return jax.shard_map(
        per_device,
        mesh=mesh,
        in_specs=(
            P("shard", "ctx", None),
            P("shard", "ctx"),
            P("shard", "ctx", None),
            P(both),
            P(both, None),
            P(both, None),
            P(both, None),
            P(both),
            P(both),
            P(both, None),
            P(both),
            P(both, None),
            P("shard", "ctx", None),
            P("shard", "ctx", None),
            P("shard", None, "ctx"),
            P(),
            P("shard", "ctx", None),
        ),
        out_specs=(
            P("shard", "ctx", None),
            P("shard", "ctx", None),
            P(both),
            P(both, None),
            P(both, None),
            P(both, None),
            P(both),
            P(both),
            P(both, None),
            P(both),
            P(both, None),
            P("shard", "ctx", None),
            P("shard", "ctx", None),
            P("shard", None, "ctx"),
            P(both, None),
            P(both, None),
            P(),
        ),
        check_vma=False,
    )
```

```python
import functools

import jax
import jax.numpy as jnp
from jax import lax
from jax.experimental import pallas as pl
from jax.experimental.pallas import tpu as pltpu
from jax.sharding import PartitionSpec as P

HEADS = 16
HEAD = 128
SCALE = HEAD ** (-0.5)
Q_BLOCK = 256
LANES = 128

norm_eps = 1e-06
rope_base = 10000.0
f32 = jnp.float32
bf16 = jnp.bfloat16


def dot(a, b):
    return jnp.dot(a, b, preferred_element_type=f32)


def contract_rows(a, b):
    return lax.dot_general(a, b, (((0,), (0,)), ((), ())), preferred_element_type=f32)


def contract_cols(a, b):
    return lax.dot_general(a, b, (((1,), (1,)), ((), ())), preferred_element_type=f32)


def inverse_rms(values):
    return lax.rsqrt(jnp.mean(values * values, axis=-1, keepdims=True) + norm_eps)


def rope_tables(count):
    half = HEAD // 2
    freq = rope_base ** (-jnp.arange(half).astype(f32) / half)
    angles = jnp.arange(count).astype(f32)[:, None] * freq[None, :]
    return jnp.cos(angles), jnp.sin(angles)


def rotate(values, cosine, sine):
    parts = []
    for col in range(0, values.shape[1], HEAD):
        a = values[:, col : col + HEAD // 2]
        b = values[:, col + HEAD // 2 : col + HEAD]
        parts += [a * cosine - b * sine, b * cosine + a * sine]
    return jnp.concatenate(parts, axis=1)


def attend_forward_kernel(q_ref, k_ref, v_ref, doc_q_ref, doc_k_ref, o_ref, lse_ref, peak_ref):
    s = SCALE * contract_cols(q_ref[...], k_ref[...])
    s = jnp.where(doc_q_ref[...] == doc_k_ref[...], s, -1e30)
    top = jnp.max(s, axis=1, keepdims=True)
    e = jnp.exp(s - top)
    total = jnp.sum(e, axis=1, keepdims=True)
    p = (e * (1.0 / total)).astype(bf16)
    o_ref[...] = dot(p, v_ref[...]).astype(bf16)
    lse_ref[0] = top + jnp.log(total)
    peak = jnp.broadcast_to(jnp.max(top, axis=0, keepdims=True), peak_ref.shape[1:])

    @pl.when(pl.program_id(1) == 0)
    def _():
        peak_ref[0] = peak

    @pl.when(pl.program_id(1) > 0)
    def _():
        peak_ref[0] = jnp.maximum(peak_ref[0], peak)


def attend_backward_kernel(
    q_ref, k_ref, v_ref, doc_q_ref, doc_k_ref, lse_ref, do_ref, dq_ref, dk_ref, dv_ref
):
    q, k, v, do = q_ref[...], k_ref[...], v_ref[...], do_ref[...]
    s = SCALE * contract_cols(q, k)
    p = jnp.where(doc_q_ref[...] == doc_k_ref[...], jnp.exp(s - lse_ref[0]), 0.0)
    dp = contract_cols(do, v)
    inner = jnp.sum(p * dp, axis=1, keepdims=True)
    ds = (p * (dp - inner)).astype(bf16)
    dq_ref[...] = SCALE * dot(ds, k)
    dk = SCALE * contract_rows(ds, q)
    dv = contract_rows(p.astype(bf16), do)

    @pl.when(pl.program_id(1) == 0)
    def _():
        dk_ref[...] = dk
        dv_ref[...] = dv

    @pl.when(pl.program_id(1) > 0)
    def _():
        dk_ref[...] += dk
        dv_ref[...] += dv


def attend_specs(count):
    block = pl.BlockSpec((Q_BLOCK, HEAD), lambda h, i: (i, h))
    whole = pl.BlockSpec((count, HEAD), lambda h, i: (0, h))
    doc_q = pl.BlockSpec((Q_BLOCK, 1), lambda h, i: (i, 0))
    doc_k = pl.BlockSpec((1, count), lambda h, i: (0, 0))
    lse = pl.BlockSpec((1, Q_BLOCK, 1), lambda h, i: (h, i, 0))
    return block, whole, doc_q, doc_k, lse


def attend_forward(q, k, v, docs):
    count, width = q.shape
    heads = width // HEAD
    block, whole, doc_q, doc_k, lse = attend_specs(count)
    return pl.pallas_call(
        attend_forward_kernel,
        grid=(heads, count // Q_BLOCK),
        in_specs=[block, whole, whole, doc_q, doc_k],
        out_specs=[block, lse, pl.BlockSpec((1, 8, 128), lambda h, i: (h, 0, 0))],
        out_shape=[
            jax.ShapeDtypeStruct((count, width), bf16),
            jax.ShapeDtypeStruct((heads, count, 1), f32),
            jax.ShapeDtypeStruct((heads, 8, 128), f32),
        ],
        compiler_params=pltpu.CompilerParams(vmem_limit_bytes=48 << 20),
        cost_estimate=pl.CostEstimate(
            flops=4 * count * count * width,
            transcendentals=heads * count * count,
            bytes_accessed=8 * count * width,
        ),
    )(q, k, v, docs[:, None], docs[None, :])


def attend_backward(q, k, v, docs, log_total, grad):
    count, width = q.shape
    heads = width // HEAD
    block, whole, doc_q, doc_k, lse = attend_specs(count)
    return pl.pallas_call(
        attend_backward_kernel,
        grid=(heads, count // Q_BLOCK),
        in_specs=[block, whole, whole, doc_q, doc_k, lse, block],
        out_specs=[block, whole, whole],
        out_shape=[jax.ShapeDtypeStruct((count, width), f32)] * 3,
        compiler_params=pltpu.CompilerParams(vmem_limit_bytes=56 << 20),
        cost_estimate=pl.CostEstimate(
            flops=10 * count * count * width,
            transcendentals=heads * count * count,
            bytes_accessed=20 * count * width,
        ),
    )(q, k, v, docs[:, None], docs[None, :], log_total, grad)


MESH = pl.DeviceIdType.MESH
ANY = pl.BlockSpec(memory_space=pl.ANY)
VMEM = pl.BlockSpec(memory_space=pltpu.VMEM)


def ring_peers(axis):
    n, me = lax.axis_size(axis), lax.axis_index(axis)
    return [lax.rem(me + k, n) for k in range(n)], [lax.rem(me + n - k, n) for k in range(n)]


class Greeting:
    def __init__(self):
        self.barrier, self.total = pltpu.get_barrier_semaphore(), 0

    def ring(self, axis):
        to, _ = ring_peers(axis)
        for peer in to[1:]:
            pl.semaphore_signal(
                self.barrier, inc=1, device_id={axis: peer}, device_id_type=MESH
            )
        self.total = self.total + len(to) - 1
        return self

    def line(self):
        line = Line()
        for there, peer in (
            (line.place >= 0, line.partner),
            (line.not_last, line.me + 2),
            (line.not_first, line.me - 2),
        ):

            @pl.when(there)
            def _():
                pl.semaphore_signal(
                    self.barrier, inc=1, device_id={"ctx": peer}, device_id_type=MESH
                )

            self.total = self.total + there.astype(jnp.int32)
        return self

    def pair(self):
        pl.semaphore_signal(
            self.barrier, inc=1, device_id={"ctx": Pair().peer}, device_id_type=MESH
        )
        self.total = self.total + 1
        return self

    def wait(self):
        pl.semaphore_wait(self.barrier, self.total)


class Line:
    def __init__(self):
        self.n, self.me = lax.axis_size("ctx") // 2, lax.axis_index("ctx")
        self.place, self.core = lax.div(self.me, 2), lax.rem(self.me, 2)
        self.partner = self.me + 1 - 2 * self.core
        self.not_first, self.not_last = self.place > 0, self.place < self.n - 1


class Direct:
    def __init__(self, axis, source, target, send, recv):
        self.axis, self.source, self.target = axis, source, target
        self.send, self.recv = send, recv
        self.me = lax.axis_index(axis)
        self.to, self.origin = ring_peers(axis)

    def copy(self, k, sender):
        return pltpu.make_async_remote_copy(
            src_ref=self.source(self.to[k]),
            dst_ref=self.target(sender, k),
            send_sem=self.send.at[k],
            recv_sem=self.recv.at[k],
            device_id={self.axis: self.to[k]},
            device_id_type=MESH,
        )

    def start(self):
        for k in range(1, len(self.to)):
            self.copy(k, self.me).start()

    def wait_recv(self):
        for k in range(1, len(self.to)):
            self.copy(k, self.origin[k]).wait_recv()

    def wait_send(self):
        for k in range(1, len(self.to)):
            self.copy(k, self.me).wait_send()


class LineGather:
    def __init__(self, pieces, own_sem, send_r, send_l, send_p, recv_r, recv_l, recv_p):
        self.line, self.pieces, self.own_sem = Line(), pieces, own_sem
        self.send_r, self.send_l, self.send_p = send_r, send_l, send_p
        self.recv_r, self.recv_l, self.recv_p = recv_r, recv_l, recv_p

    def own(self, c):
        source, target = self.pieces[c]
        return pltpu.make_async_copy(source, target(self.line.me), self.own_sem.at[c])

    def copy(self, block, k, c, target_device, send, recv):
        source, target = self.pieces[c]
        return pltpu.make_async_remote_copy(
            src_ref=source if k == 0 else target(block),
            dst_ref=target(block),
            send_sem=send,
            recv_sem=recv,
            device_id={"ctx": target_device},
            device_id_type=MESH,
        )

    def right(self, k, c):
        me = self.line.me
        return self.copy(me - 2 * k, k, c, me + 2, self.send_r.at[k, c], self.recv_r.at[k, c])

    def left(self, k, c):
        me = self.line.me
        return self.copy(me + 2 * k, k, c, me - 2, self.send_l.at[k, c], self.recv_l.at[k, c])

    def across(self, k, c, sign):
        line = self.line
        i = k if sign < 0 else line.n - 1 + k
        return self.copy(
            line.me + sign * 2 * k, k, c, line.partner, self.send_p.at[i, c], self.recv_p.at[i, c]
        )

    def arrived(self, block, c, recv):
        source, target = self.pieces[c]
        pltpu.make_async_remote_copy(
            src_ref=source,
            dst_ref=target(block),
            send_sem=recv,
            recv_sem=recv,
            device_id={"ctx": self.line.partner},
            device_id_type=MESH,
        ).wait_recv()

    def start(self):
        for c in range(len(self.pieces)):
            self.own(c).start()

    def hop(self, k):
        line = self.line
        for c in range(len(self.pieces)):

            @pl.when(line.place >= k)
            def _():
                if k:
                    self.arrived(line.me - 2 * k, c, self.recv_r.at[k - 1, c])

                @pl.when(line.not_last)
                def _():
                    self.right(k, c).start()

                self.across(k, c, -1).start()

            @pl.when(line.place + k <= line.n - 1)
            def _():
                if k:
                    self.arrived(line.me + 2 * k, c, self.recv_l.at[k - 1, c])

                @pl.when(line.not_first)
                def _():
                    self.left(k, c).start()

                if k:
                    self.across(k, c, 1).start()

    def finish(self, skip_own=None):
        line = self.line
        for c in range(len(self.pieces)):
            if c != skip_own:
                self.own(c).wait()
        for k in range(line.n):
            for c in range(len(self.pieces)):

                @pl.when(line.place >= k)
                def _():
                    @pl.when(line.not_last)
                    def _():
                        self.right(k, c).wait_send()

                    self.across(k, c, -1).wait_send()
                    self.arrived(line.partner - 2 * k, c, self.recv_p.at[k, c])

                @pl.when(line.place + k <= line.n - 1)
                def _():
                    @pl.when(line.not_first)
                    def _():
                        self.left(k, c).wait_send()

                    if k:
                        self.across(k, c, 1).wait_send()
                        self.arrived(line.partner + 2 * k, c, self.recv_p.at[line.n - 1 + k, c])


def line_gather_scratch(n, pieces):
    sem = pltpu.SemaphoreType.DMA
    one, two = sem((n, pieces)), sem((2 * n - 1, pieces))
    return [sem((pieces,)), one, one, two, one, one, two]


class LineReduce:
    def __init__(
        self, chunks, x, o, pair, from_left, from_right, send_p, recv_p, send_s, recv_r, recv_l
    ):
        self.line, self.chunks = Line(), chunks
        self.x, self.o, self.pair, self.out = x, o, pair, pair
        self.from_left, self.from_right = from_left, from_right
        self.send_p, self.recv_p, self.send_s = send_p, recv_p, send_s
        self.recv_r, self.recv_l = recv_r, recv_l
        self.order = []
        for j in range(self.line.n):
            self.order += [p for p in (self.line.n - 1 - j, j) if p not in self.order]

    def at(self, c):
        rows = self.x.shape[1] // self.chunks
        return pl.ds(c * rows, rows)

    def across(self, p, c):
        line, at = self.line, self.at(c)
        return pltpu.make_async_remote_copy(
            src_ref=self.x.at[2 * p + 1 - line.core, at],
            dst_ref=self.pair.at[p, at],
            send_sem=self.send_p.at[p, c],
            recv_sem=self.recv_p.at[p, c],
            device_id={"ctx": line.partner},
            device_id_type=MESH,
        )

    def along(self, p, c, step, buffer, recv):
        at = self.at(c)
        return pltpu.make_async_remote_copy(
            src_ref=self.out.at[p, at],
            dst_ref=buffer.at[p, at],
            send_sem=self.send_s.at[p, c],
            recv_sem=recv.at[p, c],
            device_id={"ctx": self.line.me + step},
            device_id_type=MESH,
        )

    def right(self, p, c):
        return self.along(p, c, 2, self.from_left, self.recv_r)

    def left(self, p, c):
        return self.along(p, c, -2, self.from_right, self.recv_l)

    def start(self):
        for p in self.order:
            for c in range(self.chunks):
                self.across(p, c).start()

    def both(self, p, c):
        at = self.at(c)
        return self.x[2 * p + self.line.core, at].astype(f32) + self.pair[p, at].astype(f32)

    def pass_on(self):
        line = self.line
        for p in self.order:
            for c in range(self.chunks):
                at = self.at(c)
                self.across(p, c).wait_recv()

                @pl.when(line.place < p)
                def _():
                    @pl.when(line.not_first)
                    def _():
                        self.right(p, c).wait_recv()
                        total = self.both(p, c) + self.from_left[p, at].astype(f32)
                        self.out[p, at] = total.astype(bf16)

                    @pl.when(line.place == 0)
                    def _():
                        self.out[p, at] = self.both(p, c).astype(bf16)

                    self.right(p, c).start()

                @pl.when(line.place > p)
                def _():
                    @pl.when(line.not_last)
                    def _():
                        self.left(p, c).wait_recv()
                        total = self.both(p, c) + self.from_right[p, at].astype(f32)
                        self.out[p, at] = total.astype(bf16)

                    @pl.when(line.place == line.n - 1)
                    def _():
                        self.out[p, at] = self.both(p, c).astype(bf16)

                    self.left(p, c).start()

    def finish(self):
        line = self.line
        for p in range(line.n):
            for c in range(self.chunks):
                at = self.at(c)

                @pl.when(line.place == p)
                def _():
                    self.o[at] = self.both(p, c)
                    if p > 0:
                        self.right(p, c).wait_recv()
                        self.o[at] += self.from_left[p, at].astype(f32)
                    if p < line.n - 1:
                        self.left(p, c).wait_recv()
                        self.o[at] += self.from_right[p, at].astype(f32)

        for p in range(line.n):
            for c in range(self.chunks):
                self.across(p, c).wait_send()

                @pl.when(line.place < p)
                def _():
                    self.right(p, c).wait_send()

                @pl.when(line.place > p)
                def _():
                    self.left(p, c).wait_send()


def add_up(x, buf, o, me):
    rows = x.shape[1]
    step = 8 if rows % 32 else 32

    @pl.loop(0, rows // step)
    def _(j):
        at = pl.ds(pl.multiple_of(j * step, step), step)
        total = x[me, at].astype(f32)
        for k in range(buf.shape[0]):
            total = total + buf[k, at].astype(f32)
        o[at] = total.astype(o.dtype)


def block_of(ref):
    return lambda device: ref.at[device]


def block_from(ref):
    return lambda device, k: ref.at[device]


def whole_of(ref):
    return lambda device: ref


def buffer_of(ref):
    return lambda device, k: ref.at[k - 1]


def row_pieces(source, target, chunks):
    rows = source.shape[0] // chunks
    return [
        (source.at[pl.ds(c * rows, rows)], lambda b, c=c: target.at[b, pl.ds(c * rows, rows)])
        for c in range(chunks)
    ]


def start_kernel(
    x, w, w_query, w_key, w_value, small, x_all, w_all, heads_all, small_all,
    heads_mid, small_mid, own_sem, ex_send, ex_recv, sp_send, sp_recv, w_send, w_recv, f_send,
    f_recv, *line_sems,
):
    shard, ctx = lax.axis_index("shard"), lax.axis_index("ctx")
    n_ctx = lax.axis_size("ctx")
    cols = w_query.shape[1] // n_ctx
    Greeting().ring("ctx").ring("shard").wait()

    def columns(ref):
        return lambda d: ref.at[:, pl.ds(pl.multiple_of(d * cols, HEAD), cols)]

    def place(i):
        if i == 3:
            return block_from(small_mid)
        return lambda d, k: heads_mid.at[d, :, i * cols : (i + 1) * cols]

    sources = [columns(w_query), columns(w_key), columns(w_value), whole_of(small)]
    swaps = [
        Direct("ctx", source, place(i), ex_send.at[i], ex_recv.at[i])
        for i, source in enumerate(sources)
    ]

    def by_shard(ref):
        return lambda d, k: ref.at[:, d]

    spreads = [
        Direct("shard", whole_of(heads_mid), by_shard(heads_all), sp_send.at[0], sp_recv.at[0]),
        Direct("shard", whole_of(small_mid), by_shard(small_all), sp_send.at[1], sp_recv.at[1]),
    ]
    pieces = row_pieces(x, x_all, LINE_CHUNKS) + [(w, lambda b: w_all.at[b, shard])]
    line = LineGather(pieces, *line_sems)
    at = line.line
    own = [
        pltpu.make_async_copy(source(ctx), place(i)(ctx, 0), own_sem.at[i])
        for i, source in enumerate(sources)
    ]
    later = [
        pltpu.make_async_copy(heads_mid, heads_all.at[:, shard], own_sem.at[4]),
        pltpu.make_async_copy(small_mid, small_all.at[:, shard], own_sem.at[5]),
    ]
    for swap in swaps:
        swap.start()
    for copy in own:
        copy.start()
    line.start()
    line.hop(0)
    for swap in swaps:
        swap.wait_recv()
    for copy in own:
        copy.wait()
    for one in (*spreads, *later):
        one.start()
    for k in range(1, at.n):
        line.hop(k)

    to, origin = ring_peers("shard")

    def row(k, p, sender):
        block = 2 * p + at.core
        return pltpu.make_async_remote_copy(
            src_ref=w_all.at[block, shard],
            dst_ref=w_all.at[block, sender],
            send_sem=w_send.at[k, p],
            recv_sem=w_recv.at[k, p],
            device_id={"shard": to[k]},
            device_id_type=MESH,
        )

    def forward(k, p, core):
        block = w_all.at[2 * p + core, origin[k]]
        return pltpu.make_async_remote_copy(
            src_ref=block,
            dst_ref=block,
            send_sem=f_send.at[k, p],
            recv_sem=f_recv.at[k, p],
            device_id={"ctx": at.partner},
            device_id_type=MESH,
        )

    some = [(k, p) for k in range(1, len(to)) for p in range(at.n)]
    line.own(LINE_CHUNKS).wait()
    for k, p in some:
        row(k, p, shard).start()
    for k, p in some:
        row(k, p, origin[k]).wait_recv()
        forward(k, p, at.core).start()
    line.finish(skip_own=LINE_CHUNKS)
    for k, p in some:
        row(k, p, shard).wait_send()
        forward(k, p, at.core).wait_send()
        forward(k, p, 1 - at.core).wait_recv()
    for direct in spreads:
        direct.wait_recv()
    for direct in (*swaps, *spreads):
        direct.wait_send()
    for copy in later:
        copy.wait()


def exchange_kernel(to_rows, *refs):
    more = len(refs) > 5
    if more:
        x, cot, o, cot_all, own_sem, send, recv, cot_send, cot_recv = refs
    else:
        x, o, own_sem, send, recv = refs
    n, me = lax.axis_size("ctx"), lax.axis_index("ctx")
    cols, rows = (x.shape[1] // n, x.shape[0]) if to_rows else (x.shape[1], o.shape[0])

    def row_block(ref):
        return lambda d, k=0: ref.at[pl.ds(pl.multiple_of(d * rows, rows), rows)]

    def column_block(ref):
        return lambda d, k=0: ref.at[:, pl.ds(pl.multiple_of(d * cols, cols), cols)]

    source, target = (
        (column_block(x), row_block(o)) if to_rows else (row_block(x), column_block(o))
    )
    greeting = Greeting().ring("ctx")
    if more:
        greeting.ring("shard")
    greeting.wait()
    all_of = [Direct("ctx", source, target, send, recv)]
    own = [pltpu.make_async_copy(source(me), target(me), own_sem.at[0])]
    if more:
        all_of.append(Direct("shard", whole_of(cot), block_from(cot_all), cot_send, cot_recv))
        own.append(
            pltpu.make_async_copy(cot, cot_all.at[lax.axis_index("shard")], own_sem.at[1])
        )
    for one in (*all_of, *own):
        one.start()
    for copy in own:
        copy.wait()
    for direct in all_of:
        direct.wait_recv()
        direct.wait_send()


class Pair:
    def __init__(self):
        ctx, half = lax.axis_index("ctx"), lax.axis_size("ctx") // 2
        self.role = lax.div(ctx, half)
        self.peer = ctx + half - 2 * half * self.role

    def copy(self, source, target, send, recv):
        return pltpu.make_async_remote_copy(
            src_ref=source,
            dst_ref=target,
            send_sem=send,
            recv_sem=recv,
            device_id={"ctx": self.peer},
            device_id_type=MESH,
        )


def pair_gather_kernel(x, peaks, o, peaks_all, own_sem, send, recv, pair_send, pair_recv):
    shard, pair = lax.axis_index("shard"), Pair()
    Greeting().ring("shard").pair().wait()
    own_rows = Direct(
        "shard", whole_of(x), lambda d, k: o.at[0, d], send.at[0], recv.at[0]
    )
    peer_rows = Direct(
        "shard", lambda d: o.at[1, shard], lambda d, k: o.at[1, d], send.at[1], recv.at[1]
    )
    tops = Direct("shard", whole_of(peaks), block_from(peaks_all), send.at[2], recv.at[2])
    across = pair.copy(x, o.at[1, shard], pair_send, pair_recv)
    across.start()
    own_rows.start()
    tops.start()
    own = [
        pltpu.make_async_copy(x, o.at[0, shard], own_sem.at[0]),
        pltpu.make_async_copy(peaks, peaks_all.at[shard], own_sem.at[1]),
    ]
    for copy in own:
        copy.start()
    across.wait_recv()
    peer_rows.start()
    for copy in own:
        copy.wait()
    across.wait_send()
    for direct in (own_rows, peer_rows, tops):
        direct.wait_recv()
        direct.wait_send()


class PairReduce:
    def __init__(self, x, o, buf, part, peer, send, recv, pair_send, pair_recv):
        self.x, self.o, self.buf, self.part, self.peer = x, o, buf, part, peer
        self.pair = Pair()
        self.first = Direct(
            "shard", lambda d: x.at[1, d], lambda d, k: buf.at[1, k - 1], send.at[1], recv.at[1]
        )
        self.second = Direct(
            "shard", lambda d: x.at[0, d], lambda d, k: buf.at[0, k - 1], send.at[0], recv.at[0]
        )
        self.across = self.pair.copy(part, peer, pair_send, pair_recv)

    def start(self):
        self.first.start()
        self.second.start()

    def add_up(self, half, o, more=None):
        x, buf, shard = self.x, self.buf, self.first.me
        rows = x.shape[2]
        step = 8 if rows % 32 else 32

        @pl.loop(0, rows // step)
        def _(j):
            at = pl.ds(pl.multiple_of(j * step, step), step)
            total = x[half, shard, at].astype(f32)
            for k in range(buf.shape[1]):
                total = total + buf[half, k, at].astype(f32)
            if more is not None:
                total = total + more[at].astype(f32)
            o[at] = total.astype(o.dtype)

    def turn(self):
        self.first.wait_recv()
        self.add_up(1, self.part)
        self.across.start()

    def finish(self):
        self.second.wait_recv()
        self.across.wait_recv()
        self.add_up(0, self.o, self.peer)
        self.across.wait_send()
        self.first.wait_send()
        self.second.wait_send()


def pair_reduce_scratch(n_shard, x):
    sem = pltpu.SemaphoreType.DMA
    return [
        pltpu.VMEM((2, n_shard - 1, *x.shape[2:]), x.dtype),
        pltpu.VMEM(x.shape[2:], x.dtype),
        pltpu.VMEM(x.shape[2:], x.dtype),
        sem((2, n_shard)),
        sem((2, n_shard)),
        sem,
        sem,
    ]


def pair_reduce_kernel(count, *refs):
    ins, outs, rest = refs[:count], refs[count : 2 * count], refs[2 * count :]
    Greeting().ring("shard").pair().wait()
    all_of = [PairReduce(ins[i], outs[i], *rest[7 * i : 7 * i + 7]) for i in range(count)]
    for one in all_of:
        one.start()
    for one in all_of:
        one.turn()
    for one in all_of:
        one.finish()


def many_sum_kernel(axis, x, o, buf, send, recv):
    Greeting().ring(axis).wait()
    direct = Direct(axis, whole_of(x), buffer_of(buf), send, recv)
    direct.start()
    direct.wait_recv()
    total = x[...]
    for k in range(buf.shape[0]):
        total = total + buf[k]
    o[...] = total
    direct.wait_send()


def end_kernel(
    x, wide, out, y, x_sum, wide_all, out_sum, y_sum, wide_buf, out_buf, wide_sum,
    own_sem, wide_send, wide_recv, out_send, out_recv, swap_send, swap_recv, *rest,
):
    ctx = lax.axis_index("ctx")
    Greeting().ring("ctx").ring("shard").wait()
    wides = Direct("shard", block_of(wide), buffer_of(wide_buf), wide_send, wide_recv)
    outs = Direct("shard", block_of(out), buffer_of(out_buf), out_send, out_recv)
    swap = Direct("ctx", block_of(wide_sum), block_from(wide_all), swap_send, swap_recv)
    line = LineReduce(LINE_CHUNKS, x, x_sum, *rest[7:])
    returns = PairReduce(y, y_sum, *rest[:7])
    line.start()
    wides.start()
    returns.start()
    outs.start()
    line.pass_on()
    wides.wait_recv()
    for b in range(lax.axis_size("ctx")):
        rows = wide_sum.shape[1]
        total = wide[wides.me, b * rows : (b + 1) * rows].astype(f32)
        for k in range(wide_buf.shape[0]):
            total = total + wide_buf[k, b * rows : (b + 1) * rows].astype(f32)
        wide_sum[b] = total.astype(bf16)
    swap.start()
    own = pltpu.make_async_copy(wide_sum.at[ctx], wide_all.at[ctx], own_sem)
    own.start()
    line.finish()
    returns.turn()
    outs.wait_recv()
    add_up(out, out_buf, out_sum, outs.me)
    returns.finish()
    own.wait()
    swap.wait_recv()
    for direct in (swap, wides, outs):
        direct.wait_send()


def remote_params(collective_id, megabytes):
    return pltpu.CompilerParams(
        collective_id=collective_id, has_side_effects=True, vmem_limit_bytes=megabytes << 20
    )


LINE_CHUNKS = 4


def start_call(collective_id, x, w, w_query, w_key, w_value, small):
    n_ctx, n_shard = lax.axis_size("ctx"), lax.axis_size("shard")
    n = n_ctx // 2
    heads = (w.shape[0], 3 * w.shape[1] // n_ctx)
    sem = pltpu.SemaphoreType.DMA
    return pl.pallas_call(
        start_kernel,
        out_shape=[
            jax.ShapeDtypeStruct((n_ctx, *x.shape), bf16),
            jax.ShapeDtypeStruct((n_ctx, n_shard, *w.shape), bf16),
            jax.ShapeDtypeStruct((n_ctx, n_shard, *heads), bf16),
            jax.ShapeDtypeStruct((n_ctx, n_shard, *small.shape), bf16),
        ],
        in_specs=[ANY] * 6,
        out_specs=[ANY] * 4,
        scratch_shapes=[
            pltpu.VMEM((n_ctx, *heads), bf16),
            pltpu.VMEM((n_ctx, *small.shape), bf16),
            sem((6,)),
            sem((4, n_ctx)),
            sem((4, n_ctx)),
        ]
        + [sem((2, n_shard))] * 2
        + [sem((n_shard, n))] * 4
        + line_gather_scratch(n, LINE_CHUNKS + 1),
        compiler_params=remote_params(collective_id, 8),
    )(x, w, w_query, w_key, w_value, small)


def exchange(collective_id, x, to_rows, *more):
    n, n_shard = lax.axis_size("ctx"), lax.axis_size("shard")
    shape = (x.shape[0] * n, x.shape[1] // n) if to_rows else (x.shape[0] // n, x.shape[1] * n)
    sem = pltpu.SemaphoreType.DMA
    return pl.pallas_call(
        functools.partial(exchange_kernel, to_rows),
        out_shape=[jax.ShapeDtypeStruct(shape, x.dtype)]
        + [jax.ShapeDtypeStruct((n_shard, *u.shape), u.dtype) for u in more],
        in_specs=[ANY] * (1 + len(more)),
        out_specs=[ANY] * (1 + len(more)),
        scratch_shapes=[sem((2,)), sem((n,)), sem((n,))] + [sem((n_shard,))] * (2 * len(more)),
        compiler_params=remote_params(collective_id, 8),
    )(x, *more)


def pair_gather(collective_id, x, peaks):
    n = lax.axis_size("shard")
    sem = pltpu.SemaphoreType.DMA
    return pl.pallas_call(
        pair_gather_kernel,
        out_shape=[
            jax.ShapeDtypeStruct((2, n, *x.shape), x.dtype),
            jax.ShapeDtypeStruct((n, *peaks.shape), peaks.dtype),
        ],
        in_specs=[ANY] * 2,
        out_specs=[ANY] * 2,
        scratch_shapes=[sem((2,)), sem((3, n)), sem((3, n)), sem, sem],
        compiler_params=remote_params(collective_id, 8),
    )(x, peaks)


def pair_reduce(collective_id, *arrays):
    n = lax.axis_size("shard")
    return pl.pallas_call(
        functools.partial(pair_reduce_kernel, len(arrays)),
        out_shape=[jax.ShapeDtypeStruct(a.shape[2:], f32) for a in arrays],
        in_specs=[VMEM] * len(arrays),
        out_specs=[VMEM] * len(arrays),
        scratch_shapes=sum((pair_reduce_scratch(n, a) for a in arrays), []),
        compiler_params=remote_params(collective_id, 40),
    )(*arrays)


def many_sum(axis, collective_id, x):
    n = lax.axis_size(axis)
    sem = pltpu.SemaphoreType.DMA
    return pl.pallas_call(
        functools.partial(many_sum_kernel, axis),
        out_shape=jax.ShapeDtypeStruct(x.shape, x.dtype),
        in_specs=[VMEM],
        out_specs=VMEM,
        scratch_shapes=[pltpu.VMEM((n - 1, *x.shape), x.dtype), sem((n,)), sem((n,))],
        compiler_params=remote_params(collective_id, 8),
    )(x)


def end_call(collective_id, x, wide, out, y):
    n_ctx, rows, width = x.shape
    n_shard = lax.axis_size("shard")
    n = n_ctx // 2
    wide_rows, wide_cols = wide.shape[1] // n_ctx, wide.shape[2]
    sem = pltpu.SemaphoreType.DMA
    return pl.pallas_call(
        end_kernel,
        out_shape=[
            jax.ShapeDtypeStruct((rows, width), f32),
            jax.ShapeDtypeStruct((n_ctx, wide_rows, wide_cols), bf16),
            jax.ShapeDtypeStruct(out.shape[1:], f32),
            jax.ShapeDtypeStruct(y.shape[2:], f32),
        ],
        in_specs=[VMEM] * 4,
        out_specs=[VMEM] * 4,
        scratch_shapes=[
            pltpu.VMEM((n_shard - 1, *wide.shape[1:]), bf16),
            pltpu.VMEM((n_shard - 1, *out.shape[1:]), bf16),
            pltpu.VMEM((n_ctx, wide_rows, wide_cols), bf16),
            sem,
        ]
        + [sem((n_shard,))] * 4
        + [sem((n_ctx,))] * 2
        + pair_reduce_scratch(n_shard, y)
        + [pltpu.VMEM((n, rows, width), bf16)] * 3
        + [sem((n, LINE_CHUNKS))] * 5,
        compiler_params=remote_params(collective_id, 56),
    )(x, wide, out, y)


def per_device(
    tokens,
    doc_ids,
    routes,
    attn_gain,
    w_query,
    w_key,
    w_value,
    query_gain,
    key_gain,
    w_out,
    ffn_gain,
    w_router,
    w_gate,
    w_up,
    w_down,
    clip_threshold,
    cotangent,
):
    both = ("ctx", "shard")
    n_ctx, n_shard = lax.axis_size("ctx"), lax.axis_size("shard")
    ctx, shard = lax.axis_index("ctx"), lax.axis_index("shard")
    x_own = tokens[0]
    rows, width = x_own.shape
    part = w_query.shape[0]
    cols = width // n_ctx
    heads = cols // HEAD
    count = rows * n_ctx
    local = w_gate.shape[0]
    experts = local * n_shard

    top = routes.shape[2]
    spare = jnp.zeros((part, LANES - 4 - experts - rows // part * (1 + top)), bf16)
    small = jnp.concatenate(
        [
            jnp.stack([attn_gain, query_gain, key_gain, ffn_gain], axis=1),
            w_router,
            doc_ids.reshape(part, rows // part).astype(bf16),
            routes.reshape(part, rows // part * top).astype(bf16),
            spare,
        ],
        axis=1,
    )
    grad_own = cotangent[0]
    x_all, out_w, weights, small_all = start_call(
        1, x_own, w_out, w_query, w_key, w_value, small
    )
    x_all = x_all.reshape(count, width)
    out_w = out_w.reshape(width, width)
    weights = weights.reshape(width, 3 * cols)
    gains = small_all[..., : 4 + experts].reshape(width, 4 + experts)
    gain_attn, gain_query, gain_key, gain_ffn = (gains[:, i].astype(f32) for i in range(4))
    router_w = gains[:, 4:]
    gain_query = lax.dynamic_slice_in_dim(gain_query, ctx * cols, cols)
    gain_key = lax.dynamic_slice_in_dim(gain_key, ctx * cols, cols)
    tail = small_all[..., 4 + experts :].astype(jnp.int32)
    docs = lax.dynamic_index_in_dim(tail[..., : rows // part], shard, 1, False).reshape(count)
    span = n_ctx // 2
    role = lax.div(ctx, span)
    routes_all = tail[..., rows // part : rows // part * (1 + top)].reshape(
        n_ctx, n_shard, rows, top
    )
    routes_all = jnp.stack(
        [
            lax.dynamic_index_in_dim(routes_all, ctx, 0, False),
            lax.dynamic_index_in_dim(routes_all, lax.rem(ctx + span, n_ctx), 0, False),
        ]
    ).reshape(2 * n_shard * rows, top)

    def swap(u):
        return lax.ppermute(u, "ctx", [(i, (i + span) % n_ctx) for i in range(n_ctx)])

    def queued_swap(u):
        both = lax.all_gather(
            u, "ctx", axis=0, axis_index_groups=[[i, i + span] for i in range(span)]
        )
        return lax.dynamic_index_in_dim(both, 1 - role, 0, False)

    def in_order(mine, theirs):
        return jnp.where(role == 0, jnp.stack([mine, theirs]), jnp.stack([theirs, mine]))

    half = local // 2
    ff = w_gate.shape[2]
    own_w = jnp.concatenate([w_gate, w_up, w_down.transpose(0, 2, 1)], axis=2)
    keep_w = lax.dynamic_slice_in_dim(own_w, role * half, half, 0)
    give_w = lax.dynamic_slice_in_dim(own_w, (1 - role) * half, half, 0)
    spans = [list(range(r * span, (r + 1) * span)) for r in (0, 1)]
    grad_theirs = queued_swap(grad_own)
    first_w = queued_swap(give_w[0])
    x_all, first_w, later_w = lax.optimization_barrier((x_all, first_w, give_w[1:]))
    early = [first_w] + [queued_swap(later_w[e]) for e in range(half - 1)]

    def expert_weights(e, theirs):
        return lax.all_gather(
            in_order(keep_w[e], theirs),
            "ctx",
            axis=1,
            tiled=True,
            axis_index_groups=spans,
        ).reshape(width, 3 * ff)

    expert_w = [expert_weights(0, early[0])]

    x_wide = x_all.astype(f32)
    inverse_one = inverse_rms(x_wide)
    hidden_one = (x_wide * inverse_one * gain_attn).astype(bf16)
    linear = dot(hidden_one, weights)
    query_lin, key_lin = linear[:, :cols], linear[:, cols : 2 * cols]
    value = linear[:, 2 * cols :].astype(bf16)
    squares = jnp.stack(
        [jnp.sum(query_lin * query_lin, axis=1), jnp.sum(key_lin * key_lin, axis=1)]
    )
    squares = many_sum("ctx", 6, squares)
    inverse_qk = lax.rsqrt(squares / width + norm_eps)
    inverse_q, inverse_k = inverse_qk[0][:, None], inverse_qk[1][:, None]
    cosine, sine = rope_tables(count)
    query_n, key_n = query_lin * inverse_q, key_lin * inverse_k
    query = rotate(query_n * gain_query, cosine, sine).astype(bf16)
    key = rotate(key_n * gain_key, cosine, sine).astype(bf16)
    mixed, log_total, peaks = attend_forward(query, key, value, docs)
    x_f = x_own.astype(f32)
    mixed_own, grad_mine = exchange(2, mixed, False, grad_own)
    grad_mine = grad_mine.reshape(n_shard * rows, width)
    after = x_f + dot(mixed_own, out_w)
    inverse_two = inverse_rms(after)
    normed_two = after * inverse_two
    hidden_two = (normed_two * gain_ffn).astype(bf16)

    hidden_all, peaks = pair_gather(3, hidden_two, peaks)
    hidden_all, early, grad_theirs = lax.optimization_barrier(
        (hidden_all, early[1:], grad_theirs)
    )
    grad_theirs = lax.all_gather(grad_theirs, "shard", axis=0, tiled=True)
    expert_w += [expert_weights(e + 1, u) for e, u in enumerate(early)]
    hidden_all = hidden_all.reshape(2 * n_shard * rows, width)
    peaks = jnp.max(peaks, axis=0)[:, 0, 0]
    logits = dot(hidden_all, router_w)
    named = jnp.any(routes_all[:, :, None] == jnp.arange(experts)[None, None, :], axis=1)
    probs = jax.nn.softmax(logits, axis=1)
    selected = jnp.where(named, probs, 0.0)
    selected_sum = jnp.sum(selected, axis=1, keepdims=True)
    gates = selected / selected_sum
    first = shard * local + role * half
    gates_own = lax.dynamic_slice_in_dim(gates, first, half, 1)
    named_own = lax.dynamic_slice_in_dim(named, first, half, 1)
    moe_part = jnp.zeros(hidden_all.shape, f32)
    back_part = jnp.zeros(hidden_all.shape, f32)

    def by_half(grad_theirs, function, *arrays):
        split = grad_mine.shape[0]
        return jnp.concatenate(
            [
                function(grad_mine.astype(f32), *(u[:split] for u in arrays)),
                function(grad_theirs.astype(f32), *(u[split:] for u in arrays)),
            ]
        )

    grad_gates, expert_grads = [], []
    for e in range(half):
        wide, down = expert_w[e][:, : 2 * ff], expert_w[e][:, 2 * ff :]
        gate_col = gates_own[:, e : e + 1]
        hidden = dot(hidden_all, wide)
        gate_h, up_h = hidden[:, :ff], hidden[:, ff:]
        sig = jax.nn.sigmoid(gate_h)
        silu = gate_h * sig
        act = (silu * up_h).astype(bf16)
        if e == 0:
            act, grad_theirs = lax.optimization_barrier((act, grad_theirs))
        result = contract_cols(act, down).astype(bf16).astype(f32)
        moe_part = moe_part + gate_col * result
        along = by_half(grad_theirs, lambda d, u: jnp.sum(d * u, axis=1), result)
        grad_gates.append(jnp.where(named_own[:, e], along, 0.0))
        grad_y = by_half(grad_theirs, lambda d, u: (u * d).astype(bf16), gate_col)
        grad_act = dot(grad_y, down)
        grad_h = jnp.concatenate(
            [grad_act * up_h * sig * (1.0 + gate_h * (1.0 - sig)), grad_act * silu], axis=1
        ).astype(bf16)
        back_part = back_part + contract_cols(grad_h, wide).astype(bf16).astype(f32)
        grad_w = [
            contract_rows(hidden_all, grad_h).astype(bf16),
            contract_rows(grad_y, act).astype(bf16),
        ]
        hidden_all, back_part, grad_w, expert_grads = lax.optimization_barrier(
            (hidden_all, back_part, grad_w, expert_grads)
        )
        expert_grads.append(
            [
                lax.psum_scatter(
                    u.reshape(2, width // 2, -1),
                    "ctx",
                    scatter_dimension=1,
                    tiled=True,
                    axis_index_groups=spans,
                )
                for u in grad_w
            ]
        )
    slots = jnp.stack(grad_gates).reshape(half, 2, n_shard, rows).transpose(1, 2, 0, 3)
    grad_gates = lax.dynamic_update_slice_in_dim(
        jnp.zeros((2, n_shard, experts, rows), f32), slots, first, 2
    )
    back_sum, grad_gates = pair_reduce(
        4, back_part.astype(bf16).reshape(2, n_shard, rows, width), grad_gates
    )
    grad_gates = grad_gates.T
    def own_rows(u):
        return lax.dynamic_slice_in_dim(u, shard * rows, rows, 0)

    gates_t, probs_t, named_t, sum_t = map(own_rows, (gates, probs, named, selected_sum))
    grad_selected = (
        grad_gates - jnp.sum(gates_t * grad_gates, axis=1, keepdims=True)
    ) / sum_t
    grad_probs = jnp.where(named_t, grad_selected, 0.0)
    grad_logits = (
        probs_t * (grad_probs - jnp.sum(probs_t * grad_probs, axis=1, keepdims=True))
    ).astype(bf16)
    grad_router = contract_rows(hidden_two, grad_logits)
    grad_hidden = back_sum + contract_cols(grad_logits, router_w)
    grad_gain_ffn = jnp.sum(grad_hidden * normed_two, axis=0)
    scaled_two = grad_hidden * gain_ffn
    grad_after = grad_own.astype(f32) + inverse_two * (
        scaled_two - normed_two * jnp.mean(scaled_two * normed_two, axis=1, keepdims=True)
    )

    grad_attn_own = grad_after.astype(bf16)

    def give(sums):
        return jnp.concatenate(
            [lax.dynamic_index_in_dim(u, 1 - role, 0, False) for u in sums], axis=1
        )

    peers = [swap(give(sums)) for sums in expert_grads[:-1]]
    to_gather, grad_attn_own, expert_grads[-1], peers = lax.optimization_barrier(
        (grad_attn_own, grad_attn_own, expert_grads[-1], peers)
    )
    grad_attn = lax.all_gather(to_gather, "ctx", axis=0, tiled=True)
    (grad_mixed,) = exchange(5, contract_cols(grad_attn_own, out_w).astype(bf16), True)
    grad_out_w = contract_rows(mixed, grad_attn)
    grad_query_rot, grad_key_rot, grad_value = attend_backward(
        query, key, value, docs, log_total, grad_mixed
    )
    grad_query_n = rotate(grad_query_rot, cosine, -sine)
    grad_key_n = rotate(grad_key_rot, cosine, -sine)
    grad_gain_query = jnp.sum(grad_query_n * query_n, axis=0)
    grad_gain_key = jnp.sum(grad_key_n * key_n, axis=0)
    scaled_q, scaled_k = grad_query_n * gain_query, grad_key_n * gain_key
    peak_row = lax.dynamic_update_slice_in_dim(jnp.zeros((count,), f32), peaks, ctx * heads, 0)
    inner = jnp.stack(
        [jnp.sum(scaled_q * query_n, axis=1), jnp.sum(scaled_k * key_n, axis=1), peak_row]
    )
    inner = many_sum("ctx", 7, inner)
    inner, expert_grads[-1] = lax.optimization_barrier((inner, expert_grads[-1]))
    peers.append(swap(give(expert_grads[-1])))
    kept = [[lax.dynamic_index_in_dim(u, role, 0, False) for u in sums] for sums in expert_grads]
    peers = [(peer[:, : 2 * ff], peer[:, 2 * ff :]) for peer in peers]
    both_halves = [
        in_order(jnp.stack([k[i] for k in kept]), jnp.stack([p[i] for p in peers]))
        .reshape(local, width // n_ctx, -1)
        .astype(f32)
        for i in (0, 1)
    ]
    peak_all = inner[2, :HEADS]
    inner = inner / width
    grad_linear = jnp.concatenate(
        [
            inverse_q * (scaled_q - query_n * inner[0][:, None]),
            inverse_k * (scaled_k - key_n * inner[1][:, None]),
            grad_value,
        ],
        axis=1,
    ).astype(bf16)
    grad_weights = contract_rows(hidden_one, grad_linear)
    hidden_part = contract_cols(grad_linear, weights)
    grad_gain_attn = jnp.sum(hidden_part * (x_wide * inverse_one), axis=0)
    grad_small = jnp.concatenate(
        [jnp.stack([grad_gain_attn, grad_gain_ffn], axis=1), grad_router], axis=1
    )
    grad_small = jnp.pad(grad_small, ((0, 0), (0, LANES - 2 - experts)))
    grad_weights = (
        jnp.concatenate([grad_weights, grad_small], axis=1)
        .astype(bf16)
        .reshape(n_ctx, n_shard, part, 3 * cols + LANES)
        .transpose(1, 0, 2, 3)
        .reshape(n_shard, n_ctx * part, 3 * cols + LANES)
    )
    grad_gain_qk = jnp.pad(
        jnp.stack([grad_gain_query, grad_gain_key], axis=1), ((0, 0), (0, LANES - 2))
    )
    grad_out_w = (
        jnp.concatenate([grad_out_w, grad_gain_qk], axis=1)
        .astype(bf16)
        .reshape(n_shard, part, width + LANES)
    )
    grad_hidden_one, grad_weights, grad_out_w, moe_sum = end_call(
        8,
        hidden_part.astype(bf16).reshape(n_ctx, rows, width),
        grad_weights,
        grad_out_w,
        moe_part.astype(bf16).reshape(2, n_shard, rows, width),
    )
    output = (after + moe_sum).astype(bf16)
    grad_weights = grad_weights.astype(f32)
    grad_small = jnp.sum(grad_weights[..., 3 * cols :], axis=0)
    grad_weights = (
        grad_weights[..., : 3 * cols]
        .reshape(n_ctx, part, 3, cols)
        .transpose(2, 1, 0, 3)
        .reshape(3, part, width)
    )
    inverse_own = inverse_rms(x_f)
    normed_own = x_f * inverse_own
    scaled_one = grad_hidden_one * gain_attn
    grad_inputs = grad_after + inverse_own * (
        scaled_one - normed_own * jnp.mean(scaled_one * normed_own, axis=1, keepdims=True)
    )

    factors = jnp.sqrt(clip_threshold / jnp.maximum(peak_all, clip_threshold))
    col_scale = jnp.repeat(factors, HEAD)
    query_clipped = (w_query.astype(f32) * col_scale[None, :]).astype(bf16)
    key_clipped = (w_key.astype(f32) * col_scale[None, :]).astype(bf16)
    return (
        output[None],
        grad_inputs[None],
        grad_small[:, 0],
        grad_weights[0],
        grad_weights[1],
        grad_weights[2],
        grad_out_w[:, width],
        grad_out_w[:, width + 1],
        grad_out_w[:, :width],
        grad_small[:, 1],
        grad_small[:, 2 : 2 + experts],
        both_halves[0][..., :ff],
        both_halves[0][..., ff:],
        both_halves[1].transpose(0, 2, 1),
        query_clipped,
        key_clipped,
        factors,
    )


def solution(mesh):
    both = ("ctx", "shard")
    return jax.shard_map(
        per_device,
        mesh=mesh,
        in_specs=(
            P("shard", "ctx", None),
            P("shard", "ctx"),
            P("shard", "ctx", None),
            P(both),
            P(both, None),
            P(both, None),
            P(both, None),
            P(both),
            P(both),
            P(both, None),
            P(both),
            P(both, None),
            P("shard", "ctx", None),
            P("shard", "ctx", None),
            P("shard", None, "ctx"),
            P(),
            P("shard", "ctx", None),
        ),
        out_specs=(
            P("shard", "ctx", None),
            P("shard", "ctx", None),
            P(both),
            P(both, None),
            P(both, None),
            P(both, None),
            P(both),
            P(both),
            P(both, None),
            P(both),
            P(both, None),
            P("shard", "ctx", None),
            P("shard", "ctx", None),
            P("shard", None, "ctx"),
            P(both, None),
            P(both, None),
            P(),
        ),
        check_vma=False,
    )
```

```python
import functools

import jax
import jax.numpy as jnp
from jax import lax
from jax.experimental import pallas as pl
from jax.experimental.pallas import tpu as pltpu
from jax.sharding import PartitionSpec as P

HEADS = 16
HEAD = 128
SCALE = HEAD ** (-0.5)
Q_BLOCK = 256
LANES = 128

norm_eps = 1e-06
rope_base = 10000.0
f32 = jnp.float32
bf16 = jnp.bfloat16


def dot(a, b):
    return jnp.dot(a, b, preferred_element_type=f32)


def contract_rows(a, b):
    return lax.dot_general(a, b, (((0,), (0,)), ((), ())), preferred_element_type=f32)


def contract_cols(a, b):
    return lax.dot_general(a, b, (((1,), (1,)), ((), ())), preferred_element_type=f32)


def inverse_rms(values):
    return lax.rsqrt(jnp.mean(values * values, axis=-1, keepdims=True) + norm_eps)


def rope_tables(count):
    half = HEAD // 2
    freq = rope_base ** (-jnp.arange(half).astype(f32) / half)
    angles = jnp.arange(count).astype(f32)[:, None] * freq[None, :]
    return jnp.cos(angles), jnp.sin(angles)


def rotate(values, cosine, sine):
    parts = []
    for col in range(0, values.shape[1], HEAD):
        a = values[:, col : col + HEAD // 2]
        b = values[:, col + HEAD // 2 : col + HEAD]
        parts += [a * cosine - b * sine, b * cosine + a * sine]
    return jnp.concatenate(parts, axis=1)


def attend_forward_kernel(q_ref, k_ref, v_ref, doc_q_ref, doc_k_ref, o_ref, lse_ref, peak_ref):
    s = SCALE * contract_cols(q_ref[...], k_ref[...])
    s = jnp.where(doc_q_ref[...] == doc_k_ref[...], s, -1e30)
    top = jnp.max(s, axis=1, keepdims=True)
    e = jnp.exp(s - top)
    total = jnp.sum(e, axis=1, keepdims=True)
    p = (e * (1.0 / total)).astype(bf16)
    o_ref[...] = dot(p, v_ref[...]).astype(bf16)
    lse_ref[0] = top + jnp.log(total)
    peak = jnp.broadcast_to(jnp.max(top, axis=0, keepdims=True), peak_ref.shape[1:])

    @pl.when(pl.program_id(1) == 0)
    def _():
        peak_ref[0] = peak

    @pl.when(pl.program_id(1) > 0)
    def _():
        peak_ref[0] = jnp.maximum(peak_ref[0], peak)


def attend_backward_kernel(
    q_ref, k_ref, v_ref, doc_q_ref, doc_k_ref, lse_ref, do_ref, dq_ref, dk_ref, dv_ref
):
    q, k, v, do = q_ref[...], k_ref[...], v_ref[...], do_ref[...]
    s = SCALE * contract_cols(q, k)
    p = jnp.where(doc_q_ref[...] == doc_k_ref[...], jnp.exp(s - lse_ref[0]), 0.0)
    dp = contract_cols(do, v)
    inner = jnp.sum(p * dp, axis=1, keepdims=True)
    ds = (p * (dp - inner)).astype(bf16)
    dq_ref[...] = SCALE * dot(ds, k)
    dk = SCALE * contract_rows(ds, q)
    dv = contract_rows(p.astype(bf16), do)

    @pl.when(pl.program_id(1) == 0)
    def _():
        dk_ref[...] = dk
        dv_ref[...] = dv

    @pl.when(pl.program_id(1) > 0)
    def _():
        dk_ref[...] += dk
        dv_ref[...] += dv


def attend_specs(count):
    block = pl.BlockSpec((Q_BLOCK, HEAD), lambda h, i: (i, h))
    whole = pl.BlockSpec((count, HEAD), lambda h, i: (0, h))
    doc_q = pl.BlockSpec((Q_BLOCK, 1), lambda h, i: (i, 0))
    doc_k = pl.BlockSpec((1, count), lambda h, i: (0, 0))
    lse = pl.BlockSpec((1, Q_BLOCK, 1), lambda h, i: (h, i, 0))
    return block, whole, doc_q, doc_k, lse


def attend_forward(q, k, v, docs):
    count, width = q.shape
    heads = width // HEAD
    block, whole, doc_q, doc_k, lse = attend_specs(count)
    return pl.pallas_call(
        attend_forward_kernel,
        grid=(heads, count // Q_BLOCK),
        in_specs=[block, whole, whole, doc_q, doc_k],
        out_specs=[block, lse, pl.BlockSpec((1, 8, 128), lambda h, i: (h, 0, 0))],
        out_shape=[
            jax.ShapeDtypeStruct((count, width), bf16),
            jax.ShapeDtypeStruct((heads, count, 1), f32),
            jax.ShapeDtypeStruct((heads, 8, 128), f32),
        ],
        compiler_params=pltpu.CompilerParams(vmem_limit_bytes=48 << 20),
        cost_estimate=pl.CostEstimate(
            flops=4 * count * count * width,
            transcendentals=heads * count * count,
            bytes_accessed=8 * count * width,
        ),
    )(q, k, v, docs[:, None], docs[None, :])


def attend_backward(q, k, v, docs, log_total, grad):
    count, width = q.shape
    heads = width // HEAD
    block, whole, doc_q, doc_k, lse = attend_specs(count)
    return pl.pallas_call(
        attend_backward_kernel,
        grid=(heads, count // Q_BLOCK),
        in_specs=[block, whole, whole, doc_q, doc_k, lse, block],
        out_specs=[block, whole, whole],
        out_shape=[jax.ShapeDtypeStruct((count, width), f32)] * 3,
        compiler_params=pltpu.CompilerParams(vmem_limit_bytes=56 << 20),
        cost_estimate=pl.CostEstimate(
            flops=10 * count * count * width,
            transcendentals=heads * count * count,
            bytes_accessed=20 * count * width,
        ),
    )(q, k, v, docs[:, None], docs[None, :], log_total, grad)


MESH = pl.DeviceIdType.MESH
ANY = pl.BlockSpec(memory_space=pl.ANY)
VMEM = pl.BlockSpec(memory_space=pltpu.VMEM)


def ring_peers(axis):
    n, me = lax.axis_size(axis), lax.axis_index(axis)
    return [lax.rem(me + k, n) for k in range(n)], [lax.rem(me + n - k, n) for k in range(n)]


class Greeting:
    def __init__(self):
        self.barrier, self.total = pltpu.get_barrier_semaphore(), 0

    def ring(self, axis):
        to, _ = ring_peers(axis)
        for peer in to[1:]:
            pl.semaphore_signal(
                self.barrier, inc=1, device_id={axis: peer}, device_id_type=MESH
            )
        self.total = self.total + len(to) - 1
        return self

    def line(self):
        line = Line()
        for there, peer in (
            (line.place >= 0, line.partner),
            (line.not_last, line.me + 2),
            (line.not_first, line.me - 2),
        ):

            @pl.when(there)
            def _():
                pl.semaphore_signal(
                    self.barrier, inc=1, device_id={"ctx": peer}, device_id_type=MESH
                )

            self.total = self.total + there.astype(jnp.int32)
        return self

    def pair(self):
        pl.semaphore_signal(
            self.barrier, inc=1, device_id={"ctx": Pair().peer}, device_id_type=MESH
        )
        self.total = self.total + 1
        return self

    def wait(self):
        pl.semaphore_wait(self.barrier, self.total)


class Line:
    def __init__(self):
        self.n, self.me = lax.axis_size("ctx") // 2, lax.axis_index("ctx")
        self.place, self.core = lax.div(self.me, 2), lax.rem(self.me, 2)
        self.partner = self.me + 1 - 2 * self.core
        self.not_first, self.not_last = self.place > 0, self.place < self.n - 1


class Direct:
    def __init__(self, axis, source, target, send, recv):
        self.axis, self.source, self.target = axis, source, target
        self.send, self.recv = send, recv
        self.me = lax.axis_index(axis)
        self.to, self.origin = ring_peers(axis)

    def copy(self, k, sender):
        return pltpu.make_async_remote_copy(
            src_ref=self.source(self.to[k]),
            dst_ref=self.target(sender, k),
            send_sem=self.send.at[k],
            recv_sem=self.recv.at[k],
            device_id={self.axis: self.to[k]},
            device_id_type=MESH,
        )

    def start(self):
        for k in range(1, len(self.to)):
            self.copy(k, self.me).start()

    def wait_recv(self):
        for k in range(1, len(self.to)):
            self.copy(k, self.origin[k]).wait_recv()

    def wait_send(self):
        for k in range(1, len(self.to)):
            self.copy(k, self.me).wait_send()


class LineGather:
    def __init__(self, pieces, own_sem, send_r, send_l, send_p, recv_r, recv_l, recv_p):
        self.line, self.pieces, self.own_sem = Line(), pieces, own_sem
        self.send_r, self.send_l, self.send_p = send_r, send_l, send_p
        self.recv_r, self.recv_l, self.recv_p = recv_r, recv_l, recv_p

    def own(self, c):
        source, target = self.pieces[c]
        return pltpu.make_async_copy(source, target(self.line.me), self.own_sem.at[c])

    def copy(self, block, k, c, target_device, send, recv):
        source, target = self.pieces[c]
        return pltpu.make_async_remote_copy(
            src_ref=source if k == 0 else target(block),
            dst_ref=target(block),
            send_sem=send,
            recv_sem=recv,
            device_id={"ctx": target_device},
            device_id_type=MESH,
        )

    def right(self, k, c):
        me = self.line.me
        return self.copy(me - 2 * k, k, c, me + 2, self.send_r.at[k, c], self.recv_r.at[k, c])

    def left(self, k, c):
        me = self.line.me
        return self.copy(me + 2 * k, k, c, me - 2, self.send_l.at[k, c], self.recv_l.at[k, c])

    def across(self, k, c, sign):
        line = self.line
        i = k if sign < 0 else line.n - 1 + k
        return self.copy(
            line.me + sign * 2 * k, k, c, line.partner, self.send_p.at[i, c], self.recv_p.at[i, c]
        )

    def arrived(self, block, c, recv):
        source, target = self.pieces[c]
        pltpu.make_async_remote_copy(
            src_ref=source,
            dst_ref=target(block),
            send_sem=recv,
            recv_sem=recv,
            device_id={"ctx": self.line.partner},
            device_id_type=MESH,
        ).wait_recv()

    def start(self):
        for c in range(len(self.pieces)):
            self.own(c).start()

    def hop(self, k):
        line = self.line
        for c in range(len(self.pieces)):

            @pl.when(line.place >= k)
            def _():
                if k:
                    self.arrived(line.me - 2 * k, c, self.recv_r.at[k - 1, c])

                @pl.when(line.not_last)
                def _():
                    self.right(k, c).start()

                self.across(k, c, -1).start()

            @pl.when(line.place + k <= line.n - 1)
            def _():
                if k:
                    self.arrived(line.me + 2 * k, c, self.recv_l.at[k - 1, c])

                @pl.when(line.not_first)
                def _():
                    self.left(k, c).start()

                if k:
                    self.across(k, c, 1).start()

    def finish(self, skip_own=None):
        line = self.line
        for c in range(len(self.pieces)):
            if c != skip_own:
                self.own(c).wait()
        for k in range(line.n):
            for c in range(len(self.pieces)):

                @pl.when(line.place >= k)
                def _():
                    @pl.when(line.not_last)
                    def _():
                        self.right(k, c).wait_send()

                    self.across(k, c, -1).wait_send()
                    self.arrived(line.partner - 2 * k, c, self.recv_p.at[k, c])

                @pl.when(line.place + k <= line.n - 1)
                def _():
                    @pl.when(line.not_first)
                    def _():
                        self.left(k, c).wait_send()

                    if k:
                        self.across(k, c, 1).wait_send()
                        self.arrived(line.partner + 2 * k, c, self.recv_p.at[line.n - 1 + k, c])


def line_gather_scratch(n, pieces):
    sem = pltpu.SemaphoreType.DMA
    one, two = sem((n, pieces)), sem((2 * n - 1, pieces))
    return [sem((pieces,)), one, one, two, one, one, two]


class LineReduce:
    def __init__(
        self, chunks, x, o, pair, from_left, from_right, send_p, recv_p, send_s, recv_r, recv_l
    ):
        self.line, self.chunks = Line(), chunks
        self.x, self.o, self.pair, self.out = x, o, pair, pair
        self.from_left, self.from_right = from_left, from_right
        self.send_p, self.recv_p, self.send_s = send_p, recv_p, send_s
        self.recv_r, self.recv_l = recv_r, recv_l
        self.order = []
        for j in range(self.line.n):
            self.order += [p for p in (self.line.n - 1 - j, j) if p not in self.order]

    def at(self, c):
        rows = self.x.shape[1] // self.chunks
        return pl.ds(c * rows, rows)

    def across(self, p, c):
        line, at = self.line, self.at(c)
        return pltpu.make_async_remote_copy(
            src_ref=self.x.at[2 * p + 1 - line.core, at],
            dst_ref=self.pair.at[p, at],
            send_sem=self.send_p.at[p, c],
            recv_sem=self.recv_p.at[p, c],
            device_id={"ctx": line.partner},
            device_id_type=MESH,
        )

    def along(self, p, c, step, buffer, recv):
        at = self.at(c)
        return pltpu.make_async_remote_copy(
            src_ref=self.out.at[p, at],
            dst_ref=buffer.at[p, at],
            send_sem=self.send_s.at[p, c],
            recv_sem=recv.at[p, c],
            device_id={"ctx": self.line.me + step},
            device_id_type=MESH,
        )

    def right(self, p, c):
        return self.along(p, c, 2, self.from_left, self.recv_r)

    def left(self, p, c):
        return self.along(p, c, -2, self.from_right, self.recv_l)

    def start(self):
        for p in self.order:
            for c in range(self.chunks):
                self.across(p, c).start()

    def both(self, p, c):
        at = self.at(c)
        return self.x[2 * p + self.line.core, at].astype(f32) + self.pair[p, at].astype(f32)

    def pass_on(self):
        line = self.line
        for p in self.order:
            for c in range(self.chunks):
                at = self.at(c)
                self.across(p, c).wait_recv()

                @pl.when(line.place < p)
                def _():
                    @pl.when(line.not_first)
                    def _():
                        self.right(p, c).wait_recv()
                        total = self.both(p, c) + self.from_left[p, at].astype(f32)
                        self.out[p, at] = total.astype(bf16)

                    @pl.when(line.place == 0)
                    def _():
                        self.out[p, at] = self.both(p, c).astype(bf16)

                    self.right(p, c).start()

                @pl.when(line.place > p)
                def _():
                    @pl.when(line.not_last)
                    def _():
                        self.left(p, c).wait_recv()
                        total = self.both(p, c) + self.from_right[p, at].astype(f32)
                        self.out[p, at] = total.astype(bf16)

                    @pl.when(line.place == line.n - 1)
                    def _():
                        self.out[p, at] = self.both(p, c).astype(bf16)

                    self.left(p, c).start()

    def finish(self):
        line = self.line
        for p in range(line.n):
            for c in range(self.chunks):
                at = self.at(c)

                @pl.when(line.place == p)
                def _():
                    self.o[at] = self.both(p, c)
                    if p > 0:
                        self.right(p, c).wait_recv()
                        self.o[at] += self.from_left[p, at].astype(f32)
                    if p < line.n - 1:
                        self.left(p, c).wait_recv()
                        self.o[at] += self.from_right[p, at].astype(f32)

        for p in range(line.n):
            for c in range(self.chunks):
                self.across(p, c).wait_send()

                @pl.when(line.place < p)
                def _():
                    self.right(p, c).wait_send()

                @pl.when(line.place > p)
                def _():
                    self.left(p, c).wait_send()


def add_up(x, buf, o, me):
    rows = x.shape[1]
    step = 8 if rows % 32 else 32

    @pl.loop(0, rows // step)
    def _(j):
        at = pl.ds(pl.multiple_of(j * step, step), step)
        total = x[me, at].astype(f32)
        for k in range(buf.shape[0]):
            total = total + buf[k, at].astype(f32)
        o[at] = total.astype(o.dtype)


def block_of(ref):
    return lambda device: ref.at[device]


def block_from(ref):
    return lambda device, k: ref.at[device]


def whole_of(ref):
    return lambda device: ref


def buffer_of(ref):
    return lambda device, k: ref.at[k - 1]


def row_pieces(source, target, chunks):
    rows = source.shape[0] // chunks
    return [
        (source.at[pl.ds(c * rows, rows)], lambda b, c=c: target.at[b, pl.ds(c * rows, rows)])
        for c in range(chunks)
    ]


def start_kernel(
    x, w, w_query, w_key, w_value, small, cot, x_all, w_all, heads_all, small_all, cot_peer,
    heads_mid, small_mid, own_sem, ex_send, ex_recv, sp_send, sp_recv, w_send, w_recv, f_send,
    f_recv, pair_send, pair_recv, *line_sems,
):
    shard, ctx = lax.axis_index("shard"), lax.axis_index("ctx")
    n_ctx = lax.axis_size("ctx")
    cols = w_query.shape[1] // n_ctx
    Greeting().ring("ctx").ring("shard").wait()

    def columns(ref):
        return lambda d: ref.at[:, pl.ds(pl.multiple_of(d * cols, HEAD), cols)]

    def place(i):
        if i == 3:
            return block_from(small_mid)
        return lambda d, k: heads_mid.at[d, :, i * cols : (i + 1) * cols]

    sources = [columns(w_query), columns(w_key), columns(w_value), whole_of(small)]
    swaps = [
        Direct("ctx", source, place(i), ex_send.at[i], ex_recv.at[i])
        for i, source in enumerate(sources)
    ]

    def by_shard(ref):
        return lambda d, k: ref.at[:, d]

    spreads = [
        Direct("shard", whole_of(heads_mid), by_shard(heads_all), sp_send.at[0], sp_recv.at[0]),
        Direct("shard", whole_of(small_mid), by_shard(small_all), sp_send.at[1], sp_recv.at[1]),
    ]
    pieces = row_pieces(x, x_all, LINE_CHUNKS) + [(w, lambda b: w_all.at[b, shard])]
    line = LineGather(pieces, *line_sems)
    at = line.line
    own = [
        pltpu.make_async_copy(source(ctx), place(i)(ctx, 0), own_sem.at[i])
        for i, source in enumerate(sources)
    ]
    later = [
        pltpu.make_async_copy(heads_mid, heads_all.at[:, shard], own_sem.at[4]),
        pltpu.make_async_copy(small_mid, small_all.at[:, shard], own_sem.at[5]),
    ]
    for swap in swaps:
        swap.start()
    for copy in own:
        copy.start()
    line.start()
    line.hop(0)
    for swap in swaps:
        swap.wait_recv()
    for copy in own:
        copy.wait()
    for one in (*spreads, *later):
        one.start()
    for k in range(1, at.n):
        line.hop(k)
    across = Pair().copy(cot, cot_peer, pair_send, pair_recv)
    across.start()

    to, origin = ring_peers("shard")

    def row(k, p, sender):
        block = 2 * p + at.core
        return pltpu.make_async_remote_copy(
            src_ref=w_all.at[block, shard],
            dst_ref=w_all.at[block, sender],
            send_sem=w_send.at[k, p],
            recv_sem=w_recv.at[k, p],
            device_id={"shard": to[k]},
            device_id_type=MESH,
        )

    def forward(k, p, core):
        block = w_all.at[2 * p + core, origin[k]]
        return pltpu.make_async_remote_copy(
            src_ref=block,
            dst_ref=block,
            send_sem=f_send.at[k, p],
            recv_sem=f_recv.at[k, p],
            device_id={"ctx": at.partner},
            device_id_type=MESH,
        )

    some = [(k, p) for k in range(1, len(to)) for p in range(at.n)]
    line.own(LINE_CHUNKS).wait()
    for k, p in some:
        row(k, p, shard).start()
    for k, p in some:
        row(k, p, origin[k]).wait_recv()
        forward(k, p, at.core).start()
    line.finish(skip_own=LINE_CHUNKS)
    for k, p in some:
        row(k, p, shard).wait_send()
        forward(k, p, at.core).wait_send()
        forward(k, p, 1 - at.core).wait_recv()
    across.wait()
    for direct in spreads:
        direct.wait_recv()
    for direct in (*swaps, *spreads):
        direct.wait_send()
    for copy in later:
        copy.wait()


def exchange_kernel(to_rows, *refs):
    more = len(refs) > 5
    if more:
        x, cot, o, cot_all, own_sem, send, recv, cot_send, cot_recv = refs
    else:
        x, o, own_sem, send, recv = refs
    n, me = lax.axis_size("ctx"), lax.axis_index("ctx")
    cols, rows = (x.shape[1] // n, x.shape[0]) if to_rows else (x.shape[1], o.shape[0])

    def row_block(ref):
        return lambda d, k=0: ref.at[pl.ds(pl.multiple_of(d * rows, rows), rows)]

    def column_block(ref):
        return lambda d, k=0: ref.at[:, pl.ds(pl.multiple_of(d * cols, cols), cols)]

    source, target = (
        (column_block(x), row_block(o)) if to_rows else (row_block(x), column_block(o))
    )
    greeting = Greeting().ring("ctx")
    if more:
        greeting.ring("shard")
    greeting.wait()
    all_of = [Direct("ctx", source, target, send, recv)]
    own = [pltpu.make_async_copy(source(me), target(me), own_sem.at[0])]
    if more:
        all_of.append(Direct("shard", whole_of(cot), block_from(cot_all), cot_send, cot_recv))
        own.append(
            pltpu.make_async_copy(cot, cot_all.at[lax.axis_index("shard")], own_sem.at[1])
        )
    for one in (*all_of, *own):
        one.start()
    for copy in own:
        copy.wait()
    for direct in all_of:
        direct.wait_recv()
        direct.wait_send()


class Pair:
    def __init__(self):
        ctx, half = lax.axis_index("ctx"), lax.axis_size("ctx") // 2
        self.role = lax.div(ctx, half)
        self.peer = ctx + half - 2 * half * self.role

    def copy(self, source, target, send, recv):
        return pltpu.make_async_remote_copy(
            src_ref=source,
            dst_ref=target,
            send_sem=send,
            recv_sem=recv,
            device_id={"ctx": self.peer},
            device_id_type=MESH,
        )


def pair_gather_kernel(x, peaks, o, peaks_all, own_sem, send, recv, pair_send, pair_recv):
    shard, pair = lax.axis_index("shard"), Pair()
    Greeting().ring("shard").pair().wait()
    own_rows = Direct(
        "shard", whole_of(x), lambda d, k: o.at[0, d], send.at[0], recv.at[0]
    )
    peer_rows = Direct(
        "shard", lambda d: o.at[1, shard], lambda d, k: o.at[1, d], send.at[1], recv.at[1]
    )
    tops = Direct("shard", whole_of(peaks), block_from(peaks_all), send.at[2], recv.at[2])
    across = pair.copy(x, o.at[1, shard], pair_send, pair_recv)
    across.start()
    own_rows.start()
    tops.start()
    own = [
        pltpu.make_async_copy(x, o.at[0, shard], own_sem.at[0]),
        pltpu.make_async_copy(peaks, peaks_all.at[shard], own_sem.at[1]),
    ]
    for copy in own:
        copy.start()
    across.wait_recv()
    peer_rows.start()
    for copy in own:
        copy.wait()
    across.wait_send()
    for direct in (own_rows, peer_rows, tops):
        direct.wait_recv()
        direct.wait_send()


class PairReduce:
    def __init__(self, x, o, buf, part, peer, send, recv, pair_send, pair_recv):
        self.x, self.o, self.buf, self.part, self.peer = x, o, buf, part, peer
        self.pair = Pair()
        self.first = Direct(
            "shard", lambda d: x.at[1, d], lambda d, k: buf.at[1, k - 1], send.at[1], recv.at[1]
        )
        self.second = Direct(
            "shard", lambda d: x.at[0, d], lambda d, k: buf.at[0, k - 1], send.at[0], recv.at[0]
        )
        self.across = self.pair.copy(part, peer, pair_send, pair_recv)

    def start(self):
        self.first.start()
        self.second.start()

    def add_up(self, half, o, more=None):
        x, buf, shard = self.x, self.buf, self.first.me
        rows = x.shape[2]
        step = 8 if rows % 32 else 32

        @pl.loop(0, rows // step)
        def _(j):
            at = pl.ds(pl.multiple_of(j * step, step), step)
            total = x[half, shard, at].astype(f32)
            for k in range(buf.shape[1]):
                total = total + buf[half, k, at].astype(f32)
            if more is not None:
                total = total + more[at].astype(f32)
            o[at] = total.astype(o.dtype)

    def turn(self):
        self.first.wait_recv()
        self.add_up(1, self.part)
        self.across.start()

    def finish(self):
        self.second.wait_recv()
        self.across.wait_recv()
        self.add_up(0, self.o, self.peer)
        self.across.wait_send()
        self.first.wait_send()
        self.second.wait_send()


def pair_reduce_scratch(n_shard, x):
    sem = pltpu.SemaphoreType.DMA
    return [
        pltpu.VMEM((2, n_shard - 1, *x.shape[2:]), x.dtype),
        pltpu.VMEM(x.shape[2:], x.dtype),
        pltpu.VMEM(x.shape[2:], x.dtype),
        sem((2, n_shard)),
        sem((2, n_shard)),
        sem,
        sem,
    ]


def pair_reduce_kernel(count, *refs):
    ins, outs, rest = refs[:count], refs[count : 2 * count], refs[2 * count :]
    Greeting().ring("shard").pair().wait()
    all_of = [PairReduce(ins[i], outs[i], *rest[7 * i : 7 * i + 7]) for i in range(count)]
    for one in all_of:
        one.start()
    for one in all_of:
        one.turn()
    for one in all_of:
        one.finish()


def many_sum_kernel(axis, x, o, buf, send, recv):
    Greeting().ring(axis).wait()
    direct = Direct(axis, whole_of(x), buffer_of(buf), send, recv)
    direct.start()
    direct.wait_recv()
    total = x[...]
    for k in range(buf.shape[0]):
        total = total + buf[k]
    o[...] = total
    direct.wait_send()


def end_kernel(
    x, wide, out, y, x_sum, wide_all, out_sum, y_peer, wide_buf, out_buf, wide_sum,
    own_sem, wide_send, wide_recv, out_send, out_recv, swap_send, swap_recv, pair_send, pair_recv,
    *line_refs,
):
    ctx = lax.axis_index("ctx")
    Greeting().ring("ctx").ring("shard").wait()
    wides = Direct("shard", block_of(wide), buffer_of(wide_buf), wide_send, wide_recv)
    outs = Direct("shard", block_of(out), buffer_of(out_buf), out_send, out_recv)
    swap = Direct("ctx", block_of(wide_sum), block_from(wide_all), swap_send, swap_recv)
    line = LineReduce(LINE_CHUNKS, x, x_sum, *line_refs)
    line.start()
    wides.start()
    outs.start()
    line.pass_on()
    across = Pair().copy(y, y_peer, pair_send, pair_recv)
    across.start()
    wides.wait_recv()
    for b in range(lax.axis_size("ctx")):
        rows = wide_sum.shape[1]
        total = wide[wides.me, b * rows : (b + 1) * rows].astype(f32)
        for k in range(wide_buf.shape[0]):
            total = total + wide_buf[k, b * rows : (b + 1) * rows].astype(f32)
        wide_sum[b] = total.astype(bf16)
    swap.start()
    own = pltpu.make_async_copy(wide_sum.at[ctx], wide_all.at[ctx], own_sem)
    own.start()
    outs.wait_recv()
    add_up(out, out_buf, out_sum, outs.me)
    line.finish()
    own.wait()
    across.wait()
    swap.wait_recv()
    for direct in (swap, wides, outs):
        direct.wait_send()


def remote_params(collective_id, megabytes):
    return pltpu.CompilerParams(
        collective_id=collective_id, has_side_effects=True, vmem_limit_bytes=megabytes << 20
    )


LINE_CHUNKS = 4


def start_call(collective_id, x, w, w_query, w_key, w_value, small, cot):
    n_ctx, n_shard = lax.axis_size("ctx"), lax.axis_size("shard")
    n = n_ctx // 2
    heads = (w.shape[0], 3 * w.shape[1] // n_ctx)
    sem = pltpu.SemaphoreType.DMA
    return pl.pallas_call(
        start_kernel,
        out_shape=[
            jax.ShapeDtypeStruct((n_ctx, *x.shape), bf16),
            jax.ShapeDtypeStruct((n_ctx, n_shard, *w.shape), bf16),
            jax.ShapeDtypeStruct((n_ctx, n_shard, *heads), bf16),
            jax.ShapeDtypeStruct((n_ctx, n_shard, *small.shape), bf16),
            jax.ShapeDtypeStruct(cot.shape, bf16),
        ],
        in_specs=[ANY] * 7,
        out_specs=[ANY] * 5,
        scratch_shapes=[
            pltpu.VMEM((n_ctx, *heads), bf16),
            pltpu.VMEM((n_ctx, *small.shape), bf16),
            sem((6,)),
            sem((4, n_ctx)),
            sem((4, n_ctx)),
        ]
        + [sem((2, n_shard))] * 2
        + [sem((n_shard, n))] * 4
        + [sem, sem]
        + line_gather_scratch(n, LINE_CHUNKS + 1),
        compiler_params=remote_params(collective_id, 8),
    )(x, w, w_query, w_key, w_value, small, cot)


def exchange(collective_id, x, to_rows, *more):
    n, n_shard = lax.axis_size("ctx"), lax.axis_size("shard")
    shape = (x.shape[0] * n, x.shape[1] // n) if to_rows else (x.shape[0] // n, x.shape[1] * n)
    sem = pltpu.SemaphoreType.DMA
    return pl.pallas_call(
        functools.partial(exchange_kernel, to_rows),
        out_shape=[jax.ShapeDtypeStruct(shape, x.dtype)]
        + [jax.ShapeDtypeStruct((n_shard, *u.shape), u.dtype) for u in more],
        in_specs=[ANY] * (1 + len(more)),
        out_specs=[ANY] * (1 + len(more)),
        scratch_shapes=[sem((2,)), sem((n,)), sem((n,))] + [sem((n_shard,))] * (2 * len(more)),
        compiler_params=remote_params(collective_id, 8),
    )(x, *more)


def pair_gather(collective_id, x, peaks):
    n = lax.axis_size("shard")
    sem = pltpu.SemaphoreType.DMA
    return pl.pallas_call(
        pair_gather_kernel,
        out_shape=[
            jax.ShapeDtypeStruct((2, n, *x.shape), x.dtype),
            jax.ShapeDtypeStruct((n, *peaks.shape), peaks.dtype),
        ],
        in_specs=[ANY] * 2,
        out_specs=[ANY] * 2,
        scratch_shapes=[sem((2,)), sem((3, n)), sem((3, n)), sem, sem],
        compiler_params=remote_params(collective_id, 8),
    )(x, peaks)


def pair_reduce(collective_id, *arrays):
    n = lax.axis_size("shard")
    return pl.pallas_call(
        functools.partial(pair_reduce_kernel, len(arrays)),
        out_shape=[jax.ShapeDtypeStruct(a.shape[2:], f32) for a in arrays],
        in_specs=[VMEM] * len(arrays),
        out_specs=[VMEM] * len(arrays),
        scratch_shapes=sum((pair_reduce_scratch(n, a) for a in arrays), []),
        compiler_params=remote_params(collective_id, 40),
    )(*arrays)


def many_sum(axis, collective_id, x):
    n = lax.axis_size(axis)
    sem = pltpu.SemaphoreType.DMA
    return pl.pallas_call(
        functools.partial(many_sum_kernel, axis),
        out_shape=jax.ShapeDtypeStruct(x.shape, x.dtype),
        in_specs=[VMEM],
        out_specs=VMEM,
        scratch_shapes=[pltpu.VMEM((n - 1, *x.shape), x.dtype), sem((n,)), sem((n,))],
        compiler_params=remote_params(collective_id, 8),
    )(x)


def end_call(collective_id, x, wide, out, y):
    n_ctx, rows, width = x.shape
    n_shard = lax.axis_size("shard")
    n = n_ctx // 2
    wide_rows, wide_cols = wide.shape[1] // n_ctx, wide.shape[2]
    sem = pltpu.SemaphoreType.DMA
    return pl.pallas_call(
        end_kernel,
        out_shape=[
            jax.ShapeDtypeStruct((rows, width), f32),
            jax.ShapeDtypeStruct((n_ctx, wide_rows, wide_cols), bf16),
            jax.ShapeDtypeStruct(out.shape[1:], f32),
            jax.ShapeDtypeStruct(y.shape, y.dtype),
        ],
        in_specs=[VMEM] * 3 + [ANY],
        out_specs=[VMEM] * 3 + [ANY],
        scratch_shapes=[
            pltpu.VMEM((n_shard - 1, *wide.shape[1:]), bf16),
            pltpu.VMEM((n_shard - 1, *out.shape[1:]), bf16),
            pltpu.VMEM((n_ctx, wide_rows, wide_cols), bf16),
            sem,
        ]
        + [sem((n_shard,))] * 4
        + [sem((n_ctx,))] * 2
        + [sem, sem]
        + [pltpu.VMEM((n, rows, width), bf16)] * 3
        + [sem((n, LINE_CHUNKS))] * 5,
        compiler_params=remote_params(collective_id, 56),
    )(x, wide, out, y)


def per_device(
    tokens,
    doc_ids,
    routes,
    attn_gain,
    w_query,
    w_key,
    w_value,
    query_gain,
    key_gain,
    w_out,
    ffn_gain,
    w_router,
    w_gate,
    w_up,
    w_down,
    clip_threshold,
    cotangent,
):
    both = ("ctx", "shard")
    n_ctx, n_shard = lax.axis_size("ctx"), lax.axis_size("shard")
    ctx, shard = lax.axis_index("ctx"), lax.axis_index("shard")
    x_own = tokens[0]
    rows, width = x_own.shape
    part = w_query.shape[0]
    cols = width // n_ctx
    heads = cols // HEAD
    count = rows * n_ctx
    local = w_gate.shape[0]
    experts = local * n_shard

    top = routes.shape[2]
    spare = jnp.zeros((part, LANES - 4 - experts - rows // part * (1 + top)), bf16)
    small = jnp.concatenate(
        [
            jnp.stack([attn_gain, query_gain, key_gain, ffn_gain], axis=1),
            w_router,
            doc_ids.reshape(part, rows // part).astype(bf16),
            routes.reshape(part, rows // part * top).astype(bf16),
            spare,
        ],
        axis=1,
    )
    grad_own = cotangent[0]
    x_all, out_w, weights, small_all, grad_theirs = start_call(
        1, x_own, w_out, w_query, w_key, w_value, small, grad_own
    )
    x_all = x_all.reshape(count, width)
    out_w = out_w.reshape(width, width)
    weights = weights.reshape(width, 3 * cols)
    gains = small_all[..., : 4 + experts].reshape(width, 4 + experts)
    gain_attn, gain_query, gain_key, gain_ffn = (gains[:, i].astype(f32) for i in range(4))
    router_w = gains[:, 4:]
    gain_query = lax.dynamic_slice_in_dim(gain_query, ctx * cols, cols)
    gain_key = lax.dynamic_slice_in_dim(gain_key, ctx * cols, cols)
    tail = small_all[..., 4 + experts :].astype(jnp.int32)
    docs = lax.dynamic_index_in_dim(tail[..., : rows // part], shard, 1, False).reshape(count)
    span = n_ctx // 2
    role = lax.div(ctx, span)
    routes_all = tail[..., rows // part : rows // part * (1 + top)].reshape(
        n_ctx, n_shard, rows, top
    )
    routes_all = jnp.stack(
        [
            lax.dynamic_index_in_dim(routes_all, ctx, 0, False),
            lax.dynamic_index_in_dim(routes_all, lax.rem(ctx + span, n_ctx), 0, False),
        ]
    ).reshape(2 * n_shard * rows, top)

    def swap(u):
        return lax.ppermute(u, "ctx", [(i, (i + span) % n_ctx) for i in range(n_ctx)])

    def queued_swap(u):
        both = lax.all_gather(
            u, "ctx", axis=0, axis_index_groups=[[i, i + span] for i in range(span)]
        )
        return lax.dynamic_index_in_dim(both, 1 - role, 0, False)

    def in_order(mine, theirs):
        return jnp.where(role == 0, jnp.stack([mine, theirs]), jnp.stack([theirs, mine]))

    half = local // 2
    ff = w_gate.shape[2]
    own_w = jnp.concatenate([w_gate, w_up, w_down.transpose(0, 2, 1)], axis=2)
    keep_w = lax.dynamic_slice_in_dim(own_w, role * half, half, 0)
    give_w = lax.dynamic_slice_in_dim(own_w, (1 - role) * half, half, 0)
    spans = [list(range(r * span, (r + 1) * span)) for r in (0, 1)]
    x_all, give_w = lax.optimization_barrier((x_all, give_w))
    early = queued_swap(give_w[0])

    def expert_weights(e, theirs):
        return lax.all_gather(
            in_order(keep_w[e], theirs),
            "ctx",
            axis=1,
            tiled=True,
            axis_index_groups=spans,
        ).reshape(width, 3 * ff)

    x_wide = x_all.astype(f32)
    inverse_one = inverse_rms(x_wide)
    hidden_one = (x_wide * inverse_one * gain_attn).astype(bf16)
    linear = dot(hidden_one, weights)
    query_lin, key_lin = linear[:, :cols], linear[:, cols : 2 * cols]
    value = linear[:, 2 * cols :].astype(bf16)
    squares = jnp.stack(
        [jnp.sum(query_lin * query_lin, axis=1), jnp.sum(key_lin * key_lin, axis=1)]
    )
    squares = many_sum("ctx", 6, squares)
    inverse_qk = lax.rsqrt(squares / width + norm_eps)
    inverse_q, inverse_k = inverse_qk[0][:, None], inverse_qk[1][:, None]
    cosine, sine = rope_tables(count)
    query_n, key_n = query_lin * inverse_q, key_lin * inverse_k
    query = rotate(query_n * gain_query, cosine, sine).astype(bf16)
    key = rotate(key_n * gain_key, cosine, sine).astype(bf16)
    mixed, log_total, peaks = attend_forward(query, key, value, docs)
    mixed, early = lax.optimization_barrier((mixed, early))
    expert_w = [expert_weights(0, early)]
    x_f = x_own.astype(f32)
    mixed_own, grad_mine = exchange(2, mixed, False, grad_own)
    mixed_own, give_w = lax.optimization_barrier((mixed_own, give_w))
    early = [queued_swap(give_w[e]) for e in range(1, half)]
    grad_mine = grad_mine.reshape(n_shard * rows, width)
    after = x_f + dot(mixed_own, out_w)
    inverse_two = inverse_rms(after)
    normed_two = after * inverse_two
    hidden_two = (normed_two * gain_ffn).astype(bf16)

    hidden_all, peaks = pair_gather(3, hidden_two, peaks)
    hidden_all, early, grad_theirs = lax.optimization_barrier((hidden_all, early, grad_theirs))
    grad_theirs = lax.all_gather(grad_theirs, "shard", axis=0, tiled=True)
    expert_w += [expert_weights(e + 1, u) for e, u in enumerate(early)]
    hidden_all = hidden_all.reshape(2 * n_shard * rows, width)
    peaks = jnp.max(peaks, axis=0)[:, 0, 0]
    logits = dot(hidden_all, router_w)
    named = jnp.any(routes_all[:, :, None] == jnp.arange(experts)[None, None, :], axis=1)
    probs = jax.nn.softmax(logits, axis=1)
    selected = jnp.where(named, probs, 0.0)
    selected_sum = jnp.sum(selected, axis=1, keepdims=True)
    gates = selected / selected_sum
    first = shard * local + role * half
    gates_own = lax.dynamic_slice_in_dim(gates, first, half, 1)
    named_own = lax.dynamic_slice_in_dim(named, first, half, 1)
    moe_part = jnp.zeros(hidden_all.shape, f32)
    back_part = jnp.zeros(hidden_all.shape, f32)

    def by_half(grad_theirs, function, *arrays):
        split = grad_mine.shape[0]
        return jnp.concatenate(
            [
                function(grad_mine.astype(f32), *(u[:split] for u in arrays)),
                function(grad_theirs.astype(f32), *(u[split:] for u in arrays)),
            ]
        )

    grad_gates, expert_grads = [], []
    for e in range(half):
        wide, down = expert_w[e][:, : 2 * ff], expert_w[e][:, 2 * ff :]
        gate_col = gates_own[:, e : e + 1]
        hidden = dot(hidden_all, wide)
        gate_h, up_h = hidden[:, :ff], hidden[:, ff:]
        sig = jax.nn.sigmoid(gate_h)
        silu = gate_h * sig
        act = (silu * up_h).astype(bf16)
        if e == 0:
            act, grad_theirs = lax.optimization_barrier((act, grad_theirs))
        result = contract_cols(act, down).astype(bf16).astype(f32)
        moe_part = moe_part + gate_col * result
        along = by_half(grad_theirs, lambda d, u: jnp.sum(d * u, axis=1), result)
        grad_gates.append(jnp.where(named_own[:, e], along, 0.0))
        grad_y = by_half(grad_theirs, lambda d, u: (u * d).astype(bf16), gate_col)
        grad_act = dot(grad_y, down)
        grad_h = jnp.concatenate(
            [grad_act * up_h * sig * (1.0 + gate_h * (1.0 - sig)), grad_act * silu], axis=1
        ).astype(bf16)
        back_part = back_part + contract_cols(grad_h, wide).astype(bf16).astype(f32)
        grad_w = [
            contract_rows(hidden_all, grad_h).astype(bf16),
            contract_rows(grad_y, act).astype(bf16),
        ]
        hidden_all, back_part, grad_w, expert_grads = lax.optimization_barrier(
            (hidden_all, back_part, grad_w, expert_grads)
        )
        expert_grads.append(
            [
                lax.psum_scatter(
                    u.reshape(2, width // 2, -1),
                    "ctx",
                    scatter_dimension=1,
                    tiled=True,
                    axis_index_groups=spans,
                )
                for u in grad_w
            ]
        )
    slots = jnp.stack(grad_gates).reshape(half, 2, n_shard, rows).transpose(1, 2, 0, 3)
    grad_gates = lax.dynamic_update_slice_in_dim(
        jnp.zeros((2, n_shard, experts, rows), f32), slots, first, 2
    )
    back_sum, grad_gates = pair_reduce(
        4, back_part.astype(bf16).reshape(2, n_shard, rows, width), grad_gates
    )
    grad_gates = grad_gates.T
    def own_rows(u):
        return lax.dynamic_slice_in_dim(u, shard * rows, rows, 0)

    gates_t, probs_t, named_t, sum_t = map(own_rows, (gates, probs, named, selected_sum))
    grad_selected = (
        grad_gates - jnp.sum(gates_t * grad_gates, axis=1, keepdims=True)
    ) / sum_t
    grad_probs = jnp.where(named_t, grad_selected, 0.0)
    grad_logits = (
        probs_t * (grad_probs - jnp.sum(probs_t * grad_probs, axis=1, keepdims=True))
    ).astype(bf16)
    grad_router = contract_rows(hidden_two, grad_logits)
    grad_hidden = back_sum + contract_cols(grad_logits, router_w)
    grad_gain_ffn = jnp.sum(grad_hidden * normed_two, axis=0)
    scaled_two = grad_hidden * gain_ffn
    grad_after = grad_own.astype(f32) + inverse_two * (
        scaled_two - normed_two * jnp.mean(scaled_two * normed_two, axis=1, keepdims=True)
    )

    grad_attn_own = grad_after.astype(bf16)

    def give(sums):
        return jnp.concatenate(
            [lax.dynamic_index_in_dim(u, 1 - role, 0, False) for u in sums], axis=1
        )

    peers = [swap(give(sums)) for sums in expert_grads[:-1]]
    to_gather, grad_attn_own, expert_grads[-1], peers = lax.optimization_barrier(
        (grad_attn_own, grad_attn_own, expert_grads[-1], peers)
    )
    grad_attn = lax.all_gather(to_gather, "ctx", axis=0, tiled=True)
    (grad_mixed,) = exchange(5, contract_cols(grad_attn_own, out_w).astype(bf16), True)
    grad_query_rot, grad_key_rot, grad_value = attend_backward(
        query, key, value, docs, log_total, grad_mixed
    )
    grad_query_n = rotate(grad_query_rot, cosine, -sine)
    grad_key_n = rotate(grad_key_rot, cosine, -sine)
    grad_gain_query = jnp.sum(grad_query_n * query_n, axis=0)
    grad_gain_key = jnp.sum(grad_key_n * key_n, axis=0)
    scaled_q, scaled_k = grad_query_n * gain_query, grad_key_n * gain_key
    peak_row = lax.dynamic_update_slice_in_dim(jnp.zeros((count,), f32), peaks, ctx * heads, 0)
    inner = jnp.stack(
        [jnp.sum(scaled_q * query_n, axis=1), jnp.sum(scaled_k * key_n, axis=1), peak_row]
    )
    inner = many_sum("ctx", 7, inner)
    inner, expert_grads[-1], moe_part, grad_attn = lax.optimization_barrier(
        (inner, expert_grads[-1], moe_part, grad_attn)
    )
    grad_out_w = contract_rows(mixed, grad_attn)
    moe_sums = lax.psum_scatter(
        moe_part.astype(bf16).reshape(2, n_shard * rows, width),
        "shard",
        scatter_dimension=1,
        tiled=True,
    )
    peers.append(swap(give(expert_grads[-1])))
    kept = [[lax.dynamic_index_in_dim(u, role, 0, False) for u in sums] for sums in expert_grads]
    peak_all = inner[2, :HEADS]
    inner = inner / width
    grad_linear = jnp.concatenate(
        [
            inverse_q * (scaled_q - query_n * inner[0][:, None]),
            inverse_k * (scaled_k - key_n * inner[1][:, None]),
            grad_value,
        ],
        axis=1,
    ).astype(bf16)
    grad_weights = contract_rows(hidden_one, grad_linear)
    hidden_part = contract_cols(grad_linear, weights)
    grad_gain_attn = jnp.sum(hidden_part * (x_wide * inverse_one), axis=0)
    grad_small = jnp.concatenate(
        [jnp.stack([grad_gain_attn, grad_gain_ffn], axis=1), grad_router], axis=1
    )
    grad_small = jnp.pad(grad_small, ((0, 0), (0, LANES - 2 - experts)))
    grad_weights = (
        jnp.concatenate([grad_weights, grad_small], axis=1)
        .astype(bf16)
        .reshape(n_ctx, n_shard, part, 3 * cols + LANES)
        .transpose(1, 0, 2, 3)
        .reshape(n_shard, n_ctx * part, 3 * cols + LANES)
    )
    grad_gain_qk = jnp.pad(
        jnp.stack([grad_gain_query, grad_gain_key], axis=1), ((0, 0), (0, LANES - 2))
    )
    grad_out_w = (
        jnp.concatenate([grad_out_w, grad_gain_qk], axis=1)
        .astype(bf16)
        .reshape(n_shard, part, width + LANES)
    )
    hidden_part = hidden_part.astype(bf16).reshape(n_ctx, rows, width)
    hidden_part, peers = lax.optimization_barrier((hidden_part, peers))
    grad_hidden_one, grad_weights, grad_out_w, moe_peer = end_call(
        8, hidden_part, grad_weights, grad_out_w, moe_sums[1]
    )
    output = (after + (moe_sums[0].astype(f32) + moe_peer.astype(f32))).astype(bf16)
    peers = [(peer[:, : 2 * ff], peer[:, 2 * ff :]) for peer in peers]
    both_halves = [
        in_order(jnp.stack([k[i] for k in kept]), jnp.stack([p[i] for p in peers]))
        .reshape(local, width // n_ctx, -1)
        .astype(f32)
        for i in (0, 1)
    ]
    grad_weights = grad_weights.astype(f32)
    grad_small = jnp.sum(grad_weights[..., 3 * cols :], axis=0)
    grad_weights = (
        grad_weights[..., : 3 * cols]
        .reshape(n_ctx, part, 3, cols)
        .transpose(2, 1, 0, 3)
        .reshape(3, part, width)
    )
    inverse_own = inverse_rms(x_f)
    normed_own = x_f * inverse_own
    scaled_one = grad_hidden_one * gain_attn
    grad_inputs = grad_after + inverse_own * (
        scaled_one - normed_own * jnp.mean(scaled_one * normed_own, axis=1, keepdims=True)
    )

    factors = jnp.sqrt(clip_threshold / jnp.maximum(peak_all, clip_threshold))
    col_scale = jnp.repeat(factors, HEAD)
    query_clipped = (w_query.astype(f32) * col_scale[None, :]).astype(bf16)
    key_clipped = (w_key.astype(f32) * col_scale[None, :]).astype(bf16)
    return (
        output[None],
        grad_inputs[None],
        grad_small[:, 0],
        grad_weights[0],
        grad_weights[1],
        grad_weights[2],
        grad_out_w[:, width],
        grad_out_w[:, width + 1],
        grad_out_w[:, :width],
        grad_small[:, 1],
        grad_small[:, 2 : 2 + experts],
        both_halves[0][..., :ff],
        both_halves[0][..., ff:],
        both_halves[1].transpose(0, 2, 1),
        query_clipped,
        key_clipped,
        factors,
    )


def solution(mesh):
    both = ("ctx", "shard")
    return jax.shard_map(
        per_device,
        mesh=mesh,
        in_specs=(
            P("shard", "ctx", None),
            P("shard", "ctx"),
            P("shard", "ctx", None),
            P(both),
            P(both, None),
            P(both, None),
            P(both, None),
            P(both),
            P(both),
            P(both, None),
            P(both),
            P(both, None),
            P("shard", "ctx", None),
            P("shard", "ctx", None),
            P("shard", None, "ctx"),
            P(),
            P("shard", "ctx", None),
        ),
        out_specs=(
            P("shard", "ctx", None),
            P("shard", "ctx", None),
            P(both),
            P(both, None),
            P(both, None),
            P(both, None),
            P(both),
            P(both),
            P(both, None),
            P(both),
            P(both, None),
            P("shard", "ctx", None),
            P("shard", "ctx", None),
            P("shard", None, "ctx"),
            P(both, None),
            P(both, None),
            P(),
        ),
        check_vma=False,
    )
```

```python
import functools

import jax
import jax.numpy as jnp
from jax import lax
from jax.experimental import pallas as pl
from jax.experimental.pallas import tpu as pltpu
from jax.sharding import PartitionSpec as P

HEADS = 16
HEAD = 128
SCALE = HEAD ** (-0.5)
Q_BLOCK = 256
LANES = 128

norm_eps = 1e-06
rope_base = 10000.0
f32 = jnp.float32
bf16 = jnp.bfloat16


def dot(a, b):
    return jnp.dot(a, b, preferred_element_type=f32)


def contract_rows(a, b):
    return lax.dot_general(a, b, (((0,), (0,)), ((), ())), preferred_element_type=f32)


def contract_cols(a, b):
    return lax.dot_general(a, b, (((1,), (1,)), ((), ())), preferred_element_type=f32)


def inverse_rms(values):
    return lax.rsqrt(jnp.mean(values * values, axis=-1, keepdims=True) + norm_eps)


def rope_tables(count):
    half = HEAD // 2
    freq = rope_base ** (-jnp.arange(half).astype(f32) / half)
    angles = jnp.arange(count).astype(f32)[:, None] * freq[None, :]
    return jnp.cos(angles), jnp.sin(angles)


def rotate(values, cosine, sine):
    parts = []
    for col in range(0, values.shape[1], HEAD):
        a = values[:, col : col + HEAD // 2]
        b = values[:, col + HEAD // 2 : col + HEAD]
        parts += [a * cosine - b * sine, b * cosine + a * sine]
    return jnp.concatenate(parts, axis=1)


def attend_forward_kernel(q_ref, k_ref, v_ref, doc_q_ref, doc_k_ref, o_ref, lse_ref, peak_ref):
    s = SCALE * contract_cols(q_ref[...], k_ref[...])
    s = jnp.where(doc_q_ref[...] == doc_k_ref[...], s, -1e30)
    top = jnp.max(s, axis=1, keepdims=True)
    e = jnp.exp(s - top)
    total = jnp.sum(e, axis=1, keepdims=True)
    p = (e * (1.0 / total)).astype(bf16)
    o_ref[...] = dot(p, v_ref[...]).astype(bf16)
    lse_ref[0] = top + jnp.log(total)
    peak = jnp.broadcast_to(jnp.max(top, axis=0, keepdims=True), peak_ref.shape[1:])

    @pl.when(pl.program_id(1) == 0)
    def _():
        peak_ref[0] = peak

    @pl.when(pl.program_id(1) > 0)
    def _():
        peak_ref[0] = jnp.maximum(peak_ref[0], peak)


def attend_backward_kernel(
    q_ref, k_ref, v_ref, doc_q_ref, doc_k_ref, lse_ref, do_ref, dq_ref, dk_ref, dv_ref
):
    q, k, v, do = q_ref[...], k_ref[...], v_ref[...], do_ref[...]
    s = SCALE * contract_cols(q, k)
    p = jnp.where(doc_q_ref[...] == doc_k_ref[...], jnp.exp(s - lse_ref[0]), 0.0)
    dp = contract_cols(do, v)
    inner = jnp.sum(p * dp, axis=1, keepdims=True)
    ds = (p * (dp - inner)).astype(bf16)
    dq_ref[...] = SCALE * dot(ds, k)
    dk = SCALE * contract_rows(ds, q)
    dv = contract_rows(p.astype(bf16), do)

    @pl.when(pl.program_id(1) == 0)
    def _():
        dk_ref[...] = dk
        dv_ref[...] = dv

    @pl.when(pl.program_id(1) > 0)
    def _():
        dk_ref[...] += dk
        dv_ref[...] += dv


def attend_specs(count):
    block = pl.BlockSpec((Q_BLOCK, HEAD), lambda h, i: (i, h))
    whole = pl.BlockSpec((count, HEAD), lambda h, i: (0, h))
    doc_q = pl.BlockSpec((Q_BLOCK, 1), lambda h, i: (i, 0))
    doc_k = pl.BlockSpec((1, count), lambda h, i: (0, 0))
    lse = pl.BlockSpec((1, Q_BLOCK, 1), lambda h, i: (h, i, 0))
    return block, whole, doc_q, doc_k, lse


def attend_forward(q, k, v, docs):
    count, width = q.shape
    heads = width // HEAD
    block, whole, doc_q, doc_k, lse = attend_specs(count)
    return pl.pallas_call(
        attend_forward_kernel,
        grid=(heads, count // Q_BLOCK),
        in_specs=[block, whole, whole, doc_q, doc_k],
        out_specs=[block, lse, pl.BlockSpec((1, 8, 128), lambda h, i: (h, 0, 0))],
        out_shape=[
            jax.ShapeDtypeStruct((count, width), bf16),
            jax.ShapeDtypeStruct((heads, count, 1), f32),
            jax.ShapeDtypeStruct((heads, 8, 128), f32),
        ],
        compiler_params=pltpu.CompilerParams(vmem_limit_bytes=48 << 20),
        cost_estimate=pl.CostEstimate(
            flops=4 * count * count * width,
            transcendentals=heads * count * count,
            bytes_accessed=8 * count * width,
        ),
    )(q, k, v, docs[:, None], docs[None, :])


def attend_backward(q, k, v, docs, log_total, grad):
    count, width = q.shape
    heads = width // HEAD
    block, whole, doc_q, doc_k, lse = attend_specs(count)
    return pl.pallas_call(
        attend_backward_kernel,
        grid=(heads, count // Q_BLOCK),
        in_specs=[block, whole, whole, doc_q, doc_k, lse, block],
        out_specs=[block, whole, whole],
        out_shape=[jax.ShapeDtypeStruct((count, width), f32)] * 3,
        compiler_params=pltpu.CompilerParams(vmem_limit_bytes=56 << 20),
        cost_estimate=pl.CostEstimate(
            flops=10 * count * count * width,
            transcendentals=heads * count * count,
            bytes_accessed=20 * count * width,
        ),
    )(q, k, v, docs[:, None], docs[None, :], log_total, grad)


MESH = pl.DeviceIdType.MESH
ANY = pl.BlockSpec(memory_space=pl.ANY)
VMEM = pl.BlockSpec(memory_space=pltpu.VMEM)


def ring_peers(axis):
    n, me = lax.axis_size(axis), lax.axis_index(axis)
    return [lax.rem(me + k, n) for k in range(n)], [lax.rem(me + n - k, n) for k in range(n)]


class Greeting:
    def __init__(self):
        self.barrier, self.total = pltpu.get_barrier_semaphore(), 0

    def ring(self, axis):
        to, _ = ring_peers(axis)
        for peer in to[1:]:
            pl.semaphore_signal(
                self.barrier, inc=1, device_id={axis: peer}, device_id_type=MESH
            )
        self.total = self.total + len(to) - 1
        return self

    def line(self):
        line = Line()
        for there, peer in (
            (line.place >= 0, line.partner),
            (line.not_last, line.me + 2),
            (line.not_first, line.me - 2),
        ):

            @pl.when(there)
            def _():
                pl.semaphore_signal(
                    self.barrier, inc=1, device_id={"ctx": peer}, device_id_type=MESH
                )

            self.total = self.total + there.astype(jnp.int32)
        return self

    def wait(self):
        pl.semaphore_wait(self.barrier, self.total)


class Line:
    def __init__(self):
        self.n, self.me = lax.axis_size("ctx") // 2, lax.axis_index("ctx")
        self.place, self.core = lax.div(self.me, 2), lax.rem(self.me, 2)
        self.partner = self.me + 1 - 2 * self.core
        self.not_first, self.not_last = self.place > 0, self.place < self.n - 1


class Direct:
    def __init__(self, axis, source, target, send, recv):
        self.axis, self.source, self.target = axis, source, target
        self.send, self.recv = send, recv
        self.me = lax.axis_index(axis)
        self.to, self.origin = ring_peers(axis)

    def copy(self, k, sender):
        return pltpu.make_async_remote_copy(
            src_ref=self.source(self.to[k]),
            dst_ref=self.target(sender, k),
            send_sem=self.send.at[k],
            recv_sem=self.recv.at[k],
            device_id={self.axis: self.to[k]},
            device_id_type=MESH,
        )

    def start(self):
        for k in range(1, len(self.to)):
            self.copy(k, self.me).start()

    def wait_recv(self):
        for k in range(1, len(self.to)):
            self.copy(k, self.origin[k]).wait_recv()

    def wait_send(self):
        for k in range(1, len(self.to)):
            self.copy(k, self.me).wait_send()


class LineGather:
    def __init__(self, pieces, own_sem, send_r, send_l, send_p, recv_r, recv_l, recv_p):
        self.line, self.pieces, self.own_sem = Line(), pieces, own_sem
        self.send_r, self.send_l, self.send_p = send_r, send_l, send_p
        self.recv_r, self.recv_l, self.recv_p = recv_r, recv_l, recv_p

    def own(self, c):
        source, target = self.pieces[c]
        return pltpu.make_async_copy(source, target(self.line.me), self.own_sem.at[c])

    def copy(self, block, k, c, target_device, send, recv):
        source, target = self.pieces[c]
        return pltpu.make_async_remote_copy(
            src_ref=source if k == 0 else target(block),
            dst_ref=target(block),
            send_sem=send,
            recv_sem=recv,
            device_id={"ctx": target_device},
            device_id_type=MESH,
        )

    def right(self, k, c):
        me = self.line.me
        return self.copy(me - 2 * k, k, c, me + 2, self.send_r.at[k, c], self.recv_r.at[k, c])

    def left(self, k, c):
        me = self.line.me
        return self.copy(me + 2 * k, k, c, me - 2, self.send_l.at[k, c], self.recv_l.at[k, c])

    def across(self, k, c, sign):
        line = self.line
        i = k if sign < 0 else line.n - 1 + k
        return self.copy(
            line.me + sign * 2 * k, k, c, line.partner, self.send_p.at[i, c], self.recv_p.at[i, c]
        )

    def arrived(self, block, c, recv):
        source, target = self.pieces[c]
        pltpu.make_async_remote_copy(
            src_ref=source,
            dst_ref=target(block),
            send_sem=recv,
            recv_sem=recv,
            device_id={"ctx": self.line.partner},
            device_id_type=MESH,
        ).wait_recv()

    def start(self):
        for c in range(len(self.pieces)):
            self.own(c).start()

    def hop(self, k):
        line = self.line
        for c in range(len(self.pieces)):

            @pl.when(line.place >= k)
            def _():
                if k:
                    self.arrived(line.me - 2 * k, c, self.recv_r.at[k - 1, c])

                @pl.when(line.not_last)
                def _():
                    self.right(k, c).start()

                self.across(k, c, -1).start()

            @pl.when(line.place + k <= line.n - 1)
            def _():
                if k:
                    self.arrived(line.me + 2 * k, c, self.recv_l.at[k - 1, c])

                @pl.when(line.not_first)
                def _():
                    self.left(k, c).start()

                if k:
                    self.across(k, c, 1).start()

    def finish(self, skip_own=None):
        line = self.line
        for c in range(len(self.pieces)):
            if c != skip_own:
                self.own(c).wait()
        for k in range(line.n):
            for c in range(len(self.pieces)):

                @pl.when(line.place >= k)
                def _():
                    @pl.when(line.not_last)
                    def _():
                        self.right(k, c).wait_send()

                    self.across(k, c, -1).wait_send()
                    self.arrived(line.partner - 2 * k, c, self.recv_p.at[k, c])

                @pl.when(line.place + k <= line.n - 1)
                def _():
                    @pl.when(line.not_first)
                    def _():
                        self.left(k, c).wait_send()

                    if k:
                        self.across(k, c, 1).wait_send()
                        self.arrived(line.partner + 2 * k, c, self.recv_p.at[line.n - 1 + k, c])


def line_gather_scratch(n, pieces):
    sem = pltpu.SemaphoreType.DMA
    one, two = sem((n, pieces)), sem((2 * n - 1, pieces))
    return [sem((pieces,)), one, one, two, one, one, two]


class LineReduce:
    def __init__(
        self, chunks, x, o, pair, from_left, from_right, send_p, recv_p, send_s, recv_r, recv_l
    ):
        self.line, self.chunks = Line(), chunks
        self.x, self.o, self.pair, self.out = x, o, pair, pair
        self.from_left, self.from_right = from_left, from_right
        self.send_p, self.recv_p, self.send_s = send_p, recv_p, send_s
        self.recv_r, self.recv_l = recv_r, recv_l
        self.order = []
        for j in range(self.line.n):
            self.order += [p for p in (self.line.n - 1 - j, j) if p not in self.order]

    def at(self, c):
        rows = self.x.shape[1] // self.chunks
        return pl.ds(c * rows, rows)

    def across(self, p, c):
        line, at = self.line, self.at(c)
        return pltpu.make_async_remote_copy(
            src_ref=self.x.at[2 * p + 1 - line.core, at],
            dst_ref=self.pair.at[p, at],
            send_sem=self.send_p.at[p, c],
            recv_sem=self.recv_p.at[p, c],
            device_id={"ctx": line.partner},
            device_id_type=MESH,
        )

    def along(self, p, c, step, buffer, recv):
        at = self.at(c)
        return pltpu.make_async_remote_copy(
            src_ref=self.out.at[p, at],
            dst_ref=buffer.at[p, at],
            send_sem=self.send_s.at[p, c],
            recv_sem=recv.at[p, c],
            device_id={"ctx": self.line.me + step},
            device_id_type=MESH,
        )

    def right(self, p, c):
        return self.along(p, c, 2, self.from_left, self.recv_r)

    def left(self, p, c):
        return self.along(p, c, -2, self.from_right, self.recv_l)

    def start(self):
        for p in self.order:
            for c in range(self.chunks):
                self.across(p, c).start()

    def both(self, p, c):
        at = self.at(c)
        return self.x[2 * p + self.line.core, at].astype(f32) + self.pair[p, at].astype(f32)

    def pass_on(self):
        line = self.line
        for p in self.order:
            for c in range(self.chunks):
                at = self.at(c)
                self.across(p, c).wait_recv()

                @pl.when(line.place < p)
                def _():
                    @pl.when(line.not_first)
                    def _():
                        self.right(p, c).wait_recv()
                        total = self.both(p, c) + self.from_left[p, at].astype(f32)
                        self.out[p, at] = total.astype(bf16)

                    @pl.when(line.place == 0)
                    def _():
                        self.out[p, at] = self.both(p, c).astype(bf16)

                    self.right(p, c).start()

                @pl.when(line.place > p)
                def _():
                    @pl.when(line.not_last)
                    def _():
                        self.left(p, c).wait_recv()
                        total = self.both(p, c) + self.from_right[p, at].astype(f32)
                        self.out[p, at] = total.astype(bf16)

                    @pl.when(line.place == line.n - 1)
                    def _():
                        self.out[p, at] = self.both(p, c).astype(bf16)

                    self.left(p, c).start()

    def finish(self):
        line = self.line
        for p in range(line.n):
            for c in range(self.chunks):
                at = self.at(c)

                @pl.when(line.place == p)
                def _():
                    self.o[at] = self.both(p, c)
                    if p > 0:
                        self.right(p, c).wait_recv()
                        self.o[at] += self.from_left[p, at].astype(f32)
                    if p < line.n - 1:
                        self.left(p, c).wait_recv()
                        self.o[at] += self.from_right[p, at].astype(f32)

        for p in range(line.n):
            for c in range(self.chunks):
                self.across(p, c).wait_send()

                @pl.when(line.place < p)
                def _():
                    self.right(p, c).wait_send()

                @pl.when(line.place > p)
                def _():
                    self.left(p, c).wait_send()


def add_up(x, buf, o, me):
    rows = x.shape[1]
    step = 8 if rows % 32 else 32

    @pl.loop(0, rows // step)
    def _(j):
        at = pl.ds(pl.multiple_of(j * step, step), step)
        total = x[me, at].astype(f32)
        for k in range(buf.shape[0]):
            total = total + buf[k, at].astype(f32)
        o[at] = total.astype(o.dtype)


def block_of(ref):
    return lambda device: ref.at[device]


def block_from(ref):
    return lambda device, k: ref.at[device]


def whole_of(ref):
    return lambda device: ref


def buffer_of(ref):
    return lambda device, k: ref.at[k - 1]


def row_pieces(source, target, chunks):
    rows = source.shape[0] // chunks
    return [
        (source.at[pl.ds(c * rows, rows)], lambda b, c=c: target.at[b, pl.ds(c * rows, rows)])
        for c in range(chunks)
    ]


def start_kernel(
    x, w, w_query, w_key, w_value, small, cot, x_all, w_all, heads_all, small_all, cot_all,
    heads_mid, small_mid, own_sem, ex_send, ex_recv, sp_send, sp_recv, w_send, w_recv, f_send,
    f_recv, *line_sems,
):
    shard, ctx = lax.axis_index("shard"), lax.axis_index("ctx")
    n_ctx = lax.axis_size("ctx")
    cols = w_query.shape[1] // n_ctx
    Greeting().ring("ctx").ring("shard").wait()

    def columns(ref):
        return lambda d: ref.at[:, pl.ds(pl.multiple_of(d * cols, HEAD), cols)]

    def place(i):
        if i == 3:
            return block_from(small_mid)
        return lambda d, k: heads_mid.at[d, :, i * cols : (i + 1) * cols]

    sources = [columns(w_query), columns(w_key), columns(w_value), whole_of(small)]
    swaps = [
        Direct("ctx", source, place(i), ex_send.at[i], ex_recv.at[i])
        for i, source in enumerate(sources)
    ]

    def by_shard(ref):
        return lambda d, k: ref.at[:, d]

    spreads = [
        Direct("shard", whole_of(heads_mid), by_shard(heads_all), sp_send.at[0], sp_recv.at[0]),
        Direct("shard", whole_of(small_mid), by_shard(small_all), sp_send.at[1], sp_recv.at[1]),
    ]
    other = Direct("shard", whole_of(cot), block_from(cot_all), sp_send.at[2], sp_recv.at[2])
    rows_w = LineGather([(w, lambda b: w_all.at[b, shard])], *line_sems[:7])
    rows_x = LineGather(row_pieces(x, x_all, LINE_CHUNKS), *line_sems[7:])
    at = rows_x.line
    own = [
        pltpu.make_async_copy(source(ctx), place(i)(ctx, 0), own_sem.at[i])
        for i, source in enumerate(sources)
    ]
    later = [
        pltpu.make_async_copy(heads_mid, heads_all.at[:, shard], own_sem.at[4]),
        pltpu.make_async_copy(small_mid, small_all.at[:, shard], own_sem.at[5]),
        pltpu.make_async_copy(cot, cot_all.at[shard], own_sem.at[6]),
    ]
    other.start()
    for swap in swaps:
        swap.start()
    for copy in own:
        copy.start()
    rows_w.start()
    rows_w.hop(0)
    rows_x.start()
    rows_x.hop(0)
    for swap in swaps:
        swap.wait_recv()
    for copy in own:
        copy.wait()
    for one in (*spreads, *later):
        one.start()
    for k in range(1, at.n):
        rows_w.hop(k)

    to, origin = ring_peers("shard")

    def row(k, p, sender):
        block = 2 * p + at.core
        return pltpu.make_async_remote_copy(
            src_ref=w_all.at[block, shard],
            dst_ref=w_all.at[block, sender],
            send_sem=w_send.at[k, p],
            recv_sem=w_recv.at[k, p],
            device_id={"shard": to[k]},
            device_id_type=MESH,
        )

    def forward(k, p, core):
        block = w_all.at[2 * p + core, origin[k]]
        return pltpu.make_async_remote_copy(
            src_ref=block,
            dst_ref=block,
            send_sem=f_send.at[k, p],
            recv_sem=f_recv.at[k, p],
            device_id={"ctx": at.partner},
            device_id_type=MESH,
        )

    some = [(k, p) for k in range(1, len(to)) for p in range(at.n)]
    rows_w.own(0).wait()
    for k, p in some:
        row(k, p, shard).start()
    for k in range(1, at.n):
        rows_x.hop(k)
    for k, p in some:
        row(k, p, origin[k]).wait_recv()
        forward(k, p, at.core).start()
    rows_w.finish(skip_own=0)
    rows_x.finish()
    for k, p in some:
        row(k, p, shard).wait_send()
        forward(k, p, at.core).wait_send()
        forward(k, p, 1 - at.core).wait_recv()
    for direct in (other, *spreads):
        direct.wait_recv()
    for direct in (other, *swaps, *spreads):
        direct.wait_send()
    for copy in later:
        copy.wait()


def exchange_kernel(to_rows, *refs):
    more = len(refs) > 5
    if more:
        x, cot, o, cot_all, own_sem, send, recv, cot_send, cot_recv = refs
    else:
        x, o, own_sem, send, recv = refs
    n, me = lax.axis_size("ctx"), lax.axis_index("ctx")
    cols, rows = (x.shape[1] // n, x.shape[0]) if to_rows else (x.shape[1], o.shape[0])

    def row_block(ref):
        return lambda d, k=0: ref.at[pl.ds(pl.multiple_of(d * rows, rows), rows)]

    def column_block(ref):
        return lambda d, k=0: ref.at[:, pl.ds(pl.multiple_of(d * cols, cols), cols)]

    source, target = (
        (column_block(x), row_block(o)) if to_rows else (row_block(x), column_block(o))
    )
    greeting = Greeting().ring("ctx")
    if more:
        greeting.ring("shard")
    greeting.wait()
    all_of = [Direct("ctx", source, target, send, recv)]
    own = [pltpu.make_async_copy(source(me), target(me), own_sem.at[0])]
    if more:
        all_of.append(Direct("shard", whole_of(cot), block_from(cot_all), cot_send, cot_recv))
        own.append(
            pltpu.make_async_copy(cot, cot_all.at[lax.axis_index("shard")], own_sem.at[1])
        )
    for one in (*all_of, *own):
        one.start()
    for copy in own:
        copy.wait()
    for direct in all_of:
        direct.wait_recv()
        direct.wait_send()


def gather_kernel(axis, count, *refs):
    ins, outs = refs[:count], refs[count : 2 * count]
    own_sem, send, recv = refs[2 * count :]
    me = lax.axis_index(axis)
    Greeting().ring(axis).wait()
    all_of = [
        Direct(axis, whole_of(ins[i]), block_from(outs[i]), send.at[i], recv.at[i])
        for i in range(count)
    ]
    own = [pltpu.make_async_copy(ins[i], outs[i].at[me], own_sem.at[i]) for i in range(count)]
    for direct in all_of:
        direct.start()
    for copy in own:
        copy.start()
    for copy in own:
        copy.wait()
    for direct in all_of:
        direct.wait_recv()
        direct.wait_send()


def reduce_kernel(axis, count, *refs):
    ins, outs, bufs = refs[:count], refs[count : 2 * count], refs[2 * count : 3 * count]
    send, recv = refs[3 * count :]
    Greeting().ring(axis).wait()
    all_of = [
        Direct(axis, block_of(ins[i]), buffer_of(bufs[i]), send.at[i], recv.at[i])
        for i in range(count)
    ]
    for direct in all_of:
        direct.start()
    for i, direct in enumerate(all_of):
        direct.wait_recv()
        add_up(ins[i], bufs[i], outs[i], direct.me)
        direct.wait_send()


def many_sum_kernel(axis, x, o, buf, send, recv):
    Greeting().ring(axis).wait()
    direct = Direct(axis, whole_of(x), buffer_of(buf), send, recv)
    direct.start()
    direct.wait_recv()
    total = x[...]
    for k in range(buf.shape[0]):
        total = total + buf[k]
    o[...] = total
    direct.wait_send()


def end_kernel(
    x, wide, out, y, x_sum, wide_all, out_sum, y_sum, wide_buf, out_buf, y_buf, wide_sum,
    own_sem, wide_send, wide_recv, out_send, out_recv, y_send, y_recv, swap_send, swap_recv,
    *line_refs,
):
    ctx = lax.axis_index("ctx")
    Greeting().ring("ctx").ring("shard").wait()
    wides = Direct("shard", block_of(wide), buffer_of(wide_buf), wide_send, wide_recv)
    outs = Direct("shard", block_of(out), buffer_of(out_buf), out_send, out_recv)
    swap = Direct("ctx", block_of(wide_sum), block_from(wide_all), swap_send, swap_recv)
    line = LineReduce(LINE_CHUNKS, x, x_sum, *line_refs)
    returns = Direct("shard", block_of(y), buffer_of(y_buf), y_send, y_recv)
    line.start()
    wides.start()
    outs.start()
    returns.start()
    line.pass_on()
    wides.wait_recv()
    for b in range(lax.axis_size("ctx")):
        rows = wide_sum.shape[1]
        total = wide[wides.me, b * rows : (b + 1) * rows].astype(f32)
        for k in range(wide_buf.shape[0]):
            total = total + wide_buf[k, b * rows : (b + 1) * rows].astype(f32)
        wide_sum[b] = total.astype(bf16)
    swap.start()
    own = pltpu.make_async_copy(wide_sum.at[ctx], wide_all.at[ctx], own_sem)
    own.start()
    outs.wait_recv()
    add_up(out, out_buf, out_sum, outs.me)
    line.finish()
    returns.wait_recv()
    add_up(y, y_buf, y_sum, returns.me)
    own.wait()
    swap.wait_recv()
    for direct in (swap, wides, outs, returns):
        direct.wait_send()


def remote_params(collective_id, megabytes):
    return pltpu.CompilerParams(
        collective_id=collective_id, has_side_effects=True, vmem_limit_bytes=megabytes << 20
    )


LINE_CHUNKS = 4


def start_call(collective_id, x, w, w_query, w_key, w_value, small, cot):
    n_ctx, n_shard = lax.axis_size("ctx"), lax.axis_size("shard")
    n = n_ctx // 2
    heads = (w.shape[0], 3 * w.shape[1] // n_ctx)
    sem = pltpu.SemaphoreType.DMA
    return pl.pallas_call(
        start_kernel,
        out_shape=[
            jax.ShapeDtypeStruct((n_ctx, *x.shape), bf16),
            jax.ShapeDtypeStruct((n_ctx, n_shard, *w.shape), bf16),
            jax.ShapeDtypeStruct((n_ctx, n_shard, *heads), bf16),
            jax.ShapeDtypeStruct((n_ctx, n_shard, *small.shape), bf16),
            jax.ShapeDtypeStruct((n_shard, *cot.shape), bf16),
        ],
        in_specs=[ANY] * 7,
        out_specs=[ANY] * 5,
        scratch_shapes=[
            pltpu.VMEM((n_ctx, *heads), bf16),
            pltpu.VMEM((n_ctx, *small.shape), bf16),
            sem((7,)),
            sem((4, n_ctx)),
            sem((4, n_ctx)),
        ]
        + [sem((3, n_shard))] * 2
        + [sem((n_shard, n))] * 4
        + line_gather_scratch(n, 1)
        + line_gather_scratch(n, LINE_CHUNKS),
        compiler_params=remote_params(collective_id, 8),
    )(x, w, w_query, w_key, w_value, small, cot)


def exchange(collective_id, x, to_rows, *more):
    n, n_shard = lax.axis_size("ctx"), lax.axis_size("shard")
    shape = (x.shape[0] * n, x.shape[1] // n) if to_rows else (x.shape[0] // n, x.shape[1] * n)
    sem = pltpu.SemaphoreType.DMA
    return pl.pallas_call(
        functools.partial(exchange_kernel, to_rows),
        out_shape=[jax.ShapeDtypeStruct(shape, x.dtype)]
        + [jax.ShapeDtypeStruct((n_shard, *u.shape), u.dtype) for u in more],
        in_specs=[ANY] * (1 + len(more)),
        out_specs=[ANY] * (1 + len(more)),
        scratch_shapes=[sem((2,)), sem((n,)), sem((n,))] + [sem((n_shard,))] * (2 * len(more)),
        compiler_params=remote_params(collective_id, 8),
    )(x, *more)


def gather(axis, collective_id, *arrays):
    count, n = len(arrays), lax.axis_size(axis)
    sem = pltpu.SemaphoreType.DMA
    return pl.pallas_call(
        functools.partial(gather_kernel, axis, count),
        out_shape=[jax.ShapeDtypeStruct((n, *a.shape), a.dtype) for a in arrays],
        in_specs=[ANY] * count,
        out_specs=[ANY] * count,
        scratch_shapes=[sem((count,)), sem((count, n)), sem((count, n))],
        compiler_params=remote_params(collective_id, 8),
    )(*arrays)


def reduce(axis, collective_id, *arrays):
    count, n = len(arrays), lax.axis_size(axis)
    sem = pltpu.SemaphoreType.DMA
    return pl.pallas_call(
        functools.partial(reduce_kernel, axis, count),
        out_shape=[jax.ShapeDtypeStruct(a.shape[1:], f32) for a in arrays],
        in_specs=[VMEM] * count,
        out_specs=[VMEM] * count,
        scratch_shapes=[pltpu.VMEM((n - 1, *a.shape[1:]), a.dtype) for a in arrays]
        + [sem((count, n)), sem((count, n))],
        compiler_params=remote_params(collective_id, 32),
    )(*arrays)


def many_sum(axis, collective_id, x):
    n = lax.axis_size(axis)
    sem = pltpu.SemaphoreType.DMA
    return pl.pallas_call(
        functools.partial(many_sum_kernel, axis),
        out_shape=jax.ShapeDtypeStruct(x.shape, x.dtype),
        in_specs=[VMEM],
        out_specs=VMEM,
        scratch_shapes=[pltpu.VMEM((n - 1, *x.shape), x.dtype), sem((n,)), sem((n,))],
        compiler_params=remote_params(collective_id, 8),
    )(x)


def end_call(collective_id, x, wide, out, y):
    n_ctx, rows, width = x.shape
    n_shard = lax.axis_size("shard")
    n = n_ctx // 2
    wide_rows, wide_cols = wide.shape[1] // n_ctx, wide.shape[2]
    sem = pltpu.SemaphoreType.DMA
    return pl.pallas_call(
        end_kernel,
        out_shape=[
            jax.ShapeDtypeStruct((rows, width), f32),
            jax.ShapeDtypeStruct((n_ctx, wide_rows, wide_cols), bf16),
            jax.ShapeDtypeStruct(out.shape[1:], f32),
            jax.ShapeDtypeStruct(y.shape[1:], f32),
        ],
        in_specs=[VMEM] * 4,
        out_specs=[VMEM] * 4,
        scratch_shapes=[
            pltpu.VMEM((n_shard - 1, *wide.shape[1:]), bf16),
            pltpu.VMEM((n_shard - 1, *out.shape[1:]), bf16),
            pltpu.VMEM((n_shard - 1, *y.shape[1:]), bf16),
            pltpu.VMEM((n_ctx, wide_rows, wide_cols), bf16),
            sem,
        ]
        + [sem((n_shard,))] * 6
        + [sem((n_ctx,))] * 2
        + [pltpu.VMEM((n, rows, width), bf16)] * 3
        + [sem((n, LINE_CHUNKS))] * 5,
        compiler_params=remote_params(collective_id, 56),
    )(x, wide, out, y)


def per_device(
    tokens,
    doc_ids,
    routes,
    attn_gain,
    w_query,
    w_key,
    w_value,
    query_gain,
    key_gain,
    w_out,
    ffn_gain,
    w_router,
    w_gate,
    w_up,
    w_down,
    clip_threshold,
    cotangent,
):
    both = ("ctx", "shard")
    n_ctx, n_shard = lax.axis_size("ctx"), lax.axis_size("shard")
    ctx, shard = lax.axis_index("ctx"), lax.axis_index("shard")
    x_own = tokens[0]
    rows, width = x_own.shape
    part = w_query.shape[0]
    cols = width // n_ctx
    heads = cols // HEAD
    count = rows * n_ctx
    local = w_gate.shape[0]
    experts = local * n_shard

    top = routes.shape[2]
    spare = jnp.zeros((part, LANES - 4 - experts - rows // part * (1 + top)), bf16)
    small = jnp.concatenate(
        [
            jnp.stack([attn_gain, query_gain, key_gain, ffn_gain], axis=1),
            w_router,
            doc_ids.reshape(part, rows // part).astype(bf16),
            routes.reshape(part, rows // part * top).astype(bf16),
            spare,
        ],
        axis=1,
    )
    grad_own = cotangent[0]
    x_all, out_w, weights, small_all, grad_all = start_call(
        1, x_own, w_out, w_query, w_key, w_value, small, grad_own
    )
    x_all = x_all.reshape(count, width)
    out_w = out_w.reshape(width, width)
    weights = weights.reshape(width, 3 * cols)
    gains = small_all[..., : 4 + experts].reshape(width, 4 + experts)
    gain_attn, gain_query, gain_key, gain_ffn = (gains[:, i].astype(f32) for i in range(4))
    router_w = gains[:, 4:]
    gain_query = lax.dynamic_slice_in_dim(gain_query, ctx * cols, cols)
    gain_key = lax.dynamic_slice_in_dim(gain_key, ctx * cols, cols)
    tail = small_all[..., 4 + experts :].astype(jnp.int32)
    docs = lax.dynamic_index_in_dim(tail[..., : rows // part], shard, 1, False).reshape(count)
    grad_all = grad_all.reshape(n_shard * rows, width)
    routes_all = lax.dynamic_index_in_dim(
        tail[..., rows // part : rows // part * (1 + top)], ctx, 0, False
    ).reshape(n_shard * rows, top)

    ff = w_gate.shape[2]
    own_w = jnp.concatenate([w_gate, w_up, w_down.transpose(0, 2, 1)], axis=2)
    x_all, own_w = lax.optimization_barrier((x_all, own_w))
    expert_w = [lax.all_gather(own_w[e], "ctx", axis=0, tiled=True) for e in range(local)]

    x_wide = x_all.astype(f32)
    inverse_one = inverse_rms(x_wide)
    hidden_one = (x_wide * inverse_one * gain_attn).astype(bf16)
    linear = dot(hidden_one, weights)
    query_lin, key_lin = linear[:, :cols], linear[:, cols : 2 * cols]
    value = linear[:, 2 * cols :].astype(bf16)
    squares = jnp.stack(
        [jnp.sum(query_lin * query_lin, axis=1), jnp.sum(key_lin * key_lin, axis=1)]
    )
    squares = many_sum("ctx", 6, squares)
    inverse_qk = lax.rsqrt(squares / width + norm_eps)
    inverse_q, inverse_k = inverse_qk[0][:, None], inverse_qk[1][:, None]
    cosine, sine = rope_tables(count)
    query_n, key_n = query_lin * inverse_q, key_lin * inverse_k
    query = rotate(query_n * gain_query, cosine, sine).astype(bf16)
    key = rotate(key_n * gain_key, cosine, sine).astype(bf16)
    mixed, log_total, peaks = attend_forward(query, key, value, docs)
    x_f = x_own.astype(f32)
    (mixed_own,) = exchange(2, mixed, False)
    after = x_f + dot(mixed_own, out_w)
    inverse_two = inverse_rms(after)
    normed_two = after * inverse_two
    hidden_two = (normed_two * gain_ffn).astype(bf16)

    hidden_all, peaks = gather("shard", 3, hidden_two, peaks)
    hidden_all = hidden_all.reshape(n_shard * rows, width)
    peaks = jnp.max(peaks, axis=0)[:, 0, 0]
    logits = dot(hidden_all, router_w)
    named = jnp.any(routes_all[:, :, None] == jnp.arange(experts)[None, None, :], axis=1)
    probs = jax.nn.softmax(logits, axis=1)
    selected = jnp.where(named, probs, 0.0)
    selected_sum = jnp.sum(selected, axis=1, keepdims=True)
    gates = selected / selected_sum
    gates_own = lax.dynamic_slice_in_dim(gates, shard * local, local, 1)
    named_own = lax.dynamic_slice_in_dim(named, shard * local, local, 1)
    moe_part = jnp.zeros(hidden_all.shape, f32)
    back_part = jnp.zeros(hidden_all.shape, f32)

    grad_wide = grad_all.astype(f32)
    def to_owners(parts):
        return [lax.psum_scatter(u, "ctx", scatter_dimension=0, tiled=True) for u in parts]

    grad_gates, expert_grads = [], []
    for e in range(local):
        wide, down = expert_w[e][:, : 2 * ff], expert_w[e][:, 2 * ff :]
        gate_col = gates_own[:, e : e + 1]
        hidden = dot(hidden_all, wide)
        gate_h, up_h = hidden[:, :ff], hidden[:, ff:]
        sig = jax.nn.sigmoid(gate_h)
        silu = gate_h * sig
        act = (silu * up_h).astype(bf16)
        result = contract_cols(act, down).astype(bf16).astype(f32)
        moe_part = moe_part + gate_col * result
        along = jnp.sum(grad_wide * result, axis=1)
        grad_gates.append(jnp.where(named_own[:, e], along, 0.0))
        grad_y = (gate_col * grad_wide).astype(bf16)
        grad_act = dot(grad_y, down)
        grad_h = jnp.concatenate(
            [grad_act * up_h * sig * (1.0 + gate_h * (1.0 - sig)), grad_act * silu], axis=1
        ).astype(bf16)
        back_part = back_part + contract_cols(grad_h, wide).astype(bf16).astype(f32)
        grad_w = [
            contract_rows(hidden_all, grad_h).astype(bf16),
            contract_rows(grad_y, act).astype(bf16),
        ]
        hidden_all, back_part, grad_w = lax.optimization_barrier((hidden_all, back_part, grad_w))
        expert_grads.append(grad_w)
    early = local // 2
    expert_grads[:early] = [to_owners(grad_w) for grad_w in expert_grads[:early]]
    slots = jnp.stack(grad_gates).reshape(local, n_shard, rows).transpose(1, 0, 2)
    grad_gates = lax.dynamic_update_slice_in_dim(
        jnp.zeros((n_shard, experts, rows), f32), slots, shard * local, 1
    )
    back_sum, grad_gates = reduce(
        "shard", 4, back_part.astype(bf16).reshape(n_shard, rows, width), grad_gates
    )
    grad_gates = grad_gates.T

    def own_rows(u):
        return lax.dynamic_slice_in_dim(u, shard * rows, rows, 0)

    gates_t, probs_t, named_t, sum_t = map(own_rows, (gates, probs, named, selected_sum))
    grad_selected = (
        grad_gates - jnp.sum(gates_t * grad_gates, axis=1, keepdims=True)
    ) / sum_t
    grad_probs = jnp.where(named_t, grad_selected, 0.0)
    grad_logits = (
        probs_t * (grad_probs - jnp.sum(probs_t * grad_probs, axis=1, keepdims=True))
    ).astype(bf16)
    grad_router = contract_rows(hidden_two, grad_logits)
    grad_hidden = back_sum + contract_cols(grad_logits, router_w)
    grad_gain_ffn = jnp.sum(grad_hidden * normed_two, axis=0)
    scaled_two = grad_hidden * gain_ffn
    grad_after = grad_own.astype(f32) + inverse_two * (
        scaled_two - normed_two * jnp.mean(scaled_two * normed_two, axis=1, keepdims=True)
    )

    grad_attn_own = grad_after.astype(bf16)
    to_gather, expert_grads[0] = lax.optimization_barrier((grad_attn_own, expert_grads[0]))
    grad_attn = lax.all_gather(to_gather, "ctx", axis=0, tiled=True)
    (grad_mixed,) = exchange(5, contract_cols(grad_attn_own, out_w).astype(bf16), True)
    grad_mixed, late = lax.optimization_barrier((grad_mixed, expert_grads[early:]))
    expert_grads[early:] = [to_owners(grad_w) for grad_w in late]
    grad_query_rot, grad_key_rot, grad_value = attend_backward(
        query, key, value, docs, log_total, grad_mixed
    )
    grad_query_n = rotate(grad_query_rot, cosine, -sine)
    grad_key_n = rotate(grad_key_rot, cosine, -sine)
    grad_gain_query = jnp.sum(grad_query_n * query_n, axis=0)
    grad_gain_key = jnp.sum(grad_key_n * key_n, axis=0)
    scaled_q, scaled_k = grad_query_n * gain_query, grad_key_n * gain_key
    peak_row = lax.dynamic_update_slice_in_dim(jnp.zeros((count,), f32), peaks, ctx * heads, 0)
    inner = jnp.stack(
        [jnp.sum(scaled_q * query_n, axis=1), jnp.sum(scaled_k * key_n, axis=1), peak_row]
    )
    inner = many_sum("ctx", 7, inner)
    grad_out_w = contract_rows(mixed, grad_attn)
    peak_all = inner[2, :HEADS]
    inner = inner / width
    grad_linear = jnp.concatenate(
        [
            inverse_q * (scaled_q - query_n * inner[0][:, None]),
            inverse_k * (scaled_k - key_n * inner[1][:, None]),
            grad_value,
        ],
        axis=1,
    ).astype(bf16)
    grad_weights = contract_rows(hidden_one, grad_linear)
    hidden_part = contract_cols(grad_linear, weights)
    grad_gain_attn = jnp.sum(hidden_part * (x_wide * inverse_one), axis=0)
    grad_small = jnp.concatenate(
        [jnp.stack([grad_gain_attn, grad_gain_ffn], axis=1), grad_router], axis=1
    )
    grad_small = jnp.pad(grad_small, ((0, 0), (0, LANES - 2 - experts)))
    grad_weights = (
        jnp.concatenate([grad_weights, grad_small], axis=1)
        .astype(bf16)
        .reshape(n_ctx, n_shard, part, 3 * cols + LANES)
        .transpose(1, 0, 2, 3)
        .reshape(n_shard, n_ctx * part, 3 * cols + LANES)
    )
    grad_gain_qk = jnp.pad(
        jnp.stack([grad_gain_query, grad_gain_key], axis=1), ((0, 0), (0, LANES - 2))
    )
    grad_out_w = (
        jnp.concatenate([grad_out_w, grad_gain_qk], axis=1)
        .astype(bf16)
        .reshape(n_shard, part, width + LANES)
    )
    hidden_part = hidden_part.astype(bf16).reshape(n_ctx, rows, width)
    grad_hidden_one, grad_weights, grad_out_w, moe_sum = end_call(
        8,
        hidden_part,
        grad_weights,
        grad_out_w,
        moe_part.astype(bf16).reshape(n_shard, rows, width),
    )
    output = (after + moe_sum).astype(bf16)
    grad_hidden_one, expert_grads = lax.optimization_barrier((grad_hidden_one, expert_grads))
    grad_weights = grad_weights.astype(f32)
    grad_small = jnp.sum(grad_weights[..., 3 * cols :], axis=0)
    grad_weights = (
        grad_weights[..., : 3 * cols]
        .reshape(n_ctx, part, 3, cols)
        .transpose(2, 1, 0, 3)
        .reshape(3, part, width)
    )
    inverse_own = inverse_rms(x_f)
    normed_own = x_f * inverse_own
    scaled_one = grad_hidden_one * gain_attn
    grad_inputs = grad_after + inverse_own * (
        scaled_one - normed_own * jnp.mean(scaled_one * normed_own, axis=1, keepdims=True)
    )

    wide_grads = jnp.stack([u for u, _ in expert_grads])
    down_grads = jnp.stack([u for _, u in expert_grads])
    factors = jnp.sqrt(clip_threshold / jnp.maximum(peak_all, clip_threshold))
    col_scale = jnp.repeat(factors, HEAD)
    query_clipped = (w_query.astype(f32) * col_scale[None, :]).astype(bf16)
    key_clipped = (w_key.astype(f32) * col_scale[None, :]).astype(bf16)
    return (
        output[None],
        grad_inputs[None],
        grad_small[:, 0],
        grad_weights[0],
        grad_weights[1],
        grad_weights[2],
        grad_out_w[:, width],
        grad_out_w[:, width + 1],
        grad_out_w[:, :width],
        grad_small[:, 1],
        grad_small[:, 2 : 2 + experts],
        wide_grads[..., :ff].astype(f32),
        wide_grads[..., ff:].astype(f32),
        down_grads.transpose(0, 2, 1).astype(f32),
        query_clipped,
        key_clipped,
        factors,
    )


def solution(mesh):
    both = ("ctx", "shard")
    return jax.shard_map(
        per_device,
        mesh=mesh,
        in_specs=(
            P("shard", "ctx", None),
            P("shard", "ctx"),
            P("shard", "ctx", None),
            P(both),
            P(both, None),
            P(both, None),
            P(both, None),
            P(both),
            P(both),
            P(both, None),
            P(both),
            P(both, None),
            P("shard", "ctx", None),
            P("shard", "ctx", None),
            P("shard", None, "ctx"),
            P(),
            P("shard", "ctx", None),
        ),
        out_specs=(
            P("shard", "ctx", None),
            P("shard", "ctx", None),
            P(both),
            P(both, None),
            P(both, None),
            P(both, None),
            P(both),
            P(both),
            P(both, None),
            P(both),
            P(both, None),
            P("shard", "ctx", None),
            P("shard", "ctx", None),
            P("shard", None, "ctx"),
            P(both, None),
            P(both, None),
            P(),
        ),
        check_vma=False,
    )
```

```python
import functools

import jax
import jax.numpy as jnp
from jax import lax
from jax.experimental import pallas as pl
from jax.experimental.pallas import tpu as pltpu
from jax.sharding import PartitionSpec as P

HEADS = 16
HEAD = 128
SCALE = HEAD ** (-0.5)
Q_BLOCK = 256
LANES = 128

norm_eps = 1e-06
rope_base = 10000.0
f32 = jnp.float32
bf16 = jnp.bfloat16


def dot(a, b):
    return jnp.dot(a, b, preferred_element_type=f32)


def contract_rows(a, b):
    return lax.dot_general(a, b, (((0,), (0,)), ((), ())), preferred_element_type=f32)


def contract_cols(a, b):
    return lax.dot_general(a, b, (((1,), (1,)), ((), ())), preferred_element_type=f32)


def inverse_rms(values):
    return lax.rsqrt(jnp.mean(values * values, axis=-1, keepdims=True) + norm_eps)


def rope_tables(count):
    half = HEAD // 2
    freq = rope_base ** (-jnp.arange(half).astype(f32) / half)
    angles = jnp.arange(count).astype(f32)[:, None] * freq[None, :]
    return jnp.cos(angles), jnp.sin(angles)


def rotate(values, cosine, sine):
    parts = []
    for col in range(0, values.shape[1], HEAD):
        a = values[:, col : col + HEAD // 2]
        b = values[:, col + HEAD // 2 : col + HEAD]
        parts += [a * cosine - b * sine, b * cosine + a * sine]
    return jnp.concatenate(parts, axis=1)


def attend_forward_kernel(q_ref, k_ref, v_ref, doc_q_ref, doc_k_ref, o_ref, lse_ref, peak_ref):
    s = SCALE * contract_cols(q_ref[...], k_ref[...])
    s = jnp.where(doc_q_ref[...] == doc_k_ref[...], s, -1e30)
    top = jnp.max(s, axis=1, keepdims=True)
    e = jnp.exp(s - top)
    total = jnp.sum(e, axis=1, keepdims=True)
    p = (e * (1.0 / total)).astype(bf16)
    o_ref[...] = dot(p, v_ref[...]).astype(bf16)
    lse_ref[0] = top + jnp.log(total)
    peak = jnp.broadcast_to(jnp.max(top, axis=0, keepdims=True), peak_ref.shape[1:])

    @pl.when(pl.program_id(1) == 0)
    def _():
        peak_ref[0] = peak

    @pl.when(pl.program_id(1) > 0)
    def _():
        peak_ref[0] = jnp.maximum(peak_ref[0], peak)


def attend_backward_kernel(
    q_ref, k_ref, v_ref, doc_q_ref, doc_k_ref, lse_ref, do_ref, dq_ref, dk_ref, dv_ref
):
    q, k, v, do = q_ref[...], k_ref[...], v_ref[...], do_ref[...]
    s = SCALE * contract_cols(q, k)
    p = jnp.where(doc_q_ref[...] == doc_k_ref[...], jnp.exp(s - lse_ref[0]), 0.0)
    dp = contract_cols(do, v)
    inner = jnp.sum(p * dp, axis=1, keepdims=True)
    ds = (p * (dp - inner)).astype(bf16)
    dq_ref[...] = SCALE * dot(ds, k)
    dk = SCALE * contract_rows(ds, q)
    dv = contract_rows(p.astype(bf16), do)

    @pl.when(pl.program_id(1) == 0)
    def _():
        dk_ref[...] = dk
        dv_ref[...] = dv

    @pl.when(pl.program_id(1) > 0)
    def _():
        dk_ref[...] += dk
        dv_ref[...] += dv


def attend_specs(count):
    block = pl.BlockSpec((Q_BLOCK, HEAD), lambda h, i: (i, h))
    whole = pl.BlockSpec((count, HEAD), lambda h, i: (0, h))
    doc_q = pl.BlockSpec((Q_BLOCK, 1), lambda h, i: (i, 0))
    doc_k = pl.BlockSpec((1, count), lambda h, i: (0, 0))
    lse = pl.BlockSpec((1, Q_BLOCK, 1), lambda h, i: (h, i, 0))
    return block, whole, doc_q, doc_k, lse


def attend_forward(q, k, v, docs):
    count, width = q.shape
    heads = width // HEAD
    block, whole, doc_q, doc_k, lse = attend_specs(count)
    return pl.pallas_call(
        attend_forward_kernel,
        grid=(heads, count // Q_BLOCK),
        in_specs=[block, whole, whole, doc_q, doc_k],
        out_specs=[block, lse, pl.BlockSpec((1, 8, 128), lambda h, i: (h, 0, 0))],
        out_shape=[
            jax.ShapeDtypeStruct((count, width), bf16),
            jax.ShapeDtypeStruct((heads, count, 1), f32),
            jax.ShapeDtypeStruct((heads, 8, 128), f32),
        ],
        compiler_params=pltpu.CompilerParams(vmem_limit_bytes=48 << 20),
        cost_estimate=pl.CostEstimate(
            flops=4 * count * count * width,
            transcendentals=heads * count * count,
            bytes_accessed=8 * count * width,
        ),
    )(q, k, v, docs[:, None], docs[None, :])


def attend_backward(q, k, v, docs, log_total, grad):
    count, width = q.shape
    heads = width // HEAD
    block, whole, doc_q, doc_k, lse = attend_specs(count)
    return pl.pallas_call(
        attend_backward_kernel,
        grid=(heads, count // Q_BLOCK),
        in_specs=[block, whole, whole, doc_q, doc_k, lse, block],
        out_specs=[block, whole, whole],
        out_shape=[jax.ShapeDtypeStruct((count, width), f32)] * 3,
        compiler_params=pltpu.CompilerParams(vmem_limit_bytes=56 << 20),
        cost_estimate=pl.CostEstimate(
            flops=10 * count * count * width,
            transcendentals=heads * count * count,
            bytes_accessed=20 * count * width,
        ),
    )(q, k, v, docs[:, None], docs[None, :], log_total, grad)


MESH = pl.DeviceIdType.MESH
ANY = pl.BlockSpec(memory_space=pl.ANY)
VMEM = pl.BlockSpec(memory_space=pltpu.VMEM)


def ring_peers(axis):
    n, me = lax.axis_size(axis), lax.axis_index(axis)
    return [lax.rem(me + k, n) for k in range(n)], [lax.rem(me + n - k, n) for k in range(n)]


class Greeting:
    def __init__(self):
        self.barrier, self.total = pltpu.get_barrier_semaphore(), 0

    def ring(self, axis):
        to, _ = ring_peers(axis)
        for peer in to[1:]:
            pl.semaphore_signal(
                self.barrier, inc=1, device_id={axis: peer}, device_id_type=MESH
            )
        self.total = self.total + len(to) - 1
        return self

    def line(self):
        line = Line()
        for there, peer in (
            (line.place >= 0, line.partner),
            (line.not_last, line.me + 2),
            (line.not_first, line.me - 2),
        ):

            @pl.when(there)
            def _():
                pl.semaphore_signal(
                    self.barrier, inc=1, device_id={"ctx": peer}, device_id_type=MESH
                )

            self.total = self.total + there.astype(jnp.int32)
        return self

    def wait(self):
        pl.semaphore_wait(self.barrier, self.total)


class Line:
    def __init__(self):
        self.n, self.me = lax.axis_size("ctx") // 2, lax.axis_index("ctx")
        self.place, self.core = lax.div(self.me, 2), lax.rem(self.me, 2)
        self.partner = self.me + 1 - 2 * self.core
        self.not_first, self.not_last = self.place > 0, self.place < self.n - 1


class Direct:
    def __init__(self, axis, source, target, send, recv):
        self.axis, self.source, self.target = axis, source, target
        self.send, self.recv = send, recv
        self.me = lax.axis_index(axis)
        self.to, self.origin = ring_peers(axis)

    def copy(self, k, sender):
        return pltpu.make_async_remote_copy(
            src_ref=self.source(self.to[k]),
            dst_ref=self.target(sender, k),
            send_sem=self.send.at[k],
            recv_sem=self.recv.at[k],
            device_id={self.axis: self.to[k]},
            device_id_type=MESH,
        )

    def start(self):
        for k in range(1, len(self.to)):
            self.copy(k, self.me).start()

    def wait_recv(self):
        for k in range(1, len(self.to)):
            self.copy(k, self.origin[k]).wait_recv()

    def wait_send(self):
        for k in range(1, len(self.to)):
            self.copy(k, self.me).wait_send()


class LineGather:
    def __init__(self, pieces, own_sem, send_r, send_l, send_p, recv_r, recv_l, recv_p):
        self.line, self.pieces, self.own_sem = Line(), pieces, own_sem
        self.send_r, self.send_l, self.send_p = send_r, send_l, send_p
        self.recv_r, self.recv_l, self.recv_p = recv_r, recv_l, recv_p

    def own(self, c):
        source, target = self.pieces[c]
        return pltpu.make_async_copy(source, target(self.line.me), self.own_sem.at[c])

    def copy(self, block, k, c, target_device, send, recv):
        source, target = self.pieces[c]
        return pltpu.make_async_remote_copy(
            src_ref=source if k == 0 else target(block),
            dst_ref=target(block),
            send_sem=send,
            recv_sem=recv,
            device_id={"ctx": target_device},
            device_id_type=MESH,
        )

    def right(self, k, c):
        me = self.line.me
        return self.copy(me - 2 * k, k, c, me + 2, self.send_r.at[k, c], self.recv_r.at[k, c])

    def left(self, k, c):
        me = self.line.me
        return self.copy(me + 2 * k, k, c, me - 2, self.send_l.at[k, c], self.recv_l.at[k, c])

    def across(self, k, c, sign):
        line = self.line
        i = k if sign < 0 else line.n - 1 + k
        return self.copy(
            line.me + sign * 2 * k, k, c, line.partner, self.send_p.at[i, c], self.recv_p.at[i, c]
        )

    def arrived(self, block, c, recv):
        source, target = self.pieces[c]
        pltpu.make_async_remote_copy(
            src_ref=source,
            dst_ref=target(block),
            send_sem=recv,
            recv_sem=recv,
            device_id={"ctx": self.line.partner},
            device_id_type=MESH,
        ).wait_recv()

    def start(self):
        for c in range(len(self.pieces)):
            self.own(c).start()

    def hop(self, k):
        line = self.line
        for c in range(len(self.pieces)):

            @pl.when(line.place >= k)
            def _():
                if k:
                    self.arrived(line.me - 2 * k, c, self.recv_r.at[k - 1, c])

                @pl.when(line.not_last)
                def _():
                    self.right(k, c).start()

                self.across(k, c, -1).start()

            @pl.when(line.place + k <= line.n - 1)
            def _():
                if k:
                    self.arrived(line.me + 2 * k, c, self.recv_l.at[k - 1, c])

                @pl.when(line.not_first)
                def _():
                    self.left(k, c).start()

                if k:
                    self.across(k, c, 1).start()

    def finish(self, skip_own=None):
        line = self.line
        for c in range(len(self.pieces)):
            if c != skip_own:
                self.own(c).wait()
        for k in range(line.n):
            for c in range(len(self.pieces)):

                @pl.when(line.place >= k)
                def _():
                    @pl.when(line.not_last)
                    def _():
                        self.right(k, c).wait_send()

                    self.across(k, c, -1).wait_send()
                    self.arrived(line.partner - 2 * k, c, self.recv_p.at[k, c])

                @pl.when(line.place + k <= line.n - 1)
                def _():
                    @pl.when(line.not_first)
                    def _():
                        self.left(k, c).wait_send()

                    if k:
                        self.across(k, c, 1).wait_send()
                        self.arrived(line.partner + 2 * k, c, self.recv_p.at[line.n - 1 + k, c])


def line_gather_scratch(n, pieces):
    sem = pltpu.SemaphoreType.DMA
    one, two = sem((n, pieces)), sem((2 * n - 1, pieces))
    return [sem((pieces,)), one, one, two, one, one, two]


class LineReduce:
    def __init__(
        self, chunks, x, o, pair, from_left, from_right, send_p, recv_p, send_s, recv_r, recv_l
    ):
        self.line, self.chunks = Line(), chunks
        self.x, self.o, self.pair, self.out = x, o, pair, pair
        self.from_left, self.from_right = from_left, from_right
        self.send_p, self.recv_p, self.send_s = send_p, recv_p, send_s
        self.recv_r, self.recv_l = recv_r, recv_l
        self.order = []
        for j in range(self.line.n):
            self.order += [p for p in (self.line.n - 1 - j, j) if p not in self.order]

    def at(self, c):
        rows = self.x.shape[1] // self.chunks
        return pl.ds(c * rows, rows)

    def across(self, p, c):
        line, at = self.line, self.at(c)
        return pltpu.make_async_remote_copy(
            src_ref=self.x.at[2 * p + 1 - line.core, at],
            dst_ref=self.pair.at[p, at],
            send_sem=self.send_p.at[p, c],
            recv_sem=self.recv_p.at[p, c],
            device_id={"ctx": line.partner},
            device_id_type=MESH,
        )

    def along(self, p, c, step, buffer, recv):
        at = self.at(c)
        return pltpu.make_async_remote_copy(
            src_ref=self.out.at[p, at],
            dst_ref=buffer.at[p, at],
            send_sem=self.send_s.at[p, c],
            recv_sem=recv.at[p, c],
            device_id={"ctx": self.line.me + step},
            device_id_type=MESH,
        )

    def right(self, p, c):
        return self.along(p, c, 2, self.from_left, self.recv_r)

    def left(self, p, c):
        return self.along(p, c, -2, self.from_right, self.recv_l)

    def start(self):
        for p in self.order:
            for c in range(self.chunks):
                self.across(p, c).start()

    def both(self, p, c):
        at = self.at(c)
        return self.x[2 * p + self.line.core, at].astype(f32) + self.pair[p, at].astype(f32)

    def pass_on(self):
        line = self.line
        for p in self.order:
            for c in range(self.chunks):
                at = self.at(c)
                self.across(p, c).wait_recv()

                @pl.when(line.place < p)
                def _():
                    @pl.when(line.not_first)
                    def _():
                        self.right(p, c).wait_recv()
                        total = self.both(p, c) + self.from_left[p, at].astype(f32)
                        self.out[p, at] = total.astype(bf16)

                    @pl.when(line.place == 0)
                    def _():
                        self.out[p, at] = self.both(p, c).astype(bf16)

                    self.right(p, c).start()

                @pl.when(line.place > p)
                def _():
                    @pl.when(line.not_last)
                    def _():
                        self.left(p, c).wait_recv()
                        total = self.both(p, c) + self.from_right[p, at].astype(f32)
                        self.out[p, at] = total.astype(bf16)

                    @pl.when(line.place == line.n - 1)
                    def _():
                        self.out[p, at] = self.both(p, c).astype(bf16)

                    self.left(p, c).start()

    def finish(self):
        line = self.line
        for p in range(line.n):
            for c in range(self.chunks):
                at = self.at(c)

                @pl.when(line.place == p)
                def _():
                    self.o[at] = self.both(p, c)
                    if p > 0:
                        self.right(p, c).wait_recv()
                        self.o[at] += self.from_left[p, at].astype(f32)
                    if p < line.n - 1:
                        self.left(p, c).wait_recv()
                        self.o[at] += self.from_right[p, at].astype(f32)

        for p in range(line.n):
            for c in range(self.chunks):
                self.across(p, c).wait_send()

                @pl.when(line.place < p)
                def _():
                    self.right(p, c).wait_send()

                @pl.when(line.place > p)
                def _():
                    self.left(p, c).wait_send()


def add_up(x, buf, o, me):
    rows = x.shape[1]
    step = 8 if rows % 32 else 32

    @pl.loop(0, rows // step)
    def _(j):
        at = pl.ds(pl.multiple_of(j * step, step), step)
        total = x[me, at].astype(f32)
        for k in range(buf.shape[0]):
            total = total + buf[k, at].astype(f32)
        o[at] = total.astype(o.dtype)


def block_of(ref):
    return lambda device: ref.at[device]


def block_from(ref):
    return lambda device, k: ref.at[device]


def whole_of(ref):
    return lambda device: ref


def buffer_of(ref):
    return lambda device, k: ref.at[k - 1]


def row_pieces(source, target, chunks):
    rows = source.shape[0] // chunks
    return [
        (source.at[pl.ds(c * rows, rows)], lambda b, c=c: target.at[b, pl.ds(c * rows, rows)])
        for c in range(chunks)
    ]


def start_kernel(
    x, w, w_query, w_key, w_value, small, cot, x_all, w_all, heads_all, small_all, cot_all,
    heads_mid, small_mid, own_sem, ex_send, ex_recv, sp_send, sp_recv, w_send, w_recv, f_send,
    f_recv, *line_sems,
):
    shard, ctx = lax.axis_index("shard"), lax.axis_index("ctx")
    n_ctx = lax.axis_size("ctx")
    cols = w_query.shape[1] // n_ctx
    Greeting().ring("ctx").ring("shard").wait()

    def columns(ref):
        return lambda d: ref.at[:, pl.ds(pl.multiple_of(d * cols, HEAD), cols)]

    def place(i):
        if i == 3:
            return block_from(small_mid)
        return lambda d, k: heads_mid.at[d, :, i * cols : (i + 1) * cols]

    sources = [columns(w_query), columns(w_key), columns(w_value), whole_of(small)]
    swaps = [
        Direct("ctx", source, place(i), ex_send.at[i], ex_recv.at[i])
        for i, source in enumerate(sources)
    ]

    def by_shard(ref):
        return lambda d, k: ref.at[:, d]

    spreads = [
        Direct("shard", whole_of(heads_mid), by_shard(heads_all), sp_send.at[0], sp_recv.at[0]),
        Direct("shard", whole_of(small_mid), by_shard(small_all), sp_send.at[1], sp_recv.at[1]),
    ]
    other = Direct("shard", whole_of(cot), block_from(cot_all), sp_send.at[2], sp_recv.at[2])
    rows_w = LineGather([(w, lambda b: w_all.at[b, shard])], *line_sems[:7])
    rows_x = LineGather(row_pieces(x, x_all, LINE_CHUNKS), *line_sems[7:])
    at = rows_x.line
    own = [
        pltpu.make_async_copy(source(ctx), place(i)(ctx, 0), own_sem.at[i])
        for i, source in enumerate(sources)
    ]
    later = [
        pltpu.make_async_copy(heads_mid, heads_all.at[:, shard], own_sem.at[4]),
        pltpu.make_async_copy(small_mid, small_all.at[:, shard], own_sem.at[5]),
        pltpu.make_async_copy(cot, cot_all.at[shard], own_sem.at[6]),
    ]
    other.start()
    for swap in swaps:
        swap.start()
    for copy in own:
        copy.start()
    rows_w.start()
    rows_w.hop(0)
    rows_x.start()
    rows_x.hop(0)
    for swap in swaps:
        swap.wait_recv()
    for copy in own:
        copy.wait()
    for one in (*spreads, *later):
        one.start()
    for k in range(1, at.n):
        rows_w.hop(k)

    to, origin = ring_peers("shard")

    def row(k, p, sender):
        block = 2 * p + at.core
        return pltpu.make_async_remote_copy(
            src_ref=w_all.at[block, shard],
            dst_ref=w_all.at[block, sender],
            send_sem=w_send.at[k, p],
            recv_sem=w_recv.at[k, p],
            device_id={"shard": to[k]},
            device_id_type=MESH,
        )

    def forward(k, p, core):
        block = w_all.at[2 * p + core, origin[k]]
        return pltpu.make_async_remote_copy(
            src_ref=block,
            dst_ref=block,
            send_sem=f_send.at[k, p],
            recv_sem=f_recv.at[k, p],
            device_id={"ctx": at.partner},
            device_id_type=MESH,
        )

    some = [(k, p) for k in range(1, len(to)) for p in range(at.n)]
    rows_w.own(0).wait()
    for k, p in some:
        row(k, p, shard).start()
    for k in range(1, at.n):
        rows_x.hop(k)
    for k, p in some:
        row(k, p, origin[k]).wait_recv()
        forward(k, p, at.core).start()
    rows_w.finish(skip_own=0)
    rows_x.finish()
    for k, p in some:
        row(k, p, shard).wait_send()
        forward(k, p, at.core).wait_send()
        forward(k, p, 1 - at.core).wait_recv()
    for direct in (other, *spreads):
        direct.wait_recv()
    for direct in (other, *swaps, *spreads):
        direct.wait_send()
    for copy in later:
        copy.wait()


def exchange_kernel(to_rows, *refs):
    more = len(refs) > 5
    if more:
        x, cot, o, cot_all, own_sem, send, recv, cot_send, cot_recv = refs
    else:
        x, o, own_sem, send, recv = refs
    n, me = lax.axis_size("ctx"), lax.axis_index("ctx")
    cols, rows = (x.shape[1] // n, x.shape[0]) if to_rows else (x.shape[1], o.shape[0])

    def row_block(ref):
        return lambda d, k=0: ref.at[pl.ds(pl.multiple_of(d * rows, rows), rows)]

    def column_block(ref):
        return lambda d, k=0: ref.at[:, pl.ds(pl.multiple_of(d * cols, cols), cols)]

    source, target = (
        (column_block(x), row_block(o)) if to_rows else (row_block(x), column_block(o))
    )
    greeting = Greeting().ring("ctx")
    if more:
        greeting.ring("shard")
    greeting.wait()
    all_of = [Direct("ctx", source, target, send, recv)]
    own = [pltpu.make_async_copy(source(me), target(me), own_sem.at[0])]
    if more:
        all_of.append(Direct("shard", whole_of(cot), block_from(cot_all), cot_send, cot_recv))
        own.append(
            pltpu.make_async_copy(cot, cot_all.at[lax.axis_index("shard")], own_sem.at[1])
        )
    for one in (*all_of, *own):
        one.start()
    for copy in own:
        copy.wait()
    for direct in all_of:
        direct.wait_recv()
        direct.wait_send()


def gather_kernel(axis, count, *refs):
    ins, outs = refs[:count], refs[count : 2 * count]
    own_sem, send, recv = refs[2 * count :]
    me = lax.axis_index(axis)
    Greeting().ring(axis).wait()
    all_of = [
        Direct(axis, whole_of(ins[i]), block_from(outs[i]), send.at[i], recv.at[i])
        for i in range(count)
    ]
    own = [pltpu.make_async_copy(ins[i], outs[i].at[me], own_sem.at[i]) for i in range(count)]
    for direct in all_of:
        direct.start()
    for copy in own:
        copy.start()
    for copy in own:
        copy.wait()
    for direct in all_of:
        direct.wait_recv()
        direct.wait_send()


def reduce_kernel(axis, count, *refs):
    ins, outs, bufs = refs[:count], refs[count : 2 * count], refs[2 * count : 3 * count]
    send, recv = refs[3 * count :]
    Greeting().ring(axis).wait()
    all_of = [
        Direct(axis, block_of(ins[i]), buffer_of(bufs[i]), send.at[i], recv.at[i])
        for i in range(count)
    ]
    for direct in all_of:
        direct.start()
    for i, direct in enumerate(all_of):
        direct.wait_recv()
        add_up(ins[i], bufs[i], outs[i], direct.me)
        direct.wait_send()


def many_sum_kernel(axis, x, o, buf, send, recv):
    Greeting().ring(axis).wait()
    direct = Direct(axis, whole_of(x), buffer_of(buf), send, recv)
    direct.start()
    direct.wait_recv()
    total = x[...]
    for k in range(buf.shape[0]):
        total = total + buf[k]
    o[...] = total
    direct.wait_send()


def end_kernel(
    x, wide, out, y, x_sum, wide_all, out_sum, y_sum, wide_buf, out_buf, y_buf, wide_sum,
    own_sem, wide_send, wide_recv, out_send, out_recv, y_send, y_recv, swap_send, swap_recv,
    *line_refs,
):
    ctx = lax.axis_index("ctx")
    Greeting().ring("ctx").ring("shard").wait()
    wides = Direct("shard", block_of(wide), buffer_of(wide_buf), wide_send, wide_recv)
    outs = Direct("shard", block_of(out), buffer_of(out_buf), out_send, out_recv)
    swap = Direct("ctx", block_of(wide_sum), block_from(wide_all), swap_send, swap_recv)
    line = LineReduce(LINE_CHUNKS, x, x_sum, *line_refs)
    returns = Direct("shard", block_of(y), buffer_of(y_buf), y_send, y_recv)
    line.start()
    wides.start()
    outs.start()
    returns.start()
    line.pass_on()
    wides.wait_recv()
    for b in range(lax.axis_size("ctx")):
        rows = wide_sum.shape[1]
        total = wide[wides.me, b * rows : (b + 1) * rows].astype(f32)
        for k in range(wide_buf.shape[0]):
            total = total + wide_buf[k, b * rows : (b + 1) * rows].astype(f32)
        wide_sum[b] = total.astype(bf16)
    swap.start()
    own = pltpu.make_async_copy(wide_sum.at[ctx], wide_all.at[ctx], own_sem)
    own.start()
    outs.wait_recv()
    add_up(out, out_buf, out_sum, outs.me)
    line.finish()
    returns.wait_recv()
    add_up(y, y_buf, y_sum, returns.me)
    own.wait()
    swap.wait_recv()
    for direct in (swap, wides, outs, returns):
        direct.wait_send()


def line_reduce_kernel(count, *refs):
    ins, outs, rest = refs[:count], refs[count : 2 * count], refs[2 * count :]
    Greeting().line().wait()
    all_of = [
        LineReduce(LINE_CHUNKS, ins[i], outs[i], *rest[8 * i : 8 * i + 8]) for i in range(count)
    ]
    for one in all_of:
        one.start()
    for one in all_of:
        one.pass_on()
    for one in all_of:
        one.finish()


def line_reduce_scratch(x):
    n_ctx, rows, width = x.shape
    n = n_ctx // 2
    return [pltpu.VMEM((n, rows, width), bf16)] * 3 + [
        pltpu.SemaphoreType.DMA((n, LINE_CHUNKS))
    ] * 5


def line_reduce(collective_id, *arrays):
    return pl.pallas_call(
        functools.partial(line_reduce_kernel, len(arrays)),
        out_shape=[jax.ShapeDtypeStruct(x.shape[1:], f32) for x in arrays],
        in_specs=[VMEM] * len(arrays),
        out_specs=[VMEM] * len(arrays),
        scratch_shapes=sum((line_reduce_scratch(x) for x in arrays), []),
        compiler_params=remote_params(collective_id, 48),
    )(*arrays)


def remote_params(collective_id, megabytes):
    return pltpu.CompilerParams(
        collective_id=collective_id, has_side_effects=True, vmem_limit_bytes=megabytes << 20
    )


LINE_CHUNKS = 4


def start_call(collective_id, x, w, w_query, w_key, w_value, small, cot):
    n_ctx, n_shard = lax.axis_size("ctx"), lax.axis_size("shard")
    n = n_ctx // 2
    heads = (w.shape[0], 3 * w.shape[1] // n_ctx)
    sem = pltpu.SemaphoreType.DMA
    return pl.pallas_call(
        start_kernel,
        out_shape=[
            jax.ShapeDtypeStruct((n_ctx, *x.shape), bf16),
            jax.ShapeDtypeStruct((n_ctx, n_shard, *w.shape), bf16),
            jax.ShapeDtypeStruct((n_ctx, n_shard, *heads), bf16),
            jax.ShapeDtypeStruct((n_ctx, n_shard, *small.shape), bf16),
            jax.ShapeDtypeStruct((n_shard, *cot.shape), bf16),
        ],
        in_specs=[ANY] * 7,
        out_specs=[ANY] * 5,
        scratch_shapes=[
            pltpu.VMEM((n_ctx, *heads), bf16),
            pltpu.VMEM((n_ctx, *small.shape), bf16),
            sem((7,)),
            sem((4, n_ctx)),
            sem((4, n_ctx)),
        ]
        + [sem((3, n_shard))] * 2
        + [sem((n_shard, n))] * 4
        + line_gather_scratch(n, 1)
        + line_gather_scratch(n, LINE_CHUNKS),
        compiler_params=remote_params(collective_id, 8),
    )(x, w, w_query, w_key, w_value, small, cot)


def exchange(collective_id, x, to_rows, *more):
    n, n_shard = lax.axis_size("ctx"), lax.axis_size("shard")
    shape = (x.shape[0] * n, x.shape[1] // n) if to_rows else (x.shape[0] // n, x.shape[1] * n)
    sem = pltpu.SemaphoreType.DMA
    return pl.pallas_call(
        functools.partial(exchange_kernel, to_rows),
        out_shape=[jax.ShapeDtypeStruct(shape, x.dtype)]
        + [jax.ShapeDtypeStruct((n_shard, *u.shape), u.dtype) for u in more],
        in_specs=[ANY] * (1 + len(more)),
        out_specs=[ANY] * (1 + len(more)),
        scratch_shapes=[sem((2,)), sem((n,)), sem((n,))] + [sem((n_shard,))] * (2 * len(more)),
        compiler_params=remote_params(collective_id, 8),
    )(x, *more)


def gather(axis, collective_id, *arrays):
    count, n = len(arrays), lax.axis_size(axis)
    sem = pltpu.SemaphoreType.DMA
    return pl.pallas_call(
        functools.partial(gather_kernel, axis, count),
        out_shape=[jax.ShapeDtypeStruct((n, *a.shape), a.dtype) for a in arrays],
        in_specs=[ANY] * count,
        out_specs=[ANY] * count,
        scratch_shapes=[sem((count,)), sem((count, n)), sem((count, n))],
        compiler_params=remote_params(collective_id, 8),
    )(*arrays)


def reduce(axis, collective_id, *arrays):
    count, n = len(arrays), lax.axis_size(axis)
    sem = pltpu.SemaphoreType.DMA
    return pl.pallas_call(
        functools.partial(reduce_kernel, axis, count),
        out_shape=[jax.ShapeDtypeStruct(a.shape[1:], f32) for a in arrays],
        in_specs=[VMEM] * count,
        out_specs=[VMEM] * count,
        scratch_shapes=[pltpu.VMEM((n - 1, *a.shape[1:]), a.dtype) for a in arrays]
        + [sem((count, n)), sem((count, n))],
        compiler_params=remote_params(collective_id, 32),
    )(*arrays)


def many_sum(axis, collective_id, x):
    n = lax.axis_size(axis)
    sem = pltpu.SemaphoreType.DMA
    return pl.pallas_call(
        functools.partial(many_sum_kernel, axis),
        out_shape=jax.ShapeDtypeStruct(x.shape, x.dtype),
        in_specs=[VMEM],
        out_specs=VMEM,
        scratch_shapes=[pltpu.VMEM((n - 1, *x.shape), x.dtype), sem((n,)), sem((n,))],
        compiler_params=remote_params(collective_id, 8),
    )(x)


def end_call(collective_id, x, wide, out, y):
    n_ctx, rows, width = x.shape
    n_shard = lax.axis_size("shard")
    n = n_ctx // 2
    wide_rows, wide_cols = wide.shape[1] // n_ctx, wide.shape[2]
    sem = pltpu.SemaphoreType.DMA
    return pl.pallas_call(
        end_kernel,
        out_shape=[
            jax.ShapeDtypeStruct((rows, width), f32),
            jax.ShapeDtypeStruct((n_ctx, wide_rows, wide_cols), bf16),
            jax.ShapeDtypeStruct(out.shape[1:], f32),
            jax.ShapeDtypeStruct(y.shape[1:], f32),
        ],
        in_specs=[VMEM] * 4,
        out_specs=[VMEM] * 4,
        scratch_shapes=[
            pltpu.VMEM((n_shard - 1, *wide.shape[1:]), bf16),
            pltpu.VMEM((n_shard - 1, *out.shape[1:]), bf16),
            pltpu.VMEM((n_shard - 1, *y.shape[1:]), bf16),
            pltpu.VMEM((n_ctx, wide_rows, wide_cols), bf16),
            sem,
        ]
        + [sem((n_shard,))] * 6
        + [sem((n_ctx,))] * 2
        + [pltpu.VMEM((n, rows, width), bf16)] * 3
        + [sem((n, LINE_CHUNKS))] * 5,
        compiler_params=remote_params(collective_id, 56),
    )(x, wide, out, y)


def per_device(
    tokens,
    doc_ids,
    routes,
    attn_gain,
    w_query,
    w_key,
    w_value,
    query_gain,
    key_gain,
    w_out,
    ffn_gain,
    w_router,
    w_gate,
    w_up,
    w_down,
    clip_threshold,
    cotangent,
):
    both = ("ctx", "shard")
    n_ctx, n_shard = lax.axis_size("ctx"), lax.axis_size("shard")
    ctx, shard = lax.axis_index("ctx"), lax.axis_index("shard")
    x_own = tokens[0]
    rows, width = x_own.shape
    part = w_query.shape[0]
    cols = width // n_ctx
    heads = cols // HEAD
    count = rows * n_ctx
    local = w_gate.shape[0]
    experts = local * n_shard

    top = routes.shape[2]
    spare = jnp.zeros((part, LANES - 4 - experts - rows // part * (1 + top)), bf16)
    small = jnp.concatenate(
        [
            jnp.stack([attn_gain, query_gain, key_gain, ffn_gain], axis=1),
            w_router,
            doc_ids.reshape(part, rows // part).astype(bf16),
            routes.reshape(part, rows // part * top).astype(bf16),
            spare,
        ],
        axis=1,
    )
    grad_own = cotangent[0]
    x_all, out_w, weights, small_all, grad_all = start_call(
        1, x_own, w_out, w_query, w_key, w_value, small, grad_own
    )
    x_all = x_all.reshape(count, width)
    out_w = out_w.reshape(width, width)
    weights = weights.reshape(width, 3 * cols)
    gains = small_all[..., : 4 + experts].reshape(width, 4 + experts)
    gain_attn, gain_query, gain_key, gain_ffn = (gains[:, i].astype(f32) for i in range(4))
    router_w = gains[:, 4:]
    gain_query = lax.dynamic_slice_in_dim(gain_query, ctx * cols, cols)
    gain_key = lax.dynamic_slice_in_dim(gain_key, ctx * cols, cols)
    tail = small_all[..., 4 + experts :].astype(jnp.int32)
    docs = lax.dynamic_index_in_dim(tail[..., : rows // part], shard, 1, False).reshape(count)
    grad_all = grad_all.reshape(n_shard * rows, width)
    routes_all = lax.dynamic_index_in_dim(
        tail[..., rows // part : rows // part * (1 + top)], ctx, 0, False
    ).reshape(n_shard * rows, top)

    ff = w_gate.shape[2]
    own_w = jnp.concatenate([w_gate, w_up, w_down.transpose(0, 2, 1)], axis=2)
    first_w = own_w[0]
    x_all, own_w = lax.optimization_barrier((x_all, own_w))
    own_w = [first_w] + [own_w[e] for e in range(1, local)]
    expert_w = [lax.all_gather(u, "ctx", axis=0, tiled=True) for u in own_w]

    x_wide = x_all.astype(f32)
    inverse_one = inverse_rms(x_wide)
    hidden_one = (x_wide * inverse_one * gain_attn).astype(bf16)
    linear = dot(hidden_one, weights)
    query_lin, key_lin = linear[:, :cols], linear[:, cols : 2 * cols]
    value = linear[:, 2 * cols :].astype(bf16)
    squares = jnp.stack(
        [jnp.sum(query_lin * query_lin, axis=1), jnp.sum(key_lin * key_lin, axis=1)]
    )
    squares = many_sum("ctx", 6, squares)
    inverse_qk = lax.rsqrt(squares / width + norm_eps)
    inverse_q, inverse_k = inverse_qk[0][:, None], inverse_qk[1][:, None]
    cosine, sine = rope_tables(count)
    query_n, key_n = query_lin * inverse_q, key_lin * inverse_k
    query = rotate(query_n * gain_query, cosine, sine).astype(bf16)
    key = rotate(key_n * gain_key, cosine, sine).astype(bf16)
    mixed, log_total, peaks = attend_forward(query, key, value, docs)
    x_f = x_own.astype(f32)
    (mixed_own,) = exchange(2, mixed, False)
    after = x_f + dot(mixed_own, out_w)
    inverse_two = inverse_rms(after)
    normed_two = after * inverse_two
    hidden_two = (normed_two * gain_ffn).astype(bf16)

    hidden_all, peaks = gather("shard", 3, hidden_two, peaks)
    hidden_all = hidden_all.reshape(n_shard * rows, width)
    peaks = jnp.max(peaks, axis=0)[:, 0, 0]
    logits = dot(hidden_all, router_w)
    named = jnp.any(routes_all[:, :, None] == jnp.arange(experts)[None, None, :], axis=1)
    probs = jax.nn.softmax(logits, axis=1)
    selected = jnp.where(named, probs, 0.0)
    selected_sum = jnp.sum(selected, axis=1, keepdims=True)
    gates = selected / selected_sum
    gates_own = lax.dynamic_slice_in_dim(gates, shard * local, local, 1)
    named_own = lax.dynamic_slice_in_dim(named, shard * local, local, 1)
    moe_part = jnp.zeros(hidden_all.shape, f32)
    back_part = jnp.zeros(hidden_all.shape, f32)

    grad_wide = grad_all.astype(f32)
    def to_owners(parts):
        return [lax.psum_scatter(u, "ctx", scatter_dimension=0, tiled=True) for u in parts]

    grad_gates, expert_grads = [], []
    for e in range(local):
        wide, down = expert_w[e][:, : 2 * ff], expert_w[e][:, 2 * ff :]
        gate_col = gates_own[:, e : e + 1]
        hidden = dot(hidden_all, wide)
        gate_h, up_h = hidden[:, :ff], hidden[:, ff:]
        sig = jax.nn.sigmoid(gate_h)
        silu = gate_h * sig
        act = (silu * up_h).astype(bf16)
        result = contract_cols(act, down).astype(bf16).astype(f32)
        moe_part = moe_part + gate_col * result
        along = jnp.sum(grad_wide * result, axis=1)
        grad_gates.append(jnp.where(named_own[:, e], along, 0.0))
        grad_y = (gate_col * grad_wide).astype(bf16)
        grad_act = dot(grad_y, down)
        grad_h = jnp.concatenate(
            [grad_act * up_h * sig * (1.0 + gate_h * (1.0 - sig)), grad_act * silu], axis=1
        ).astype(bf16)
        back_part = back_part + contract_cols(grad_h, wide).astype(bf16).astype(f32)
        grad_w = [
            contract_rows(hidden_all, grad_h).astype(bf16),
            contract_rows(grad_y, act).astype(bf16),
        ]
        hidden_all, back_part, grad_w = lax.optimization_barrier((hidden_all, back_part, grad_w))
        expert_grads.append(grad_w)
    early = local // 2
    expert_grads[:early] = [to_owners(grad_w) for grad_w in expert_grads[:early]]
    slots = jnp.stack(grad_gates).reshape(local, n_shard, rows).transpose(1, 0, 2)
    grad_gates = lax.dynamic_update_slice_in_dim(
        jnp.zeros((n_shard, experts, rows), f32), slots, shard * local, 1
    )
    back_sum, grad_gates = reduce(
        "shard", 4, back_part.astype(bf16).reshape(n_shard, rows, width), grad_gates
    )
    grad_gates = grad_gates.T

    def own_rows(u):
        return lax.dynamic_slice_in_dim(u, shard * rows, rows, 0)

    gates_t, probs_t, named_t, sum_t = map(own_rows, (gates, probs, named, selected_sum))
    grad_selected = (
        grad_gates - jnp.sum(gates_t * grad_gates, axis=1, keepdims=True)
    ) / sum_t
    grad_probs = jnp.where(named_t, grad_selected, 0.0)
    grad_logits = (
        probs_t * (grad_probs - jnp.sum(probs_t * grad_probs, axis=1, keepdims=True))
    ).astype(bf16)
    grad_router = contract_rows(hidden_two, grad_logits)
    grad_hidden = back_sum + contract_cols(grad_logits, router_w)
    grad_gain_ffn = jnp.sum(grad_hidden * normed_two, axis=0)
    scaled_two = grad_hidden * gain_ffn
    grad_after = grad_own.astype(f32) + inverse_two * (
        scaled_two - normed_two * jnp.mean(scaled_two * normed_two, axis=1, keepdims=True)
    )

    grad_attn_own = grad_after.astype(bf16)
    to_gather, expert_grads[0] = lax.optimization_barrier((grad_attn_own, expert_grads[0]))
    grad_attn = lax.all_gather(to_gather, "ctx", axis=0, tiled=True)
    (grad_mixed,) = exchange(5, contract_cols(grad_attn_own, out_w).astype(bf16), True)
    last_grad = expert_grads.pop()
    grad_mixed, late = lax.optimization_barrier((grad_mixed, expert_grads[early:]))
    expert_grads[early:] = [to_owners(grad_w) for grad_w in late]
    grad_query_rot, grad_key_rot, grad_value = attend_backward(
        query, key, value, docs, log_total, grad_mixed
    )
    grad_query_n = rotate(grad_query_rot, cosine, -sine)
    grad_key_n = rotate(grad_key_rot, cosine, -sine)
    grad_gain_query = jnp.sum(grad_query_n * query_n, axis=0)
    grad_gain_key = jnp.sum(grad_key_n * key_n, axis=0)
    scaled_q, scaled_k = grad_query_n * gain_query, grad_key_n * gain_key
    peak_row = lax.dynamic_update_slice_in_dim(jnp.zeros((count,), f32), peaks, ctx * heads, 0)
    inner = jnp.stack(
        [jnp.sum(scaled_q * query_n, axis=1), jnp.sum(scaled_k * key_n, axis=1), peak_row]
    )
    inner = many_sum("ctx", 7, inner)
    grad_out_w = contract_rows(mixed, grad_attn)
    peak_all = inner[2, :HEADS]
    inner = inner / width
    grad_linear = jnp.concatenate(
        [
            inverse_q * (scaled_q - query_n * inner[0][:, None]),
            inverse_k * (scaled_k - key_n * inner[1][:, None]),
            grad_value,
        ],
        axis=1,
    ).astype(bf16)
    grad_weights = contract_rows(hidden_one, grad_linear)
    hidden_part = contract_cols(grad_linear, weights)
    grad_gain_attn = jnp.sum(hidden_part * (x_wide * inverse_one), axis=0)
    grad_small = jnp.concatenate(
        [jnp.stack([grad_gain_attn, grad_gain_ffn], axis=1), grad_router], axis=1
    )
    grad_small = jnp.pad(grad_small, ((0, 0), (0, LANES - 2 - experts)))
    grad_weights = (
        jnp.concatenate([grad_weights, grad_small], axis=1)
        .astype(bf16)
        .reshape(n_ctx, n_shard, part, 3 * cols + LANES)
        .transpose(1, 0, 2, 3)
        .reshape(n_shard, n_ctx * part, 3 * cols + LANES)
    )
    grad_gain_qk = jnp.pad(
        jnp.stack([grad_gain_query, grad_gain_key], axis=1), ((0, 0), (0, LANES - 2))
    )
    grad_out_w = (
        jnp.concatenate([grad_out_w, grad_gain_qk], axis=1)
        .astype(bf16)
        .reshape(n_shard, part, width + LANES)
    )
    hidden_part = hidden_part.astype(bf16).reshape(n_ctx, rows, width)
    grad_hidden_one, grad_weights, grad_out_w, moe_sum = end_call(
        8,
        hidden_part,
        grad_weights,
        grad_out_w,
        moe_part.astype(bf16).reshape(n_shard, rows, width),
    )
    output = (after + moe_sum).astype(bf16)
    grad_hidden_one, last_grad = lax.optimization_barrier((grad_hidden_one, last_grad))
    last_grad = line_reduce(9, *(u.reshape(n_ctx, width // n_ctx, -1) for u in last_grad))
    last_grad, expert_grads = lax.optimization_barrier((last_grad, expert_grads))
    expert_grads = [[u.astype(f32) for u in sums] for sums in expert_grads] + [last_grad]
    grad_weights = grad_weights.astype(f32)
    grad_small = jnp.sum(grad_weights[..., 3 * cols :], axis=0)
    grad_weights = (
        grad_weights[..., : 3 * cols]
        .reshape(n_ctx, part, 3, cols)
        .transpose(2, 1, 0, 3)
        .reshape(3, part, width)
    )
    inverse_own = inverse_rms(x_f)
    normed_own = x_f * inverse_own
    scaled_one = grad_hidden_one * gain_attn
    grad_inputs = grad_after + inverse_own * (
        scaled_one - normed_own * jnp.mean(scaled_one * normed_own, axis=1, keepdims=True)
    )

    wide_grads = jnp.stack([u for u, _ in expert_grads])
    down_grads = jnp.stack([u for _, u in expert_grads])
    factors = jnp.sqrt(clip_threshold / jnp.maximum(peak_all, clip_threshold))
    col_scale = jnp.repeat(factors, HEAD)
    query_clipped = (w_query.astype(f32) * col_scale[None, :]).astype(bf16)
    key_clipped = (w_key.astype(f32) * col_scale[None, :]).astype(bf16)
    return (
        output[None],
        grad_inputs[None],
        grad_small[:, 0],
        grad_weights[0],
        grad_weights[1],
        grad_weights[2],
        grad_out_w[:, width],
        grad_out_w[:, width + 1],
        grad_out_w[:, :width],
        grad_small[:, 1],
        grad_small[:, 2 : 2 + experts],
        wide_grads[..., :ff],
        wide_grads[..., ff:],
        down_grads.transpose(0, 2, 1),
        query_clipped,
        key_clipped,
        factors,
    )


def solution(mesh):
    both = ("ctx", "shard")
    return jax.shard_map(
        per_device,
        mesh=mesh,
        in_specs=(
            P("shard", "ctx", None),
            P("shard", "ctx"),
            P("shard", "ctx", None),
            P(both),
            P(both, None),
            P(both, None),
            P(both, None),
            P(both),
            P(both),
            P(both, None),
            P(both),
            P(both, None),
            P("shard", "ctx", None),
            P("shard", "ctx", None),
            P("shard", None, "ctx"),
            P(),
            P("shard", "ctx", None),
        ),
        out_specs=(
            P("shard", "ctx", None),
            P("shard", "ctx", None),
            P(both),
            P(both, None),
            P(both, None),
            P(both, None),
            P(both),
            P(both),
            P(both, None),
            P(both),
            P(both, None),
            P("shard", "ctx", None),
            P("shard", "ctx", None),
            P("shard", None, "ctx"),
            P(both, None),
            P(both, None),
            P(),
        ),
        check_vma=False,
    )
```

```python
import functools

import jax
import jax.numpy as jnp
from jax import lax
from jax.experimental import pallas as pl
from jax.experimental.pallas import tpu as pltpu
from jax.sharding import PartitionSpec as P

HEADS = 16
HEAD = 128
SCALE = HEAD ** (-0.5)
Q_BLOCK = 256
LANES = 128

norm_eps = 1e-06
rope_base = 10000.0
f32 = jnp.float32
bf16 = jnp.bfloat16


def dot(a, b):
    return jnp.dot(a, b, preferred_element_type=f32)


def contract_rows(a, b):
    return lax.dot_general(a, b, (((0,), (0,)), ((), ())), preferred_element_type=f32)


def contract_cols(a, b):
    return lax.dot_general(a, b, (((1,), (1,)), ((), ())), preferred_element_type=f32)


def inverse_rms(values):
    return lax.rsqrt(jnp.mean(values * values, axis=-1, keepdims=True) + norm_eps)


def rope_tables(count):
    half = HEAD // 2
    freq = rope_base ** (-jnp.arange(half).astype(f32) / half)
    angles = jnp.arange(count).astype(f32)[:, None] * freq[None, :]
    return jnp.cos(angles), jnp.sin(angles)


def rotate(values, cosine, sine):
    parts = []
    for col in range(0, values.shape[1], HEAD):
        a = values[:, col : col + HEAD // 2]
        b = values[:, col + HEAD // 2 : col + HEAD]
        parts += [a * cosine - b * sine, b * cosine + a * sine]
    return jnp.concatenate(parts, axis=1)


def attend_forward_kernel(q_ref, k_ref, v_ref, doc_q_ref, doc_k_ref, o_ref, lse_ref, peak_ref):
    s = SCALE * contract_cols(q_ref[...], k_ref[...])
    s = jnp.where(doc_q_ref[...] == doc_k_ref[...], s, -1e30)
    top = jnp.max(s, axis=1, keepdims=True)
    e = jnp.exp(s - top)
    total = jnp.sum(e, axis=1, keepdims=True)
    p = (e * (1.0 / total)).astype(bf16)
    o_ref[...] = dot(p, v_ref[...]).astype(bf16)
    lse_ref[0] = top + jnp.log(total)
    peak = jnp.broadcast_to(jnp.max(top, axis=0, keepdims=True), peak_ref.shape[1:])

    @pl.when(pl.program_id(1) == 0)
    def _():
        peak_ref[0] = peak

    @pl.when(pl.program_id(1) > 0)
    def _():
        peak_ref[0] = jnp.maximum(peak_ref[0], peak)


def attend_backward_kernel(
    q_ref, k_ref, v_ref, doc_q_ref, doc_k_ref, lse_ref, do_ref, dq_ref, dk_ref, dv_ref
):
    q, k, v, do = q_ref[...], k_ref[...], v_ref[...], do_ref[...]
    s = SCALE * contract_cols(q, k)
    p = jnp.where(doc_q_ref[...] == doc_k_ref[...], jnp.exp(s - lse_ref[0]), 0.0)
    dp = contract_cols(do, v)
    inner = jnp.sum(p * dp, axis=1, keepdims=True)
    ds = (p * (dp - inner)).astype(bf16)
    dq_ref[...] = SCALE * dot(ds, k)
    dk = SCALE * contract_rows(ds, q)
    dv = contract_rows(p.astype(bf16), do)

    @pl.when(pl.program_id(1) == 0)
    def _():
        dk_ref[...] = dk
        dv_ref[...] = dv

    @pl.when(pl.program_id(1) > 0)
    def _():
        dk_ref[...] += dk
        dv_ref[...] += dv


def attend_specs(count):
    block = pl.BlockSpec((Q_BLOCK, HEAD), lambda h, i: (i, h))
    whole = pl.BlockSpec((count, HEAD), lambda h, i: (0, h))
    doc_q = pl.BlockSpec((Q_BLOCK, 1), lambda h, i: (i, 0))
    doc_k = pl.BlockSpec((1, count), lambda h, i: (0, 0))
    lse = pl.BlockSpec((1, Q_BLOCK, 1), lambda h, i: (h, i, 0))
    return block, whole, doc_q, doc_k, lse


def attend_forward(q, k, v, docs):
    count, width = q.shape
    heads = width // HEAD
    block, whole, doc_q, doc_k, lse = attend_specs(count)
    return pl.pallas_call(
        attend_forward_kernel,
        grid=(heads, count // Q_BLOCK),
        in_specs=[block, whole, whole, doc_q, doc_k],
        out_specs=[block, lse, pl.BlockSpec((1, 8, 128), lambda h, i: (h, 0, 0))],
        out_shape=[
            jax.ShapeDtypeStruct((count, width), bf16),
            jax.ShapeDtypeStruct((heads, count, 1), f32),
            jax.ShapeDtypeStruct((heads, 8, 128), f32),
        ],
        compiler_params=pltpu.CompilerParams(vmem_limit_bytes=48 << 20),
        cost_estimate=pl.CostEstimate(
            flops=4 * count * count * width,
            transcendentals=heads * count * count,
            bytes_accessed=8 * count * width,
        ),
    )(q, k, v, docs[:, None], docs[None, :])


def attend_backward(q, k, v, docs, log_total, grad):
    count, width = q.shape
    heads = width // HEAD
    block, whole, doc_q, doc_k, lse = attend_specs(count)
    return pl.pallas_call(
        attend_backward_kernel,
        grid=(heads, count // Q_BLOCK),
        in_specs=[block, whole, whole, doc_q, doc_k, lse, block],
        out_specs=[block, whole, whole],
        out_shape=[jax.ShapeDtypeStruct((count, width), f32)] * 3,
        compiler_params=pltpu.CompilerParams(vmem_limit_bytes=56 << 20),
        cost_estimate=pl.CostEstimate(
            flops=10 * count * count * width,
            transcendentals=heads * count * count,
            bytes_accessed=20 * count * width,
        ),
    )(q, k, v, docs[:, None], docs[None, :], log_total, grad)


MESH = pl.DeviceIdType.MESH
ANY = pl.BlockSpec(memory_space=pl.ANY)
VMEM = pl.BlockSpec(memory_space=pltpu.VMEM)


def ring_peers(axis):
    n, me = lax.axis_size(axis), lax.axis_index(axis)
    return [lax.rem(me + k, n) for k in range(n)], [lax.rem(me + n - k, n) for k in range(n)]


class Greeting:
    def __init__(self):
        self.barrier, self.total = pltpu.get_barrier_semaphore(), 0

    def ring(self, axis):
        to, _ = ring_peers(axis)
        for peer in to[1:]:
            pl.semaphore_signal(
                self.barrier, inc=1, device_id={axis: peer}, device_id_type=MESH
            )
        self.total = self.total + len(to) - 1
        return self

    def line(self):
        line = Line()
        for there, peer in (
            (line.place >= 0, line.partner),
            (line.not_last, line.me + 2),
            (line.not_first, line.me - 2),
        ):

            @pl.when(there)
            def _():
                pl.semaphore_signal(
                    self.barrier, inc=1, device_id={"ctx": peer}, device_id_type=MESH
                )

            self.total = self.total + there.astype(jnp.int32)
        return self

    def wait(self):
        pl.semaphore_wait(self.barrier, self.total)


class Line:
    def __init__(self):
        self.n, self.me = lax.axis_size("ctx") // 2, lax.axis_index("ctx")
        self.place, self.core = lax.div(self.me, 2), lax.rem(self.me, 2)
        self.partner = self.me + 1 - 2 * self.core
        self.not_first, self.not_last = self.place > 0, self.place < self.n - 1


class Direct:
    def __init__(self, axis, source, target, send, recv):
        self.axis, self.source, self.target = axis, source, target
        self.send, self.recv = send, recv
        self.me = lax.axis_index(axis)
        self.to, self.origin = ring_peers(axis)

    def copy(self, k, sender):
        return pltpu.make_async_remote_copy(
            src_ref=self.source(self.to[k]),
            dst_ref=self.target(sender, k),
            send_sem=self.send.at[k],
            recv_sem=self.recv.at[k],
            device_id={self.axis: self.to[k]},
            device_id_type=MESH,
        )

    def start(self):
        for k in range(1, len(self.to)):
            self.copy(k, self.me).start()

    def wait_recv(self):
        for k in range(1, len(self.to)):
            self.copy(k, self.origin[k]).wait_recv()

    def wait_send(self):
        for k in range(1, len(self.to)):
            self.copy(k, self.me).wait_send()


class LineGather:
    def __init__(self, pieces, own_sem, send_r, send_l, send_p, recv_r, recv_l, recv_p):
        self.line, self.pieces, self.own_sem = Line(), pieces, own_sem
        self.send_r, self.send_l, self.send_p = send_r, send_l, send_p
        self.recv_r, self.recv_l, self.recv_p = recv_r, recv_l, recv_p

    def own(self, c):
        source, target = self.pieces[c]
        return pltpu.make_async_copy(source, target(self.line.me), self.own_sem.at[c])

    def copy(self, block, k, c, target_device, send, recv):
        source, target = self.pieces[c]
        return pltpu.make_async_remote_copy(
            src_ref=source if k == 0 else target(block),
            dst_ref=target(block),
            send_sem=send,
            recv_sem=recv,
            device_id={"ctx": target_device},
            device_id_type=MESH,
        )

    def right(self, k, c):
        me = self.line.me
        return self.copy(me - 2 * k, k, c, me + 2, self.send_r.at[k, c], self.recv_r.at[k, c])

    def left(self, k, c):
        me = self.line.me
        return self.copy(me + 2 * k, k, c, me - 2, self.send_l.at[k, c], self.recv_l.at[k, c])

    def across(self, k, c, sign):
        line = self.line
        i = k if sign < 0 else line.n - 1 + k
        return self.copy(
            line.me + sign * 2 * k, k, c, line.partner, self.send_p.at[i, c], self.recv_p.at[i, c]
        )

    def arrived(self, block, c, recv):
        source, target = self.pieces[c]
        pltpu.make_async_remote_copy(
            src_ref=source,
            dst_ref=target(block),
            send_sem=recv,
            recv_sem=recv,
            device_id={"ctx": self.line.partner},
            device_id_type=MESH,
        ).wait_recv()

    def start(self):
        for c in range(len(self.pieces)):
            self.own(c).start()

    def hop(self, k):
        line = self.line
        for c in range(len(self.pieces)):

            @pl.when(line.place >= k)
            def _():
                if k:
                    self.arrived(line.me - 2 * k, c, self.recv_r.at[k - 1, c])

                @pl.when(line.not_last)
                def _():
                    self.right(k, c).start()

                self.across(k, c, -1).start()

            @pl.when(line.place + k <= line.n - 1)
            def _():
                if k:
                    self.arrived(line.me + 2 * k, c, self.recv_l.at[k - 1, c])

                @pl.when(line.not_first)
                def _():
                    self.left(k, c).start()

                if k:
                    self.across(k, c, 1).start()

    def finish(self, skip_own=None):
        line = self.line
        for c in range(len(self.pieces)):
            if c != skip_own:
                self.own(c).wait()
        for k in range(line.n):
            for c in range(len(self.pieces)):

                @pl.when(line.place >= k)
                def _():
                    @pl.when(line.not_last)
                    def _():
                        self.right(k, c).wait_send()

                    self.across(k, c, -1).wait_send()
                    self.arrived(line.partner - 2 * k, c, self.recv_p.at[k, c])

                @pl.when(line.place + k <= line.n - 1)
                def _():
                    @pl.when(line.not_first)
                    def _():
                        self.left(k, c).wait_send()

                    if k:
                        self.across(k, c, 1).wait_send()
                        self.arrived(line.partner + 2 * k, c, self.recv_p.at[line.n - 1 + k, c])


def line_gather_scratch(n, pieces):
    sem = pltpu.SemaphoreType.DMA
    one, two = sem((n, pieces)), sem((2 * n - 1, pieces))
    return [sem((pieces,)), one, one, two, one, one, two]


class LineReduce:
    def __init__(
        self, chunks, x, o, pair, from_left, from_right, send_p, recv_p, send_s, recv_r, recv_l
    ):
        self.line, self.chunks = Line(), chunks
        self.x, self.o, self.pair, self.out = x, o, pair, pair
        self.from_left, self.from_right = from_left, from_right
        self.send_p, self.recv_p, self.send_s = send_p, recv_p, send_s
        self.recv_r, self.recv_l = recv_r, recv_l
        self.order = []
        for j in range(self.line.n):
            self.order += [p for p in (self.line.n - 1 - j, j) if p not in self.order]

    def at(self, c):
        rows = self.x.shape[1] // self.chunks
        return pl.ds(c * rows, rows)

    def across(self, p, c):
        line, at = self.line, self.at(c)
        return pltpu.make_async_remote_copy(
            src_ref=self.x.at[2 * p + 1 - line.core, at],
            dst_ref=self.pair.at[p, at],
            send_sem=self.send_p.at[p, c],
            recv_sem=self.recv_p.at[p, c],
            device_id={"ctx": line.partner},
            device_id_type=MESH,
        )

    def along(self, p, c, step, buffer, recv):
        at = self.at(c)
        return pltpu.make_async_remote_copy(
            src_ref=self.out.at[p, at],
            dst_ref=buffer.at[p, at],
            send_sem=self.send_s.at[p, c],
            recv_sem=recv.at[p, c],
            device_id={"ctx": self.line.me + step},
            device_id_type=MESH,
        )

    def right(self, p, c):
        return self.along(p, c, 2, self.from_left, self.recv_r)

    def left(self, p, c):
        return self.along(p, c, -2, self.from_right, self.recv_l)

    def start(self):
        for p in self.order:
            for c in range(self.chunks):
                self.across(p, c).start()

    def both(self, p, c):
        at = self.at(c)
        return self.x[2 * p + self.line.core, at].astype(f32) + self.pair[p, at].astype(f32)

    def pass_on(self):
        line = self.line
        for p in self.order:
            for c in range(self.chunks):
                at = self.at(c)
                self.across(p, c).wait_recv()

                @pl.when(line.place < p)
                def _():
                    @pl.when(line.not_first)
                    def _():
                        self.right(p, c).wait_recv()
                        total = self.both(p, c) + self.from_left[p, at].astype(f32)
                        self.out[p, at] = total.astype(bf16)

                    @pl.when(line.place == 0)
                    def _():
                        self.out[p, at] = self.both(p, c).astype(bf16)

                    self.right(p, c).start()

                @pl.when(line.place > p)
                def _():
                    @pl.when(line.not_last)
                    def _():
                        self.left(p, c).wait_recv()
                        total = self.both(p, c) + self.from_right[p, at].astype(f32)
                        self.out[p, at] = total.astype(bf16)

                    @pl.when(line.place == line.n - 1)
                    def _():
                        self.out[p, at] = self.both(p, c).astype(bf16)

                    self.left(p, c).start()

    def finish(self):
        line = self.line
        for p in range(line.n):
            for c in range(self.chunks):
                at = self.at(c)

                @pl.when(line.place == p)
                def _():
                    self.o[at] = self.both(p, c)
                    if p > 0:
                        self.right(p, c).wait_recv()
                        self.o[at] += self.from_left[p, at].astype(f32)
                    if p < line.n - 1:
                        self.left(p, c).wait_recv()
                        self.o[at] += self.from_right[p, at].astype(f32)

        for p in range(line.n):
            for c in range(self.chunks):
                self.across(p, c).wait_send()

                @pl.when(line.place < p)
                def _():
                    self.right(p, c).wait_send()

                @pl.when(line.place > p)
                def _():
                    self.left(p, c).wait_send()


def add_up(x, buf, o, me):
    rows = x.shape[1]
    step = 8 if rows % 32 else 32

    @pl.loop(0, rows // step)
    def _(j):
        at = pl.ds(pl.multiple_of(j * step, step), step)
        total = x[me, at].astype(f32)
        for k in range(buf.shape[0]):
            total = total + buf[k, at].astype(f32)
        o[at] = total.astype(o.dtype)


def block_of(ref):
    return lambda device: ref.at[device]


def block_from(ref):
    return lambda device, k: ref.at[device]


def whole_of(ref):
    return lambda device: ref


def buffer_of(ref):
    return lambda device, k: ref.at[k - 1]


def row_pieces(source, target, chunks):
    rows = source.shape[0] // chunks
    return [
        (source.at[pl.ds(c * rows, rows)], lambda b, c=c: target.at[b, pl.ds(c * rows, rows)])
        for c in range(chunks)
    ]


def start_kernel(
    x, w, w_query, w_key, w_value, small, cot, x_all, w_all, heads_all, small_all, cot_all,
    heads_mid, small_mid, own_sem, ex_send, ex_recv, sp_send, sp_recv, w_send, w_recv, f_send,
    f_recv, *line_sems,
):
    shard, ctx = lax.axis_index("shard"), lax.axis_index("ctx")
    n_ctx = lax.axis_size("ctx")
    cols = w_query.shape[1] // n_ctx
    Greeting().ring("ctx").ring("shard").wait()

    def columns(ref):
        return lambda d: ref.at[:, pl.ds(pl.multiple_of(d * cols, HEAD), cols)]

    def place(i):
        if i == 3:
            return block_from(small_mid)
        return lambda d, k: heads_mid.at[d, :, i * cols : (i + 1) * cols]

    sources = [columns(w_query), columns(w_key), columns(w_value), whole_of(small)]
    swaps = [
        Direct("ctx", source, place(i), ex_send.at[i], ex_recv.at[i])
        for i, source in enumerate(sources)
    ]

    def by_shard(ref):
        return lambda d, k: ref.at[:, d]

    spreads = [
        Direct("shard", whole_of(heads_mid), by_shard(heads_all), sp_send.at[0], sp_recv.at[0]),
        Direct("shard", whole_of(small_mid), by_shard(small_all), sp_send.at[1], sp_recv.at[1]),
    ]
    other = Direct("shard", whole_of(cot), block_from(cot_all), sp_send.at[2], sp_recv.at[2])
    rows_w = LineGather([(w, lambda b: w_all.at[b, shard])], *line_sems[:7])
    rows_x = LineGather(row_pieces(x, x_all, LINE_CHUNKS), *line_sems[7:])
    at = rows_x.line
    own = [
        pltpu.make_async_copy(source(ctx), place(i)(ctx, 0), own_sem.at[i])
        for i, source in enumerate(sources)
    ]
    later = [
        pltpu.make_async_copy(heads_mid, heads_all.at[:, shard], own_sem.at[4]),
        pltpu.make_async_copy(small_mid, small_all.at[:, shard], own_sem.at[5]),
        pltpu.make_async_copy(cot, cot_all.at[shard], own_sem.at[6]),
    ]
    other.start()
    for swap in swaps:
        swap.start()
    for copy in own:
        copy.start()
    rows_w.start()
    rows_w.hop(0)
    rows_x.start()
    rows_x.hop(0)
    for swap in swaps:
        swap.wait_recv()
    for copy in own:
        copy.wait()
    for one in (*spreads, *later):
        one.start()
    for k in range(1, at.n):
        rows_w.hop(k)

    to, origin = ring_peers("shard")

    def row(k, p, sender):
        block = 2 * p + at.core
        return pltpu.make_async_remote_copy(
            src_ref=w_all.at[block, shard],
            dst_ref=w_all.at[block, sender],
            send_sem=w_send.at[k, p],
            recv_sem=w_recv.at[k, p],
            device_id={"shard": to[k]},
            device_id_type=MESH,
        )

    def forward(k, p, core):
        block = w_all.at[2 * p + core, origin[k]]
        return pltpu.make_async_remote_copy(
            src_ref=block,
            dst_ref=block,
            send_sem=f_send.at[k, p],
            recv_sem=f_recv.at[k, p],
            device_id={"ctx": at.partner},
            device_id_type=MESH,
        )

    some = [(k, p) for k in range(1, len(to)) for p in range(at.n)]
    rows_w.own(0).wait()
    for k, p in some:
        row(k, p, shard).start()
    for k in range(1, at.n):
        rows_x.hop(k)
    for k, p in some:
        row(k, p, origin[k]).wait_recv()
        forward(k, p, at.core).start()
    rows_w.finish(skip_own=0)
    rows_x.finish()
    for k, p in some:
        row(k, p, shard).wait_send()
        forward(k, p, at.core).wait_send()
        forward(k, p, 1 - at.core).wait_recv()
    for direct in (other, *spreads):
        direct.wait_recv()
    for direct in (other, *swaps, *spreads):
        direct.wait_send()
    for copy in later:
        copy.wait()


def exchange_kernel(to_rows, *refs):
    more = len(refs) > 5
    if more:
        x, cot, o, cot_all, own_sem, send, recv, cot_send, cot_recv = refs
    else:
        x, o, own_sem, send, recv = refs
    n, me = lax.axis_size("ctx"), lax.axis_index("ctx")
    cols, rows = (x.shape[1] // n, x.shape[0]) if to_rows else (x.shape[1], o.shape[0])

    def row_block(ref):
        return lambda d, k=0: ref.at[pl.ds(pl.multiple_of(d * rows, rows), rows)]

    def column_block(ref):
        return lambda d, k=0: ref.at[:, pl.ds(pl.multiple_of(d * cols, cols), cols)]

    source, target = (
        (column_block(x), row_block(o)) if to_rows else (row_block(x), column_block(o))
    )
    greeting = Greeting().ring("ctx")
    if more:
        greeting.ring("shard")
    greeting.wait()
    all_of = [Direct("ctx", source, target, send, recv)]
    own = [pltpu.make_async_copy(source(me), target(me), own_sem.at[0])]
    if more:
        all_of.append(Direct("shard", whole_of(cot), block_from(cot_all), cot_send, cot_recv))
        own.append(
            pltpu.make_async_copy(cot, cot_all.at[lax.axis_index("shard")], own_sem.at[1])
        )
    for one in (*all_of, *own):
        one.start()
    for copy in own:
        copy.wait()
    for direct in all_of:
        direct.wait_recv()
        direct.wait_send()


def gather_kernel(axis, count, *refs):
    ins, outs = refs[:count], refs[count : 2 * count]
    own_sem, send, recv = refs[2 * count :]
    me = lax.axis_index(axis)
    Greeting().ring(axis).wait()
    all_of = [
        Direct(axis, whole_of(ins[i]), block_from(outs[i]), send.at[i], recv.at[i])
        for i in range(count)
    ]
    own = [pltpu.make_async_copy(ins[i], outs[i].at[me], own_sem.at[i]) for i in range(count)]
    for direct in all_of:
        direct.start()
    for copy in own:
        copy.start()
    for copy in own:
        copy.wait()
    for direct in all_of:
        direct.wait_recv()
        direct.wait_send()


def reduce_kernel(axis, count, *refs):
    ins, outs, bufs = refs[:count], refs[count : 2 * count], refs[2 * count : 3 * count]
    send, recv = refs[3 * count :]
    Greeting().ring(axis).wait()
    all_of = [
        Direct(axis, block_of(ins[i]), buffer_of(bufs[i]), send.at[i], recv.at[i])
        for i in range(count)
    ]
    for direct in all_of:
        direct.start()
    for i, direct in enumerate(all_of):
        direct.wait_recv()
        add_up(ins[i], bufs[i], outs[i], direct.me)
        direct.wait_send()


def many_sum_kernel(axis, x, o, buf, send, recv):
    Greeting().ring(axis).wait()
    direct = Direct(axis, whole_of(x), buffer_of(buf), send, recv)
    direct.start()
    direct.wait_recv()
    total = x[...]
    for k in range(buf.shape[0]):
        total = total + buf[k]
    o[...] = total
    direct.wait_send()


def end_kernel(
    x, wide, out, y, x_sum, wide_all, out_sum, y_sum, wide_buf, out_buf, y_buf, wide_sum,
    own_sem, wide_send, wide_recv, out_send, out_recv, y_send, y_recv, swap_send, swap_recv,
    *line_refs,
):
    ctx = lax.axis_index("ctx")
    Greeting().ring("ctx").ring("shard").wait()
    wides = Direct("shard", block_of(wide), buffer_of(wide_buf), wide_send, wide_recv)
    outs = Direct("shard", block_of(out), buffer_of(out_buf), out_send, out_recv)
    swap = Direct("ctx", block_of(wide_sum), block_from(wide_all), swap_send, swap_recv)
    line = LineReduce(LINE_CHUNKS, x, x_sum, *line_refs)
    returns = Direct("shard", block_of(y), buffer_of(y_buf), y_send, y_recv)
    line.start()
    wides.start()
    outs.start()
    returns.start()
    line.pass_on()
    wides.wait_recv()
    for b in range(lax.axis_size("ctx")):
        rows = wide_sum.shape[1]
        total = wide[wides.me, b * rows : (b + 1) * rows].astype(f32)
        for k in range(wide_buf.shape[0]):
            total = total + wide_buf[k, b * rows : (b + 1) * rows].astype(f32)
        wide_sum[b] = total.astype(bf16)
    swap.start()
    own = pltpu.make_async_copy(wide_sum.at[ctx], wide_all.at[ctx], own_sem)
    own.start()
    outs.wait_recv()
    add_up(out, out_buf, out_sum, outs.me)
    line.finish()
    returns.wait_recv()
    add_up(y, y_buf, y_sum, returns.me)
    own.wait()
    swap.wait_recv()
    for direct in (swap, wides, outs, returns):
        direct.wait_send()


def line_reduce_kernel(count, *refs):
    ins, outs, rest = refs[:count], refs[count : 2 * count], refs[2 * count :]
    Greeting().line().wait()
    all_of = [
        LineReduce(LINE_CHUNKS, ins[i], outs[i], *rest[8 * i : 8 * i + 8]) for i in range(count)
    ]
    for one in all_of:
        one.start()
    for one in all_of:
        one.pass_on()
    for one in all_of:
        one.finish()


def line_reduce_scratch(x):
    n_ctx, rows, width = x.shape
    n = n_ctx // 2
    return [pltpu.VMEM((n, rows, width), bf16)] * 3 + [
        pltpu.SemaphoreType.DMA((n, LINE_CHUNKS))
    ] * 5


def line_reduce(collective_id, *arrays):
    return pl.pallas_call(
        functools.partial(line_reduce_kernel, len(arrays)),
        out_shape=[jax.ShapeDtypeStruct(x.shape[1:], f32) for x in arrays],
        in_specs=[VMEM] * len(arrays),
        out_specs=[VMEM] * len(arrays),
        scratch_shapes=sum((line_reduce_scratch(x) for x in arrays), []),
        compiler_params=remote_params(collective_id, 54),
    )(*arrays)


def remote_params(collective_id, megabytes):
    return pltpu.CompilerParams(
        collective_id=collective_id, has_side_effects=True, vmem_limit_bytes=megabytes << 20
    )


LINE_CHUNKS = 4


def start_call(collective_id, x, w, w_query, w_key, w_value, small, cot):
    n_ctx, n_shard = lax.axis_size("ctx"), lax.axis_size("shard")
    n = n_ctx // 2
    heads = (w.shape[0], 3 * w.shape[1] // n_ctx)
    sem = pltpu.SemaphoreType.DMA
    return pl.pallas_call(
        start_kernel,
        out_shape=[
            jax.ShapeDtypeStruct((n_ctx, *x.shape), bf16),
            jax.ShapeDtypeStruct((n_ctx, n_shard, *w.shape), bf16),
            jax.ShapeDtypeStruct((n_ctx, n_shard, *heads), bf16),
            jax.ShapeDtypeStruct((n_ctx, n_shard, *small.shape), bf16),
            jax.ShapeDtypeStruct((n_shard, *cot.shape), bf16),
        ],
        in_specs=[ANY] * 7,
        out_specs=[ANY] * 5,
        scratch_shapes=[
            pltpu.VMEM((n_ctx, *heads), bf16),
            pltpu.VMEM((n_ctx, *small.shape), bf16),
            sem((7,)),
            sem((4, n_ctx)),
            sem((4, n_ctx)),
        ]
        + [sem((3, n_shard))] * 2
        + [sem((n_shard, n))] * 4
        + line_gather_scratch(n, 1)
        + line_gather_scratch(n, LINE_CHUNKS),
        compiler_params=remote_params(collective_id, 8),
    )(x, w, w_query, w_key, w_value, small, cot)


def exchange(collective_id, x, to_rows, *more):
    n, n_shard = lax.axis_size("ctx"), lax.axis_size("shard")
    shape = (x.shape[0] * n, x.shape[1] // n) if to_rows else (x.shape[0] // n, x.shape[1] * n)
    sem = pltpu.SemaphoreType.DMA
    return pl.pallas_call(
        functools.partial(exchange_kernel, to_rows),
        out_shape=[jax.ShapeDtypeStruct(shape, x.dtype)]
        + [jax.ShapeDtypeStruct((n_shard, *u.shape), u.dtype) for u in more],
        in_specs=[ANY] * (1 + len(more)),
        out_specs=[ANY] * (1 + len(more)),
        scratch_shapes=[sem((2,)), sem((n,)), sem((n,))] + [sem((n_shard,))] * (2 * len(more)),
        compiler_params=remote_params(collective_id, 8),
    )(x, *more)


def gather(axis, collective_id, *arrays):
    count, n = len(arrays), lax.axis_size(axis)
    sem = pltpu.SemaphoreType.DMA
    return pl.pallas_call(
        functools.partial(gather_kernel, axis, count),
        out_shape=[jax.ShapeDtypeStruct((n, *a.shape), a.dtype) for a in arrays],
        in_specs=[ANY] * count,
        out_specs=[ANY] * count,
        scratch_shapes=[sem((count,)), sem((count, n)), sem((count, n))],
        compiler_params=remote_params(collective_id, 8),
    )(*arrays)


def reduce(axis, collective_id, *arrays):
    count, n = len(arrays), lax.axis_size(axis)
    sem = pltpu.SemaphoreType.DMA
    return pl.pallas_call(
        functools.partial(reduce_kernel, axis, count),
        out_shape=[jax.ShapeDtypeStruct(a.shape[1:], f32) for a in arrays],
        in_specs=[VMEM] * count,
        out_specs=[VMEM] * count,
        scratch_shapes=[pltpu.VMEM((n - 1, *a.shape[1:]), a.dtype) for a in arrays]
        + [sem((count, n)), sem((count, n))],
        compiler_params=remote_params(collective_id, 32),
    )(*arrays)


def many_sum(axis, collective_id, x):
    n = lax.axis_size(axis)
    sem = pltpu.SemaphoreType.DMA
    return pl.pallas_call(
        functools.partial(many_sum_kernel, axis),
        out_shape=jax.ShapeDtypeStruct(x.shape, x.dtype),
        in_specs=[VMEM],
        out_specs=VMEM,
        scratch_shapes=[pltpu.VMEM((n - 1, *x.shape), x.dtype), sem((n,)), sem((n,))],
        compiler_params=remote_params(collective_id, 8),
    )(x)


def end_call(collective_id, x, wide, out, y):
    n_ctx, rows, width = x.shape
    n_shard = lax.axis_size("shard")
    n = n_ctx // 2
    wide_rows, wide_cols = wide.shape[1] // n_ctx, wide.shape[2]
    sem = pltpu.SemaphoreType.DMA
    return pl.pallas_call(
        end_kernel,
        out_shape=[
            jax.ShapeDtypeStruct((rows, width), f32),
            jax.ShapeDtypeStruct((n_ctx, wide_rows, wide_cols), bf16),
            jax.ShapeDtypeStruct(out.shape[1:], f32),
            jax.ShapeDtypeStruct(y.shape[1:], f32),
        ],
        in_specs=[VMEM] * 4,
        out_specs=[VMEM] * 4,
        scratch_shapes=[
            pltpu.VMEM((n_shard - 1, *wide.shape[1:]), bf16),
            pltpu.VMEM((n_shard - 1, *out.shape[1:]), bf16),
            pltpu.VMEM((n_shard - 1, *y.shape[1:]), bf16),
            pltpu.VMEM((n_ctx, wide_rows, wide_cols), bf16),
            sem,
        ]
        + [sem((n_shard,))] * 6
        + [sem((n_ctx,))] * 2
        + [pltpu.VMEM((n, rows, width), bf16)] * 3
        + [sem((n, LINE_CHUNKS))] * 5,
        compiler_params=remote_params(collective_id, 56),
    )(x, wide, out, y)


def per_device(
    tokens,
    doc_ids,
    routes,
    attn_gain,
    w_query,
    w_key,
    w_value,
    query_gain,
    key_gain,
    w_out,
    ffn_gain,
    w_router,
    w_gate,
    w_up,
    w_down,
    clip_threshold,
    cotangent,
):
    both = ("ctx", "shard")
    n_ctx, n_shard = lax.axis_size("ctx"), lax.axis_size("shard")
    ctx, shard = lax.axis_index("ctx"), lax.axis_index("shard")
    x_own = tokens[0]
    rows, width = x_own.shape
    part = w_query.shape[0]
    cols = width // n_ctx
    heads = cols // HEAD
    count = rows * n_ctx
    local = w_gate.shape[0]
    experts = local * n_shard

    top = routes.shape[2]
    spare = jnp.zeros((part, LANES - 4 - experts - rows // part * (1 + top)), bf16)
    small = jnp.concatenate(
        [
            jnp.stack([attn_gain, query_gain, key_gain, ffn_gain], axis=1),
            w_router,
            doc_ids.reshape(part, rows // part).astype(bf16),
            routes.reshape(part, rows // part * top).astype(bf16),
            spare,
        ],
        axis=1,
    )
    grad_own = cotangent[0]
    x_all, out_w, weights, small_all, grad_all = start_call(
        1, x_own, w_out, w_query, w_key, w_value, small, grad_own
    )
    x_all = x_all.reshape(count, width)
    out_w = out_w.reshape(width, width)
    weights = weights.reshape(width, 3 * cols)
    gains = small_all[..., : 4 + experts].reshape(width, 4 + experts)
    gain_attn, gain_query, gain_key, gain_ffn = (gains[:, i].astype(f32) for i in range(4))
    router_w = gains[:, 4:]
    gain_query = lax.dynamic_slice_in_dim(gain_query, ctx * cols, cols)
    gain_key = lax.dynamic_slice_in_dim(gain_key, ctx * cols, cols)
    tail = small_all[..., 4 + experts :].astype(jnp.int32)
    docs = lax.dynamic_index_in_dim(tail[..., : rows // part], shard, 1, False).reshape(count)
    grad_all = grad_all.reshape(n_shard * rows, width)
    routes_all = lax.dynamic_index_in_dim(
        tail[..., rows // part : rows // part * (1 + top)], ctx, 0, False
    ).reshape(n_shard * rows, top)

    ff = w_gate.shape[2]
    own_w = jnp.concatenate([w_gate, w_up, w_down.transpose(0, 2, 1)], axis=2)
    first_w = own_w[0]
    x_all, own_w = lax.optimization_barrier((x_all, own_w))
    own_w = [first_w] + [own_w[e] for e in range(1, local)]
    expert_w = [lax.all_gather(u, "ctx", axis=0, tiled=True) for u in own_w]

    x_wide = x_all.astype(f32)
    inverse_one = inverse_rms(x_wide)
    hidden_one = (x_wide * inverse_one * gain_attn).astype(bf16)
    linear = dot(hidden_one, weights)
    query_lin, key_lin = linear[:, :cols], linear[:, cols : 2 * cols]
    value = linear[:, 2 * cols :].astype(bf16)
    squares = jnp.stack(
        [jnp.sum(query_lin * query_lin, axis=1), jnp.sum(key_lin * key_lin, axis=1)]
    )
    squares = many_sum("ctx", 6, squares)
    inverse_qk = lax.rsqrt(squares / width + norm_eps)
    inverse_q, inverse_k = inverse_qk[0][:, None], inverse_qk[1][:, None]
    cosine, sine = rope_tables(count)
    query_n, key_n = query_lin * inverse_q, key_lin * inverse_k
    query = rotate(query_n * gain_query, cosine, sine).astype(bf16)
    key = rotate(key_n * gain_key, cosine, sine).astype(bf16)
    mixed, log_total, peaks = attend_forward(query, key, value, docs)
    x_f = x_own.astype(f32)
    (mixed_own,) = exchange(2, mixed, False)
    after = x_f + dot(mixed_own, out_w)
    inverse_two = inverse_rms(after)
    normed_two = after * inverse_two
    hidden_two = (normed_two * gain_ffn).astype(bf16)

    hidden_all, peaks = gather("shard", 3, hidden_two, peaks)
    hidden_all = hidden_all.reshape(n_shard * rows, width)
    peaks = jnp.max(peaks, axis=0)[:, 0, 0]
    logits = dot(hidden_all, router_w)
    named = jnp.any(routes_all[:, :, None] == jnp.arange(experts)[None, None, :], axis=1)
    probs = jax.nn.softmax(logits, axis=1)
    selected = jnp.where(named, probs, 0.0)
    selected_sum = jnp.sum(selected, axis=1, keepdims=True)
    gates = selected / selected_sum
    gates_own = lax.dynamic_slice_in_dim(gates, shard * local, local, 1)
    named_own = lax.dynamic_slice_in_dim(named, shard * local, local, 1)
    moe_part = jnp.zeros(hidden_all.shape, f32)
    back_part = jnp.zeros(hidden_all.shape, f32)

    grad_wide = grad_all.astype(f32)
    def to_owners(parts):
        return [lax.psum_scatter(u, "ctx", scatter_dimension=0, tiled=True) for u in parts]

    grad_gates, expert_grads = [], []
    for e in range(local):
        wide, down = expert_w[e][:, : 2 * ff], expert_w[e][:, 2 * ff :]
        gate_col = gates_own[:, e : e + 1]
        hidden = dot(hidden_all, wide)
        gate_h, up_h = hidden[:, :ff], hidden[:, ff:]
        sig = jax.nn.sigmoid(gate_h)
        silu = gate_h * sig
        act = (silu * up_h).astype(bf16)
        result = contract_cols(act, down).astype(bf16).astype(f32)
        moe_part = moe_part + gate_col * result
        along = jnp.sum(grad_wide * result, axis=1)
        grad_gates.append(jnp.where(named_own[:, e], along, 0.0))
        grad_y = (gate_col * grad_wide).astype(bf16)
        grad_act = dot(grad_y, down)
        grad_h = jnp.concatenate(
            [grad_act * up_h * sig * (1.0 + gate_h * (1.0 - sig)), grad_act * silu], axis=1
        ).astype(bf16)
        back_part = back_part + contract_cols(grad_h, wide).astype(bf16).astype(f32)
        grad_w = [
            contract_rows(hidden_all, grad_h).astype(bf16),
            contract_rows(grad_y, act).astype(bf16),
        ]
        hidden_all, back_part, grad_w = lax.optimization_barrier((hidden_all, back_part, grad_w))
        expert_grads.append(grad_w)
    early = local // 2
    expert_grads[:early] = [to_owners(grad_w) for grad_w in expert_grads[:early]]
    slots = jnp.stack(grad_gates).reshape(local, n_shard, rows).transpose(1, 0, 2)
    grad_gates = lax.dynamic_update_slice_in_dim(
        jnp.zeros((n_shard, experts, rows), f32), slots, shard * local, 1
    )
    back_sum, grad_gates = reduce(
        "shard", 4, back_part.astype(bf16).reshape(n_shard, rows, width), grad_gates
    )
    grad_gates = grad_gates.T

    def own_rows(u):
        return lax.dynamic_slice_in_dim(u, shard * rows, rows, 0)

    gates_t, probs_t, named_t, sum_t = map(own_rows, (gates, probs, named, selected_sum))
    grad_selected = (
        grad_gates - jnp.sum(gates_t * grad_gates, axis=1, keepdims=True)
    ) / sum_t
    grad_probs = jnp.where(named_t, grad_selected, 0.0)
    grad_logits = (
        probs_t * (grad_probs - jnp.sum(probs_t * grad_probs, axis=1, keepdims=True))
    ).astype(bf16)
    grad_router = contract_rows(hidden_two, grad_logits)
    grad_hidden = back_sum + contract_cols(grad_logits, router_w)
    grad_gain_ffn = jnp.sum(grad_hidden * normed_two, axis=0)
    scaled_two = grad_hidden * gain_ffn
    grad_after = grad_own.astype(f32) + inverse_two * (
        scaled_two - normed_two * jnp.mean(scaled_two * normed_two, axis=1, keepdims=True)
    )

    grad_attn_own = grad_after.astype(bf16)
    to_gather, expert_grads[0] = lax.optimization_barrier((grad_attn_own, expert_grads[0]))
    grad_attn = lax.all_gather(to_gather, "ctx", axis=0, tiled=True)
    (grad_mixed,) = exchange(5, contract_cols(grad_attn_own, out_w).astype(bf16), True)
    *late, last_grad = expert_grads[early:]
    wide_late = [wide for wide, _ in late]
    grad_mixed, wide_late = lax.optimization_barrier((grad_mixed, wide_late))
    wide_late = to_owners(wide_late)
    grad_query_rot, grad_key_rot, grad_value = attend_backward(
        query, key, value, docs, log_total, grad_mixed
    )
    grad_query_n = rotate(grad_query_rot, cosine, -sine)
    grad_key_n = rotate(grad_key_rot, cosine, -sine)
    grad_gain_query = jnp.sum(grad_query_n * query_n, axis=0)
    grad_gain_key = jnp.sum(grad_key_n * key_n, axis=0)
    scaled_q, scaled_k = grad_query_n * gain_query, grad_key_n * gain_key
    peak_row = lax.dynamic_update_slice_in_dim(jnp.zeros((count,), f32), peaks, ctx * heads, 0)
    inner = jnp.stack(
        [jnp.sum(scaled_q * query_n, axis=1), jnp.sum(scaled_k * key_n, axis=1), peak_row]
    )
    inner = many_sum("ctx", 7, inner)
    grad_out_w = contract_rows(mixed, grad_attn)
    peak_all = inner[2, :HEADS]
    inner = inner / width
    grad_linear = jnp.concatenate(
        [
            inverse_q * (scaled_q - query_n * inner[0][:, None]),
            inverse_k * (scaled_k - key_n * inner[1][:, None]),
            grad_value,
        ],
        axis=1,
    ).astype(bf16)
    grad_weights = contract_rows(hidden_one, grad_linear)
    hidden_part = contract_cols(grad_linear, weights)
    grad_gain_attn = jnp.sum(hidden_part * (x_wide * inverse_one), axis=0)
    grad_small = jnp.concatenate(
        [jnp.stack([grad_gain_attn, grad_gain_ffn], axis=1), grad_router], axis=1
    )
    grad_small = jnp.pad(grad_small, ((0, 0), (0, LANES - 2 - experts)))
    grad_weights = (
        jnp.concatenate([grad_weights, grad_small], axis=1)
        .astype(bf16)
        .reshape(n_ctx, n_shard, part, 3 * cols + LANES)
        .transpose(1, 0, 2, 3)
        .reshape(n_shard, n_ctx * part, 3 * cols + LANES)
    )
    grad_gain_qk = jnp.pad(
        jnp.stack([grad_gain_query, grad_gain_key], axis=1), ((0, 0), (0, LANES - 2))
    )
    grad_out_w = (
        jnp.concatenate([grad_out_w, grad_gain_qk], axis=1)
        .astype(bf16)
        .reshape(n_shard, part, width + LANES)
    )
    hidden_part = hidden_part.astype(bf16).reshape(n_ctx, rows, width)
    grad_hidden_one, grad_weights, grad_out_w, moe_sum = end_call(
        8,
        hidden_part,
        grad_weights,
        grad_out_w,
        moe_part.astype(bf16).reshape(n_shard, rows, width),
    )
    output = (after + moe_sum).astype(bf16)
    by_line = [down for _, down in late] + last_grad
    grad_hidden_one, by_line = lax.optimization_barrier((grad_hidden_one, by_line))
    by_line = line_reduce(9, *(u.reshape(n_ctx, width // n_ctx, -1) for u in by_line))
    by_line, queued, wide_late = lax.optimization_barrier(
        (by_line, expert_grads[:early], wide_late)
    )
    by_line = list(by_line)
    wide_grads = [wide for wide, _ in queued] + list(wide_late) + by_line[-2:-1]
    down_grads = [down for _, down in queued] + by_line[:-2] + by_line[-1:]
    wide_grads = jnp.stack([u.astype(f32) for u in wide_grads])
    down_grads = jnp.stack([u.astype(f32) for u in down_grads])
    grad_weights = grad_weights.astype(f32)
    grad_small = jnp.sum(grad_weights[..., 3 * cols :], axis=0)
    grad_weights = (
        grad_weights[..., : 3 * cols]
        .reshape(n_ctx, part, 3, cols)
        .transpose(2, 1, 0, 3)
        .reshape(3, part, width)
    )
    inverse_own = inverse_rms(x_f)
    normed_own = x_f * inverse_own
    scaled_one = grad_hidden_one * gain_attn
    grad_inputs = grad_after + inverse_own * (
        scaled_one - normed_own * jnp.mean(scaled_one * normed_own, axis=1, keepdims=True)
    )

    factors = jnp.sqrt(clip_threshold / jnp.maximum(peak_all, clip_threshold))
    col_scale = jnp.repeat(factors, HEAD)
    query_clipped = (w_query.astype(f32) * col_scale[None, :]).astype(bf16)
    key_clipped = (w_key.astype(f32) * col_scale[None, :]).astype(bf16)
    return (
        output[None],
        grad_inputs[None],
        grad_small[:, 0],
        grad_weights[0],
        grad_weights[1],
        grad_weights[2],
        grad_out_w[:, width],
        grad_out_w[:, width + 1],
        grad_out_w[:, :width],
        grad_small[:, 1],
        grad_small[:, 2 : 2 + experts],
        wide_grads[..., :ff],
        wide_grads[..., ff:],
        down_grads.transpose(0, 2, 1),
        query_clipped,
        key_clipped,
        factors,
    )


def solution(mesh):
    both = ("ctx", "shard")
    return jax.shard_map(
        per_device,
        mesh=mesh,
        in_specs=(
            P("shard", "ctx", None),
            P("shard", "ctx"),
            P("shard", "ctx", None),
            P(both),
            P(both, None),
            P(both, None),
            P(both, None),
            P(both),
            P(both),
            P(both, None),
            P(both),
            P(both, None),
            P("shard", "ctx", None),
            P("shard", "ctx", None),
            P("shard", None, "ctx"),
            P(),
            P("shard", "ctx", None),
        ),
        out_specs=(
            P("shard", "ctx", None),
            P("shard", "ctx", None),
            P(both),
            P(both, None),
            P(both, None),
            P(both, None),
            P(both),
            P(both),
            P(both, None),
            P(both),
            P(both, None),
            P("shard", "ctx", None),
            P("shard", "ctx", None),
            P("shard", None, "ctx"),
            P(both, None),
            P(both, None),
            P(),
        ),
        check_vma=False,
    )
```

```python
import functools

import jax
import jax.numpy as jnp
from jax import lax
from jax.experimental import pallas as pl
from jax.experimental.pallas import tpu as pltpu
from jax.sharding import PartitionSpec as P

HEADS = 16
HEAD = 128
SCALE = HEAD ** (-0.5)
Q_BLOCK = 256
LANES = 128

norm_eps = 1e-06
rope_base = 10000.0
f32 = jnp.float32
bf16 = jnp.bfloat16


def dot(a, b):
    return jnp.dot(a, b, preferred_element_type=f32)


def contract_rows(a, b):
    return lax.dot_general(a, b, (((0,), (0,)), ((), ())), preferred_element_type=f32)


def contract_cols(a, b):
    return lax.dot_general(a, b, (((1,), (1,)), ((), ())), preferred_element_type=f32)


def inverse_rms(values):
    return lax.rsqrt(jnp.mean(values * values, axis=-1, keepdims=True) + norm_eps)


def rope_tables(count):
    half = HEAD // 2
    freq = rope_base ** (-jnp.arange(half).astype(f32) / half)
    angles = jnp.arange(count).astype(f32)[:, None] * freq[None, :]
    return jnp.cos(angles), jnp.sin(angles)


def rotate(values, cosine, sine):
    parts = []
    for col in range(0, values.shape[1], HEAD):
        a = values[:, col : col + HEAD // 2]
        b = values[:, col + HEAD // 2 : col + HEAD]
        parts += [a * cosine - b * sine, b * cosine + a * sine]
    return jnp.concatenate(parts, axis=1)


def attend_forward_kernel(q_ref, k_ref, v_ref, doc_q_ref, doc_k_ref, o_ref, lse_ref, peak_ref):
    s = SCALE * contract_cols(q_ref[...], k_ref[...])
    s = jnp.where(doc_q_ref[...] == doc_k_ref[...], s, -1e30)
    top = jnp.max(s, axis=1, keepdims=True)
    e = jnp.exp(s - top)
    total = jnp.sum(e, axis=1, keepdims=True)
    p = (e * (1.0 / total)).astype(bf16)
    o_ref[...] = dot(p, v_ref[...]).astype(bf16)
    lse_ref[0] = top + jnp.log(total)
    peak = jnp.broadcast_to(jnp.max(top, axis=0, keepdims=True), peak_ref.shape[1:])

    @pl.when(pl.program_id(1) == 0)
    def _():
        peak_ref[0] = peak

    @pl.when(pl.program_id(1) > 0)
    def _():
        peak_ref[0] = jnp.maximum(peak_ref[0], peak)


def attend_backward_kernel(
    q_ref, k_ref, v_ref, doc_q_ref, doc_k_ref, lse_ref, do_ref, dq_ref, dk_ref, dv_ref
):
    q, k, v, do = q_ref[...], k_ref[...], v_ref[...], do_ref[...]
    s = SCALE * contract_cols(q, k)
    p = jnp.where(doc_q_ref[...] == doc_k_ref[...], jnp.exp(s - lse_ref[0]), 0.0)
    dp = contract_cols(do, v)
    inner = jnp.sum(p * dp, axis=1, keepdims=True)
    ds = (p * (dp - inner)).astype(bf16)
    dq_ref[...] = SCALE * dot(ds, k)
    dk = SCALE * contract_rows(ds, q)
    dv = contract_rows(p.astype(bf16), do)

    @pl.when(pl.program_id(1) == 0)
    def _():
        dk_ref[...] = dk
        dv_ref[...] = dv

    @pl.when(pl.program_id(1) > 0)
    def _():
        dk_ref[...] += dk
        dv_ref[...] += dv


def attend_specs(count):
    block = pl.BlockSpec((Q_BLOCK, HEAD), lambda h, i: (i, h))
    whole = pl.BlockSpec((count, HEAD), lambda h, i: (0, h))
    doc_q = pl.BlockSpec((Q_BLOCK, 1), lambda h, i: (i, 0))
    doc_k = pl.BlockSpec((1, count), lambda h, i: (0, 0))
    lse = pl.BlockSpec((1, Q_BLOCK, 1), lambda h, i: (h, i, 0))
    return block, whole, doc_q, doc_k, lse


def attend_forward(q, k, v, docs):
    count, width = q.shape
    heads = width // HEAD
    block, whole, doc_q, doc_k, lse = attend_specs(count)
    return pl.pallas_call(
        attend_forward_kernel,
        grid=(heads, count // Q_BLOCK),
        in_specs=[block, whole, whole, doc_q, doc_k],
        out_specs=[block, lse, pl.BlockSpec((1, 8, 128), lambda h, i: (h, 0, 0))],
        out_shape=[
            jax.ShapeDtypeStruct((count, width), bf16),
            jax.ShapeDtypeStruct((heads, count, 1), f32),
            jax.ShapeDtypeStruct((heads, 8, 128), f32),
        ],
        compiler_params=pltpu.CompilerParams(vmem_limit_bytes=48 << 20),
        cost_estimate=pl.CostEstimate(
            flops=4 * count * count * width,
            transcendentals=heads * count * count,
            bytes_accessed=8 * count * width,
        ),
    )(q, k, v, docs[:, None], docs[None, :])


def attend_backward(q, k, v, docs, log_total, grad):
    count, width = q.shape
    heads = width // HEAD
    block, whole, doc_q, doc_k, lse = attend_specs(count)
    return pl.pallas_call(
        attend_backward_kernel,
        grid=(heads, count // Q_BLOCK),
        in_specs=[block, whole, whole, doc_q, doc_k, lse, block],
        out_specs=[block, whole, whole],
        out_shape=[jax.ShapeDtypeStruct((count, width), f32)] * 3,
        compiler_params=pltpu.CompilerParams(vmem_limit_bytes=56 << 20),
        cost_estimate=pl.CostEstimate(
            flops=10 * count * count * width,
            transcendentals=heads * count * count,
            bytes_accessed=20 * count * width,
        ),
    )(q, k, v, docs[:, None], docs[None, :], log_total, grad)


MESH = pl.DeviceIdType.MESH
ANY = pl.BlockSpec(memory_space=pl.ANY)
VMEM = pl.BlockSpec(memory_space=pltpu.VMEM)


def ring_peers(axis):
    n, me = lax.axis_size(axis), lax.axis_index(axis)
    return [lax.rem(me + k, n) for k in range(n)], [lax.rem(me + n - k, n) for k in range(n)]


class Greeting:
    def __init__(self):
        self.barrier, self.total = pltpu.get_barrier_semaphore(), 0

    def ring(self, axis):
        to, _ = ring_peers(axis)
        for peer in to[1:]:
            pl.semaphore_signal(
                self.barrier, inc=1, device_id={axis: peer}, device_id_type=MESH
            )
        self.total = self.total + len(to) - 1
        return self

    def line(self):
        line = Line()
        for there, peer in (
            (line.place >= 0, line.partner),
            (line.not_last, line.me + 2),
            (line.not_first, line.me - 2),
        ):

            @pl.when(there)
            def _():
                pl.semaphore_signal(
                    self.barrier, inc=1, device_id={"ctx": peer}, device_id_type=MESH
                )

            self.total = self.total + there.astype(jnp.int32)
        return self

    def wait(self):
        pl.semaphore_wait(self.barrier, self.total)


class Line:
    def __init__(self):
        self.n, self.me = lax.axis_size("ctx") // 2, lax.axis_index("ctx")
        self.place, self.core = lax.div(self.me, 2), lax.rem(self.me, 2)
        self.partner = self.me + 1 - 2 * self.core
        self.not_first, self.not_last = self.place > 0, self.place < self.n - 1


class Direct:
    def __init__(self, axis, source, target, send, recv):
        self.axis, self.source, self.target = axis, source, target
        self.send, self.recv = send, recv
        self.me = lax.axis_index(axis)
        self.to, self.origin = ring_peers(axis)

    def copy(self, k, sender):
        return pltpu.make_async_remote_copy(
            src_ref=self.source(self.to[k]),
            dst_ref=self.target(sender, k),
            send_sem=self.send.at[k],
            recv_sem=self.recv.at[k],
            device_id={self.axis: self.to[k]},
            device_id_type=MESH,
        )

    def start(self):
        for k in range(1, len(self.to)):
            self.copy(k, self.me).start()

    def wait_recv(self):
        for k in range(1, len(self.to)):
            self.copy(k, self.origin[k]).wait_recv()

    def wait_send(self):
        for k in range(1, len(self.to)):
            self.copy(k, self.me).wait_send()


class LineGather:
    def __init__(self, pieces, own_sem, send_r, send_l, send_p, recv_r, recv_l, recv_p):
        self.line, self.pieces, self.own_sem = Line(), pieces, own_sem
        self.send_r, self.send_l, self.send_p = send_r, send_l, send_p
        self.recv_r, self.recv_l, self.recv_p = recv_r, recv_l, recv_p

    def own(self, c):
        source, target = self.pieces[c]
        return pltpu.make_async_copy(source, target(self.line.me), self.own_sem.at[c])

    def copy(self, block, k, c, target_device, send, recv):
        source, target = self.pieces[c]
        return pltpu.make_async_remote_copy(
            src_ref=source if k == 0 else target(block),
            dst_ref=target(block),
            send_sem=send,
            recv_sem=recv,
            device_id={"ctx": target_device},
            device_id_type=MESH,
        )

    def right(self, k, c):
        me = self.line.me
        return self.copy(me - 2 * k, k, c, me + 2, self.send_r.at[k, c], self.recv_r.at[k, c])

    def left(self, k, c):
        me = self.line.me
        return self.copy(me + 2 * k, k, c, me - 2, self.send_l.at[k, c], self.recv_l.at[k, c])

    def across(self, k, c, sign):
        line = self.line
        i = k if sign < 0 else line.n - 1 + k
        return self.copy(
            line.me + sign * 2 * k, k, c, line.partner, self.send_p.at[i, c], self.recv_p.at[i, c]
        )

    def arrived(self, block, c, recv):
        source, target = self.pieces[c]
        pltpu.make_async_remote_copy(
            src_ref=source,
            dst_ref=target(block),
            send_sem=recv,
            recv_sem=recv,
            device_id={"ctx": self.line.partner},
            device_id_type=MESH,
        ).wait_recv()

    def start(self):
        for c in range(len(self.pieces)):
            self.own(c).start()

    def hop(self, k):
        line = self.line
        for c in range(len(self.pieces)):

            @pl.when(line.place >= k)
            def _():
                if k:
                    self.arrived(line.me - 2 * k, c, self.recv_r.at[k - 1, c])

                @pl.when(line.not_last)
                def _():
                    self.right(k, c).start()

                self.across(k, c, -1).start()

            @pl.when(line.place + k <= line.n - 1)
            def _():
                if k:
                    self.arrived(line.me + 2 * k, c, self.recv_l.at[k - 1, c])

                @pl.when(line.not_first)
                def _():
                    self.left(k, c).start()

                if k:
                    self.across(k, c, 1).start()

    def finish(self, skip_own=None):
        line = self.line
        for c in range(len(self.pieces)):
            if c != skip_own:
                self.own(c).wait()
        for k in range(line.n):
            for c in range(len(self.pieces)):

                @pl.when(line.place >= k)
                def _():
                    @pl.when(line.not_last)
                    def _():
                        self.right(k, c).wait_send()

                    self.across(k, c, -1).wait_send()
                    self.arrived(line.partner - 2 * k, c, self.recv_p.at[k, c])

                @pl.when(line.place + k <= line.n - 1)
                def _():
                    @pl.when(line.not_first)
                    def _():
                        self.left(k, c).wait_send()

                    if k:
                        self.across(k, c, 1).wait_send()
                        self.arrived(line.partner + 2 * k, c, self.recv_p.at[line.n - 1 + k, c])


def line_gather_scratch(n, pieces):
    sem = pltpu.SemaphoreType.DMA
    one, two = sem((n, pieces)), sem((2 * n - 1, pieces))
    return [sem((pieces,)), one, one, two, one, one, two]


class LineReduce:
    def __init__(
        self, chunks, x, o, pair, from_left, from_right, send_p, recv_p, send_s, recv_r, recv_l
    ):
        self.line, self.chunks = Line(), chunks
        self.x, self.o, self.pair, self.out = x, o, pair, pair
        self.from_left, self.from_right = from_left, from_right
        self.send_p, self.recv_p, self.send_s = send_p, recv_p, send_s
        self.recv_r, self.recv_l = recv_r, recv_l
        self.order = []
        for j in range(self.line.n):
            self.order += [p for p in (self.line.n - 1 - j, j) if p not in self.order]

    def at(self, c):
        rows = self.x.shape[1] // self.chunks
        return pl.ds(c * rows, rows)

    def across(self, p, c):
        line, at = self.line, self.at(c)
        return pltpu.make_async_remote_copy(
            src_ref=self.x.at[2 * p + 1 - line.core, at],
            dst_ref=self.pair.at[p, at],
            send_sem=self.send_p.at[p, c],
            recv_sem=self.recv_p.at[p, c],
            device_id={"ctx": line.partner},
            device_id_type=MESH,
        )

    def along(self, p, c, step, buffer, recv):
        at = self.at(c)
        return pltpu.make_async_remote_copy(
            src_ref=self.out.at[p, at],
            dst_ref=buffer.at[p, at],
            send_sem=self.send_s.at[p, c],
            recv_sem=recv.at[p, c],
            device_id={"ctx": self.line.me + step},
            device_id_type=MESH,
        )

    def right(self, p, c):
        return self.along(p, c, 2, self.from_left, self.recv_r)

    def left(self, p, c):
        return self.along(p, c, -2, self.from_right, self.recv_l)

    def start(self):
        for p in self.order:
            for c in range(self.chunks):
                self.across(p, c).start()

    def both(self, p, c):
        at = self.at(c)
        return self.x[2 * p + self.line.core, at].astype(f32) + self.pair[p, at].astype(f32)

    def pass_on(self):
        line = self.line
        for p in self.order:
            for c in range(self.chunks):
                at = self.at(c)
                self.across(p, c).wait_recv()

                @pl.when(line.place < p)
                def _():
                    @pl.when(line.not_first)
                    def _():
                        self.right(p, c).wait_recv()
                        total = self.both(p, c) + self.from_left[p, at].astype(f32)
                        self.out[p, at] = total.astype(bf16)

                    @pl.when(line.place == 0)
                    def _():
                        self.out[p, at] = self.both(p, c).astype(bf16)

                    self.right(p, c).start()

                @pl.when(line.place > p)
                def _():
                    @pl.when(line.not_last)
                    def _():
                        self.left(p, c).wait_recv()
                        total = self.both(p, c) + self.from_right[p, at].astype(f32)
                        self.out[p, at] = total.astype(bf16)

                    @pl.when(line.place == line.n - 1)
                    def _():
                        self.out[p, at] = self.both(p, c).astype(bf16)

                    self.left(p, c).start()

    def finish(self):
        line = self.line
        for p in range(line.n):
            for c in range(self.chunks):
                at = self.at(c)

                @pl.when(line.place == p)
                def _():
                    self.o[at] = self.both(p, c)
                    if p > 0:
                        self.right(p, c).wait_recv()
                        self.o[at] += self.from_left[p, at].astype(f32)
                    if p < line.n - 1:
                        self.left(p, c).wait_recv()
                        self.o[at] += self.from_right[p, at].astype(f32)

        for p in range(line.n):
            for c in range(self.chunks):
                self.across(p, c).wait_send()

                @pl.when(line.place < p)
                def _():
                    self.right(p, c).wait_send()

                @pl.when(line.place > p)
                def _():
                    self.left(p, c).wait_send()


def add_up(x, buf, o, me):
    rows = x.shape[1]
    step = 8 if rows % 32 else 32

    @pl.loop(0, rows // step)
    def _(j):
        at = pl.ds(pl.multiple_of(j * step, step), step)
        total = x[me, at].astype(f32)
        for k in range(buf.shape[0]):
            total = total + buf[k, at].astype(f32)
        o[at] = total.astype(o.dtype)


def block_of(ref):
    return lambda device: ref.at[device]


def block_from(ref):
    return lambda device, k: ref.at[device]


def whole_of(ref):
    return lambda device: ref


def buffer_of(ref):
    return lambda device, k: ref.at[k - 1]


def row_pieces(source, target, chunks):
    rows = source.shape[0] // chunks
    return [
        (source.at[pl.ds(c * rows, rows)], lambda b, c=c: target.at[b, pl.ds(c * rows, rows)])
        for c in range(chunks)
    ]


def start_kernel(
    x, w, w_query, w_key, w_value, small, cot, x_all, w_all, heads_all, small_all, cot_all,
    heads_mid, small_mid, own_sem, ex_send, ex_recv, sp_send, sp_recv, w_send, w_recv, f_send,
    f_recv, *line_sems,
):
    shard, ctx = lax.axis_index("shard"), lax.axis_index("ctx")
    n_ctx = lax.axis_size("ctx")
    cols = w_query.shape[1] // n_ctx
    Greeting().ring("ctx").ring("shard").wait()

    def columns(ref):
        return lambda d: ref.at[:, pl.ds(pl.multiple_of(d * cols, HEAD), cols)]

    def place(i):
        if i == 3:
            return block_from(small_mid)
        return lambda d, k: heads_mid.at[d, :, i * cols : (i + 1) * cols]

    sources = [columns(w_query), columns(w_key), columns(w_value), whole_of(small)]
    swaps = [
        Direct("ctx", source, place(i), ex_send.at[i], ex_recv.at[i])
        for i, source in enumerate(sources)
    ]

    def by_shard(ref):
        return lambda d, k: ref.at[:, d]

    spreads = [
        Direct("shard", whole_of(heads_mid), by_shard(heads_all), sp_send.at[0], sp_recv.at[0]),
        Direct("shard", whole_of(small_mid), by_shard(small_all), sp_send.at[1], sp_recv.at[1]),
    ]
    other = Direct("shard", whole_of(cot), block_from(cot_all), sp_send.at[2], sp_recv.at[2])
    rows_w = LineGather([(w, lambda b: w_all.at[b, shard])], *line_sems[:7])
    rows_x = LineGather(row_pieces(x, x_all, LINE_CHUNKS), *line_sems[7:])
    at = rows_x.line
    own = [
        pltpu.make_async_copy(source(ctx), place(i)(ctx, 0), own_sem.at[i])
        for i, source in enumerate(sources)
    ]
    later = [
        pltpu.make_async_copy(heads_mid, heads_all.at[:, shard], own_sem.at[4]),
        pltpu.make_async_copy(small_mid, small_all.at[:, shard], own_sem.at[5]),
        pltpu.make_async_copy(cot, cot_all.at[shard], own_sem.at[6]),
    ]
    other.start()
    for swap in swaps:
        swap.start()
    for copy in own:
        copy.start()
    rows_w.start()
    rows_w.hop(0)
    rows_x.start()
    rows_x.hop(0)
    for swap in swaps:
        swap.wait_recv()
    for copy in own:
        copy.wait()
    for one in (*spreads, *later):
        one.start()
    for k in range(1, at.n):
        rows_w.hop(k)

    to, origin = ring_peers("shard")

    def row(k, p, sender):
        block = 2 * p + at.core
        return pltpu.make_async_remote_copy(
            src_ref=w_all.at[block, shard],
            dst_ref=w_all.at[block, sender],
            send_sem=w_send.at[k, p],
            recv_sem=w_recv.at[k, p],
            device_id={"shard": to[k]},
            device_id_type=MESH,
        )

    def forward(k, p, core):
        block = w_all.at[2 * p + core, origin[k]]
        return pltpu.make_async_remote_copy(
            src_ref=block,
            dst_ref=block,
            send_sem=f_send.at[k, p],
            recv_sem=f_recv.at[k, p],
            device_id={"ctx": at.partner},
            device_id_type=MESH,
        )

    some = [(k, p) for k in range(1, len(to)) for p in range(at.n)]
    rows_w.own(0).wait()
    for k, p in some:
        row(k, p, shard).start()
    for k in range(1, at.n):
        rows_x.hop(k)
    for k, p in some:
        row(k, p, origin[k]).wait_recv()
        forward(k, p, at.core).start()
    rows_w.finish(skip_own=0)
    rows_x.finish()
    for k, p in some:
        row(k, p, shard).wait_send()
        forward(k, p, at.core).wait_send()
        forward(k, p, 1 - at.core).wait_recv()
    for direct in (other, *spreads):
        direct.wait_recv()
    for direct in (other, *swaps, *spreads):
        direct.wait_send()
    for copy in later:
        copy.wait()


def exchange_kernel(to_rows, *refs):
    more = len(refs) > 5
    if more:
        x, cot, o, cot_all, own_sem, send, recv, cot_send, cot_recv = refs
    else:
        x, o, own_sem, send, recv = refs
    n, me = lax.axis_size("ctx"), lax.axis_index("ctx")
    cols, rows = (x.shape[1] // n, x.shape[0]) if to_rows else (x.shape[1], o.shape[0])

    def row_block(ref):
        return lambda d, k=0: ref.at[pl.ds(pl.multiple_of(d * rows, rows), rows)]

    def column_block(ref):
        return lambda d, k=0: ref.at[:, pl.ds(pl.multiple_of(d * cols, cols), cols)]

    source, target = (
        (column_block(x), row_block(o)) if to_rows else (row_block(x), column_block(o))
    )
    greeting = Greeting().ring("ctx")
    if more:
        greeting.ring("shard")
    greeting.wait()
    all_of = [Direct("ctx", source, target, send, recv)]
    own = [pltpu.make_async_copy(source(me), target(me), own_sem.at[0])]
    if more:
        all_of.append(Direct("shard", whole_of(cot), block_from(cot_all), cot_send, cot_recv))
        own.append(
            pltpu.make_async_copy(cot, cot_all.at[lax.axis_index("shard")], own_sem.at[1])
        )
    for one in (*all_of, *own):
        one.start()
    for copy in own:
        copy.wait()
    for direct in all_of:
        direct.wait_recv()
        direct.wait_send()


def gather_kernel(axis, count, *refs):
    ins, outs = refs[:count], refs[count : 2 * count]
    own_sem, send, recv = refs[2 * count :]
    me = lax.axis_index(axis)
    Greeting().ring(axis).wait()
    all_of = [
        Direct(axis, whole_of(ins[i]), block_from(outs[i]), send.at[i], recv.at[i])
        for i in range(count)
    ]
    own = [pltpu.make_async_copy(ins[i], outs[i].at[me], own_sem.at[i]) for i in range(count)]
    for direct in all_of:
        direct.start()
    for copy in own:
        copy.start()
    for copy in own:
        copy.wait()
    for direct in all_of:
        direct.wait_recv()
        direct.wait_send()


def reduce_kernel(axis, count, *refs):
    ins, outs, bufs = refs[:count], refs[count : 2 * count], refs[2 * count : 3 * count]
    send, recv = refs[3 * count :]
    Greeting().ring(axis).wait()
    all_of = [
        Direct(axis, block_of(ins[i]), buffer_of(bufs[i]), send.at[i], recv.at[i])
        for i in range(count)
    ]
    for direct in all_of:
        direct.start()
    for i, direct in enumerate(all_of):
        direct.wait_recv()
        add_up(ins[i], bufs[i], outs[i], direct.me)
        direct.wait_send()


def many_sum_kernel(axis, x, o, buf, send, recv):
    Greeting().ring(axis).wait()
    direct = Direct(axis, whole_of(x), buffer_of(buf), send, recv)
    direct.start()
    direct.wait_recv()
    total = x[...]
    for k in range(buf.shape[0]):
        total = total + buf[k]
    o[...] = total
    direct.wait_send()


def end_kernel(
    x, wide, out, y, x_sum, wide_all, out_sum, y_sum, wide_buf, out_buf, y_buf, wide_sum,
    own_sem, wide_send, wide_recv, out_send, out_recv, y_send, y_recv, swap_send, swap_recv,
    *line_refs,
):
    ctx = lax.axis_index("ctx")
    Greeting().ring("ctx").ring("shard").wait()
    wides = Direct("shard", block_of(wide), buffer_of(wide_buf), wide_send, wide_recv)
    outs = Direct("shard", block_of(out), buffer_of(out_buf), out_send, out_recv)
    swap = Direct("ctx", block_of(wide_sum), block_from(wide_all), swap_send, swap_recv)
    line = LineReduce(LINE_CHUNKS, x, x_sum, *line_refs)
    returns = Direct("shard", block_of(y), buffer_of(y_buf), y_send, y_recv)
    line.start()
    wides.start()
    outs.start()
    returns.start()
    line.pass_on()
    wides.wait_recv()
    for b in range(lax.axis_size("ctx")):
        rows = wide_sum.shape[1]
        total = wide[wides.me, b * rows : (b + 1) * rows].astype(f32)
        for k in range(wide_buf.shape[0]):
            total = total + wide_buf[k, b * rows : (b + 1) * rows].astype(f32)
        wide_sum[b] = total.astype(bf16)
    swap.start()
    own = pltpu.make_async_copy(wide_sum.at[ctx], wide_all.at[ctx], own_sem)
    own.start()
    outs.wait_recv()
    add_up(out, out_buf, out_sum, outs.me)
    line.finish()
    returns.wait_recv()
    add_up(y, y_buf, y_sum, returns.me)
    own.wait()
    swap.wait_recv()
    for direct in (swap, wides, outs, returns):
        direct.wait_send()


def line_reduce_kernel(count, *refs):
    ins, outs, rest = refs[:count], refs[count : 2 * count], refs[2 * count :]
    Greeting().line().wait()
    all_of = [
        LineReduce(LINE_CHUNKS, ins[i], outs[i], *rest[8 * i : 8 * i + 8]) for i in range(count)
    ]
    for one in all_of:
        one.start()
    for one in all_of:
        one.pass_on()
    for one in all_of:
        one.finish()


def line_reduce_scratch(x):
    n_ctx, rows, width = x.shape
    n = n_ctx // 2
    return [pltpu.VMEM((n, rows, width), bf16)] * 3 + [
        pltpu.SemaphoreType.DMA((n, LINE_CHUNKS))
    ] * 5


def line_reduce(collective_id, *arrays):
    return pl.pallas_call(
        functools.partial(line_reduce_kernel, len(arrays)),
        out_shape=[jax.ShapeDtypeStruct(x.shape[1:], f32) for x in arrays],
        in_specs=[VMEM] * len(arrays),
        out_specs=[VMEM] * len(arrays),
        scratch_shapes=sum((line_reduce_scratch(x) for x in arrays), []),
        compiler_params=remote_params(collective_id, 54),
    )(*arrays)


def remote_params(collective_id, megabytes):
    return pltpu.CompilerParams(
        collective_id=collective_id, has_side_effects=True, vmem_limit_bytes=megabytes << 20
    )


LINE_CHUNKS = 4


def start_call(collective_id, x, w, w_query, w_key, w_value, small, cot):
    n_ctx, n_shard = lax.axis_size("ctx"), lax.axis_size("shard")
    n = n_ctx // 2
    heads = (w.shape[0], 3 * w.shape[1] // n_ctx)
    sem = pltpu.SemaphoreType.DMA
    return pl.pallas_call(
        start_kernel,
        out_shape=[
            jax.ShapeDtypeStruct((n_ctx, *x.shape), bf16),
            jax.ShapeDtypeStruct((n_ctx, n_shard, *w.shape), bf16),
            jax.ShapeDtypeStruct((n_ctx, n_shard, *heads), bf16),
            jax.ShapeDtypeStruct((n_ctx, n_shard, *small.shape), bf16),
            jax.ShapeDtypeStruct((n_shard, *cot.shape), bf16),
        ],
        in_specs=[ANY] * 7,
        out_specs=[ANY] * 5,
        scratch_shapes=[
            pltpu.VMEM((n_ctx, *heads), bf16),
            pltpu.VMEM((n_ctx, *small.shape), bf16),
            sem((7,)),
            sem((4, n_ctx)),
            sem((4, n_ctx)),
        ]
        + [sem((3, n_shard))] * 2
        + [sem((n_shard, n))] * 4
        + line_gather_scratch(n, 1)
        + line_gather_scratch(n, LINE_CHUNKS),
        compiler_params=remote_params(collective_id, 8),
    )(x, w, w_query, w_key, w_value, small, cot)


def exchange(collective_id, x, to_rows, *more):
    n, n_shard = lax.axis_size("ctx"), lax.axis_size("shard")
    shape = (x.shape[0] * n, x.shape[1] // n) if to_rows else (x.shape[0] // n, x.shape[1] * n)
    sem = pltpu.SemaphoreType.DMA
    return pl.pallas_call(
        functools.partial(exchange_kernel, to_rows),
        out_shape=[jax.ShapeDtypeStruct(shape, x.dtype)]
        + [jax.ShapeDtypeStruct((n_shard, *u.shape), u.dtype) for u in more],
        in_specs=[ANY] * (1 + len(more)),
        out_specs=[ANY] * (1 + len(more)),
        scratch_shapes=[sem((2,)), sem((n,)), sem((n,))] + [sem((n_shard,))] * (2 * len(more)),
        compiler_params=remote_params(collective_id, 8),
    )(x, *more)


def gather(axis, collective_id, *arrays):
    count, n = len(arrays), lax.axis_size(axis)
    sem = pltpu.SemaphoreType.DMA
    return pl.pallas_call(
        functools.partial(gather_kernel, axis, count),
        out_shape=[jax.ShapeDtypeStruct((n, *a.shape), a.dtype) for a in arrays],
        in_specs=[ANY] * count,
        out_specs=[ANY] * count,
        scratch_shapes=[sem((count,)), sem((count, n)), sem((count, n))],
        compiler_params=remote_params(collective_id, 8),
    )(*arrays)


def reduce(axis, collective_id, *arrays):
    count, n = len(arrays), lax.axis_size(axis)
    sem = pltpu.SemaphoreType.DMA
    return pl.pallas_call(
        functools.partial(reduce_kernel, axis, count),
        out_shape=[jax.ShapeDtypeStruct(a.shape[1:], f32) for a in arrays],
        in_specs=[VMEM] * count,
        out_specs=[VMEM] * count,
        scratch_shapes=[pltpu.VMEM((n - 1, *a.shape[1:]), a.dtype) for a in arrays]
        + [sem((count, n)), sem((count, n))],
        compiler_params=remote_params(collective_id, 32),
    )(*arrays)


def many_sum(axis, collective_id, x):
    n = lax.axis_size(axis)
    sem = pltpu.SemaphoreType.DMA
    return pl.pallas_call(
        functools.partial(many_sum_kernel, axis),
        out_shape=jax.ShapeDtypeStruct(x.shape, x.dtype),
        in_specs=[VMEM],
        out_specs=VMEM,
        scratch_shapes=[pltpu.VMEM((n - 1, *x.shape), x.dtype), sem((n,)), sem((n,))],
        compiler_params=remote_params(collective_id, 8),
    )(x)


def end_call(collective_id, x, wide, out, y):
    n_ctx, rows, width = x.shape
    n_shard = lax.axis_size("shard")
    n = n_ctx // 2
    wide_rows, wide_cols = wide.shape[1] // n_ctx, wide.shape[2]
    sem = pltpu.SemaphoreType.DMA
    return pl.pallas_call(
        end_kernel,
        out_shape=[
            jax.ShapeDtypeStruct((rows, width), f32),
            jax.ShapeDtypeStruct((n_ctx, wide_rows, wide_cols), bf16),
            jax.ShapeDtypeStruct(out.shape[1:], f32),
            jax.ShapeDtypeStruct(y.shape[1:], f32),
        ],
        in_specs=[VMEM] * 4,
        out_specs=[VMEM] * 4,
        scratch_shapes=[
            pltpu.VMEM((n_shard - 1, *wide.shape[1:]), bf16),
            pltpu.VMEM((n_shard - 1, *out.shape[1:]), bf16),
            pltpu.VMEM((n_shard - 1, *y.shape[1:]), bf16),
            pltpu.VMEM((n_ctx, wide_rows, wide_cols), bf16),
            sem,
        ]
        + [sem((n_shard,))] * 6
        + [sem((n_ctx,))] * 2
        + [pltpu.VMEM((n, rows, width), bf16)] * 3
        + [sem((n, LINE_CHUNKS))] * 5,
        compiler_params=remote_params(collective_id, 56),
    )(x, wide, out, y)


def per_device(
    tokens,
    doc_ids,
    routes,
    attn_gain,
    w_query,
    w_key,
    w_value,
    query_gain,
    key_gain,
    w_out,
    ffn_gain,
    w_router,
    w_gate,
    w_up,
    w_down,
    clip_threshold,
    cotangent,
):
    both = ("ctx", "shard")
    n_ctx, n_shard = lax.axis_size("ctx"), lax.axis_size("shard")
    ctx, shard = lax.axis_index("ctx"), lax.axis_index("shard")
    x_own = tokens[0]
    rows, width = x_own.shape
    part = w_query.shape[0]
    cols = width // n_ctx
    heads = cols // HEAD
    count = rows * n_ctx
    local = w_gate.shape[0]
    experts = local * n_shard

    top = routes.shape[2]
    spare = jnp.zeros((part, LANES - 4 - experts - rows // part * (1 + top)), bf16)
    small = jnp.concatenate(
        [
            jnp.stack([attn_gain, query_gain, key_gain, ffn_gain], axis=1),
            w_router,
            doc_ids.reshape(part, rows // part).astype(bf16),
            routes.reshape(part, rows // part * top).astype(bf16),
            spare,
        ],
        axis=1,
    )
    grad_own = cotangent[0]
    x_all, out_w, weights, small_all, grad_all = start_call(
        1, x_own, w_out, w_query, w_key, w_value, small, grad_own
    )
    x_all = x_all.reshape(count, width)
    out_w = out_w.reshape(width, width)
    weights = weights.reshape(width, 3 * cols)
    gains = small_all[..., : 4 + experts].reshape(width, 4 + experts)
    gain_attn, gain_query, gain_key, gain_ffn = (gains[:, i].astype(f32) for i in range(4))
    router_w = gains[:, 4:]
    gain_query = lax.dynamic_slice_in_dim(gain_query, ctx * cols, cols)
    gain_key = lax.dynamic_slice_in_dim(gain_key, ctx * cols, cols)
    tail = small_all[..., 4 + experts :].astype(jnp.int32)
    docs = lax.dynamic_index_in_dim(tail[..., : rows // part], shard, 1, False).reshape(count)
    grad_all = grad_all.reshape(n_shard * rows, width)
    routes_all = lax.dynamic_index_in_dim(
        tail[..., rows // part : rows // part * (1 + top)], ctx, 0, False
    ).reshape(n_shard * rows, top)

    ff = w_gate.shape[2]
    own_w = jnp.concatenate([w_gate, w_up, w_down.transpose(0, 2, 1)], axis=2)
    first_w = own_w[0]
    x_all, own_w = lax.optimization_barrier((x_all, own_w))
    own_w = [first_w] + [own_w[e] for e in range(1, local)]
    expert_w = [lax.all_gather(u, "ctx", axis=0, tiled=True) for u in own_w]

    x_wide = x_all.astype(f32)
    inverse_one = inverse_rms(x_wide)
    hidden_one = (x_wide * inverse_one * gain_attn).astype(bf16)
    linear = dot(hidden_one, weights)
    query_lin, key_lin = linear[:, :cols], linear[:, cols : 2 * cols]
    value = linear[:, 2 * cols :].astype(bf16)
    squares = jnp.stack(
        [jnp.sum(query_lin * query_lin, axis=1), jnp.sum(key_lin * key_lin, axis=1)]
    )
    squares = many_sum("ctx", 6, squares)
    inverse_qk = lax.rsqrt(squares / width + norm_eps)
    inverse_q, inverse_k = inverse_qk[0][:, None], inverse_qk[1][:, None]
    cosine, sine = rope_tables(count)
    query_n, key_n = query_lin * inverse_q, key_lin * inverse_k
    query = rotate(query_n * gain_query, cosine, sine).astype(bf16)
    key = rotate(key_n * gain_key, cosine, sine).astype(bf16)
    mixed, log_total, peaks = attend_forward(query, key, value, docs)
    x_f = x_own.astype(f32)
    (mixed_own,) = exchange(2, mixed, False)
    after = x_f + dot(mixed_own, out_w)
    inverse_two = inverse_rms(after)
    normed_two = after * inverse_two
    hidden_two = (normed_two * gain_ffn).astype(bf16)

    hidden_all, peaks = gather("shard", 3, hidden_two, peaks)
    hidden_all = hidden_all.reshape(n_shard * rows, width)
    peaks = jnp.max(peaks, axis=0)[:, 0, 0]
    logits = dot(hidden_all, router_w)
    named = jnp.any(routes_all[:, :, None] == jnp.arange(experts)[None, None, :], axis=1)
    probs = jax.nn.softmax(logits, axis=1)
    selected = jnp.where(named, probs, 0.0)
    selected_sum = jnp.sum(selected, axis=1, keepdims=True)
    gates = selected / selected_sum
    gates_own = lax.dynamic_slice_in_dim(gates, shard * local, local, 1)
    named_own = lax.dynamic_slice_in_dim(named, shard * local, local, 1)
    moe_part = jnp.zeros(hidden_all.shape, f32)
    back_part = jnp.zeros(hidden_all.shape, f32)

    grad_wide = grad_all.astype(f32)
    def to_owners(parts):
        return [lax.psum_scatter(u, "ctx", scatter_dimension=0, tiled=True) for u in parts]

    grad_gates, expert_grads = [], []
    for e in range(local):
        wide, down = expert_w[e][:, : 2 * ff], expert_w[e][:, 2 * ff :]
        gate_col = gates_own[:, e : e + 1]
        hidden = dot(hidden_all, wide)
        gate_h, up_h = hidden[:, :ff], hidden[:, ff:]
        sig = jax.nn.sigmoid(gate_h)
        silu = gate_h * sig
        act = (silu * up_h).astype(bf16)
        result = contract_cols(act, down).astype(bf16).astype(f32)
        moe_part = moe_part + gate_col * result
        along = jnp.sum(grad_wide * result, axis=1)
        grad_gates.append(jnp.where(named_own[:, e], along, 0.0))
        grad_y = (gate_col * grad_wide).astype(bf16)
        grad_act = dot(grad_y, down)
        grad_h = jnp.concatenate(
            [grad_act * up_h * sig * (1.0 + gate_h * (1.0 - sig)), grad_act * silu], axis=1
        ).astype(bf16)
        back_part = back_part + contract_cols(grad_h, wide).astype(bf16).astype(f32)
        grad_w = [
            contract_rows(hidden_all, grad_h).astype(bf16),
            contract_rows(grad_y, act).astype(bf16),
        ]
        hidden_all, back_part, grad_w = lax.optimization_barrier((hidden_all, back_part, grad_w))
        expert_grads.append(grad_w)
    early = local // 2
    expert_grads[:early] = [to_owners(grad_w) for grad_w in expert_grads[:early]]
    slots = jnp.stack(grad_gates).reshape(local, n_shard, rows).transpose(1, 0, 2)
    grad_gates = lax.dynamic_update_slice_in_dim(
        jnp.zeros((n_shard, experts, rows), f32), slots, shard * local, 1
    )
    back_sum, grad_gates = reduce(
        "shard", 4, back_part.astype(bf16).reshape(n_shard, rows, width), grad_gates
    )
    grad_gates = grad_gates.T

    def own_rows(u):
        return lax.dynamic_slice_in_dim(u, shard * rows, rows, 0)

    gates_t, probs_t, named_t, sum_t = map(own_rows, (gates, probs, named, selected_sum))
    grad_selected = (
        grad_gates - jnp.sum(gates_t * grad_gates, axis=1, keepdims=True)
    ) / sum_t
    grad_probs = jnp.where(named_t, grad_selected, 0.0)
    grad_logits = (
        probs_t * (grad_probs - jnp.sum(probs_t * grad_probs, axis=1, keepdims=True))
    ).astype(bf16)
    grad_router = contract_rows(hidden_two, grad_logits)
    grad_hidden = back_sum + contract_cols(grad_logits, router_w)
    grad_gain_ffn = jnp.sum(grad_hidden * normed_two, axis=0)
    scaled_two = grad_hidden * gain_ffn
    grad_after = grad_own.astype(f32) + inverse_two * (
        scaled_two - normed_two * jnp.mean(scaled_two * normed_two, axis=1, keepdims=True)
    )

    grad_attn_own = grad_after.astype(bf16)
    to_gather, expert_grads[0] = lax.optimization_barrier((grad_attn_own, expert_grads[0]))
    grad_attn = lax.all_gather(to_gather, "ctx", axis=0, tiled=True)
    (grad_mixed,) = exchange(5, contract_cols(grad_attn_own, out_w).astype(bf16), True)
    grad_query_rot, grad_key_rot, grad_value = attend_backward(
        query, key, value, docs, log_total, grad_mixed
    )
    grad_query_n = rotate(grad_query_rot, cosine, -sine)
    grad_key_n = rotate(grad_key_rot, cosine, -sine)
    grad_gain_query = jnp.sum(grad_query_n * query_n, axis=0)
    grad_gain_key = jnp.sum(grad_key_n * key_n, axis=0)
    scaled_q, scaled_k = grad_query_n * gain_query, grad_key_n * gain_key
    peak_row = lax.dynamic_update_slice_in_dim(jnp.zeros((count,), f32), peaks, ctx * heads, 0)
    inner = jnp.stack(
        [jnp.sum(scaled_q * query_n, axis=1), jnp.sum(scaled_k * key_n, axis=1), peak_row]
    )
    inner = many_sum("ctx", 7, inner)
    grad_out_w = contract_rows(mixed, grad_attn)
    peak_all = inner[2, :HEADS]
    inner = inner / width
    grad_linear = jnp.concatenate(
        [
            inverse_q * (scaled_q - query_n * inner[0][:, None]),
            inverse_k * (scaled_k - key_n * inner[1][:, None]),
            grad_value,
        ],
        axis=1,
    ).astype(bf16)
    grad_weights = contract_rows(hidden_one, grad_linear)
    hidden_part = contract_cols(grad_linear, weights)
    grad_gain_attn = jnp.sum(hidden_part * (x_wide * inverse_one), axis=0)
    grad_small = jnp.concatenate(
        [jnp.stack([grad_gain_attn, grad_gain_ffn], axis=1), grad_router], axis=1
    )
    grad_small = jnp.pad(grad_small, ((0, 0), (0, LANES - 2 - experts)))
    grad_weights = (
        jnp.concatenate([grad_weights, grad_small], axis=1)
        .astype(bf16)
        .reshape(n_ctx, n_shard, part, 3 * cols + LANES)
        .transpose(1, 0, 2, 3)
        .reshape(n_shard, n_ctx * part, 3 * cols + LANES)
    )
    grad_gain_qk = jnp.pad(
        jnp.stack([grad_gain_query, grad_gain_key], axis=1), ((0, 0), (0, LANES - 2))
    )
    grad_out_w = (
        jnp.concatenate([grad_out_w, grad_gain_qk], axis=1)
        .astype(bf16)
        .reshape(n_shard, part, width + LANES)
    )
    hidden_part = hidden_part.astype(bf16).reshape(n_ctx, rows, width)
    grad_hidden_one, grad_weights, grad_out_w, moe_sum = end_call(
        8,
        hidden_part,
        grad_weights,
        grad_out_w,
        moe_part.astype(bf16).reshape(n_shard, rows, width),
    )
    output = (after + moe_sum).astype(bf16)
    last = grad_hidden_one
    for e in range(early, local):
        last, grad_w = lax.optimization_barrier((last, expert_grads[e]))
        expert_grads[e] = list(line_reduce(9, *(u.reshape(n_ctx, width // n_ctx, -1) for u in grad_w)))
        last = expert_grads[e][0]
    grad_hidden_one, expert_grads = lax.optimization_barrier((grad_hidden_one, expert_grads))
    wide_grads = jnp.stack([wide.astype(f32) for wide, _ in expert_grads])
    down_grads = jnp.stack([down.astype(f32) for _, down in expert_grads])
    grad_weights = grad_weights.astype(f32)
    grad_small = jnp.sum(grad_weights[..., 3 * cols :], axis=0)
    grad_weights = (
        grad_weights[..., : 3 * cols]
        .reshape(n_ctx, part, 3, cols)
        .transpose(2, 1, 0, 3)
        .reshape(3, part, width)
    )
    inverse_own = inverse_rms(x_f)
    normed_own = x_f * inverse_own
    scaled_one = grad_hidden_one * gain_attn
    grad_inputs = grad_after + inverse_own * (
        scaled_one - normed_own * jnp.mean(scaled_one * normed_own, axis=1, keepdims=True)
    )

    factors = jnp.sqrt(clip_threshold / jnp.maximum(peak_all, clip_threshold))
    col_scale = jnp.repeat(factors, HEAD)
    query_clipped = (w_query.astype(f32) * col_scale[None, :]).astype(bf16)
    key_clipped = (w_key.astype(f32) * col_scale[None, :]).astype(bf16)
    return (
        output[None],
        grad_inputs[None],
        grad_small[:, 0],
        grad_weights[0],
        grad_weights[1],
        grad_weights[2],
        grad_out_w[:, width],
        grad_out_w[:, width + 1],
        grad_out_w[:, :width],
        grad_small[:, 1],
        grad_small[:, 2 : 2 + experts],
        wide_grads[..., :ff],
        wide_grads[..., ff:],
        down_grads.transpose(0, 2, 1),
        query_clipped,
        key_clipped,
        factors,
    )


def solution(mesh):
    both = ("ctx", "shard")
    return jax.shard_map(
        per_device,
        mesh=mesh,
        in_specs=(
            P("shard", "ctx", None),
            P("shard", "ctx"),
            P("shard", "ctx", None),
            P(both),
            P(both, None),
            P(both, None),
            P(both, None),
            P(both),
            P(both),
            P(both, None),
            P(both),
            P(both, None),
            P("shard", "ctx", None),
            P("shard", "ctx", None),
            P("shard", None, "ctx"),
            P(),
            P("shard", "ctx", None),
        ),
        out_specs=(
            P("shard", "ctx", None),
            P("shard", "ctx", None),
            P(both),
            P(both, None),
            P(both, None),
            P(both, None),
            P(both),
            P(both),
            P(both, None),
            P(both),
            P(both, None),
            P("shard", "ctx", None),
            P("shard", "ctx", None),
            P("shard", None, "ctx"),
            P(both, None),
            P(both, None),
            P(),
        ),
        check_vma=False,
    )
```
